32 devices in a mesh: dp: 16 (over z, x, core), tensor: 2 (over y).
Axes of the slice: x: 2, y: 2, z: 4, core: 2. Of those that a mesh axis runs over, the one named last changes fastest.
Arguments:
- inputs: bfloat16 [5120, 2048], P('dp'), may hold values from -6 to 6
- attn_gain: bfloat16 [2048], P('dp'), may hold values from 0.5 to 1.5
- w_query: bfloat16 [2048, 2048], P('dp', 'tensor'), may hold values from -0.125 to 0.125
- w_key: bfloat16 [2048, 2048], P('dp', 'tensor'), may hold values from -0.125 to 0.125
- w_value: bfloat16 [2048, 2048], P('dp', 'tensor'), may hold values from -0.125 to 0.125
- query_gain: bfloat16 [2048], P('dp'), may hold values from 0.796875 to 2
- key_gain: bfloat16 [2048], P('dp'), may hold values from 0.59765625 to 1.3984375
- w_out: bfloat16 [2048, 2048], P('tensor', 'dp'), may hold values from -0.75 to 0.75
- moe_gain: bfloat16 [2048], P('dp'), may hold values from 0.5 to 1.5
- w_gate: bfloat16 [16, 2048, 1024], P('dp', None, 'tensor'), may hold values from -0.125 to 0.125
- w_up: bfloat16 [16, 2048, 1024], P('dp', None, 'tensor'), may hold values from -0.125 to 0.125
- w_down: bfloat16 [16, 1024, 2048], P('dp', 'tensor'), may hold values from -0.1875 to 0.1875
- experts: int32 [5120, 8], P('dp'), may hold values from 0 to 15, all different within a row; in each aligned block of 320 rows (0 to 319, 320 to 639, ...) at most 288 rows name the same one
- gates: float32 [5120, 8], P('dp'), may hold values from 0.25 to 1
- segments: int32 [16, 192], P('dp'), may hold values from 0 to 1, never falling along the last dimension, each value on 1 to 128 neighbouring positions
- gaps: int32 [16, 2], P('dp'), may hold values from 0 to 512
- cotangent: float32 [5120, 2048], P('dp'), may hold values from -6 to 6
Outputs:
- output: float32 [5120, 2048], P('dp')
- input_grad: float32 [5120, 2048], P('dp')
- attn_gain_grad: float32 [2048], P('dp')
- w_query_grad: float32 [2048, 2048], P('dp', 'tensor')
- w_key_grad: float32 [2048, 2048], P('dp', 'tensor')
- w_value_grad: float32 [2048, 2048], P('dp', 'tensor')
- query_gain_grad: float32 [2048], P('dp')
- key_gain_grad: float32 [2048], P('dp')
- w_out_grad: float32 [2048, 2048], P('tensor', 'dp')
- moe_gain_grad: float32 [2048], P('dp')
- w_gate_grad: float32 [16, 2048, 1024], P('dp', None, 'tensor')
- w_up_grad: float32 [16, 2048, 1024], P('dp', None, 'tensor')
- w_down_grad: float32 [16, 1024, 2048], P('dp', 'tensor')
The draws below stay inside these ranges and needn't reach their ends.
Inputs may be any that keep to these rules, and one draw needn't show every extreme that they name: Each row names 8 different experts. In the rows of one dp index at most 288 name the same expert, and some dp index reaches 288. `segments`: in each row the numbers never fall; each continuation has 1 to 128 tokens.
All inputs are finite; a program needn't handle non-finite values.
Results may differ from the reference program's by a relative error of at most 0.018.
Values may be sent and summed in bfloat16 or wider, within the bound.
No kernel may reach another device: no remote copies, remote signals or barrier semaphores. Data moves between devices by JAX's collectives and lax.ppermute only.
A program may use at most 384 MiB of HBM per device.

```python
import math
import jax
import jax.numpy as jnp
import numpy as np
from jax import lax

D = 2048
HEADS = 16
HEAD = 128
FF = 1024
TOP = 8
GROUP = 8
PR_DEV = 128
CLEN = 128
CONT_ROWS = 192
SEGS = 2
GAP = 512
TOK_DEV = 320
TOKENS = 5120
EXPERTS = 16
SLOTS = 288
CAP = 2880
N_DP = 16
N_TENSOR = 2


def place_ends(values, key, smallest, largest):
    shape = values.shape
    place = [jax.random.randint(jax.random.fold_in(key, axis), (), 0, shape[axis]) for axis in range(len(shape))]
    values = values.at[tuple(place)].set(smallest)
    longest = shape.index(max(shape))
    place[longest] = (place[longest] + 1) % shape[longest]
    return values.at[tuple(place)].set(largest)


def shard_levels(key, shape, pieces, least, top_value):
    factor_of, own = 1.0, jax.random.fold_in(key, 6)
    for dim, shards_of in pieces:
        steps = jnp.exp(jax.random.uniform(jax.random.fold_in(own, dim), (shards_of,), jnp.float32, least / len(pieces), top_value / len(pieces)))
        factor_of = factor_of * jnp.repeat(steps, shape[dim] // shards_of).reshape([-1 if axis == dim else 1 for axis in range(len(shape))])
    return factor_of


def profile(number_of, total, limit, skew):
    weights = [(1 << 20) // math.isqrt(rank ** skew) + 1 for rank in range(2, number_of + 1)]
    surplus, holding = total - limit - (number_of - 1), [1] * (number_of - 1)
    while surplus > 0:
        movable = [i for i in range(number_of - 1) if holding[i] < limit]
        pool, left = sum([weights[i] for i in movable]), surplus
        for i in movable:
            more = min(limit - holding[i], max(1, left * weights[i] // pool), surplus)
            holding[i] = holding[i] + more
            surplus = surplus - more
    return np.array([limit] + holding)


def ragged_sizes(key, amount, total, reach, skew):
    if amount == 2:
        one = jax.random.randint(key, (), max(1, total - reach), min(reach, total - 1) + 1)
        return jnp.stack([one, total - one])
    sizes = jnp.asarray(profile(amount, total, reach, skew), jnp.int32)
    pairs = (amount - 1) // 2
    giver, taker = sizes[1:1 + 2 * pairs:2], sizes[2:2 + 2 * pairs:2]
    room = jnp.minimum(giver - 1, reach - taker)
    moved = jax.random.randint(jax.random.fold_in(key, 1), (pairs,), 0, 1 << 20) % (room + 1)
    sizes = sizes.at[1:1 + 2 * pairs:2].set(giver - moved).at[2:2 + 2 * pairs:2].set(taker + moved)
    return sizes[jax.random.permutation(jax.random.fold_in(key, 2), amount)]


def assign_block(own_key, own, number, rows, number_of, top, most, slope):
    ranking = jax.random.permutation(own_key, number_of)
    crowded, ordinary = shares(number_of, rows * top, most, slope, True), shares(number_of, rows * top, most, slope, False)
    places = jnp.arange(number_of)

    def named(sizes, offset_by):
        used = int((sizes > 0).sum())
        fixed = max(1, used // 4)
        passed = fixed + (places - fixed + offset_by * (used - fixed)) % max(1, number_of - fixed)
        return jnp.zeros((number_of,), jnp.int32).at[ranking[jnp.where(places < fixed, places, passed)]].set(jnp.asarray(sizes, jnp.int32))

    sizes = jnp.where(number % 4 == 0, named(crowded, number // 4), named(ordinary, number - number // 4 - 1))
    mixed = jax.random.permutation(jax.random.fold_in(own, 3), number_of)
    giver, sink = mixed[0:number_of // 2 * 2:2], mixed[1:number_of // 2 * 2:2]
    margin = jnp.minimum(sizes[giver] - 1, most - sizes[sink]) // 2
    margin = jnp.where((giver == ranking[0]) | (sink == ranking[0]) | (sizes[sink] == 0), 0, jnp.maximum(margin, 0))
    passed = jax.random.randint(jax.random.fold_in(own, 4), (number_of // 2,), 0, 1 << 20) % (margin + 1)
    sizes = sizes.at[giver].add(-passed).at[sink].add(passed)
    members = jnp.searchsorted(jnp.cumsum(sizes), jnp.arange(rows * top), side="right").astype(jnp.int32)
    listing = members.reshape(top, rows).T
    listing = listing[jax.random.permutation(jax.random.fold_in(own, 1), rows)]
    offset_by = jax.random.randint(jax.random.fold_in(own, 2), (rows, 1), 0, top)
    return jnp.take_along_axis(listing, (jnp.arange(top)[None, :] + offset_by) % top, axis=1)


def shares(amount, total, most, lean, full):
    loads = [(1 << 20) // math.isqrt(grade ** lean) + 1 for grade in range(1, amount + 1)]
    largest = most if full else min(most, max(-(-total // amount), total * loads[0] // sum(loads)))
    least = 1 if total - largest >= amount - 1 else 0
    counts, rest = [largest] + [least] * (amount - 1), total - largest - least * (amount - 1)
    while rest > 0:
        candidates = [i for i in range(1, amount) if counts[i] < largest] or [i for i in range(1, amount) if counts[i] < most]
        whole, left = sum([loads[i] for i in candidates]), rest
        for i in candidates:
            addition = min(most - counts[i], max(1, left * loads[i] // whole), rest)
            counts[i] = counts[i] + addition
            rest = rest - addition
    return np.array(counts)


def normal_values(rng, dims, width, limit, pieces=(), kind=jnp.bfloat16):
    loudness = shard_levels(rng, dims, pieces, -0.22, 0.18) if pieces else 1.0
    values = jax.random.normal(rng, dims, jnp.float32) * width * loudness
    return jnp.minimum(jnp.maximum(values, -limit), limit).astype(kind)


def setup_inputs(seed: int = 0) -> dict:
    key_list = jax.random.split(jax.random.key(seed), 18)
    inputs = normal_values(key_list[0], (TOKENS, D), 1.0, 6.0, ((0, 16),))
    attn_gain = jnp.clip(1.0 + 0.1 * jax.random.normal(key_list[1], (D,), jnp.float32), 0.5, 1.5).astype(jnp.bfloat16)
    w_query = normal_values(key_list[2], (D, HEADS * HEAD), D ** -0.5, 0.125, ((0, 16), (1, 2)))
    w_key = normal_values(key_list[3], (D, HEADS * HEAD), D ** -0.5, 0.125, ((0, 16), (1, 2)))
    w_value = normal_values(key_list[4], (D, HEADS * HEAD), D ** -0.5, 0.125, ((0, 16), (1, 2)))
    query_gain = jnp.clip(0.796875 + 1.203125 * jax.random.uniform(key_list[5], (HEADS * HEAD,), jnp.float32) ** shard_levels(key_list[5], (HEADS * HEAD,), ((0, 16),), -0.2, 0.2), 0.796875, 2.0).astype(jnp.bfloat16)
    key_gain = jnp.clip(0.59765625 + 0.80078125 * jax.random.uniform(key_list[6], (HEADS * HEAD,), jnp.float32) ** shard_levels(key_list[6], (HEADS * HEAD,), ((0, 16),), -0.2, 0.2), 0.59765625, 1.3984375).astype(jnp.bfloat16)
    w_out = normal_values(key_list[7], (HEADS * HEAD, D), (HEADS * HEAD // 32) ** -0.5, 0.75, ((0, 2), (1, 16)))
    moe_gain = jnp.clip(1.0 + 0.1 * jax.random.normal(key_list[8], (D,), jnp.float32), 0.5, 1.5).astype(jnp.bfloat16)
    w_gate = normal_values(key_list[9], (EXPERTS, D, FF), D ** -0.5, 0.125, ((0, 16), (2, 2)))
    w_up = normal_values(key_list[10], (EXPERTS, D, FF), D ** -0.5, 0.125, ((0, 16), (2, 2)))
    w_down = normal_values(key_list[11], (EXPERTS, FF, D), FF ** -0.5, 0.1875, ((0, 16), (1, 2)))
    experts_keys = jax.random.split(jax.random.fold_in(key_list[12], 1), TOKENS // TOK_DEV)
    experts_turns = jax.random.permutation(jax.random.fold_in(key_list[12], 3), TOKENS // TOK_DEV)
    experts = jax.vmap(lambda own, number: assign_block(jax.random.fold_in(key_list[12], 2), own, number, TOK_DEV, EXPERTS, TOP, SLOTS, 2))(experts_keys, experts_turns).reshape((TOKENS, TOP))
    gates = jnp.clip(jnp.exp(math.log(1.0) - 1.3862944 * jax.random.uniform(key_list[13], (TOKENS, TOP), jnp.float32) ** shard_levels(key_list[13], (TOKENS, TOP), ((0, 16),), -0.2, 0.2)), 0.25, 1.0)
    segments = jax.vmap(lambda own: jnp.searchsorted(jnp.cumsum(ragged_sizes(own, SEGS, CONT_ROWS, CLEN, 0)), jnp.arange(CONT_ROWS), side="right"))(jax.random.split(key_list[14], N_DP)).reshape((N_DP, CONT_ROWS)).astype(jnp.int32)
    gaps = place_ends(jax.random.randint(key_list[15], (N_DP, SEGS), 0, GAP + 1), jax.random.fold_in(key_list[15], 1), 0, GAP).astype(jnp.int32)
    cotangent = normal_values(key_list[16], (TOKENS, D), 1.0, 6.0, ((0, 16),), jnp.float32)
    return dict(inputs=inputs, attn_gain=attn_gain, w_query=w_query, w_key=w_key, w_value=w_value, query_gain=query_gain, key_gain=key_gain, w_out=w_out, moe_gain=moe_gain, w_gate=w_gate, w_up=w_up, w_down=w_down, experts=experts, gates=gates, segments=segments, gaps=gaps, cotangent=cotangent)


@jax.custom_vjp
def low(v):
    return lax.optimization_barrier(v.astype(jnp.bfloat16)).astype(jnp.float32)

@jax.custom_vjp
def low_back(v):
    return v

def low_keep(v):
    return (low(v), None)

def low_pass(kept, grad):
    return (grad,)

def back_keep(v):
    return (v, None)

def back_low(kept, grad):
    return (low(grad),)
low.defvjp(low_keep, low_pass)
low_back.defvjp(back_keep, back_low)
EPSILON = 1e-05
HIGHEST = lax.Precision.HIGHEST

def rms_norm(values, gain):
    return values * lax.rsqrt(lax.optimization_barrier(jnp.mean(values * values, axis=-1, keepdims=True)) + EPSILON) * gain

def rope_tables(positions, head_size):
    half_size = head_size // 2
    inverse = 10000.0 ** (-(jnp.arange(half_size, dtype=jnp.float32) * 2.0) / head_size)
    angles = positions.astype(jnp.float32)[:, None] * inverse[None, :]
    cosine = jnp.concatenate([jnp.cos(angles), jnp.cos(angles)], axis=-1)
    sine = jnp.concatenate([jnp.sin(angles), jnp.sin(angles)], axis=-1)
    return (cosine, sine)

def rotate(values, cosine, sine):
    half_size = values.shape[-1] // 2
    turned = jnp.concatenate([-values[..., half_size:], values[..., :half_size]], axis=-1)
    return values * cosine[:, None, :] + turned * sine[:, None, :]

def cont_positions(segment_row, gap_row, prompt_length):
    order = jnp.arange(segment_row.shape[0], dtype=jnp.int32)
    same = segment_row[:, None] == segment_row[None, :]
    earlier = order[None, :] < order[:, None]
    offset = lax.optimization_barrier(jnp.sum((same & earlier).astype(jnp.int32), axis=1))
    labels = jnp.arange(gap_row.shape[0], dtype=jnp.int32)
    shifted = lax.optimization_barrier(jnp.sum(jnp.where(segment_row[:, None] == labels[None, :], gap_row[None, :], 0), axis=1))
    return (prompt_length + shifted + offset).astype(jnp.int32)

def attend_group(block):
    query, keyset, valueset, position, segment, device = block
    prompt_side = segment < 0
    allowed_prompt = (~prompt_side)[:, None] | (position[None, :] <= position[:, None])
    allowed_cont = (~prompt_side)[:, None] & (device[:, None] == device[None, :]) & (segment[:, None] == segment[None, :]) & (position[None, :] <= position[:, None])
    allowed = jnp.where(prompt_side[None, :], allowed_prompt, allowed_cont)
    scores = jnp.einsum('qhd,khd->hqk', query, keyset, precision=HIGHEST) * HEAD ** (-0.5)
    scores = low_back(scores)
    scores = jnp.where(allowed[None], scores, -1e+30)
    peak = lax.optimization_barrier(jnp.max(scores, axis=-1, keepdims=True))
    weights = jnp.exp(scores - peak)
    weights = weights / lax.optimization_barrier(jnp.sum(weights, axis=-1, keepdims=True))
    weights = low(weights)
    return jnp.einsum('hqk,khd->qhd', weights, valueset, precision=HIGHEST)

def expert_rows(padded, gate_mat, up_mat, down_mat, row_index):
    chosen = padded[row_index]
    half_width = gate_mat.shape[1] // N_TENSOR
    total = jnp.zeros((row_index.shape[0], padded.shape[1]), jnp.float32)
    for half_index in range(N_TENSOR):
        begin_col = half_index * half_width
        end_col = begin_col + half_width
        rows_in = low_back(chosen)
        gate_val = low_back(jnp.dot(rows_in, gate_mat[:, begin_col:end_col], precision=HIGHEST))
        up_val = low_back(jnp.dot(rows_in, up_mat[:, begin_col:end_col], precision=HIGHEST))
        hidden = low(jax.nn.silu(gate_val) * up_val)
        total = total + low(jnp.dot(hidden, down_mat[begin_col:end_col], precision=HIGHEST))
    return low_back(total)

def reference(inputs, attn_gain, w_query, w_key, w_value, query_gain, key_gain, w_out, moe_gain, w_gate, w_up, w_down, experts, gates, segments, gaps, cotangent):
    device_ids = jnp.arange(N_DP, dtype=jnp.int32)
    prompt_pos = ((device_ids % GROUP)[:, None] * PR_DEV + jnp.arange(PR_DEV, dtype=jnp.int32)[None, :]).astype(jnp.int32)
    later_pos = jax.vmap(lambda seg_row, gap_row: cont_positions(seg_row, gap_row, PR_DEV * GROUP))(segments, gaps)
    positions = jnp.concatenate([prompt_pos, later_pos], axis=1).reshape(-1)
    segment_all = jnp.concatenate([jnp.full((N_DP, PR_DEV), -1, jnp.int32), segments], axis=1).reshape(-1)
    device_all = jnp.repeat(device_ids, TOK_DEV)
    cosine, sine = rope_tables(positions, HEAD)
    flat_experts = experts.reshape(-1).astype(jnp.int32)
    onehot = (flat_experts[:, None] == jnp.arange(EXPERTS, dtype=jnp.int32)[None, :]).astype(jnp.int32)
    before = jnp.cumsum(onehot, axis=0) - onehot
    slot = lax.optimization_barrier(jnp.sum(before * onehot, axis=1))
    kept = slot < CAP
    slot_or_out = jnp.where(kept, slot, CAP).astype(jnp.int32)
    token_of_pair = (jnp.arange(TOKENS * TOP, dtype=jnp.int32) // TOP).astype(jnp.int32)
    table = jnp.full((EXPERTS, CAP), TOKENS, jnp.int32).at[flat_experts, slot_or_out].set(token_of_pair, mode='drop')
    gate_table = jnp.zeros((EXPERTS, CAP), jnp.float32).at[flat_experts, slot_or_out].set(gates.reshape(-1).astype(jnp.float32), mode='drop')
    group_count = N_DP // GROUP
    group_rows = GROUP * TOK_DEV

    def grouped(array):
        return array.reshape((group_count, group_rows) + array.shape[1:])

    def forward(tokens_in, gain_attn, query_w, key_w, value_w, gain_query, gain_key, out_w, gain_moe, gate_w, up_w, down_w):
        normed = low(rms_norm(tokens_in, gain_attn))
        query_flat = low_back(jnp.dot(normed, query_w, precision=HIGHEST))
        key_flat = low_back(jnp.dot(normed, key_w, precision=HIGHEST))
        query_pre = rms_norm(query_flat, gain_query).reshape(TOKENS, HEADS, HEAD)
        key_pre = rms_norm(key_flat, gain_key).reshape(TOKENS, HEADS, HEAD)
        queries = low(rotate(query_pre, cosine, sine))
        keyset = low(rotate(key_pre, cosine, sine))
        valueset = low(low_back(jnp.dot(normed, value_w, precision=HIGHEST))).reshape(TOKENS, HEADS, HEAD)
        context = lax.map(jax.checkpoint(attend_group), (grouped(queries), grouped(keyset), grouped(valueset), grouped(positions), grouped(segment_all), grouped(device_all)))
        context = low_back(low(context.reshape(TOKENS, HEADS * HEAD)))
        attn = low_back(jnp.dot(context, out_w, precision=HIGHEST))
        hidden_state = tokens_in + attn
        normed_two = low(rms_norm(hidden_state, gain_moe))
        padded = jnp.concatenate([normed_two, jnp.zeros((1, D), jnp.float32)], axis=0)

        def expert_step(carry, item):
            gate_mat, up_mat, down_mat, row_index, row_gate = item
            result = jax.checkpoint(expert_rows)(padded, gate_mat, up_mat, down_mat, row_index)
            return (carry.at[row_index].add(row_gate[:, None] * result), None)
        mixed, unused = lax.scan(expert_step, jnp.zeros((TOKENS + 1, D), jnp.float32), (gate_w, up_w, down_w, table, gate_table))
        return hidden_state + mixed[:TOKENS]
    floats = (inputs.astype(jnp.float32), attn_gain.astype(jnp.float32), w_query.astype(jnp.float32), w_key.astype(jnp.float32), w_value.astype(jnp.float32), query_gain.astype(jnp.float32), key_gain.astype(jnp.float32), w_out.astype(jnp.float32), moe_gain.astype(jnp.float32), w_gate.astype(jnp.float32), w_up.astype(jnp.float32), w_down.astype(jnp.float32))
    output, backward = jax.vjp(forward, *floats)
    grads = backward(cotangent.astype(jnp.float32))
    return (output, grads[0], grads[1], grads[2], grads[3], grads[4], grads[5], grads[6], grads[7], grads[8], grads[9], grads[10], grads[11])
```

```python
import jax
import jax.numpy as jnp
from jax import lax
from jax.experimental import pallas as pl
from jax.experimental.pallas import tpu as pltpu
from jax.sharding import PartitionSpec as P

HEADS = 16
HEAD = 128
GROUP = 8
PR_DEV = 128


EPSILON = 1e-05
LOW = jnp.bfloat16
FULL = jnp.float32


def swap_bit(block, axis, bit):
    count = lax.axis_size(axis)
    return lax.ppermute(block, axis, [(i, i ^ (1 << bit)) for i in range(count)])


def swap_tensor(block):
    return lax.ppermute(block, "tensor", [(0, 1), (1, 0)])


def rms_norm(values, gain):
    return values * lax.rsqrt(jnp.mean(values * values, axis=-1, keepdims=True) + EPSILON) * gain


def rope_tables(positions, head_size):
    half_size = head_size // 2
    inverse = 10000.0 ** (-(jnp.arange(half_size, dtype=FULL) * 2.0) / head_size)
    angles = positions.astype(FULL)[:, None] * inverse[None, :]
    cosine = jnp.concatenate([jnp.cos(angles), jnp.cos(angles)], axis=-1)
    sine = jnp.concatenate([jnp.sin(angles), jnp.sin(angles)], axis=-1)
    return (cosine, sine)


def rotate(values, cosine, sine):
    half_size = values.shape[-1] // 2
    turned = jnp.concatenate([-values[..., half_size:], values[..., :half_size]], axis=-1)
    return values * cosine[:, None, :] + turned * sine[:, None, :]


def rotate_back(values, cosine, sine):
    half_size = values.shape[-1] // 2
    scaled = values * sine[:, None, :]
    turned = jnp.concatenate([scaled[..., half_size:], -scaled[..., :half_size]], axis=-1)
    return values * cosine[:, None, :] + turned


def cont_positions(segment_row, gap_row, prompt_length):
    order = jnp.arange(segment_row.shape[0], dtype=jnp.int32)
    same = segment_row[:, None] == segment_row[None, :]
    earlier = order[None, :] < order[:, None]
    offset = jnp.sum((same & earlier).astype(jnp.int32), axis=1)
    labels = jnp.arange(gap_row.shape[0], dtype=jnp.int32)
    shifted = jnp.sum(
        jnp.where(segment_row[:, None] == labels[None, :], gap_row[None, :], 0), axis=1
    )
    return prompt_length + shifted + offset


def dot_nn(left, right):
    return jnp.dot(left, right, preferred_element_type=FULL)


def dot_tn(left, right):
    return lax.dot_general(left, right, (((0,), (0,)), ((), ())), preferred_element_type=FULL)


def dot_nt(left, right):
    return lax.dot_general(left, right, (((1,), (1,)), ((), ())), preferred_element_type=FULL)


def collect_prompt(keys, values):
    own = jnp.stack([keys, values], axis=0)
    near = swap_bit(own, "dp", 1)
    far = swap_bit(own, "dp", 2)
    last_keys = swap_bit(far[0], "dp", 1)
    last_values = swap_bit(near[1], "dp", 2)
    blocks = [None] * GROUP
    for at, piece in ((0, own), (2, near), (4, far)):
        blocks[at] = piece
        blocks[at + 1] = swap_bit(piece, "dp", 0)
    last = jnp.stack([last_keys, last_values], axis=0)
    blocks[6] = last
    blocks[7] = swap_bit(last, "dp", 0)
    return [b[0] for b in blocks], [b[1] for b in blocks]


def return_prompt(grads, order):
    parts = {j: grads[j] for j in range(GROUP)}
    for bit in order:
        gone = [j for j in sorted(parts) if j >> bit & 1]
        sent = jnp.stack([parts[j] for j in gone], axis=0).astype(LOW)
        got = swap_bit(sent, "dp", bit)
        for at, j in enumerate(gone):
            stay = j ^ (1 << bit)
            parts[stay] = parts[stay] + got[at].astype(FULL)
            del parts[j]
    return parts[0]


def masked_scores(queries, keyset, allowed):
    scores = jnp.einsum("qhd,khd->hqk", queries, keyset, preferred_element_type=FULL) * HEAD ** (
        -0.5
    )
    return jnp.where(allowed[None], scores, -1e30)


def expert_kernel(
    rows_ref, back_ref, gate_ref, wg0, wg1, wu0, wu1, wd0, wd1, grad_ref, h0, h1, g0, g1, u0, u1
):
    rows = rows_ref[...]
    back = back_ref[...]
    gate = gate_ref[...]
    total = None
    for wg, wu, wd, h, g, u in ((wg0, wu0, wd0, h0, g0, u0), (wg1, wu1, wd1, h1, g1, u1)):
        gate_pre = dot_nn(rows, wg[...])
        up_pre = dot_nn(rows, wu[...])
        hidden_grad = gate * dot_nt(back, wd[...])
        sig = 1.0 / (1.0 + jnp.exp(-gate_pre))
        act = gate_pre * sig
        h[...] = (gate * (act * up_pre)).astype(LOW)
        gate_grad = (hidden_grad * up_pre * (sig * (1.0 + gate_pre * (1.0 - sig)))).astype(LOW)
        up_grad = (hidden_grad * act).astype(LOW)
        g[...] = gate_grad
        u[...] = up_grad
        part = dot_nt(gate_grad, wg[...]) + dot_nt(up_grad, wu[...])
        total = part if total is None else total + part
    grad_ref[...] = total.astype(LOW)


def expert_pass(rows, back, gate, gate_mats, up_mats, down_mats):
    count, width = rows.shape
    hidden = gate_mats[0].shape[1]
    tile = 256
    whole = lambda array: pl.BlockSpec(
        array.shape, lambda i: (0, 0), pipeline_mode=pl.Buffered(1)
    )
    tall = lambda columns: pl.BlockSpec((tile, columns), lambda i: (i, 0))
    mats = [*gate_mats, *up_mats, *down_mats]
    flops = 2 * 5 * count * width * hidden * 2
    return pl.pallas_call(
        expert_kernel,
        grid=(count // tile,),
        in_specs=[tall(width), tall(width), tall(1)] + [whole(m) for m in mats],
        out_specs=[tall(width)] + [tall(hidden)] * 6,
        out_shape=[jax.ShapeDtypeStruct((count, width), LOW)]
        + [jax.ShapeDtypeStruct((count, hidden), LOW)] * 6,
        compiler_params=pltpu.CompilerParams(vmem_limit_bytes=58 * 1024 * 1024),
        cost_estimate=pl.CostEstimate(
            flops=flops,
            bytes_accessed=2 * (3 * count * width + 6 * count * hidden + 6 * width * hidden),
            transcendentals=2 * count * hidden,
        ),
    )(rows, back, gate, *mats)


def body(
    inputs,
    attn_gain,
    w_query,
    w_key,
    w_value,
    query_gain,
    key_gain,
    w_out,
    moe_gain,
    w_gate,
    w_up,
    w_down,
    experts,
    gates,
    segments,
    gaps,
    cotangent,
):
    dp_count = lax.axis_size("dp")
    dp_index = lax.axis_index("dp")
    side = lax.axis_index("tensor")
    token_count, model_width = inputs.shape
    half_count = token_count // 2
    top_count = experts.shape[1]
    expert_count = w_gate.shape[0] * dp_count
    capacity = token_count * top_count * dp_count * 9 // (8 * expert_count)
    prompt_length = PR_DEV * GROUP
    column_total = HEADS * HEAD
    block = w_query.shape[0]
    local_width = w_query.shape[1]
    local_heads = local_width // HEAD

    def own_half(array):
        return lax.dynamic_slice_in_dim(array, side * half_count, half_count, axis=0)

    def other_half(array):
        return lax.dynamic_slice_in_dim(array, (1 - side) * half_count, half_count, axis=0)

    def both_halves(own, other):
        first = side == 0
        return jnp.concatenate(
            [jnp.where(first, own, other), jnp.where(first, other, own)], axis=0
        )

    gate_mats = (w_gate[0], swap_tensor(w_gate[0]))
    up_mats = (w_up[0], swap_tensor(w_up[0]))
    down_mats = (w_down[0], swap_tensor(w_down[0]))

    gates_high = gates.astype(LOW)
    gates_low = (gates - gates_high.astype(FULL)).astype(LOW)
    routing = jnp.concatenate([experts.astype(LOW).T, gates_high.T, gates_low.T], axis=1)
    routing = jnp.pad(routing, ((0, 0), (0, local_width - 3 * token_count)))
    gains = jnp.concatenate([attn_gain, moe_gain, query_gain, key_gain])
    gains = jnp.pad(gains[None], ((0, 7), (0, local_width - 4 * block)))
    packed = jnp.concatenate([w_query, w_key, w_value, w_out.T, gains, routing], axis=0)
    gathered = lax.all_gather(packed, "dp", axis=0, tiled=False)
    full_q = gathered[:, :block].reshape(model_width, local_width)
    full_k = gathered[:, block : 2 * block].reshape(model_width, local_width)
    full_v = gathered[:, 2 * block : 3 * block].reshape(model_width, local_width)
    full_o = gathered[:, 3 * block : 4 * block].reshape(model_width, local_width)
    gain_rows = gathered[:, 4 * block].astype(FULL)
    gain_one, gain_two, gain_q, gain_k = (
        gain_rows[:, j * block : (j + 1) * block].reshape(-1) for j in range(4)
    )
    gain_query_local = lax.dynamic_slice_in_dim(gain_q, side * local_width, local_width)
    gain_key_local = lax.dynamic_slice_in_dim(gain_k, side * local_width, local_width)

    names = gathered[:, 4 * block + 8 :, :token_count]
    weights = gathered[:, 4 * block + 8 :, token_count : 2 * token_count].astype(
        FULL
    ) + gathered[:, 4 * block + 8 :, 2 * token_count : 3 * token_count].astype(FULL)
    named = names == dp_index.astype(LOW)
    picked = jnp.sum(named.astype(FULL), axis=1)
    weight = jnp.sum(jnp.where(named, weights, 0.0), axis=1)
    order = jnp.arange(token_count, dtype=jnp.int32)
    earlier = (order[:, None] < order[None, :]).astype(LOW)
    within = dot_nn(picked.astype(LOW), earlier)
    per_row = jnp.sum(picked, axis=1)
    rows_order = jnp.arange(dp_count, dtype=jnp.int32)
    ahead = jnp.sum(
        jnp.where(rows_order[None, :] < rows_order[:, None], per_row[None, :], 0.0), axis=1
    )
    kept = (picked > 0.0) & (within + ahead[:, None] < capacity)
    weight = jnp.where(kept, weight, 0.0)
    weight = lax.dynamic_slice_in_dim(weight, side * half_count, half_count, axis=1)
    weight = weight.reshape(-1, 1)

    cotangent_half = own_half(cotangent)
    back_rows = lax.all_gather(cotangent_half.astype(LOW), "dp", axis=0, tiled=True)

    tokens_f = inputs.astype(FULL)
    prompt_pos = dp_index % GROUP * PR_DEV + jnp.arange(PR_DEV, dtype=jnp.int32)
    later_pos = cont_positions(segments[0], gaps[0], prompt_length)
    positions = jnp.concatenate([prompt_pos, later_pos], axis=0)
    cosine, sine = rope_tables(positions, HEAD)
    normed_b = rms_norm(tokens_f, gain_one).astype(LOW)
    query_flat = dot_nn(normed_b, full_q)
    key_flat = dot_nn(normed_b, full_k)
    values_b = dot_nn(normed_b, full_v).astype(LOW)
    query_sq, key_sq = lax.psum(
        (jnp.sum(query_flat * query_flat, axis=1), jnp.sum(key_flat * key_flat, axis=1)), "tensor"
    )
    query_scale = lax.rsqrt(query_sq / column_total + EPSILON)[:, None]
    key_scale = lax.rsqrt(key_sq / column_total + EPSILON)[:, None]
    by_head = (token_count, local_heads, HEAD)
    queries_b = rotate(
        (query_flat * query_scale * gain_query_local).reshape(by_head), cosine, sine
    ).astype(LOW)
    keys_b = rotate(
        (key_flat * key_scale * gain_key_local).reshape(by_head), cosine, sine
    ).astype(LOW)
    key_blocks, value_blocks = collect_prompt(
        keys_b[:PR_DEV].reshape(PR_DEV, local_width), values_b[:PR_DEV]
    )
    keyset = jnp.concatenate(
        key_blocks + [keys_b[PR_DEV:].reshape(-1, local_width)], axis=0
    ).reshape(-1, local_heads, HEAD)
    valueset = jnp.concatenate(value_blocks + [values_b[PR_DEV:]], axis=0).reshape(
        -1, local_heads, HEAD
    )
    prompt_query = jnp.arange(token_count, dtype=jnp.int32) < PR_DEV
    prompt_at = jnp.arange(prompt_length, dtype=jnp.int32)
    prompt_keypos = ((dp_index % GROUP) ^ (prompt_at // PR_DEV)) * PR_DEV + prompt_at % PR_DEV
    allowed_prompt = (~prompt_query)[:, None] | (prompt_keypos[None, :] <= positions[:, None])
    query_segment = jnp.concatenate([jnp.full((PR_DEV,), -1, jnp.int32), segments[0]], axis=0)
    allowed_cont = (query_segment[:, None] == segments[0][None, :]) & (
        later_pos[None, :] <= positions[:, None]
    )
    allowed = jnp.concatenate([allowed_prompt, allowed_cont], axis=1)
    scores = masked_scores(queries_b, keyset, allowed)
    peak = jnp.max(scores, axis=-1, keepdims=True)
    expo = jnp.exp(scores - peak)
    total = jnp.sum(expo, axis=-1, keepdims=True)
    log_total = peak + jnp.log(total)
    probs_b = (expo / total).astype(LOW)
    context = jnp.einsum("hqk,khd->qhd", probs_b, valueset, preferred_element_type=FULL)
    context_b = context.reshape(token_count, local_width).astype(LOW)
    attn_part = dot_nt(context_b, full_o)
    attn_other = swap_tensor(other_half(attn_part).astype(LOW))
    hidden_state = (
        own_half(tokens_f) + own_half(attn_part) + attn_other.astype(FULL)
    )
    normed_two_b = rms_norm(hidden_state, gain_two).astype(LOW)

    expert_in = lax.all_gather(normed_two_b, "dp", axis=0, tiled=True)
    grad_rows, h0, h1, g0, g1, u0, u1 = expert_pass(
        expert_in, back_rows, weight, gate_mats, up_mats, down_mats
    )
    normed_two_grad = lax.psum_scatter(grad_rows, "dp", scatter_dimension=0, tiled=True).astype(
        FULL
    )
    mixed_rows = (dot_nn(h0, down_mats[0]) + dot_nn(h1, down_mats[1])).astype(LOW)
    mixed = lax.psum_scatter(mixed_rows, "dp", scatter_dimension=0, tiled=True).astype(FULL)
    output_half = hidden_state + mixed
    output = both_halves(output_half, swap_tensor(output_half))
    gate_w_grad = dot_tn(expert_in, g0) + swap_tensor(
        dot_tn(expert_in, g1).astype(LOW)
    ).astype(FULL)
    up_w_grad = dot_tn(expert_in, u0) + swap_tensor(dot_tn(expert_in, u1).astype(LOW)).astype(
        FULL
    )
    down_grad = dot_tn(h0, back_rows) + swap_tensor(dot_tn(h1, back_rows).astype(LOW)).astype(
        FULL
    )

    unused_two, norm_two_back = jax.vjp(rms_norm, hidden_state, gain_two)
    state_part, gain_two_grad = norm_two_back(normed_two_grad)
    state_half = cotangent_half + state_part
    attn_grad_half = state_half.astype(LOW)
    attn_grad_b = both_halves(attn_grad_half, swap_tensor(attn_grad_half))
    out_w_grad = dot_tn(attn_grad_b, context_b).astype(LOW)
    out_sum = lax.psum_scatter(out_w_grad, "dp", scatter_dimension=0, tiled=True)
    context_grad_b = dot_nn(attn_grad_b, full_o).astype(LOW).reshape(by_head)
    again = masked_scores(queries_b, keyset, allowed)
    probs = jnp.exp(again - log_total)
    prob_grad = jnp.einsum(
        "qhd,khd->hqk", context_grad_b, valueset, preferred_element_type=FULL
    )
    value_grad = jnp.einsum("hqk,qhd->khd", probs_b, context_grad_b, preferred_element_type=FULL)
    row_dot = jnp.sum(probs * prob_grad, axis=-1, keepdims=True)
    score_grad_b = (probs * (prob_grad - row_dot)).astype(LOW)
    query_grad = jnp.einsum(
        "hqk,khd->qhd", score_grad_b, keyset, preferred_element_type=FULL
    ) * HEAD ** (-0.5)
    key_grad = jnp.einsum(
        "hqk,qhd->khd", score_grad_b, queries_b, preferred_element_type=FULL
    ) * HEAD ** (-0.5)
    key_grad = key_grad.reshape(-1, local_width)
    value_grad = value_grad.reshape(-1, local_width)
    blocks_of = lambda array: [array[j * PR_DEV : (j + 1) * PR_DEV] for j in range(GROUP)]
    key_own = return_prompt(blocks_of(key_grad), (0, 1, 2))
    value_own = return_prompt(blocks_of(value_grad), (0, 2, 1))
    key_local = jnp.concatenate([key_own, key_grad[prompt_length:]], axis=0)
    value_local = jnp.concatenate([value_own, value_grad[prompt_length:]], axis=0)
    query_normed_grad = rotate_back(query_grad, cosine, sine).reshape(token_count, -1)
    key_normed_grad = rotate_back(key_local.reshape(by_head), cosine, sine).reshape(
        token_count, -1
    )
    query_inner, key_inner = lax.psum(
        (
            jnp.sum(query_flat * gain_query_local * query_normed_grad, axis=1),
            jnp.sum(key_flat * gain_key_local * key_normed_grad, axis=1),
        ),
        "tensor",
    )
    query_cube = query_scale * query_scale * query_scale
    key_cube = key_scale * key_scale * key_scale
    query_pre_grad = (
        query_scale * gain_query_local * query_normed_grad
        - query_flat * query_cube * (query_inner / column_total)[:, None]
    ).astype(LOW)
    key_pre_grad = (
        key_scale * gain_key_local * key_normed_grad
        - key_flat * key_cube * (key_inner / column_total)[:, None]
    ).astype(LOW)
    query_gain_part = jnp.sum(query_normed_grad * query_flat * query_scale, axis=0)
    key_gain_part = jnp.sum(key_normed_grad * key_flat * key_scale, axis=0)
    wide = lambda part: lax.dynamic_update_slice_in_dim(
        jnp.zeros((column_total,), FULL), part, side * local_width, 0
    )
    value_pre_grad = value_local.astype(LOW)
    w_grads = jnp.stack(
        [
            dot_tn(normed_b, query_pre_grad).astype(LOW).reshape(dp_count, block, local_width),
            dot_tn(normed_b, key_pre_grad).astype(LOW).reshape(dp_count, block, local_width),
            dot_tn(normed_b, value_pre_grad).astype(LOW).reshape(dp_count, block, local_width),
        ],
        axis=1,
    ).reshape(dp_count * 3 * block, local_width)
    w_sum = lax.psum_scatter(w_grads, "dp", scatter_dimension=0, tiled=True).astype(FULL)
    normed_part = (
        dot_nt(query_pre_grad, full_q)
        + dot_nt(key_pre_grad, full_k)
        + dot_nt(value_pre_grad, full_v)
    )
    normed_other = swap_tensor(other_half(normed_part).astype(LOW))
    normed_grad = own_half(normed_part) + normed_other.astype(FULL)
    unused_one, norm_one_back = jax.vjp(rms_norm, own_half(tokens_f), gain_one)
    input_part, gain_one_grad = norm_one_back(normed_grad)
    input_half = state_half + input_part
    input_grad = both_halves(input_half, swap_tensor(input_half))
    gain_grads = jnp.stack(
        [gain_one_grad, gain_two_grad, wide(query_gain_part), wide(key_gain_part)]
    ).reshape(4, dp_count, block)
    gain_sums = lax.psum_scatter(gain_grads, "dp", scatter_dimension=1, tiled=True)
    gain_sums = lax.psum(gain_sums.reshape(4, block), "tensor")
    return (
        output,
        input_grad,
        gain_sums[0],
        w_sum[:block],
        w_sum[block : 2 * block],
        w_sum[2 * block :],
        gain_sums[2],
        gain_sums[3],
        out_sum.astype(FULL).T,
        gain_sums[1],
        gate_w_grad[None],
        up_w_grad[None],
        down_grad[None],
    )


def solution(mesh):
    return jax.shard_map(
        body,
        mesh=mesh,
        in_specs=(
            P("dp", None),
            P("dp"),
            P("dp", "tensor"),
            P("dp", "tensor"),
            P("dp", "tensor"),
            P("dp"),
            P("dp"),
            P("tensor", "dp"),
            P("dp"),
            P("dp", None, "tensor"),
            P("dp", None, "tensor"),
            P("dp", "tensor", None),
            P("dp", None),
            P("dp", None),
            P("dp", None),
            P("dp", None),
            P("dp", None),
        ),
        out_specs=(
            P("dp", None),
            P("dp", None),
            P("dp"),
            P("dp", "tensor"),
            P("dp", "tensor"),
            P("dp", "tensor"),
            P("dp"),
            P("dp"),
            P("tensor", "dp"),
            P("dp"),
            P("dp", None, "tensor"),
            P("dp", None, "tensor"),
            P("dp", "tensor", None),
        ),
        check_vma=False,
    )
```

```python
import jax
import jax.numpy as jnp
from jax import lax
from jax.experimental import pallas as pl
from jax.experimental.pallas import tpu as pltpu
from jax.sharding import PartitionSpec as P

HEADS = 16
HEAD = 128
GROUP = 8
PR_DEV = 128


EPSILON = 1e-05
LOW = jnp.bfloat16
FULL = jnp.float32


def swap_bit(block, axis, bit):
    count = lax.axis_size(axis)
    return lax.ppermute(block, axis, [(i, i ^ (1 << bit)) for i in range(count)])


def swap_tensor(block):
    return lax.ppermute(block, "tensor", [(0, 1), (1, 0)])


RING = (0, 2, 4, 6, 7, 5, 3, 1)
AHEAD = [
    (RING[p] * 2 + c, RING[(p + 1) % len(RING)] * 2 + c) for p in range(len(RING)) for c in range(2)
]
BEHIND = [(to, at) for at, to in AHEAD]


def ahead(block):
    return lax.ppermute(block, "dp", AHEAD)


def behind(block):
    return lax.ppermute(block, "dp", BEHIND)


def ring_blocks(dp_index):
    chip, core = dp_index // 2, dp_index % 2
    place = jnp.where(chip % 2 == 0, chip // 2, 7 - chip // 2)
    steps, cross = [], []
    for hop in (1, 2, 3):
        steps += [-hop, hop, -hop, hop]
        cross += [0, 0, 1, 1]
    steps += [0, 0, 4, 4]
    cross += [0, 1, 0, 1]
    there = (place + jnp.array(steps, jnp.int32)) % 8
    chips = jnp.where(there < 4, 2 * there, 2 * (7 - there) + 1)
    return 2 * chips + (core ^ jnp.array(cross, jnp.int32))


def add_low(*parts):
    total = parts[0].astype(FULL)
    for part in parts[1:]:
        total = total + part.astype(FULL)
    return total.astype(LOW)


def together(value, *others):
    return lax.optimization_barrier((value, *others))


def ring_sum(same, cross, fillers):
    both = {hop: add_low(same[hop], swap_bit(cross[hop], "dp", 0)) for hop in (4, 3, 2, 1, 0)}
    rows = both[0].shape[0]
    cut = rows // 2
    done = []

    def fill(gate):
        for work, *operands in fillers[len(done)]:
            gate, *operands = together(gate, *operands)
            done_here.append(work(*operands))
        done.append(list(done_here))
        done_here.clear()
        return gate

    done_here = []
    right, left = ahead(both[4][:cut]), behind(both[4][cut:])
    left = fill(left)
    outward, inward = both[3][rows:], both[3][:rows]
    right = jnp.concatenate([add_low(outward[:cut], right), outward[cut:]], axis=0)
    left = jnp.concatenate([inward[:cut], add_low(inward[cut:], left)], axis=0)
    right, left = ahead(right), behind(left)
    left = fill(left)
    for hop in (2, 1):
        right = ahead(add_low(both[hop][rows:], right))
        left = behind(add_low(both[hop][:rows], left))
        if hop == 2:
            left = fill(left)
    total = both[0].astype(FULL) + right.astype(FULL) + left.astype(FULL)
    return total, [out for outs in done for out in outs]


def rms_norm(values, gain):
    return values * lax.rsqrt(jnp.mean(values * values, axis=-1, keepdims=True) + EPSILON) * gain


def rope_tables(positions, head_size):
    half_size = head_size // 2
    inverse = 10000.0 ** (-(jnp.arange(half_size, dtype=FULL) * 2.0) / head_size)
    angles = positions.astype(FULL)[:, None] * inverse[None, :]
    cosine = jnp.concatenate([jnp.cos(angles), jnp.cos(angles)], axis=-1)
    sine = jnp.concatenate([jnp.sin(angles), jnp.sin(angles)], axis=-1)
    return (cosine, sine)


def rotate(values, cosine, sine):
    half_size = values.shape[-1] // 2
    turned = jnp.concatenate([-values[..., half_size:], values[..., :half_size]], axis=-1)
    return values * cosine[:, None, :] + turned * sine[:, None, :]


def rotate_back(values, cosine, sine):
    half_size = values.shape[-1] // 2
    scaled = values * sine[:, None, :]
    turned = jnp.concatenate([scaled[..., half_size:], -scaled[..., :half_size]], axis=-1)
    return values * cosine[:, None, :] + turned


def cont_positions(segment_row, gap_row, prompt_length):
    order = jnp.arange(segment_row.shape[0], dtype=jnp.int32)
    same = segment_row[:, None] == segment_row[None, :]
    earlier = order[None, :] < order[:, None]
    offset = jnp.sum((same & earlier).astype(jnp.int32), axis=1)
    labels = jnp.arange(gap_row.shape[0], dtype=jnp.int32)
    shifted = jnp.sum(
        jnp.where(segment_row[:, None] == labels[None, :], gap_row[None, :], 0), axis=1
    )
    return prompt_length + shifted + offset


def dot_nn(left, right):
    return jnp.dot(left, right, preferred_element_type=FULL)


def dot_tn(left, right):
    return lax.dot_general(left, right, (((0,), (0,)), ((), ())), preferred_element_type=FULL)


def dot_nt(left, right):
    return lax.dot_general(left, right, (((1,), (1,)), ((), ())), preferred_element_type=FULL)


def collect_prompt(keys, values):
    own = jnp.stack([keys, values], axis=0)
    near = swap_bit(own, "dp", 1)
    far = swap_bit(own, "dp", 2)
    last_keys = swap_bit(far[0], "dp", 1)
    last_values = swap_bit(near[1], "dp", 2)
    blocks = [None] * GROUP
    for at, piece in ((0, own), (2, near), (4, far)):
        blocks[at] = piece
        blocks[at + 1] = swap_bit(piece, "dp", 0)
    last = jnp.stack([last_keys, last_values], axis=0)
    blocks[6] = last
    blocks[7] = swap_bit(last, "dp", 0)
    return [b[0] for b in blocks], [b[1] for b in blocks]


def return_prompt(grads, order):
    parts = {j: grads[j] for j in range(GROUP)}
    for bit in order:
        gone = [j for j in sorted(parts) if j >> bit & 1]
        sent = jnp.stack([parts[j] for j in gone], axis=0).astype(LOW)
        got = swap_bit(sent, "dp", bit)
        for at, j in enumerate(gone):
            stay = j ^ (1 << bit)
            parts[stay] = parts[stay] + got[at].astype(FULL)
            del parts[j]
    return parts[0]


def masked_scores(queries, keyset, allowed):
    scores = jnp.einsum("qhd,khd->hqk", queries, keyset, preferred_element_type=FULL) * HEAD ** (
        -0.5
    )
    return jnp.where(allowed[None], scores, -1e30)


def expert_kernel(
    rows_ref, back_ref, gate_ref, wg0, wg1, wu0, wu1, wd0, wd1, grad_ref, h0, h1, g0, g1, u0, u1
):
    rows = rows_ref[...]
    back = back_ref[...]
    gate = gate_ref[...]
    total = None
    for wg, wu, wd, h, g, u in ((wg0, wu0, wd0, h0, g0, u0), (wg1, wu1, wd1, h1, g1, u1)):
        gate_pre = dot_nn(rows, wg[...])
        up_pre = dot_nn(rows, wu[...])
        hidden_grad = gate * dot_nt(back, wd[...])
        sig = 1.0 / (1.0 + jnp.exp(-gate_pre))
        act = gate_pre * sig
        h[...] = (gate * (act * up_pre)).astype(LOW)
        gate_grad = (hidden_grad * up_pre * (sig * (1.0 + gate_pre * (1.0 - sig)))).astype(LOW)
        up_grad = (hidden_grad * act).astype(LOW)
        g[...] = gate_grad
        u[...] = up_grad
        part = dot_nt(gate_grad, wg[...]) + dot_nt(up_grad, wu[...])
        total = part if total is None else total + part
    grad_ref[...] = total.astype(LOW)


def expert_pass(rows, back, gate, gate_mats, up_mats, down_mats):
    count, width = rows.shape
    hidden = gate_mats[0].shape[1]
    tile = 256
    whole = lambda array: pl.BlockSpec(
        array.shape, lambda i: (0, 0), pipeline_mode=pl.Buffered(1)
    )
    tall = lambda columns: pl.BlockSpec((tile, columns), lambda i: (i, 0))
    mats = [*gate_mats, *up_mats, *down_mats]
    flops = 2 * 5 * count * width * hidden * 2
    return pl.pallas_call(
        expert_kernel,
        grid=(count // tile,),
        in_specs=[tall(width), tall(width), tall(1)] + [whole(m) for m in mats],
        out_specs=[tall(width)] + [tall(hidden)] * 6,
        out_shape=[jax.ShapeDtypeStruct((count, width), LOW)]
        + [jax.ShapeDtypeStruct((count, hidden), LOW)] * 6,
        compiler_params=pltpu.CompilerParams(vmem_limit_bytes=58 * 1024 * 1024),
        cost_estimate=pl.CostEstimate(
            flops=flops,
            bytes_accessed=2 * (3 * count * width + 6 * count * hidden + 6 * width * hidden),
            transcendentals=2 * count * hidden,
        ),
    )(rows, back, gate, *mats)


def chunk_kernel(pieces, first, *refs):
    piece_refs, refs = refs[:pieces], refs[pieces:]
    back_ref, gate_ref, wg0, wg1, wu0, wu1, wd0, wd1, vg0, vg1, vu0, vu1 = refs[:12]
    same_ref, cross_ref, rows_ref, h0, h1, g0, g1, u0, u1, kept_g, kept_u = refs[
        12 if first else 19 :
    ]
    step = pl.program_id(0)

    @pl.when(step == 0)
    def _():
        at = 0
        for piece in piece_refs:
            rows_ref[at : at + piece.shape[0]] = piece[...]
            at += piece.shape[0]

    def work(wg, wu, wd, h, g, u):
        rows = rows_ref[...]
        gate = gate_ref[...]
        gate_pre = dot_nn(rows, wg[...])
        up_pre = dot_nn(rows, wu[...])
        hidden_grad = gate * dot_nt(back_ref[...], wd[...])
        sig = 1.0 / (1.0 + jnp.exp(-gate_pre))
        act = gate_pre * sig
        h[...] = (gate * (act * up_pre)).astype(LOW)
        gate_grad = (hidden_grad * up_pre * (sig * (1.0 + gate_pre * (1.0 - sig)))).astype(LOW)
        up_grad = (hidden_grad * act).astype(LOW)
        g[...] = gate_grad
        u[...] = up_grad
        kept_g[step] = gate_grad
        kept_u[step] = up_grad

    @pl.when(step < 2)
    def _():
        work(wg0, wu0, wd0, h0, g0, u0)

    @pl.when((step >= 2) & (step < 4))
    def _():
        work(wg1, wu1, wd1, h1, g1, u1)

    @pl.when(step >= 4)
    def _():
        total = None
        for kept, first_half, second_half in ((kept_g, vg0, vg1), (kept_u, vu0, vu1)):
            for at, mat in ((0, first_half), (2, second_half)):
                left = jnp.concatenate([kept[at], kept[at + 1]], axis=1)
                part = dot_nt(left, mat[...])
                total = part if total is None else total + part
        half = same_ref.shape[0]
        same_ref[...] = total[:half].astype(LOW)
        cross_ref[...] = total[half:].astype(LOW)


def expert_chunk(pieces, back, gate, mats, at, held):
    width = back.shape[1]
    hidden = mats[0].shape[1]
    part = hidden // 2
    slab = width // 4
    count = sum(piece.shape[0] for piece in pieces)
    all_rows = back.shape[0]
    own = lambda j: jnp.minimum(j, 1)
    other = lambda j: jnp.clip(j - 2, 0, 1)
    late = lambda j: jnp.maximum(j - 4, 0)
    once = pl.Buffered(1)
    fixed = lambda array: pl.BlockSpec(array.shape, lambda j: (0, 0), pipeline_mode=once)
    chunk = lambda columns, **mode: pl.BlockSpec((count, columns), lambda j: (at, 0), **mode)
    tall = lambda pick: pl.BlockSpec((width, part), lambda j: (0, pick(j)))
    flat = lambda pick: pl.BlockSpec((part, width), lambda j: (pick(j), 0))
    narrow = lambda pick: pl.BlockSpec((count, part), lambda j: (at, pick(j)))
    again = lambda: pl.BlockSpec((slab, hidden), lambda j: (late(j), 0))
    whole = lambda: pl.BlockSpec((count // 2, slab), lambda j: (0, late(j)))
    held_specs = [] if held is None else [pl.BlockSpec(memory_space=pl.ANY)] * 7
    held_args = [] if held is None else list(held)
    base = len(pieces) + 12
    wide = jax.ShapeDtypeStruct((all_rows, hidden), LOW)
    out = pl.pallas_call(
        lambda *refs: chunk_kernel(len(pieces), held is None, *refs),
        grid=(8,),
        in_specs=[fixed(piece) for piece in pieces]
        + [chunk(width, pipeline_mode=once), chunk(1, pipeline_mode=once)]
        + [tall(own), tall(other), tall(own), tall(other), flat(own), flat(other)]
        + [again(), again(), again(), again()]
        + held_specs,
        out_specs=[whole(), whole(), chunk(width)] + [narrow(own), narrow(other)] * 3,
        out_shape=[jax.ShapeDtypeStruct((count // 2, width), LOW)] * 2
        + [jax.ShapeDtypeStruct((all_rows, width), LOW)]
        + [wide] * 6,
        scratch_shapes=[pltpu.VMEM((4, count, part), LOW)] * 2,
        input_output_aliases={} if held is None else {base + k: 2 + k for k in range(7)},
        compiler_params=pltpu.CompilerParams(vmem_limit_bytes=58 * 1024 * 1024),
        cost_estimate=pl.CostEstimate(
            flops=2 * 5 * count * width * hidden * 2,
            bytes_accessed=2 * (3 * count * width + 6 * count * hidden + 6 * width * hidden),
            transcendentals=2 * count * hidden,
        ),
    )(*pieces, back, gate, *mats, *mats[:4], *held_args)
    return out[0], out[1], out[2:]


def expert_ring(rows, back, gate, mats):
    cut = rows.shape[0] // 2
    same, cross = {}, {}
    left, right = ahead(rows), behind(rows)
    swap = lambda block: swap_bit(block, "dp", 0)
    same[0], cross[0], held = expert_chunk([rows, swap(rows)], back, gate, mats, 6, None)
    for hop in (1, 2, 3):
        pieces = [left, right, swap(left), swap(right)]
        if hop < 3:
            left, right = ahead(left), behind(right)
        else:
            left, right = ahead(left[:cut]), behind(right[cut:])
        same[hop], cross[hop], held = expert_chunk(pieces, back, gate, mats, hop - 1, held)
    pieces = [left, right, swap(left), swap(right)]
    same[4], cross[4], held = expert_chunk(pieces, back, gate, mats, 7, held)
    return same, cross, held


def halving_sum(parts):
    bits = parts.shape[0].bit_length() - 1
    index = lax.axis_index("dp")
    for bit in reversed(range(bits)):
        rows = parts.shape[0] // 2
        upper = index >> bit & 1
        kept = lax.dynamic_slice_in_dim(parts, upper * rows, rows, axis=0)
        sent = lax.dynamic_slice_in_dim(parts, (1 - upper) * rows, rows, axis=0)
        parts = kept + swap_bit(sent, "dp", bit)
    return parts[0]


def body(
    inputs,
    attn_gain,
    w_query,
    w_key,
    w_value,
    query_gain,
    key_gain,
    w_out,
    moe_gain,
    w_gate,
    w_up,
    w_down,
    experts,
    gates,
    segments,
    gaps,
    cotangent,
):
    dp_count = lax.axis_size("dp")
    dp_index = lax.axis_index("dp")
    side = lax.axis_index("tensor")
    token_count, model_width = inputs.shape
    half_count = token_count // 2
    top_count = experts.shape[1]
    expert_count = w_gate.shape[0] * dp_count
    capacity = token_count * top_count * dp_count * 9 // (8 * expert_count)
    prompt_length = PR_DEV * GROUP
    column_total = HEADS * HEAD
    block = w_query.shape[0]
    local_width = w_query.shape[1]
    local_heads = local_width // HEAD

    def own_half(array):
        return lax.dynamic_slice_in_dim(array, side * half_count, half_count, axis=0)

    def other_half(array):
        return lax.dynamic_slice_in_dim(array, (1 - side) * half_count, half_count, axis=0)

    def both_halves(own, other):
        first = side == 0
        return jnp.concatenate(
            [jnp.where(first, own, other), jnp.where(first, other, own)], axis=0
        )

    gate_mats = (w_gate[0], swap_tensor(w_gate[0]))
    up_mats = (w_up[0], swap_tensor(w_up[0]))

    ring = dp_count == 2 * len(RING)

    gates_high = gates.astype(LOW)
    gates_low = (gates - gates_high.astype(FULL)).astype(LOW)
    routing = jnp.concatenate([experts.astype(LOW).T, gates_high.T, gates_low.T], axis=1)
    routing = jnp.pad(routing, ((0, 0), (0, local_width - 3 * token_count)))
    gains = jnp.concatenate([attn_gain, moe_gain, query_gain, key_gain])
    gains = jnp.pad(gains[None], ((0, 7), (0, local_width - 4 * block)))
    packed = jnp.concatenate([w_query, w_key, w_value, w_out.T, gains, routing], axis=0)
    gathered = lax.all_gather(packed, "dp", axis=0, tiled=False)
    gathered, *early = lax.optimization_barrier((gathered, gate_mats[1], up_mats[1]))
    gate_mats, up_mats = (gate_mats[0], early[0]), (up_mats[0], early[1])
    full_q = gathered[:, :block].reshape(model_width, local_width)
    full_k = gathered[:, block : 2 * block].reshape(model_width, local_width)
    full_v = gathered[:, 2 * block : 3 * block].reshape(model_width, local_width)
    full_o = gathered[:, 3 * block : 4 * block].reshape(model_width, local_width)
    gain_rows = gathered[:, 4 * block].astype(FULL)
    gain_one, gain_two, gain_q, gain_k = (
        gain_rows[:, j * block : (j + 1) * block].reshape(-1) for j in range(4)
    )
    gain_query_local = lax.dynamic_slice_in_dim(gain_q, side * local_width, local_width)
    gain_key_local = lax.dynamic_slice_in_dim(gain_k, side * local_width, local_width)

    names = gathered[:, 4 * block + 8 :, :token_count]
    weights = gathered[:, 4 * block + 8 :, token_count : 2 * token_count].astype(
        FULL
    ) + gathered[:, 4 * block + 8 :, 2 * token_count : 3 * token_count].astype(FULL)
    named = names == dp_index.astype(LOW)
    picked = jnp.sum(named.astype(FULL), axis=1)
    weight = jnp.sum(jnp.where(named, weights, 0.0), axis=1)
    order = jnp.arange(token_count, dtype=jnp.int32)
    earlier = (order[:, None] < order[None, :]).astype(LOW)
    within = dot_nn(picked.astype(LOW), earlier)
    per_row = jnp.sum(picked, axis=1)
    rows_order = jnp.arange(dp_count, dtype=jnp.int32)
    ahead = jnp.sum(
        jnp.where(rows_order[None, :] < rows_order[:, None], per_row[None, :], 0.0), axis=1
    )
    kept = (picked > 0.0) & (within + ahead[:, None] < capacity)
    weight = jnp.where(kept, weight, 0.0)
    weight = lax.dynamic_slice_in_dim(weight, side * half_count, half_count, axis=1)
    if ring:
        blocks = ring_blocks(dp_index)
        weight = weight[blocks]
    weight = weight.reshape(-1, 1)

    cotangent_half = own_half(cotangent)
    back_rows = lax.all_gather(cotangent_half.astype(LOW), "dp", axis=0, tiled=False)
    back_rows = (back_rows[blocks] if ring else back_rows).reshape(-1, model_width)

    tokens_f = inputs.astype(FULL)
    prompt_pos = dp_index % GROUP * PR_DEV + jnp.arange(PR_DEV, dtype=jnp.int32)
    later_pos = cont_positions(segments[0], gaps[0], prompt_length)
    positions = jnp.concatenate([prompt_pos, later_pos], axis=0)
    cosine, sine = rope_tables(positions, HEAD)
    normed_b = rms_norm(tokens_f, gain_one).astype(LOW)
    query_flat = dot_nn(normed_b, full_q)
    key_flat = dot_nn(normed_b, full_k)
    values_b = dot_nn(normed_b, full_v).astype(LOW)
    query_sq, key_sq = lax.psum(
        (jnp.sum(query_flat * query_flat, axis=1), jnp.sum(key_flat * key_flat, axis=1)), "tensor"
    )
    query_sq, down_mat = lax.optimization_barrier((query_sq, w_down[0]))
    down_mats = (down_mat, swap_tensor(down_mat))
    query_scale = lax.rsqrt(query_sq / column_total + EPSILON)[:, None]
    key_scale = lax.rsqrt(key_sq / column_total + EPSILON)[:, None]
    by_head = (token_count, local_heads, HEAD)
    queries_b = rotate(
        (query_flat * query_scale * gain_query_local).reshape(by_head), cosine, sine
    ).astype(LOW)
    keys_b = rotate(
        (key_flat * key_scale * gain_key_local).reshape(by_head), cosine, sine
    ).astype(LOW)
    key_blocks, value_blocks = collect_prompt(
        keys_b[:PR_DEV].reshape(PR_DEV, local_width), values_b[:PR_DEV]
    )
    keyset = jnp.concatenate(
        key_blocks + [keys_b[PR_DEV:].reshape(-1, local_width)], axis=0
    ).reshape(-1, local_heads, HEAD)
    valueset = jnp.concatenate(value_blocks + [values_b[PR_DEV:]], axis=0).reshape(
        -1, local_heads, HEAD
    )
    prompt_query = jnp.arange(token_count, dtype=jnp.int32) < PR_DEV
    prompt_at = jnp.arange(prompt_length, dtype=jnp.int32)
    prompt_keypos = ((dp_index % GROUP) ^ (prompt_at // PR_DEV)) * PR_DEV + prompt_at % PR_DEV
    allowed_prompt = (~prompt_query)[:, None] | (prompt_keypos[None, :] <= positions[:, None])
    query_segment = jnp.concatenate([jnp.full((PR_DEV,), -1, jnp.int32), segments[0]], axis=0)
    allowed_cont = (query_segment[:, None] == segments[0][None, :]) & (
        later_pos[None, :] <= positions[:, None]
    )
    allowed = jnp.concatenate([allowed_prompt, allowed_cont], axis=1)
    scores = masked_scores(queries_b, keyset, allowed)
    peak = jnp.max(scores, axis=-1, keepdims=True)
    expo = jnp.exp(scores - peak)
    total = jnp.sum(expo, axis=-1, keepdims=True)
    log_total = peak + jnp.log(total)
    probs_b = (expo / total).astype(LOW)
    context = jnp.einsum("hqk,khd->qhd", probs_b, valueset, preferred_element_type=FULL)
    context_b = context.reshape(token_count, local_width).astype(LOW)
    attn_part = dot_nt(context_b, full_o)
    attn_part, late = lax.optimization_barrier((attn_part, down_mats[1]))
    down_mats = (down_mats[0], late)
    mats = (*gate_mats, *up_mats, *down_mats)
    attn_other = swap_tensor(other_half(attn_part).astype(LOW))
    hidden_state = (
        own_half(tokens_f) + own_half(attn_part) + attn_other.astype(FULL)
    )
    normed_two_b = rms_norm(hidden_state, gain_two).astype(LOW)

    low_tn = lambda left, right: dot_tn(left, right).astype(LOW)
    if ring:
        same, cross, held = expert_ring(normed_two_b, back_rows, weight, mats)
        expert_in, h0, h1, g0, g1, u0, u1 = held
        down_sent = low_tn(h1, back_rows)
        down_got = swap_tensor(down_sent)
        normed_two_grad, outs = ring_sum(
            same,
            cross,
            [
                [(low_tn, expert_in, g1), (low_tn, expert_in, u1)],
                [(lambda a, b: dot_nn(a, down_mats[0]) + dot_nn(b, down_mats[1]), h0, h1)],
                [(dot_tn, h0, back_rows), (dot_tn, expert_in, g0), (dot_tn, expert_in, u0)],
            ],
        )
        gate_sent, up_sent, mixed_rows, down_grad, gate_w_grad, up_w_grad = outs
        mixed_rows = mixed_rows.astype(LOW)
        gate_got = swap_tensor(gate_sent)
    else:
        expert_in = lax.all_gather(normed_two_b, "dp", axis=0, tiled=True)
        grad_rows, h0, h1, g0, g1, u0, u1 = expert_pass(
            expert_in, back_rows, weight, gate_mats, up_mats, down_mats
        )
        normed_two_grad = lax.psum_scatter(
            grad_rows, "dp", scatter_dimension=0, tiled=True
        ).astype(FULL)
        mixed_rows = (dot_nn(h0, down_mats[0]) + dot_nn(h1, down_mats[1])).astype(LOW)
        down_got = swap_tensor(low_tn(h1, back_rows))
        gate_got = swap_tensor(low_tn(expert_in, g1))
        up_sent = low_tn(expert_in, u1)
        down_grad = dot_tn(h0, back_rows)
        gate_w_grad = dot_tn(expert_in, g0)
        up_w_grad = dot_tn(expert_in, u0)
    normed_two_grad, down_got, gate_got, mixed_rows, down_grad, gate_w_grad, up_w_grad = together(
        normed_two_grad, down_got, gate_got, mixed_rows, down_grad, gate_w_grad, up_w_grad
    )
    if ring:
        back_to = jnp.argsort(blocks)
        mixed_rows = mixed_rows.reshape(dp_count, half_count, model_width)[back_to].reshape(
            -1, model_width
        )
    mixed = lax.psum_scatter(mixed_rows, "dp", scatter_dimension=0, tiled=True).astype(FULL)
    output_half = hidden_state + mixed

    unused_two, norm_two_back = jax.vjp(rms_norm, hidden_state, gain_two)
    state_part, gain_two_grad = norm_two_back(normed_two_grad)
    state_half = cotangent_half + state_part
    attn_grad_half = state_half.astype(LOW)
    attn_grad_b = both_halves(attn_grad_half, swap_tensor(attn_grad_half))
    attn_grad_b, up_sent = together(attn_grad_b, up_sent)
    up_got = swap_tensor(up_sent)
    out_w_grad = dot_tn(attn_grad_b, context_b).astype(LOW)
    context_grad_b = dot_nn(attn_grad_b, full_o).astype(LOW).reshape(by_head)
    again = masked_scores(queries_b, keyset, allowed)
    probs = jnp.exp(again - log_total)
    prob_grad = jnp.einsum(
        "qhd,khd->hqk", context_grad_b, valueset, preferred_element_type=FULL
    )
    value_grad = jnp.einsum("hqk,qhd->khd", probs_b, context_grad_b, preferred_element_type=FULL)
    row_dot = jnp.sum(probs * prob_grad, axis=-1, keepdims=True)
    score_grad_b = (probs * (prob_grad - row_dot)).astype(LOW)
    query_grad = jnp.einsum(
        "hqk,khd->qhd", score_grad_b, keyset, preferred_element_type=FULL
    ) * HEAD ** (-0.5)
    key_grad = jnp.einsum(
        "hqk,qhd->khd", score_grad_b, queries_b, preferred_element_type=FULL
    ) * HEAD ** (-0.5)
    key_grad = key_grad.reshape(-1, local_width)
    value_grad = value_grad.reshape(-1, local_width)
    blocks_of = lambda array: [array[j * PR_DEV : (j + 1) * PR_DEV] for j in range(GROUP)]
    key_own = return_prompt(blocks_of(key_grad), (0, 1, 2))
    value_own = return_prompt(blocks_of(value_grad), (0, 2, 1))
    key_local = jnp.concatenate([key_own, key_grad[prompt_length:]], axis=0)
    value_local = jnp.concatenate([value_own, value_grad[prompt_length:]], axis=0)
    query_normed_grad = rotate_back(query_grad, cosine, sine).reshape(token_count, -1)
    key_normed_grad = rotate_back(key_local.reshape(by_head), cosine, sine).reshape(
        token_count, -1
    )
    query_normed_grad, key_normed_grad, up_got = together(
        query_normed_grad, key_normed_grad, up_got
    )
    query_inner, key_inner = lax.psum(
        (
            jnp.sum(query_flat * gain_query_local * query_normed_grad, axis=1),
            jnp.sum(key_flat * gain_key_local * key_normed_grad, axis=1),
        ),
        "tensor",
    )
    query_cube = query_scale * query_scale * query_scale
    key_cube = key_scale * key_scale * key_scale
    query_pre_grad = (
        query_scale * gain_query_local * query_normed_grad
        - query_flat * query_cube * (query_inner / column_total)[:, None]
    ).astype(LOW)
    key_pre_grad = (
        key_scale * gain_key_local * key_normed_grad
        - key_flat * key_cube * (key_inner / column_total)[:, None]
    ).astype(LOW)
    query_gain_part = jnp.sum(query_normed_grad * query_flat * query_scale, axis=0)
    key_gain_part = jnp.sum(key_normed_grad * key_flat * key_scale, axis=0)
    wide = lambda part: lax.dynamic_update_slice_in_dim(
        jnp.zeros((column_total,), FULL), part, side * local_width, 0
    )
    value_pre_grad = value_local.astype(LOW)
    w_grads = jnp.stack(
        [
            dot_tn(normed_b, query_pre_grad).astype(LOW).reshape(dp_count, block, local_width),
            dot_tn(normed_b, key_pre_grad).astype(LOW).reshape(dp_count, block, local_width),
            dot_tn(normed_b, value_pre_grad).astype(LOW).reshape(dp_count, block, local_width),
            out_w_grad.reshape(dp_count, block, local_width),
        ],
        axis=1,
    ).reshape(dp_count * 4 * block, local_width)
    down_grad = down_grad + down_got.astype(FULL)
    gate_w_grad = gate_w_grad + gate_got.astype(FULL)
    up_w_grad = up_w_grad + up_got.astype(FULL)
    output = both_halves(output_half, swap_tensor(output_half))
    w_sum = lax.psum_scatter(w_grads, "dp", scatter_dimension=0, tiled=True).astype(FULL)
    normed_part = (
        dot_nt(query_pre_grad, full_q)
        + dot_nt(key_pre_grad, full_k)
        + dot_nt(value_pre_grad, full_v)
    )
    normed_other = swap_tensor(other_half(normed_part).astype(LOW))
    normed_grad = own_half(normed_part) + normed_other.astype(FULL)
    unused_one, norm_one_back = jax.vjp(rms_norm, own_half(tokens_f), gain_one)
    input_part, gain_one_grad = norm_one_back(normed_grad)
    input_half = state_half + input_part
    input_grad = both_halves(input_half, swap_tensor(input_half))
    gain_grads = jnp.stack(
        [gain_one_grad, gain_two_grad, wide(query_gain_part), wide(key_gain_part)]
    ).reshape(4, dp_count, block)
    gain_sums = halving_sum(jnp.swapaxes(gain_grads, 0, 1))
    gain_sums = gain_sums + swap_tensor(gain_sums)
    return (
        output,
        input_grad,
        gain_sums[0],
        w_sum[:block],
        w_sum[block : 2 * block],
        w_sum[2 * block : 3 * block],
        gain_sums[2],
        gain_sums[3],
        w_sum[3 * block :].T,
        gain_sums[1],
        gate_w_grad[None],
        up_w_grad[None],
        down_grad[None],
    )


def solution(mesh):
    return jax.shard_map(
        body,
        mesh=mesh,
        in_specs=(
            P("dp", None),
            P("dp"),
            P("dp", "tensor"),
            P("dp", "tensor"),
            P("dp", "tensor"),
            P("dp"),
            P("dp"),
            P("tensor", "dp"),
            P("dp"),
            P("dp", None, "tensor"),
            P("dp", None, "tensor"),
            P("dp", "tensor", None),
            P("dp", None),
            P("dp", None),
            P("dp", None),
            P("dp", None),
            P("dp", None),
        ),
        out_specs=(
            P("dp", None),
            P("dp", None),
            P("dp"),
            P("dp", "tensor"),
            P("dp", "tensor"),
            P("dp", "tensor"),
            P("dp"),
            P("dp"),
            P("tensor", "dp"),
            P("dp"),
            P("dp", None, "tensor"),
            P("dp", None, "tensor"),
            P("dp", "tensor", None),
        ),
        check_vma=False,
    )
```

```python
import jax
import jax.numpy as jnp
from jax import lax
from jax.experimental import pallas as pl
from jax.experimental.pallas import tpu as pltpu
from jax.sharding import PartitionSpec as P

HEADS = 16
HEAD = 128
GROUP = 8
PR_DEV = 128


EPSILON = 1e-05
LOW = jnp.bfloat16
FULL = jnp.float32


def swap_bit(block, axis, bit):
    count = lax.axis_size(axis)
    return lax.ppermute(block, axis, [(i, i ^ (1 << bit)) for i in range(count)])


def swap_tensor(block):
    return lax.ppermute(block, "tensor", [(0, 1), (1, 0)])


RING = (0, 2, 4, 6, 7, 5, 3, 1)
AHEAD = [
    (RING[p] * 2 + c, RING[(p + 1) % len(RING)] * 2 + c) for p in range(len(RING)) for c in range(2)
]
BEHIND = [(to, at) for at, to in AHEAD]


def ahead(block):
    return lax.ppermute(block, "dp", AHEAD)


def behind(block):
    return lax.ppermute(block, "dp", BEHIND)


def ring_blocks(dp_index):
    chip, core = dp_index // 2, dp_index % 2
    place = jnp.where(chip % 2 == 0, chip // 2, 7 - chip // 2)
    steps, cross = [], []
    for hop in (1, 2, 3):
        steps += [-hop, hop, -hop, hop]
        cross += [0, 0, 1, 1]
    steps += [0, 0, 4, 4]
    cross += [0, 1, 0, 1]
    there = (place + jnp.array(steps, jnp.int32)) % 8
    chips = jnp.where(there < 4, 2 * there, 2 * (7 - there) + 1)
    return 2 * chips + (core ^ jnp.array(cross, jnp.int32))


def add_low(*parts):
    total = parts[0].astype(FULL)
    for part in parts[1:]:
        total = total + part.astype(FULL)
    return total.astype(LOW)


def together(value, *others):
    return lax.optimization_barrier((value, *others))


def ring_sum(same, cross, fillers):
    both = {hop: add_low(same[hop], swap_bit(cross[hop], "dp", 0)) for hop in (4, 3, 2, 1, 0)}
    rows = both[0].shape[0]
    cut = rows // 2
    done = []

    def fill(gate):
        for work, *operands in fillers[len(done)]:
            gate, *operands = together(gate, *operands)
            done_here.append(work(*operands))
        done.append(list(done_here))
        done_here.clear()
        return gate

    done_here = []
    right, left = ahead(both[4][:cut]), behind(both[4][cut:])
    left = fill(left)
    outward, inward = both[3][rows:], both[3][:rows]
    right = jnp.concatenate([add_low(outward[:cut], right), outward[cut:]], axis=0)
    left = jnp.concatenate([inward[:cut], add_low(inward[cut:], left)], axis=0)
    right, left = ahead(right), behind(left)
    left = fill(left)
    for hop in (2, 1):
        right = ahead(add_low(both[hop][rows:], right))
        left = behind(add_low(both[hop][:rows], left))
        if hop == 2:
            left = fill(left)
    total = both[0].astype(FULL) + right.astype(FULL) + left.astype(FULL)
    return total, [out for outs in done for out in outs]


def rms_norm(values, gain):
    return values * lax.rsqrt(jnp.mean(values * values, axis=-1, keepdims=True) + EPSILON) * gain


def rope_tables(positions, head_size):
    half_size = head_size // 2
    inverse = 10000.0 ** (-(jnp.arange(half_size, dtype=FULL) * 2.0) / head_size)
    angles = positions.astype(FULL)[:, None] * inverse[None, :]
    cosine = jnp.concatenate([jnp.cos(angles), jnp.cos(angles)], axis=-1)
    sine = jnp.concatenate([jnp.sin(angles), jnp.sin(angles)], axis=-1)
    return (cosine, sine)


def cont_positions(segment_row, gap_row, prompt_length):
    order = jnp.arange(segment_row.shape[0], dtype=jnp.int32)
    same = segment_row[:, None] == segment_row[None, :]
    earlier = order[None, :] < order[:, None]
    offset = jnp.sum((same & earlier).astype(jnp.int32), axis=1)
    labels = jnp.arange(gap_row.shape[0], dtype=jnp.int32)
    shifted = jnp.sum(
        jnp.where(segment_row[:, None] == labels[None, :], gap_row[None, :], 0), axis=1
    )
    return prompt_length + shifted + offset


def dot_nn(left, right):
    return jnp.dot(left, right, preferred_element_type=FULL)


def dot_tn(left, right):
    return lax.dot_general(left, right, (((0,), (0,)), ((), ())), preferred_element_type=FULL)


def dot_nt(left, right):
    return lax.dot_general(left, right, (((1,), (1,)), ((), ())), preferred_element_type=FULL)


def collect_prompt(own):
    near = swap_bit(own, "dp", 1)
    far = swap_bit(own, "dp", 2)
    last = jnp.stack([swap_bit(far[0], "dp", 1), swap_bit(near[1], "dp", 2)], axis=0)
    others = [swap_bit(piece, "dp", 0) for piece in (own, near, far, last)]
    return [others[0], near, others[1], far, others[2], last, others[3]]


def return_prompt(odd, even):
    got = swap_bit(odd, "dp", 0)
    near, far, last = (add_low(even[i], got[i + 1]) for i in range(3))
    keys = swap_bit(jnp.stack([near[0], last[0]], axis=0), "dp", 1)
    values = swap_bit(jnp.stack([far[1], last[1]], axis=0), "dp", 2)
    last_keys = swap_bit(add_low(far[0], keys[1]), "dp", 2)
    last_values = swap_bit(add_low(near[1], values[1]), "dp", 1)
    return (got[0, 0], keys[0], last_keys), (got[0, 1], values[0], last_values)


def turn(values):
    return pltpu.roll(values, HEAD // 2, 1)


def rope_kernel(q_ref, k_ref, gq_ref, gk_ref, sq_ref, sk_ref, cos_ref, sin_ref, qo_ref, ko_ref):
    for pre, gain, scale, out in (
        (q_ref, gq_ref, sq_ref, qo_ref),
        (k_ref, gk_ref, sk_ref, ko_ref),
    ):
        normed = pre[...] * scale[...] * gain[...]
        out[...] = (normed * cos_ref[...] + turn(normed) * sin_ref[...]).astype(LOW)


def head_spec(rows):
    return pl.BlockSpec((rows, HEAD), lambda h: (0, h))


def kept_spec(array):
    zeros = (0,) * array.ndim
    return pl.BlockSpec(array.shape, lambda h: zeros, pipeline_mode=pl.Buffered(1))


def piece_spec(count):
    return pl.BlockSpec((count, 2, PR_DEV, HEAD), lambda h: (0, 0, 0, h))


def rope_pass(query_flat, key_flat, gain_q, gain_k, scale_q, scale_k, cosine, sine):
    rows, width = query_flat.shape
    return pl.pallas_call(
        rope_kernel,
        grid=(width // HEAD,),
        in_specs=[head_spec(rows)] * 2
        + [head_spec(1)] * 2
        + [kept_spec(a) for a in (scale_q, scale_k, cosine, sine)],
        out_specs=[head_spec(rows)] * 2,
        out_shape=[jax.ShapeDtypeStruct((rows, width), LOW)] * 2,
    )(query_flat, key_flat, gain_q, gain_k, scale_q, scale_k, cosine, sine)


def all_keys(own_ref, pieces, which):
    return jnp.concatenate(
        [own_ref[:PR_DEV]] + [piece[0, which] for piece in pieces] + [own_ref[PR_DEV:]], axis=0
    )


def softmax_rows(query, keys, bias):
    scores = dot_nt(query, keys) * HEAD ** (-0.5) + bias
    weights = jnp.exp(scores - jnp.max(scores, axis=1, keepdims=True))
    return weights * (1.0 / jnp.sum(weights, axis=1, keepdims=True))


def attend_kernel(q_ref, k_ref, v_ref, bias_ref, *refs):
    pieces, out_ref = refs[:-1], refs[-1]
    probs = softmax_rows(
        q_ref[...], all_keys(k_ref, pieces, 0), bias_ref[...].astype(FULL)
    ).astype(LOW)
    out_ref[...] = dot_nn(probs, all_keys(v_ref, pieces, 1)).astype(LOW)


def attend(queries, keys, values, bias, pieces):
    rows, width = queries.shape
    pieces = [piece[None] for piece in pieces]
    return pl.pallas_call(
        attend_kernel,
        grid=(width // HEAD,),
        in_specs=[head_spec(rows)] * 3 + [kept_spec(bias)] + [piece_spec(1)] * len(pieces),
        out_specs=head_spec(rows),
        out_shape=jax.ShapeDtypeStruct((rows, width), LOW),
        compiler_params=pltpu.CompilerParams(vmem_limit_bytes=40 * 1024 * 1024),
    )(queries, keys, values, bias, *pieces)


def norm_parts(step, grad, flat_ref, gain_ref, scale_ref, inner_ref, gain_grad_ref):
    product = flat_ref[...] * grad
    inner = jnp.sum(product * gain_ref[...], axis=1, keepdims=True)
    gain_grad_ref[...] = jnp.sum(product * scale_ref[...], axis=0, keepdims=True)

    @pl.when(step == 0)
    def _():
        inner_ref[...] = inner

    @pl.when(step > 0)
    def _():
        inner_ref[...] += inner


def attend_back_kernel(*refs):
    q_ref, k_ref, v_ref, bias_ref, back_ref, flat_ref, gain_ref, scale_ref, cos_ref, sin_ref = (
        refs[:10]
    )
    pieces = refs[10 : 10 + GROUP - 1]
    qg_ref, inner_ref, gain_grad_ref, kg_ref, vg_ref, odd_ref, even_ref = refs[10 + GROUP - 1 :]
    step = pl.program_id(0)
    query, keys, values = q_ref[...], all_keys(k_ref, pieces, 0), all_keys(v_ref, pieces, 1)
    back = back_ref[...]
    probs = softmax_rows(query, keys, bias_ref[...].astype(FULL))
    prob_grad = dot_nt(back, values)
    value_grad = dot_tn(probs.astype(LOW), back)
    row_dot = jnp.sum(probs * prob_grad, axis=1, keepdims=True)
    score_grad = (probs * (prob_grad - row_dot)).astype(LOW)
    query_grad = dot_nn(score_grad, keys) * HEAD ** (-0.5)
    key_grad = dot_tn(score_grad, query) * HEAD ** (-0.5)
    query_grad = query_grad * cos_ref[...] - turn(query_grad) * sin_ref[...]
    qg_ref[...] = query_grad
    norm_parts(step, query_grad, flat_ref, gain_ref, scale_ref, inner_ref, gain_grad_ref)
    prompt = PR_DEV * GROUP
    for which, grad, own_ref in ((0, key_grad, kg_ref), (1, value_grad, vg_ref)):
        own_ref[:PR_DEV] = grad[:PR_DEV]
        own_ref[PR_DEV:] = grad[prompt:]
        for j in range(1, GROUP):
            to = odd_ref if j % 2 else even_ref
            to[(j - 1) // 2, which] = grad[j * PR_DEV : (j + 1) * PR_DEV].astype(LOW)


def attend_back(queries, keys, values, bias, back, flat, gain, scale, cosine, sine, pieces):
    rows, width = queries.shape
    pieces = [piece[None] for piece in pieces]
    wide = jax.ShapeDtypeStruct((rows, width), FULL)
    return pl.pallas_call(
        attend_back_kernel,
        grid=(width // HEAD,),
        in_specs=[head_spec(rows)] * 3
        + [kept_spec(bias), head_spec(rows), head_spec(rows), head_spec(1)]
        + [kept_spec(a) for a in (scale, cosine, sine)]
        + [piece_spec(1)] * len(pieces),
        out_specs=[
            head_spec(rows),
            pl.BlockSpec((rows, 1), lambda h: (0, 0)),
            head_spec(1),
            head_spec(rows),
            head_spec(rows),
            piece_spec(4),
            piece_spec(3),
        ],
        out_shape=[
            wide,
            jax.ShapeDtypeStruct((rows, 1), FULL),
            jax.ShapeDtypeStruct((1, width), FULL),
            wide,
            wide,
            jax.ShapeDtypeStruct((4, 2, PR_DEV, width), LOW),
            jax.ShapeDtypeStruct((3, 2, PR_DEV, width), LOW),
        ],
        compiler_params=pltpu.CompilerParams(vmem_limit_bytes=58 * 1024 * 1024),
    )(queries, keys, values, bias, back, flat, gain, scale, cosine, sine, *pieces)


def key_back_kernel(*refs):
    kg_ref, vg_ref, flat_ref, gain_ref, scale_ref, cos_ref, sin_ref = refs[:7]
    key_parts, value_parts = refs[7:10], refs[10:13]
    out_ref, inner_ref, gain_grad_ref, value_ref = refs[13:]
    step = pl.program_id(0)
    grads = []
    for own_ref, parts in ((kg_ref, key_parts), (vg_ref, value_parts)):
        first = own_ref[:PR_DEV]
        for part in parts:
            first = first + part[...].astype(FULL)
        grads.append(jnp.concatenate([first, own_ref[PR_DEV:]], axis=0))
    key_grad = grads[0] * cos_ref[...] - turn(grads[0]) * sin_ref[...]
    out_ref[...] = key_grad
    norm_parts(step, key_grad, flat_ref, gain_ref, scale_ref, inner_ref, gain_grad_ref)
    value_ref[...] = grads[1].astype(LOW)


def key_back(key_grad, value_grad, flat, gain, scale, cosine, sine, key_parts, value_parts):
    rows, width = flat.shape
    return pl.pallas_call(
        key_back_kernel,
        grid=(width // HEAD,),
        in_specs=[head_spec(rows)] * 3
        + [head_spec(1)]
        + [kept_spec(a) for a in (scale, cosine, sine)]
        + [head_spec(PR_DEV)] * 6,
        out_specs=[
            head_spec(rows),
            pl.BlockSpec((rows, 1), lambda h: (0, 0)),
            head_spec(1),
            head_spec(rows),
        ],
        out_shape=[
            jax.ShapeDtypeStruct((rows, width), FULL),
            jax.ShapeDtypeStruct((rows, 1), FULL),
            jax.ShapeDtypeStruct((1, width), FULL),
            jax.ShapeDtypeStruct((rows, width), LOW),
        ],
    )(key_grad, value_grad, flat, gain, scale, cosine, sine, *key_parts, *value_parts)


def ring_weights(first, second):
    rows = first.shape[0] // len(RING)
    cut = (first.shape[1] + second.shape[1]) // 2
    chip = lax.axis_index("dp") // 2
    place = jnp.where(chip % 2 == 0, chip // 2, 7 - chip // 2)

    def part(hop):
        there = (place + hop) % len(RING)
        at = jnp.where(there < 4, 2 * there, 2 * (7 - there) + 1) * rows
        return jnp.concatenate(
            [lax.dynamic_slice_in_dim(a, at, rows, axis=0) for a in (first, second)], axis=1
        )

    far = part(4)
    right, left = ahead(far[:, :cut]), behind(far[:, cut:])
    outward, inward = part(3), part(-3)
    right = jnp.concatenate([add_low(outward[:, :cut], right), outward[:, cut:]], axis=1)
    left = jnp.concatenate([inward[:, :cut], add_low(inward[:, cut:], left)], axis=1)
    right, left = ahead(right), behind(left)
    for hop in (2, 1):
        right, left = ahead(add_low(part(hop), right)), behind(add_low(part(-hop), left))
    return part(0).astype(FULL) + right.astype(FULL) + left.astype(FULL)


def expert_kernel(
    rows_ref, back_ref, gate_ref, wg0, wg1, wu0, wu1, wd0, wd1, grad_ref, h0, h1, g0, g1, u0, u1
):
    rows = rows_ref[...]
    back = back_ref[...]
    gate = gate_ref[...]
    total = None
    for wg, wu, wd, h, g, u in ((wg0, wu0, wd0, h0, g0, u0), (wg1, wu1, wd1, h1, g1, u1)):
        gate_pre = dot_nn(rows, wg[...])
        up_pre = dot_nn(rows, wu[...])
        hidden_grad = gate * dot_nt(back, wd[...])
        sig = 1.0 / (1.0 + jnp.exp(-gate_pre))
        act = gate_pre * sig
        h[...] = (gate * (act * up_pre)).astype(LOW)
        gate_grad = (hidden_grad * up_pre * (sig * (1.0 + gate_pre * (1.0 - sig)))).astype(LOW)
        up_grad = (hidden_grad * act).astype(LOW)
        g[...] = gate_grad
        u[...] = up_grad
        part = dot_nt(gate_grad, wg[...]) + dot_nt(up_grad, wu[...])
        total = part if total is None else total + part
    grad_ref[...] = total.astype(LOW)


def expert_pass(rows, back, gate, gate_mats, up_mats, down_mats):
    count, width = rows.shape
    hidden = gate_mats[0].shape[1]
    tile = 256
    whole = lambda array: pl.BlockSpec(
        array.shape, lambda i: (0, 0), pipeline_mode=pl.Buffered(1)
    )
    tall = lambda columns: pl.BlockSpec((tile, columns), lambda i: (i, 0))
    mats = [*gate_mats, *up_mats, *down_mats]
    flops = 2 * 5 * count * width * hidden * 2
    return pl.pallas_call(
        expert_kernel,
        grid=(count // tile,),
        in_specs=[tall(width), tall(width), tall(1)] + [whole(m) for m in mats],
        out_specs=[tall(width)] + [tall(hidden)] * 6,
        out_shape=[jax.ShapeDtypeStruct((count, width), LOW)]
        + [jax.ShapeDtypeStruct((count, hidden), LOW)] * 6,
        compiler_params=pltpu.CompilerParams(vmem_limit_bytes=58 * 1024 * 1024),
        cost_estimate=pl.CostEstimate(
            flops=flops,
            bytes_accessed=2 * (3 * count * width + 6 * count * hidden + 6 * width * hidden),
            transcendentals=2 * count * hidden,
        ),
    )(rows, back, gate, *mats)


def chunk_kernel(pieces, first, *refs):
    piece_refs, refs = refs[:pieces], refs[pieces:]
    back_ref, gate_ref, wg0, wg1, wu0, wu1, wd0, wd1, vg0, vg1, vu0, vu1 = refs[:12]
    same_ref, cross_ref, rows_ref, h0, h1, g0, g1, u0, u1, kept_g, kept_u = refs[
        12 if first else 19 :
    ]
    step = pl.program_id(0)

    @pl.when(step == 0)
    def _():
        at = 0
        for piece in piece_refs:
            rows_ref[at : at + piece.shape[0]] = piece[...]
            at += piece.shape[0]

    def work(wg, wu, wd, h, g, u):
        rows = rows_ref[...]
        gate = gate_ref[...]
        gate_pre = dot_nn(rows, wg[...])
        up_pre = dot_nn(rows, wu[...])
        hidden_grad = gate * dot_nt(back_ref[...], wd[...])
        sig = 1.0 / (1.0 + jnp.exp(-gate_pre))
        act = gate_pre * sig
        h[...] = (gate * (act * up_pre)).astype(LOW)
        gate_grad = (hidden_grad * up_pre * (sig * (1.0 + gate_pre * (1.0 - sig)))).astype(LOW)
        up_grad = (hidden_grad * act).astype(LOW)
        g[...] = gate_grad
        u[...] = up_grad
        kept_g[step] = gate_grad
        kept_u[step] = up_grad

    @pl.when(step < 2)
    def _():
        work(wg0, wu0, wd0, h0, g0, u0)

    @pl.when((step >= 2) & (step < 4))
    def _():
        work(wg1, wu1, wd1, h1, g1, u1)

    @pl.when(step >= 4)
    def _():
        total = None
        for kept, first_half, second_half in ((kept_g, vg0, vg1), (kept_u, vu0, vu1)):
            for at, mat in ((0, first_half), (2, second_half)):
                left = jnp.concatenate([kept[at], kept[at + 1]], axis=1)
                part = dot_nt(left, mat[...])
                total = part if total is None else total + part
        half = same_ref.shape[0]
        same_ref[...] = total[:half].astype(LOW)
        cross_ref[...] = total[half:].astype(LOW)


def expert_chunk(pieces, back, gate, mats, at, held):
    width = back.shape[1]
    hidden = mats[0].shape[1]
    part = hidden // 2
    slab = width // 4
    count = sum(piece.shape[0] for piece in pieces)
    all_rows = back.shape[0]
    own = lambda j: jnp.minimum(j, 1)
    other = lambda j: jnp.clip(j - 2, 0, 1)
    late = lambda j: jnp.maximum(j - 4, 0)
    once = pl.Buffered(1)
    fixed = lambda array: pl.BlockSpec(array.shape, lambda j: (0, 0), pipeline_mode=once)
    chunk = lambda columns, **mode: pl.BlockSpec((count, columns), lambda j: (at, 0), **mode)
    tall = lambda pick: pl.BlockSpec((width, part), lambda j: (0, pick(j)))
    flat = lambda pick: pl.BlockSpec((part, width), lambda j: (pick(j), 0))
    narrow = lambda pick: pl.BlockSpec((count, part), lambda j: (at, pick(j)))
    again = lambda: pl.BlockSpec((slab, hidden), lambda j: (late(j), 0))
    whole = lambda: pl.BlockSpec((count // 2, slab), lambda j: (0, late(j)))
    held_specs = [] if held is None else [pl.BlockSpec(memory_space=pl.ANY)] * 7
    held_args = [] if held is None else list(held)
    base = len(pieces) + 12
    wide = jax.ShapeDtypeStruct((all_rows, hidden), LOW)
    out = pl.pallas_call(
        lambda *refs: chunk_kernel(len(pieces), held is None, *refs),
        grid=(8,),
        in_specs=[fixed(piece) for piece in pieces]
        + [chunk(width, pipeline_mode=once), chunk(1, pipeline_mode=once)]
        + [tall(own), tall(other), tall(own), tall(other), flat(own), flat(other)]
        + [again(), again(), again(), again()]
        + held_specs,
        out_specs=[whole(), whole(), chunk(width)] + [narrow(own), narrow(other)] * 3,
        out_shape=[jax.ShapeDtypeStruct((count // 2, width), LOW)] * 2
        + [jax.ShapeDtypeStruct((all_rows, width), LOW)]
        + [wide] * 6,
        scratch_shapes=[pltpu.VMEM((4, count, part), LOW)] * 2,
        input_output_aliases={} if held is None else {base + k: 2 + k for k in range(7)},
        compiler_params=pltpu.CompilerParams(vmem_limit_bytes=58 * 1024 * 1024),
        cost_estimate=pl.CostEstimate(
            flops=2 * 5 * count * width * hidden * 2,
            bytes_accessed=2 * (3 * count * width + 6 * count * hidden + 6 * width * hidden),
            transcendentals=2 * count * hidden,
        ),
    )(*pieces, back, gate, *mats, *mats[:4], *held_args)
    return out[0], out[1], out[2:]


def expert_ring(rows, back, gate, mats):
    cut = rows.shape[0] // 2
    same, cross = {}, {}
    left, right = ahead(rows), behind(rows)
    swap = lambda block: swap_bit(block, "dp", 0)
    same[0], cross[0], held = expert_chunk([rows, swap(rows)], back, gate, mats, 6, None)
    for hop in (1, 2, 3):
        pieces = [left, right, swap(left), swap(right)]
        if hop < 3:
            left, right = ahead(left), behind(right)
        else:
            left, right = ahead(left[:cut]), behind(right[cut:])
        same[hop], cross[hop], held = expert_chunk(pieces, back, gate, mats, hop - 1, held)
    pieces = [left, right, swap(left), swap(right)]
    same[4], cross[4], held = expert_chunk(pieces, back, gate, mats, 7, held)
    return same, cross, held


def halving_sum(parts):
    bits = parts.shape[0].bit_length() - 1
    index = lax.axis_index("dp")
    for bit in reversed(range(bits)):
        rows = parts.shape[0] // 2
        upper = index >> bit & 1
        kept = lax.dynamic_slice_in_dim(parts, upper * rows, rows, axis=0)
        sent = lax.dynamic_slice_in_dim(parts, (1 - upper) * rows, rows, axis=0)
        parts = kept + swap_bit(sent, "dp", bit)
    return parts[0]


def body(
    inputs,
    attn_gain,
    w_query,
    w_key,
    w_value,
    query_gain,
    key_gain,
    w_out,
    moe_gain,
    w_gate,
    w_up,
    w_down,
    experts,
    gates,
    segments,
    gaps,
    cotangent,
):
    dp_count = lax.axis_size("dp")
    dp_index = lax.axis_index("dp")
    side = lax.axis_index("tensor")
    token_count, model_width = inputs.shape
    half_count = token_count // 2
    top_count = experts.shape[1]
    expert_count = w_gate.shape[0] * dp_count
    capacity = token_count * top_count * dp_count * 9 // (8 * expert_count)
    prompt_length = PR_DEV * GROUP
    column_total = HEADS * HEAD
    block = w_query.shape[0]
    local_width = w_query.shape[1]
    local_heads = local_width // HEAD

    def own_half(array):
        return lax.dynamic_slice_in_dim(array, side * half_count, half_count, axis=0)

    def other_half(array):
        return lax.dynamic_slice_in_dim(array, (1 - side) * half_count, half_count, axis=0)

    def both_halves(own, other):
        first = side == 0
        return jnp.concatenate(
            [jnp.where(first, own, other), jnp.where(first, other, own)], axis=0
        )

    gate_mats = (w_gate[0], swap_tensor(w_gate[0]))
    up_mats = (w_up[0], swap_tensor(w_up[0]))

    ring = dp_count == 2 * len(RING)

    gates_high = gates.astype(LOW)
    gates_low = (gates - gates_high.astype(FULL)).astype(LOW)
    routing = jnp.concatenate([experts.astype(LOW).T, gates_high.T, gates_low.T], axis=1)
    routing = jnp.pad(routing, ((0, 0), (0, local_width - 3 * token_count)))
    gains = jnp.concatenate([attn_gain, moe_gain, query_gain, key_gain])
    gains = jnp.pad(gains[None], ((0, 7), (0, local_width - 4 * block)))
    packed = jnp.concatenate([w_query, w_key, w_value, w_out.T, gains, routing], axis=0)
    gathered = lax.all_gather(packed, "dp", axis=0, tiled=False)
    gathered, *early = lax.optimization_barrier((gathered, gate_mats[1], up_mats[1]))
    gate_mats, up_mats = (gate_mats[0], early[0]), (up_mats[0], early[1])
    full_q = gathered[:, :block].reshape(model_width, local_width)
    full_k = gathered[:, block : 2 * block].reshape(model_width, local_width)
    full_v = gathered[:, 2 * block : 3 * block].reshape(model_width, local_width)
    full_o = gathered[:, 3 * block : 4 * block].reshape(model_width, local_width)
    gain_rows = gathered[:, 4 * block].astype(FULL)
    gain_one, gain_two, gain_q, gain_k = (
        gain_rows[:, j * block : (j + 1) * block].reshape(-1) for j in range(4)
    )
    gain_query_local = lax.dynamic_slice_in_dim(gain_q, side * local_width, local_width)
    gain_key_local = lax.dynamic_slice_in_dim(gain_k, side * local_width, local_width)

    names = gathered[:, 4 * block + 8 :, :token_count]
    weights = gathered[:, 4 * block + 8 :, token_count : 2 * token_count].astype(
        FULL
    ) + gathered[:, 4 * block + 8 :, 2 * token_count : 3 * token_count].astype(FULL)
    named = names == dp_index.astype(LOW)
    picked = jnp.sum(named.astype(FULL), axis=1)
    weight = jnp.sum(jnp.where(named, weights, 0.0), axis=1)
    order = jnp.arange(token_count, dtype=jnp.int32)
    earlier = (order[:, None] < order[None, :]).astype(LOW)
    within = dot_nn(picked.astype(LOW), earlier)
    per_row = jnp.sum(picked, axis=1)
    rows_order = jnp.arange(dp_count, dtype=jnp.int32)
    ahead = jnp.sum(
        jnp.where(rows_order[None, :] < rows_order[:, None], per_row[None, :], 0.0), axis=1
    )
    kept = (picked > 0.0) & (within + ahead[:, None] < capacity)
    weight = jnp.where(kept, weight, 0.0)
    weight = lax.dynamic_slice_in_dim(weight, side * half_count, half_count, axis=1)
    if ring:
        blocks = ring_blocks(dp_index)
        weight = weight[blocks]
    weight = weight.reshape(-1, 1)

    cotangent_half = own_half(cotangent)
    back_rows = lax.all_gather(cotangent_half.astype(LOW), "dp", axis=0, tiled=False)
    back_rows = (back_rows[blocks] if ring else back_rows).reshape(-1, model_width)

    core = dp_index % 2
    tokens_f = inputs.astype(FULL)
    prompt_pos = dp_index % GROUP * PR_DEV + jnp.arange(PR_DEV, dtype=jnp.int32)
    later_pos = cont_positions(segments[0], gaps[0], prompt_length)
    positions = jnp.concatenate([prompt_pos, later_pos], axis=0)
    cosine, sine = rope_tables(positions, HEAD)
    sine = jnp.where(jnp.arange(HEAD) < HEAD // 2, -sine, sine)
    prompt_query = jnp.arange(token_count, dtype=jnp.int32) < PR_DEV
    prompt_at = jnp.arange(prompt_length, dtype=jnp.int32)
    prompt_keypos = ((dp_index % GROUP) ^ (prompt_at // PR_DEV)) * PR_DEV + prompt_at % PR_DEV
    allowed_prompt = (~prompt_query)[:, None] | (prompt_keypos[None, :] <= positions[:, None])
    query_segment = jnp.concatenate([jnp.full((PR_DEV,), -1, jnp.int32), segments[0]], axis=0)
    allowed_cont = (query_segment[:, None] == segments[0][None, :]) & (
        later_pos[None, :] <= positions[:, None]
    )
    allowed = jnp.concatenate([allowed_prompt, allowed_cont], axis=1)
    bias = jnp.where(allowed, 0.0, -1e30).astype(LOW)
    normed_b = rms_norm(tokens_f, gain_one).astype(LOW)
    query_flat = dot_nn(normed_b, full_q)
    key_flat = dot_nn(normed_b, full_k)
    values_b = dot_nn(normed_b, full_v).astype(LOW)
    query_sq, key_sq = lax.psum(
        (jnp.sum(query_flat * query_flat, axis=1), jnp.sum(key_flat * key_flat, axis=1)), "tensor"
    )
    query_sq, down_mat = lax.optimization_barrier((query_sq, w_down[0]))
    down_mats = (down_mat, swap_tensor(down_mat))
    query_scale = lax.rsqrt(query_sq / column_total + EPSILON)[:, None]
    key_scale = lax.rsqrt(key_sq / column_total + EPSILON)[:, None]
    queries_b, keys_b = rope_pass(
        query_flat,
        key_flat,
        gain_query_local[None],
        gain_key_local[None],
        query_scale,
        key_scale,
        cosine,
        sine,
    )
    pieces = collect_prompt(jnp.stack([keys_b[:PR_DEV], values_b[:PR_DEV]], axis=0))
    context_b = attend(queries_b, keys_b, values_b, bias, pieces)
    attn_part = dot_nt(context_b, full_o)
    attn_part, late = lax.optimization_barrier((attn_part, down_mats[1]))
    down_mats = (down_mats[0], late)
    mats = (*gate_mats, *up_mats, *down_mats)
    attn_other = swap_tensor(other_half(attn_part).astype(LOW))
    hidden_state = (
        own_half(tokens_f) + own_half(attn_part) + attn_other.astype(FULL)
    )
    normed_two_b = rms_norm(hidden_state, gain_two).astype(LOW)

    low_tn = lambda left, right: dot_tn(left, right).astype(LOW)
    if ring:
        same, cross, held = expert_ring(normed_two_b, back_rows, weight, mats)
        expert_in, h0, h1, g0, g1, u0, u1 = held
        down_sent = low_tn(h1, back_rows)
        down_got = swap_tensor(down_sent)
        normed_two_grad, outs = ring_sum(
            same,
            cross,
            [
                [(low_tn, expert_in, g1), (low_tn, expert_in, u1)],
                [(lambda a, b: dot_nn(a, down_mats[0]) + dot_nn(b, down_mats[1]), h0, h1)],
                [(dot_tn, h0, back_rows), (dot_tn, expert_in, g0), (dot_tn, expert_in, u0)],
            ],
        )
        gate_sent, up_sent, mixed_rows, down_grad, gate_w_grad, up_w_grad = outs
        mixed_rows = mixed_rows.astype(LOW)
        gate_got = swap_tensor(gate_sent)
    else:
        expert_in = lax.all_gather(normed_two_b, "dp", axis=0, tiled=True)
        grad_rows, h0, h1, g0, g1, u0, u1 = expert_pass(
            expert_in, back_rows, weight, gate_mats, up_mats, down_mats
        )
        normed_two_grad = lax.psum_scatter(
            grad_rows, "dp", scatter_dimension=0, tiled=True
        ).astype(FULL)
        mixed_rows = (dot_nn(h0, down_mats[0]) + dot_nn(h1, down_mats[1])).astype(LOW)
        down_got = swap_tensor(low_tn(h1, back_rows))
        gate_got = swap_tensor(low_tn(expert_in, g1))
        up_sent = low_tn(expert_in, u1)
        down_grad = dot_tn(h0, back_rows)
        gate_w_grad = dot_tn(expert_in, g0)
        up_w_grad = dot_tn(expert_in, u0)
    normed_two_grad, down_got, gate_got, mixed_rows, down_grad, gate_w_grad, up_w_grad = together(
        normed_two_grad, down_got, gate_got, mixed_rows, down_grad, gate_w_grad, up_w_grad
    )
    if ring:
        back_to = jnp.argsort(blocks)
        mixed_rows = mixed_rows.reshape(dp_count, half_count, model_width)[back_to].reshape(
            -1, model_width
        )
    mixed = lax.psum_scatter(mixed_rows, "dp", scatter_dimension=0, tiled=True).astype(FULL)
    output_half = hidden_state + mixed

    unused_two, norm_two_back = jax.vjp(rms_norm, hidden_state, gain_two)
    state_part, gain_two_grad = norm_two_back(normed_two_grad)
    state_half = cotangent_half + state_part
    attn_grad_half = state_half.astype(LOW)
    attn_grad_b = both_halves(attn_grad_half, swap_tensor(attn_grad_half))
    attn_grad_b, up_sent = together(attn_grad_b, up_sent)
    up_got = swap_tensor(up_sent)
    context_grad_b = dot_nn(attn_grad_b, full_o).astype(LOW)
    query_normed_grad, query_inner, query_gain_part, key_grad, value_grad, odd, even = attend_back(
        queries_b,
        keys_b,
        values_b,
        bias,
        context_grad_b,
        query_flat,
        gain_query_local[None],
        query_scale,
        cosine,
        sine,
        pieces,
    )
    key_parts, value_parts = return_prompt(odd, even)
    key_normed_grad, key_inner, key_gain_part, value_pre_grad = key_back(
        key_grad,
        value_grad,
        key_flat,
        gain_key_local[None],
        key_scale,
        cosine,
        sine,
        key_parts,
        value_parts,
    )
    query_inner, key_inner, up_got = together(query_inner, key_inner, up_got)
    query_inner, key_inner = lax.psum((query_inner[:, 0], key_inner[:, 0]), "tensor")
    query_cube = query_scale * query_scale * query_scale
    key_cube = key_scale * key_scale * key_scale
    query_pre_grad = (
        query_scale * gain_query_local * query_normed_grad
        - query_flat * query_cube * (query_inner / column_total)[:, None]
    ).astype(LOW)
    key_pre_grad = (
        key_scale * gain_key_local * key_normed_grad
        - key_flat * key_cube * (key_inner / column_total)[:, None]
    ).astype(LOW)
    wide = lambda part: lax.dynamic_update_slice_in_dim(
        jnp.zeros((column_total,), FULL), part, side * local_width, 0
    )
    pre_grads = (query_pre_grad, key_pre_grad, value_pre_grad)
    if ring:
        columns = local_width // 2
        mine = lambda a: lax.dynamic_slice_in_dim(a, core * columns, columns, axis=1)
        theirs = lambda a: lax.dynamic_slice_in_dim(a, (1 - core) * columns, columns, axis=1)
        pair = lambda own, sent: jnp.concatenate([own, swap_bit(sent, "dp", 0)], axis=0)
        normed_pair = pair(normed_b, normed_b)
        attn_grad_pair = pair(attn_grad_b, attn_grad_b)
        context_pair = pair(mine(context_b), theirs(context_b))
        grad_pair = pair(
            jnp.concatenate([mine(g) for g in pre_grads], axis=1),
            jnp.concatenate([theirs(g) for g in pre_grads], axis=1),
        )
        w_half = ring_weights(low_tn(normed_pair, grad_pair), low_tn(attn_grad_pair, context_pair))
        own_w = lax.dynamic_slice_in_dim(w_half, core * block, block, axis=0)
        got_w = swap_bit(lax.dynamic_slice_in_dim(w_half, (1 - core) * block, block, axis=0), "dp", 0)
        left_w, right_w = jnp.where(core == 0, own_w, got_w), jnp.where(core == 0, got_w, own_w)
        w_sums = [
            jnp.concatenate([w[:, j * columns : (j + 1) * columns] for w in (left_w, right_w)], axis=1)
            for j in range(4)
        ]
    else:
        w_grads = jnp.concatenate(
            [low_tn(normed_b, g) for g in pre_grads] + [low_tn(attn_grad_b, context_b)], axis=1
        )
        w_sum = lax.psum_scatter(w_grads, "dp", scatter_dimension=0, tiled=True).astype(FULL)
        w_sums = [w_sum[:, j * local_width : (j + 1) * local_width] for j in range(4)]
    down_grad = down_grad + down_got.astype(FULL)
    gate_w_grad = gate_w_grad + gate_got.astype(FULL)
    up_w_grad = up_w_grad + up_got.astype(FULL)
    output = both_halves(output_half, swap_tensor(output_half))
    normed_part = (
        dot_nt(query_pre_grad, full_q)
        + dot_nt(key_pre_grad, full_k)
        + dot_nt(value_pre_grad, full_v)
    )
    normed_other = swap_tensor(other_half(normed_part).astype(LOW))
    normed_grad = own_half(normed_part) + normed_other.astype(FULL)
    unused_one, norm_one_back = jax.vjp(rms_norm, own_half(tokens_f), gain_one)
    input_part, gain_one_grad = norm_one_back(normed_grad)
    input_half = state_half + input_part
    input_grad = both_halves(input_half, swap_tensor(input_half))
    gain_grads = jnp.stack(
        [gain_one_grad, gain_two_grad, wide(query_gain_part[0]), wide(key_gain_part[0])]
    ).reshape(4, dp_count, block)
    gain_sums = halving_sum(jnp.swapaxes(gain_grads, 0, 1))
    gain_sums = gain_sums + swap_tensor(gain_sums)
    return (
        output,
        input_grad,
        gain_sums[0],
        w_sums[0],
        w_sums[1],
        w_sums[2],
        gain_sums[2],
        gain_sums[3],
        w_sums[3].T,
        gain_sums[1],
        gate_w_grad[None],
        up_w_grad[None],
        down_grad[None],
    )


def solution(mesh):
    return jax.shard_map(
        body,
        mesh=mesh,
        in_specs=(
            P("dp", None),
            P("dp"),
            P("dp", "tensor"),
            P("dp", "tensor"),
            P("dp", "tensor"),
            P("dp"),
            P("dp"),
            P("tensor", "dp"),
            P("dp"),
            P("dp", None, "tensor"),
            P("dp", None, "tensor"),
            P("dp", "tensor", None),
            P("dp", None),
            P("dp", None),
            P("dp", None),
            P("dp", None),
            P("dp", None),
        ),
        out_specs=(
            P("dp", None),
            P("dp", None),
            P("dp"),
            P("dp", "tensor"),
            P("dp", "tensor"),
            P("dp", "tensor"),
            P("dp"),
            P("dp"),
            P("tensor", "dp"),
            P("dp"),
            P("dp", None, "tensor"),
            P("dp", None, "tensor"),
            P("dp", "tensor", None),
        ),
        check_vma=False,
    )
```

```python
import jax
import jax.numpy as jnp
from jax import lax
from jax.experimental import pallas as pl
from jax.experimental.pallas import tpu as pltpu
from jax.sharding import PartitionSpec as P

HEADS = 16
HEAD = 128
GROUP = 8
PR_DEV = 128


EPSILON = 1e-05
LOW = jnp.bfloat16
FULL = jnp.float32


def swap_bit(block, axis, bit):
    count = lax.axis_size(axis)
    return lax.ppermute(block, axis, [(i, i ^ (1 << bit)) for i in range(count)])


def swap_tensor(block):
    return lax.ppermute(block, "tensor", [(0, 1), (1, 0)])


RING = (0, 2, 4, 6, 7, 5, 3, 1)
AHEAD = [
    (RING[p] * 2 + c, RING[(p + 1) % len(RING)] * 2 + c) for p in range(len(RING)) for c in range(2)
]
BEHIND = [(to, at) for at, to in AHEAD]
HOPS = (-1, 1, -2, 2, -3, 3, 0, 4)


def ahead(block):
    return lax.ppermute(block, "dp", AHEAD)


def behind(block):
    return lax.ppermute(block, "dp", BEHIND)


def ring_blocks(dp_index):
    chip, core = dp_index // 2, dp_index % 2
    place = jnp.where(chip % 2 == 0, chip // 2, 7 - chip // 2)
    steps, cross = [], []
    for hop in HOPS:
        steps += [hop, hop]
        cross += [0, 1]
    there = (place + jnp.array(steps, jnp.int32)) % 8
    chips = jnp.where(there < 4, 2 * there, 2 * (7 - there) + 1)
    return 2 * chips + (core ^ jnp.array(cross, jnp.int32))


def add_low(*parts):
    total = parts[0].astype(FULL)
    for part in parts[1:]:
        total = total + part.astype(FULL)
    return total.astype(LOW)


def together(value, *others):
    return lax.optimization_barrier((value, *others))


class Fillers:
    def __init__(self, stages):
        self.stages = list(stages)
        self.outs = []

    def next(self, gate):
        for work, *operands in self.stages.pop(0) if self.stages else ():
            gate, *operands = together(gate, *operands)
            self.outs.append(work(*operands))
        return gate


def ring_sum(same, cross, fillers):
    both = {hop: add_low(same[hop], swap_bit(cross[hop], "dp", 0)) for hop in (4, 3, 2, 1, 0)}
    rows = both[0].shape[0]
    cut = rows // 2
    right, left = ahead(both[4][:cut]), behind(both[4][cut:])
    left = fillers.next(left)
    outward, inward = both[3][rows:], both[3][:rows]
    right = jnp.concatenate([add_low(outward[:cut], right), outward[cut:]], axis=0)
    left = jnp.concatenate([inward[:cut], add_low(inward[cut:], left)], axis=0)
    right, left = ahead(right), behind(left)
    left = fillers.next(left)
    for hop in (2, 1):
        right = ahead(add_low(both[hop][rows:], right))
        left = behind(add_low(both[hop][:rows], left))
        left = fillers.next(left)
    return both[0].astype(FULL) + right.astype(FULL) + left.astype(FULL)


def rms_norm(values, gain):
    return values * lax.rsqrt(jnp.mean(values * values, axis=-1, keepdims=True) + EPSILON) * gain


def rope_tables(positions, head_size):
    half_size = head_size // 2
    inverse = 10000.0 ** (-(jnp.arange(half_size, dtype=FULL) * 2.0) / head_size)
    angles = positions.astype(FULL)[:, None] * inverse[None, :]
    cosine = jnp.concatenate([jnp.cos(angles), jnp.cos(angles)], axis=-1)
    sine = jnp.concatenate([jnp.sin(angles), jnp.sin(angles)], axis=-1)
    return (cosine, sine)


def cont_positions(segment_row, gap_row, prompt_length):
    order = jnp.arange(segment_row.shape[0], dtype=jnp.int32)
    same = segment_row[:, None] == segment_row[None, :]
    earlier = order[None, :] < order[:, None]
    offset = jnp.sum((same & earlier).astype(jnp.int32), axis=1)
    labels = jnp.arange(gap_row.shape[0], dtype=jnp.int32)
    shifted = jnp.sum(
        jnp.where(segment_row[:, None] == labels[None, :], gap_row[None, :], 0), axis=1
    )
    return prompt_length + shifted + offset


def dot_nn(left, right):
    return jnp.dot(left, right, preferred_element_type=FULL)


def dot_tn(left, right):
    return lax.dot_general(left, right, (((0,), (0,)), ((), ())), preferred_element_type=FULL)


def dot_nt(left, right):
    return lax.dot_general(left, right, (((1,), (1,)), ((), ())), preferred_element_type=FULL)


def collect_prompt(own, first, second):
    near, far = swap_bit(own, "dp", 1), swap_bit(own, "dp", 2)
    last = swap_bit(near if first == 1 else far, "dp", second)
    stay = jnp.stack([own, near, far, last], axis=0)
    return stay, swap_bit(stay, "dp", 0)


def return_prompt(odd, even):
    got = swap_bit(odd, "dp", 0)
    near, far, last = (add_low(even[i], got[i + 1]) for i in range(3))
    keys = swap_bit(jnp.stack([near[0], last[0]], axis=0), "dp", 1)
    values = swap_bit(jnp.stack([far[1], last[1]], axis=0), "dp", 2)
    last_keys = swap_bit(add_low(far[0], keys[1]), "dp", 2)
    last_values = swap_bit(add_low(near[1], values[1]), "dp", 1)
    return (got[0, 0], keys[0], last_keys), (got[0, 1], values[0], last_values)


def turn(values):
    return pltpu.roll(values, HEAD // 2, 1)


def rope_kernel(pre_ref, gain_ref, scale_ref, cos_ref, sin_ref, out_ref):
    scale, cosine, sine = scale_ref[...], cos_ref[...], sin_ref[...]
    for at in range(0, pre_ref.shape[1], HEAD):
        span = slice(at, at + HEAD)
        normed = pre_ref[:, span] * scale * gain_ref[:, span]
        out_ref[:, span] = (normed * cosine + turn(normed) * sine).astype(LOW)


def rope_pass(flat, gain, scale, cosine, sine):
    rows, width = flat.shape
    part = width // 2
    wide = lambda rows: pl.BlockSpec((rows, part), lambda h: (0, h))
    return pl.pallas_call(
        rope_kernel,
        grid=(2,),
        in_specs=[wide(rows), wide(1)] + [kept_spec(a) for a in (scale, cosine, sine)],
        out_specs=wide(rows),
        out_shape=jax.ShapeDtypeStruct((rows, width), LOW),
    )(flat, gain, scale, cosine, sine)


PAIR = 2


def head_spec(rows):
    return pl.BlockSpec((rows, PAIR * HEAD), lambda h: (0, h))


def kept_spec(array):
    zeros = (0,) * array.ndim
    return pl.BlockSpec(array.shape, lambda h: zeros, pipeline_mode=pl.Buffered(1))


def piece_spec(count):
    return pl.BlockSpec((count, PR_DEV, PAIR * HEAD), lambda h: (0, 0, h))


def all_keys(own_ref, stay_ref, cross_ref, span):
    blocks = []
    for j in range(GROUP // 2):
        blocks += [stay_ref[j, :, span], cross_ref[j, :, span]]
    return jnp.concatenate(blocks + [own_ref[PR_DEV:, span]], axis=0)


def softmax_rows(query, keys, bias):
    scores = dot_nt(query, keys) * HEAD ** (-0.5) + bias
    weights = jnp.exp(scores - jnp.max(scores, axis=1, keepdims=True))
    return weights * (1.0 / jnp.sum(weights, axis=1, keepdims=True))


def attend_kernel(q_ref, k_ref, v_ref, bias_ref, k_stay, k_cross, v_stay, v_cross, out_ref):
    bias = bias_ref[...].astype(FULL)
    for at in range(0, PAIR * HEAD, HEAD):
        span = slice(at, at + HEAD)
        probs = softmax_rows(q_ref[:, span], all_keys(k_ref, k_stay, k_cross, span), bias)
        out_ref[:, span] = dot_nn(
            probs.astype(LOW), all_keys(v_ref, v_stay, v_cross, span)
        ).astype(LOW)


def attend(queries, keys, values, bias, pieces):
    rows, width = queries.shape
    return pl.pallas_call(
        attend_kernel,
        grid=(width // HEAD // PAIR,),
        in_specs=[head_spec(rows)] * 3 + [kept_spec(bias)] + [piece_spec(GROUP // 2)] * 4,
        out_specs=head_spec(rows),
        out_shape=jax.ShapeDtypeStruct((rows, width), LOW),
        compiler_params=pltpu.CompilerParams(vmem_limit_bytes=40 * 1024 * 1024),
    )(queries, keys, values, bias, *pieces)


def norm_parts(step, at, grad, flat_ref, gain_ref, scale_ref, inner_ref, gain_grad_ref):
    span = slice(at, at + HEAD)
    product = flat_ref[:, span] * grad
    inner = jnp.sum(product * gain_ref[:, span], axis=1, keepdims=True)
    gain_grad_ref[:, span] = jnp.sum(product * scale_ref[...], axis=0, keepdims=True)
    if at:
        inner_ref[...] += inner
    else:
        inner_ref[...] = jnp.where(step == 0, 0.0, inner_ref[...]) + inner


def attend_back_kernel(
    q_ref,
    k_ref,
    v_ref,
    bias_ref,
    back_ref,
    flat_ref,
    gain_ref,
    scale_ref,
    cos_ref,
    sin_ref,
    k_stay,
    k_cross,
    v_stay,
    v_cross,
    qg_ref,
    inner_ref,
    gain_grad_ref,
    kg_ref,
    vg_ref,
    odd_ref,
    even_ref,
):
    step = pl.program_id(0)
    bias = bias_ref[...].astype(FULL)
    cosine, sine = cos_ref[...], sin_ref[...]
    prompt = PR_DEV * GROUP
    for at in range(0, PAIR * HEAD, HEAD):
        span = slice(at, at + HEAD)
        query, back = q_ref[:, span], back_ref[:, span]
        keys = all_keys(k_ref, k_stay, k_cross, span)
        values = all_keys(v_ref, v_stay, v_cross, span)
        probs = softmax_rows(query, keys, bias)
        prob_grad = dot_nt(back, values)
        value_grad = dot_tn(probs.astype(LOW), back)
        row_dot = jnp.sum(probs * prob_grad, axis=1, keepdims=True)
        score_grad = (probs * (prob_grad - row_dot)).astype(LOW)
        query_grad = dot_nn(score_grad, keys) * HEAD ** (-0.5)
        key_grad = dot_tn(score_grad, query) * HEAD ** (-0.5)
        query_grad = query_grad * cosine - turn(query_grad) * sine
        qg_ref[:, span] = query_grad
        norm_parts(step, at, query_grad, flat_ref, gain_ref, scale_ref, inner_ref, gain_grad_ref)
        for which, grad, own_ref in ((0, key_grad, kg_ref), (1, value_grad, vg_ref)):
            own_ref[:PR_DEV, span] = grad[:PR_DEV]
            own_ref[PR_DEV:, span] = grad[prompt:]
            for j in range(1, GROUP):
                to = odd_ref if j % 2 else even_ref
                to[(j - 1) // 2, which, :, span] = grad[j * PR_DEV : (j + 1) * PR_DEV].astype(LOW)


def attend_back(queries, keys, values, bias, back, flat, gain, scale, cosine, sine, pieces):
    rows, width = queries.shape
    wide = jax.ShapeDtypeStruct((rows, width), FULL)
    both = lambda count: pl.BlockSpec((count, 2, PR_DEV, PAIR * HEAD), lambda h: (0, 0, 0, h))
    return pl.pallas_call(
        attend_back_kernel,
        grid=(width // HEAD // PAIR,),
        in_specs=[head_spec(rows)] * 3
        + [kept_spec(bias), head_spec(rows), head_spec(rows), head_spec(1)]
        + [kept_spec(a) for a in (scale, cosine, sine)]
        + [piece_spec(GROUP // 2)] * 4,
        out_specs=[
            head_spec(rows),
            pl.BlockSpec((rows, 1), lambda h: (0, 0)),
            head_spec(1),
            head_spec(rows),
            head_spec(rows),
            both(4),
            both(3),
        ],
        out_shape=[
            wide,
            jax.ShapeDtypeStruct((rows, 1), FULL),
            jax.ShapeDtypeStruct((1, width), FULL),
            wide,
            wide,
            jax.ShapeDtypeStruct((4, 2, PR_DEV, width), LOW),
            jax.ShapeDtypeStruct((3, 2, PR_DEV, width), LOW),
        ],
        compiler_params=pltpu.CompilerParams(vmem_limit_bytes=58 * 1024 * 1024),
    )(queries, keys, values, bias, back, flat, gain, scale, cosine, sine, *pieces)


def key_back_kernel(*refs):
    kg_ref, vg_ref, flat_ref, gain_ref, scale_ref, cos_ref, sin_ref = refs[:7]
    key_parts, value_parts = refs[7:10], refs[10:13]
    out_ref, inner_ref, gain_grad_ref, value_ref = refs[13:]
    step = pl.program_id(0)
    for at in range(0, PAIR * HEAD, HEAD):
        span = slice(at, at + HEAD)
        grads = []
        for own_ref, parts in ((kg_ref, key_parts), (vg_ref, value_parts)):
            first = own_ref[:PR_DEV, span]
            for part in parts:
                first = first + part[:, span].astype(FULL)
            grads.append(jnp.concatenate([first, own_ref[PR_DEV:, span]], axis=0))
        key_grad = grads[0] * cos_ref[...] - turn(grads[0]) * sin_ref[...]
        out_ref[:, span] = key_grad
        norm_parts(step, at, key_grad, flat_ref, gain_ref, scale_ref, inner_ref, gain_grad_ref)
        value_ref[:, span] = grads[1].astype(LOW)


def key_back(key_grad, value_grad, flat, gain, scale, cosine, sine, key_parts, value_parts):
    rows, width = flat.shape
    return pl.pallas_call(
        key_back_kernel,
        grid=(width // HEAD // PAIR,),
        in_specs=[head_spec(rows)] * 3
        + [head_spec(1)]
        + [kept_spec(a) for a in (scale, cosine, sine)]
        + [head_spec(PR_DEV)] * 6,
        out_specs=[
            head_spec(rows),
            pl.BlockSpec((rows, 1), lambda h: (0, 0)),
            head_spec(1),
            head_spec(rows),
        ],
        out_shape=[
            jax.ShapeDtypeStruct((rows, width), FULL),
            jax.ShapeDtypeStruct((rows, 1), FULL),
            jax.ShapeDtypeStruct((1, width), FULL),
            jax.ShapeDtypeStruct((rows, width), LOW),
        ],
    )(key_grad, value_grad, flat, gain, scale, cosine, sine, *key_parts, *value_parts)


def pack_kernel(query, key, value, out, rest, packed):
    at = 0
    for ref in (query, key, value):
        packed[at : at + ref.shape[0]] = ref[...]
        at += ref.shape[0]
    packed[at : at + out.shape[1]] = out[...].T
    packed[at + out.shape[1] :] = rest[...]


def pack_weights(w_query, w_key, w_value, w_out, rest):
    rows = 4 * w_query.shape[0] + rest.shape[0]
    return pl.pallas_call(
        pack_kernel, out_shape=jax.ShapeDtypeStruct((rows, w_query.shape[1]), LOW)
    )(w_query, w_key, w_value, w_out, rest)


def pack_specs(gathered, places, steps, at):
    count, width = gathered.shape[0] // steps, gathered.shape[2]
    block = at
    return [
        pl.BlockSpec((count, block, width), lambda i, place=place: (i, place, 0))
        for place in places
    ]


def project_kernel(mats, roundings, rows_ref, *refs):
    mat_refs, out_refs, totals = refs[:mats], refs[mats : 2 * mats], refs[2 * mats :]
    step = pl.program_id(0)
    rows = rows_ref[...]
    for mat, out, total, rounding in zip(mat_refs, out_refs, totals, roundings):
        flat = mat[...].reshape(-1, mat.shape[2])
        part = dot_nn(rows, flat)

        @pl.when(step == 0)
        def _():
            total[...] = part

        @pl.when(step > 0)
        def _():
            total[...] += part

        @pl.when(step == pl.num_programs(0) - 1)
        def _():
            out[...] = total[...].astype(rounding)


def project(rows, gathered, block, places, roundings):
    count, width = rows.shape
    columns = gathered.shape[2]
    steps = 4
    outs = [jax.ShapeDtypeStruct((count, columns), rounding) for rounding in roundings]
    return pl.pallas_call(
        lambda *refs: project_kernel(len(places), roundings, *refs),
        grid=(steps,),
        in_specs=[pl.BlockSpec((count, width // steps), lambda i: (0, i))]
        + pack_specs(gathered, places, steps, block),
        out_specs=[pl.BlockSpec((count, columns), lambda i: (0, 0)) for _ in outs],
        out_shape=outs,
        scratch_shapes=[pltpu.VMEM((count, columns), FULL)] * len(outs),
        compiler_params=pltpu.CompilerParams(vmem_limit_bytes=40 * 1024 * 1024),
        cost_estimate=pl.CostEstimate(
            flops=2 * count * width * columns * len(places),
            bytes_accessed=2 * width * columns * len(places) + 8 * count * columns,
            transcendentals=0,
        ),
    )(rows, *[gathered] * len(places))


def project_back_kernel(mats, *refs):
    out = refs[-1]
    total = None
    for rows_ref, mat in zip(refs[:mats], refs[mats:-1]):
        part = dot_nt(rows_ref[...], mat[...].reshape(-1, mat.shape[2]))
        total = part if total is None else total + part
    out[...] = total


def project_back(rows, gathered, block, places):
    count, columns = rows[0].shape
    width = gathered.shape[0] * block
    steps = 4
    fixed = pl.BlockSpec((count, columns), lambda i: (0, 0), pipeline_mode=pl.Buffered(1))
    return pl.pallas_call(
        lambda *refs: project_back_kernel(len(places), *refs),
        grid=(steps,),
        in_specs=[fixed] * len(rows) + pack_specs(gathered, places, steps, block),
        out_specs=pl.BlockSpec((count, width // steps), lambda i: (0, i)),
        out_shape=jax.ShapeDtypeStruct((count, width), FULL),
        compiler_params=pltpu.CompilerParams(vmem_limit_bytes=40 * 1024 * 1024),
        cost_estimate=pl.CostEstimate(
            flops=2 * count * width * columns * len(places),
            bytes_accessed=2 * width * columns * len(places) + 4 * count * width,
            transcendentals=0,
        ),
    )(*rows, *[gathered] * len(places))


def ring_weights(first, second, fillers):
    rows = first.shape[0] // len(RING)
    cut = (first.shape[1] + second.shape[1]) // 2
    chip = lax.axis_index("dp") // 2
    place = jnp.where(chip % 2 == 0, chip // 2, 7 - chip // 2)

    def part(hop):
        there = (place + hop) % len(RING)
        at = jnp.where(there < 4, 2 * there, 2 * (7 - there) + 1) * rows
        return jnp.concatenate(
            [lax.dynamic_slice_in_dim(a, at, rows, axis=0) for a in (first, second)], axis=1
        )

    far = part(4)
    right, left = ahead(far[:, :cut]), behind(far[:, cut:])
    left = fillers.next(left)
    outward, inward = part(3), part(-3)
    right = jnp.concatenate([add_low(outward[:, :cut], right), outward[:, cut:]], axis=1)
    left = jnp.concatenate([inward[:, :cut], add_low(inward[:, cut:], left)], axis=1)
    right, left = ahead(right), behind(left)
    left = fillers.next(left)
    for hop in (2, 1):
        right, left = ahead(add_low(part(hop), right)), behind(add_low(part(-hop), left))
        left = fillers.next(left)
    return part(0).astype(FULL) + right.astype(FULL) + left.astype(FULL)


def expert_kernel(
    rows_ref, back_ref, gate_ref, wg0, wg1, wu0, wu1, wd0, wd1, grad_ref, h0, h1, g0, g1, u0, u1
):
    rows = rows_ref[...]
    back = back_ref[...]
    gate = gate_ref[...]
    total = None
    for wg, wu, wd, h, g, u in ((wg0, wu0, wd0, h0, g0, u0), (wg1, wu1, wd1, h1, g1, u1)):
        gate_pre = dot_nn(rows, wg[...])
        up_pre = dot_nn(rows, wu[...])
        hidden_grad = gate * dot_nt(back, wd[...])
        sig = 1.0 / (1.0 + jnp.exp(-gate_pre))
        act = gate_pre * sig
        h[...] = (gate * (act * up_pre)).astype(LOW)
        gate_grad = (hidden_grad * up_pre * (sig * (1.0 + gate_pre * (1.0 - sig)))).astype(LOW)
        up_grad = (hidden_grad * act).astype(LOW)
        g[...] = gate_grad
        u[...] = up_grad
        part = dot_nt(gate_grad, wg[...]) + dot_nt(up_grad, wu[...])
        total = part if total is None else total + part
    grad_ref[...] = total.astype(LOW)


def expert_pass(rows, back, gate, gate_mats, up_mats, down_mats):
    count, width = rows.shape
    hidden = gate_mats[0].shape[1]
    tile = 256
    whole = lambda array: pl.BlockSpec(
        array.shape, lambda i: (0, 0), pipeline_mode=pl.Buffered(1)
    )
    tall = lambda columns: pl.BlockSpec((tile, columns), lambda i: (i, 0))
    mats = [*gate_mats, *up_mats, *down_mats]
    flops = 2 * 5 * count * width * hidden * 2
    return pl.pallas_call(
        expert_kernel,
        grid=(count // tile,),
        in_specs=[tall(width), tall(width), tall(1)] + [whole(m) for m in mats],
        out_specs=[tall(width)] + [tall(hidden)] * 6,
        out_shape=[jax.ShapeDtypeStruct((count, width), LOW)]
        + [jax.ShapeDtypeStruct((count, hidden), LOW)] * 6,
        compiler_params=pltpu.CompilerParams(vmem_limit_bytes=58 * 1024 * 1024),
        cost_estimate=pl.CostEstimate(
            flops=flops,
            bytes_accessed=2 * (3 * count * width + 6 * count * hidden + 6 * width * hidden),
            transcendentals=2 * count * hidden,
        ),
    )(rows, back, gate, *mats)


def chunk_kernel(pieces, held, at, size, gate_ref, *refs):
    piece_refs, refs = refs[:pieces], refs[pieces:]
    back_ref, mats, refs = refs[0], refs[1:7], refs[7 + held :]
    same_ref, cross_ref, rows_out, hidden_out, gate_out, up_out = refs[:6]
    rows, back, wg, wu, wd, hidden, gate_grad, up_grad, grads, sems = refs[6:]
    count = rows.shape[0]
    part = wg.shape[2]
    slab = wg.shape[1] // 4
    place = pl.ds(at * count, count)
    copy = pltpu.make_async_copy
    load_rows, start = [], 0
    for piece in piece_refs:
        span = pl.ds(start, piece.shape[0])
        load_rows.append(copy(piece, rows.at[span], sems.at[len(load_rows)]))
        start += piece.shape[0]
    load_back = copy(back_ref.at[place], back, sems.at[4])
    loads = [
        [copy(mats[2 * k + half], to.at[half], sems.at[5 + 3 * half + k]) for k, to in enumerate((wg, wu, wd))]
        for half in range(2)
    ]
    for one in load_rows + loads[0][:2] + [load_back] + loads[0][2:] + loads[1]:
        one.start()
    gate = gate_ref[...]
    for one in load_rows:
        one.wait()
    stores = [copy(rows, rows_out.at[place], sems.at[11])]
    stores[0].start()
    for half in range(2):
        columns = pl.ds(half * part, part)
        loads[half][0].wait()
        gate_pre = dot_nn(rows[...], wg[half])
        loads[half][1].wait()
        up_pre = dot_nn(rows[...], wu[half])
        if half == 0:
            load_back.wait()
        loads[half][2].wait()
        hidden_grad = gate * dot_nt(back[...], wd[half])
        sig = 1.0 / (1.0 + jnp.exp(-gate_pre))
        act = gate_pre * sig
        hidden[:, columns] = (gate * (act * up_pre)).astype(LOW)
        gate_grad[:, columns] = (
            hidden_grad * up_pre * (sig * (1.0 + gate_pre * (1.0 - sig)))
        ).astype(LOW)
        up_grad[:, columns] = (hidden_grad * act).astype(LOW)
        for k, (held_in, out) in enumerate(
            ((hidden, hidden_out), (gate_grad, gate_out), (up_grad, up_out))
        ):
            stores.append(
                copy(held_in.at[:, columns], out.at[place, columns], sems.at[12 + 3 * half + k])
            )
            stores[-1].start()

    @pl.loop(0, 4)
    def _(j):
        span = pl.ds(pl.multiple_of(j * slab, slab), slab)
        total = None
        for grad, mat in ((gate_grad, wg), (up_grad, wu)):
            for half in range(2):
                piece = dot_nt(grad[:, half * part : (half + 1) * part], mat[half, span])
                total = piece if total is None else total + piece
        grads[:, span] = total.astype(LOW)

    for k in range(count // size):
        to = cross_ref if k % 2 else same_ref
        stores.append(
            copy(
                grads.at[pl.ds(k * size, size)],
                to.at[pl.ds(k // 2 * size, size)],
                sems.at[18 + k],
            )
        )
        stores[-1].start()
    for one in stores:
        one.wait()


def expert_chunk(pieces, back, gate, mats, at, held, size):
    all_rows, width = back.shape
    part = mats[0].shape[1]
    hidden = 2 * part
    count = sum(piece.shape[0] for piece in pieces)
    anywhere = pl.BlockSpec(memory_space=pl.ANY)
    held = [] if held is None else list(held)
    args = [gate, *pieces, back, *mats, *held]
    out = pl.pallas_call(
        lambda *refs: chunk_kernel(len(pieces), len(held), at, size, *refs),
        grid=(1,),
        in_specs=[pl.BlockSpec((count, 1), lambda j: (at, 0))] + [anywhere] * (len(args) - 1),
        out_specs=[anywhere] * 6,
        out_shape=[jax.ShapeDtypeStruct((count // 2, width), LOW)] * 2
        + [jax.ShapeDtypeStruct((all_rows, width), LOW)]
        + [jax.ShapeDtypeStruct((all_rows, hidden), LOW)] * 3,
        scratch_shapes=[
            pltpu.VMEM((count, width), LOW),
            pltpu.VMEM((count, width), LOW),
            pltpu.VMEM((2, width, part), LOW),
            pltpu.VMEM((2, width, part), LOW),
            pltpu.VMEM((2, part, width), LOW),
            pltpu.VMEM((count, hidden), LOW),
            pltpu.VMEM((count, hidden), LOW),
            pltpu.VMEM((count, hidden), LOW),
            pltpu.VMEM((count, width), LOW),
            pltpu.SemaphoreType.DMA((22,)),
        ],
        input_output_aliases={len(args) - len(held) + k: 2 + k for k in range(len(held))},
        compiler_params=pltpu.CompilerParams(vmem_limit_bytes=50 * 1024 * 1024),
        cost_estimate=pl.CostEstimate(
            flops=2 * 5 * count * width * hidden,
            bytes_accessed=2 * (4 * count * width + 3 * count * hidden + 3 * width * hidden),
            transcendentals=count * hidden,
        ),
    )(*args)
    return out[0], out[1], out[2:]


def mixed_kernel(chip_ref, core_ref, hidden_ref, first_ref, second_ref, out_ref):
    part = first_ref.shape[0]
    rows = out_ref.shape[2]
    result = dot_nn(hidden_ref[:, :part], first_ref[...]) + dot_nn(
        hidden_ref[:, part:], second_ref[...]
    )
    result = result.astype(LOW)
    out_ref[0, core_ref[0]] = result[:rows]
    out_ref[0, 1 - core_ref[0]] = result[rows:]


def mixed_pass(hidden, down_mats, blocks):
    count, columns = hidden.shape
    width = down_mats[0].shape[1]
    chips = blocks.shape[0] // 2
    rows = count // chips
    once = pl.Buffered(1)
    fixed = lambda m: pl.BlockSpec(m.shape, lambda i, a, b: (0, 0), pipeline_mode=once)
    out = pl.pallas_call(
        mixed_kernel,
        grid_spec=pltpu.PrefetchScalarGridSpec(
            num_scalar_prefetch=2,
            grid=(chips,),
            in_specs=[pl.BlockSpec((rows, columns), lambda i, a, b: (i, 0))]
            + [fixed(m) for m in down_mats],
            out_specs=pl.BlockSpec(
                (1, 2, rows // 2, width), lambda i, chip, core: (chip[i], 0, 0, 0)
            ),
        ),
        out_shape=jax.ShapeDtypeStruct((chips, 2, rows // 2, width), LOW),
        compiler_params=pltpu.CompilerParams(vmem_limit_bytes=40 * 1024 * 1024),
        cost_estimate=pl.CostEstimate(
            flops=2 * count * columns * width,
            bytes_accessed=2 * (count * (columns + width) + columns * width),
            transcendentals=0,
        ),
    )(blocks[::2] // 2, blocks[:1] % 2, hidden, *down_mats)
    return out.reshape(count, width)


def expert_ring(rows, back, gate, mats):
    size = rows.shape[0]
    cut = size // 2
    same, cross = {}, {}
    left, right = ahead(rows), behind(rows)
    swap = lambda block: swap_bit(block, "dp", 0)
    same[0], cross[0], held = expert_chunk([rows, swap(rows)], back, gate, mats, 6, None, size)
    for hop in (1, 2, 3):
        pieces = [left, swap(left), right, swap(right)]
        if hop < 3:
            left, right = ahead(left), behind(right)
        else:
            left, right = ahead(left[:cut]), behind(right[cut:])
        same[hop], cross[hop], held = expert_chunk(pieces, back, gate, mats, hop - 1, held, size)
    pieces = [left, right, swap(left), swap(right)]
    same[4], cross[4], held = expert_chunk(pieces, back, gate, mats, 7, held, size)
    return same, cross, held


def halving_sum(parts):
    bits = parts.shape[0].bit_length() - 1
    index = lax.axis_index("dp")
    for bit in reversed(range(bits)):
        rows = parts.shape[0] // 2
        upper = index >> bit & 1
        kept = lax.dynamic_slice_in_dim(parts, upper * rows, rows, axis=0)
        sent = lax.dynamic_slice_in_dim(parts, (1 - upper) * rows, rows, axis=0)
        parts = kept + swap_bit(sent, "dp", bit)
    return parts[0]


def body(
    inputs,
    attn_gain,
    w_query,
    w_key,
    w_value,
    query_gain,
    key_gain,
    w_out,
    moe_gain,
    w_gate,
    w_up,
    w_down,
    experts,
    gates,
    segments,
    gaps,
    cotangent,
):
    dp_count = lax.axis_size("dp")
    dp_index = lax.axis_index("dp")
    side = lax.axis_index("tensor")
    token_count, model_width = inputs.shape
    half_count = token_count // 2
    top_count = experts.shape[1]
    expert_count = w_gate.shape[0] * dp_count
    capacity = token_count * top_count * dp_count * 9 // (8 * expert_count)
    prompt_length = PR_DEV * GROUP
    column_total = HEADS * HEAD
    block = w_query.shape[0]
    local_width = w_query.shape[1]
    local_heads = local_width // HEAD

    def own_half(array):
        return lax.dynamic_slice_in_dim(array, side * half_count, half_count, axis=0)

    def other_half(array):
        return lax.dynamic_slice_in_dim(array, (1 - side) * half_count, half_count, axis=0)

    def both_halves(own, other):
        first = side == 0
        return jnp.concatenate(
            [jnp.where(first, own, other), jnp.where(first, other, own)], axis=0
        )

    gate_mats = (w_gate[0], swap_tensor(w_gate[0]))
    up_mats = (w_up[0], swap_tensor(w_up[0]))

    ring = dp_count == 2 * len(RING)

    gates_high = gates.astype(LOW)
    gates_low = (gates - gates_high.astype(FULL)).astype(LOW)
    routing = jnp.concatenate([experts.astype(LOW).T, gates_high.T, gates_low.T], axis=1)
    routing = jnp.pad(routing, ((0, 0), (0, local_width - 3 * token_count)))
    gains = jnp.concatenate([attn_gain, moe_gain, query_gain, key_gain])
    gains = jnp.pad(gains[None], ((0, 7), (0, local_width - 4 * block)))
    packed = pack_weights(
        w_query, w_key, w_value, w_out, jnp.concatenate([gains, routing], axis=0)
    )
    gathered = lax.all_gather(packed, "dp", axis=0, tiled=False)
    gathered, *early = lax.optimization_barrier((gathered, gate_mats[1], up_mats[1]))
    gate_mats, up_mats = (gate_mats[0], early[0]), (up_mats[0], early[1])
    gain_rows = gathered[:, 4 * block].astype(FULL)
    gain_one, gain_two, gain_q, gain_k = (
        gain_rows[:, j * block : (j + 1) * block].reshape(-1) for j in range(4)
    )
    gain_query_local = lax.dynamic_slice_in_dim(gain_q, side * local_width, local_width)
    gain_key_local = lax.dynamic_slice_in_dim(gain_k, side * local_width, local_width)

    names = gathered[:, 4 * block + 8 :, :token_count]
    weights = gathered[:, 4 * block + 8 :, token_count : 2 * token_count].astype(
        FULL
    ) + gathered[:, 4 * block + 8 :, 2 * token_count : 3 * token_count].astype(FULL)
    named = names == dp_index.astype(LOW)
    picked = jnp.sum(named.astype(FULL), axis=1)
    weight = jnp.sum(jnp.where(named, weights, 0.0), axis=1)
    order = jnp.arange(token_count, dtype=jnp.int32)
    earlier = (order[:, None] < order[None, :]).astype(LOW)
    within = dot_nn(picked.astype(LOW), earlier)
    per_row = jnp.sum(picked, axis=1)
    rows_order = jnp.arange(dp_count, dtype=jnp.int32)
    ahead = jnp.sum(
        jnp.where(rows_order[None, :] < rows_order[:, None], per_row[None, :], 0.0), axis=1
    )
    kept = (picked > 0.0) & (within + ahead[:, None] < capacity)
    weight = jnp.where(kept, weight, 0.0)
    weight = lax.dynamic_slice_in_dim(weight, side * half_count, half_count, axis=1)
    if ring:
        blocks = ring_blocks(dp_index)
        weight = weight[blocks]
    weight = weight.reshape(-1, 1)

    cotangent_half = own_half(cotangent)
    back_rows = lax.all_gather(cotangent_half.astype(LOW), "dp", axis=0, tiled=False)
    back_rows = (back_rows[blocks] if ring else back_rows).reshape(-1, model_width)

    core = dp_index % 2
    tokens_f = inputs.astype(FULL)
    prompt_pos = dp_index % GROUP * PR_DEV + jnp.arange(PR_DEV, dtype=jnp.int32)
    later_pos = cont_positions(segments[0], gaps[0], prompt_length)
    positions = jnp.concatenate([prompt_pos, later_pos], axis=0)
    cosine, sine = rope_tables(positions, HEAD)
    sine = jnp.where(jnp.arange(HEAD) < HEAD // 2, -sine, sine)
    prompt_query = jnp.arange(token_count, dtype=jnp.int32) < PR_DEV
    prompt_at = jnp.arange(prompt_length, dtype=jnp.int32)
    prompt_keypos = ((dp_index % GROUP) ^ (prompt_at // PR_DEV)) * PR_DEV + prompt_at % PR_DEV
    allowed_prompt = (~prompt_query)[:, None] | (prompt_keypos[None, :] <= positions[:, None])
    query_segment = jnp.concatenate([jnp.full((PR_DEV,), -1, jnp.int32), segments[0]], axis=0)
    allowed_cont = (query_segment[:, None] == segments[0][None, :]) & (
        later_pos[None, :] <= positions[:, None]
    )
    allowed = jnp.concatenate([allowed_prompt, allowed_cont], axis=1)
    bias = jnp.where(allowed, 0.0, -1e30).astype(LOW)
    normed_b = rms_norm(tokens_f, gain_one).astype(LOW)
    query_flat, key_flat, values_b = project(
        normed_b, gathered, block, (0, 1, 2), (FULL, FULL, LOW)
    )
    value_pieces = collect_prompt(values_b[:PR_DEV], 1, 2)
    query_sq, key_sq = lax.psum(
        (jnp.sum(query_flat * query_flat, axis=1), jnp.sum(key_flat * key_flat, axis=1)), "tensor"
    )
    query_sq, down_mat = lax.optimization_barrier((query_sq, w_down[0]))
    down_mats = (down_mat, swap_tensor(down_mat))
    query_scale = lax.rsqrt(query_sq / column_total + EPSILON)[:, None]
    key_scale = lax.rsqrt(key_sq / column_total + EPSILON)[:, None]
    keys_b = rope_pass(key_flat, gain_key_local[None], key_scale, cosine, sine)
    pieces = (*collect_prompt(keys_b[:PR_DEV], 2, 1), *value_pieces)
    queries_b = rope_pass(query_flat, gain_query_local[None], query_scale, cosine, sine)
    context_b = attend(queries_b, keys_b, values_b, bias, pieces)
    attn_part = project_back([context_b], gathered, block, (3,))
    attn_part, late = lax.optimization_barrier((attn_part, down_mats[1]))
    down_mats = (down_mats[0], late)
    mats = (*gate_mats, *up_mats, *down_mats)
    attn_other = swap_tensor(other_half(attn_part).astype(LOW))
    attn_other, back_rows, weight = together(attn_other, back_rows, weight)
    hidden_state = (
        own_half(tokens_f) + own_half(attn_part) + attn_other.astype(FULL)
    )
    normed_two_b = rms_norm(hidden_state, gain_two).astype(LOW)

    low_tn = lambda left, right: dot_tn(left, right).astype(LOW)
    if ring:
        same, cross, held = expert_ring(normed_two_b, back_rows, weight, mats)
        expert_in, hidden, gate_grad, up_grad = held
        part = down_mats[0].shape[0]
        h0, h1 = hidden[:, :part], hidden[:, part:]
        g0, g1 = gate_grad[:, :part], gate_grad[:, part:]
        u0, u1 = up_grad[:, :part], up_grad[:, part:]
        down_got = swap_tensor(low_tn(h1, back_rows))
        fillers = Fillers(
            [
                [(low_tn, expert_in, g1)],
                [(low_tn, expert_in, u1)],
                [(lambda h: mixed_pass(h, down_mats, blocks), hidden)],
            ]
        )
        normed_two_grad = ring_sum(same, cross, fillers)
        gate_sent, up_sent, mixed_rows = fillers.outs
        gate_got = swap_tensor(gate_sent)
    else:
        expert_in = lax.all_gather(normed_two_b, "dp", axis=0, tiled=True)
        grad_rows, h0, h1, g0, g1, u0, u1 = expert_pass(
            expert_in, back_rows, weight, gate_mats, up_mats, down_mats
        )
        normed_two_grad = lax.psum_scatter(
            grad_rows, "dp", scatter_dimension=0, tiled=True
        ).astype(FULL)
        mixed_rows = (dot_nn(h0, down_mats[0]) + dot_nn(h1, down_mats[1])).astype(LOW)
        down_got = swap_tensor(low_tn(h1, back_rows))
        gate_got = swap_tensor(low_tn(expert_in, g1))
        up_sent = low_tn(expert_in, u1)
    normed_two_grad, down_got, gate_got, mixed_rows = together(
        normed_two_grad, down_got, gate_got, mixed_rows
    )
    mixed = lax.psum_scatter(mixed_rows, "dp", scatter_dimension=0, tiled=True)

    unused_two, norm_two_back = jax.vjp(rms_norm, hidden_state, gain_two)
    state_part, gain_two_grad = norm_two_back(normed_two_grad)
    state_half = cotangent_half + state_part
    attn_grad_half = state_half.astype(LOW)
    attn_grad_b = both_halves(attn_grad_half, swap_tensor(attn_grad_half))
    attn_grad_b, up_sent = together(attn_grad_b, up_sent)
    up_got = swap_tensor(up_sent)
    (context_grad_b,) = project(attn_grad_b, gathered, block, (3,), (LOW,))
    query_normed_grad, query_inner, query_gain_part, key_grad, value_grad, odd, even = attend_back(
        queries_b,
        keys_b,
        values_b,
        bias,
        context_grad_b,
        query_flat,
        gain_query_local[None],
        query_scale,
        cosine,
        sine,
        pieces,
    )
    odd, up_got = together(odd, up_got)
    key_parts, value_parts = return_prompt(odd, even)
    key_normed_grad, key_inner, key_gain_part, value_pre_grad = key_back(
        key_grad,
        value_grad,
        key_flat,
        gain_key_local[None],
        key_scale,
        cosine,
        sine,
        key_parts,
        value_parts,
    )
    query_inner, key_inner = lax.psum((query_inner[:, 0], key_inner[:, 0]), "tensor")
    query_inner, key_inner, mixed = together(query_inner, key_inner, mixed)
    output_half = hidden_state + mixed.astype(FULL)
    query_cube = query_scale * query_scale * query_scale
    key_cube = key_scale * key_scale * key_scale
    query_pre_grad = (
        query_scale * gain_query_local * query_normed_grad
        - query_flat * query_cube * (query_inner / column_total)[:, None]
    ).astype(LOW)
    key_pre_grad = (
        key_scale * gain_key_local * key_normed_grad
        - key_flat * key_cube * (key_inner / column_total)[:, None]
    ).astype(LOW)
    wide = lambda part: lax.dynamic_update_slice_in_dim(
        jnp.zeros((column_total,), FULL), part, side * local_width, 0
    )
    pre_grads = (query_pre_grad, key_pre_grad, value_pre_grad)
    grad_sum = lambda left, right, got: dot_tn(left, right) + got.astype(FULL)
    down, gate, up = (h0, back_rows, down_got), (expert_in, g0, gate_got), (expert_in, u0, up_got)
    if ring:
        columns = local_width // 2
        mine = lambda a: lax.dynamic_slice_in_dim(a, core * columns, columns, axis=1)
        theirs = lambda a: lax.dynamic_slice_in_dim(a, (1 - core) * columns, columns, axis=1)
        pair = lambda own, sent: jnp.concatenate([own, swap_bit(sent, "dp", 0)], axis=0)
        normed_pair = pair(normed_b, normed_b)
        attn_grad_pair = pair(attn_grad_b, attn_grad_b)
        context_pair = pair(mine(context_b), theirs(context_b))
        grad_pair = pair(
            jnp.concatenate([mine(g) for g in pre_grads], axis=1),
            jnp.concatenate([theirs(g) for g in pre_grads], axis=1),
        )
        normed_pair, attn_grad_pair, context_pair = together(
            normed_pair, attn_grad_pair, context_pair
        )
        out_half = low_tn(attn_grad_pair, context_pair)
        normed_pair, grad_pair = together(normed_pair, grad_pair)
        first_half = low_tn(normed_pair, grad_pair)
        first_half, *pre_grads = together(first_half, *pre_grads)
        fillers = Fillers([[(grad_sum, *down)], [(grad_sum, *gate)], [(grad_sum, *up)]])
        w_half = ring_weights(first_half, out_half, fillers)
        down_grad, gate_w_grad, up_w_grad = fillers.outs
        own_w = lax.dynamic_slice_in_dim(w_half, core * block, block, axis=0)
        got_w = swap_bit(lax.dynamic_slice_in_dim(w_half, (1 - core) * block, block, axis=0), "dp", 0)
        left_w, right_w = jnp.where(core == 0, own_w, got_w), jnp.where(core == 0, got_w, own_w)
        w_sums = [
            jnp.concatenate([w[:, j * columns : (j + 1) * columns] for w in (left_w, right_w)], axis=1)
            for j in range(4)
        ]
    else:
        w_grads = jnp.concatenate(
            [low_tn(normed_b, g) for g in pre_grads] + [low_tn(attn_grad_b, context_b)], axis=1
        )
        w_sum = lax.psum_scatter(w_grads, "dp", scatter_dimension=0, tiled=True).astype(FULL)
        w_sums = [w_sum[:, j * local_width : (j + 1) * local_width] for j in range(4)]
        down_grad, gate_w_grad, up_w_grad = grad_sum(*down), grad_sum(*gate), grad_sum(*up)
    output = both_halves(output_half, swap_tensor(output_half))
    normed_part = project_back(pre_grads, gathered, block, (0, 1, 2))
    normed_other = swap_tensor(other_half(normed_part).astype(LOW))
    normed_grad = own_half(normed_part) + normed_other.astype(FULL)
    unused_one, norm_one_back = jax.vjp(rms_norm, own_half(tokens_f), gain_one)
    input_part, gain_one_grad = norm_one_back(normed_grad)
    input_half = state_half + input_part
    input_grad = both_halves(input_half, swap_tensor(input_half))
    gain_grads = jnp.stack(
        [gain_one_grad, gain_two_grad, wide(query_gain_part[0]), wide(key_gain_part[0])]
    ).reshape(4, dp_count, block)
    gain_sums = halving_sum(jnp.swapaxes(gain_grads, 0, 1))
    gain_sums = gain_sums + swap_tensor(gain_sums)
    return (
        output,
        input_grad,
        gain_sums[0],
        w_sums[0],
        w_sums[1],
        w_sums[2],
        gain_sums[2],
        gain_sums[3],
        w_sums[3].T,
        gain_sums[1],
        gate_w_grad[None],
        up_w_grad[None],
        down_grad[None],
    )


def solution(mesh):
    return jax.shard_map(
        body,
        mesh=mesh,
        in_specs=(
            P("dp", None),
            P("dp"),
            P("dp", "tensor"),
            P("dp", "tensor"),
            P("dp", "tensor"),
            P("dp"),
            P("dp"),
            P("tensor", "dp"),
            P("dp"),
            P("dp", None, "tensor"),
            P("dp", None, "tensor"),
            P("dp", "tensor", None),
            P("dp", None),
            P("dp", None),
            P("dp", None),
            P("dp", None),
            P("dp", None),
        ),
        out_specs=(
            P("dp", None),
            P("dp", None),
            P("dp"),
            P("dp", "tensor"),
            P("dp", "tensor"),
            P("dp", "tensor"),
            P("dp"),
            P("dp"),
            P("tensor", "dp"),
            P("dp"),
            P("dp", None, "tensor"),
            P("dp", None, "tensor"),
            P("dp", "tensor", None),
        ),
        check_vma=False,
    )
```

```python
import jax
import jax.numpy as jnp
from jax import lax
from jax.experimental import pallas as pl
from jax.experimental.pallas import tpu as pltpu
from jax.sharding import PartitionSpec as P

HEADS = 16
HEAD = 128
GROUP = 8
PR_DEV = 128


EPSILON = 1e-05
LOW = jnp.bfloat16
FULL = jnp.float32


def swap_bit(block, axis, bit):
    count = lax.axis_size(axis)
    return lax.ppermute(block, axis, [(i, i ^ (1 << bit)) for i in range(count)])


def swap_tensor(block):
    return lax.ppermute(block, "tensor", [(0, 1), (1, 0)])


RING = (0, 2, 4, 6, 7, 5, 3, 1)
AHEAD = [
    (RING[p] * 2 + c, RING[(p + 1) % len(RING)] * 2 + c) for p in range(len(RING)) for c in range(2)
]
BEHIND = [(to, at) for at, to in AHEAD]
HOPS = (-1, 1, -2, 2, -3, 3, 0, 4)


def ahead(block):
    return lax.ppermute(block, "dp", AHEAD)


def behind(block):
    return lax.ppermute(block, "dp", BEHIND)


def ring_blocks(dp_index):
    chip, core = dp_index // 2, dp_index % 2
    place = jnp.where(chip % 2 == 0, chip // 2, 7 - chip // 2)
    steps, cross = [], []
    for hop in HOPS:
        steps += [hop, hop]
        cross += [0, 1]
    there = (place + jnp.array(steps, jnp.int32)) % 8
    chips = jnp.where(there < 4, 2 * there, 2 * (7 - there) + 1)
    return 2 * chips + (core ^ jnp.array(cross, jnp.int32))


def add_low(*parts):
    total = parts[0].astype(FULL)
    for part in parts[1:]:
        total = total + part.astype(FULL)
    return total.astype(LOW)


def together(value, *others):
    return lax.optimization_barrier((value, *others))


class Fillers:
    def __init__(self, stages):
        self.stages = list(stages)
        self.outs = []

    def next(self, gate):
        for work, *operands in self.stages.pop(0) if self.stages else ():
            gate, *operands = together(gate, *operands)
            self.outs.append(work(*operands))
        return gate


def ring_sum(same, cross, fillers):
    both = {hop: add_low(same[hop], swap_bit(cross[hop], "dp", 0)) for hop in (4, 3, 2, 1, 0)}
    rows = both[0].shape[0]
    cut = rows // 2
    right, left = ahead(both[4][:cut]), behind(both[4][cut:])
    left = fillers.next(left)
    outward, inward = both[3][rows:], both[3][:rows]
    right = jnp.concatenate([add_low(outward[:cut], right), outward[cut:]], axis=0)
    left = jnp.concatenate([inward[:cut], add_low(inward[cut:], left)], axis=0)
    right, left = ahead(right), behind(left)
    left = fillers.next(left)
    for hop in (2, 1):
        right = ahead(add_low(both[hop][rows:], right))
        left = behind(add_low(both[hop][:rows], left))
        left = fillers.next(left)
    return both[0].astype(FULL) + right.astype(FULL) + left.astype(FULL)


def rms_norm(values, gain):
    return values * lax.rsqrt(jnp.mean(values * values, axis=-1, keepdims=True) + EPSILON) * gain


def rope_tables(positions, head_size):
    half_size = head_size // 2
    inverse = 10000.0 ** (-(jnp.arange(half_size, dtype=FULL) * 2.0) / head_size)
    angles = positions.astype(FULL)[:, None] * inverse[None, :]
    cosine = jnp.concatenate([jnp.cos(angles), jnp.cos(angles)], axis=-1)
    sine = jnp.concatenate([jnp.sin(angles), jnp.sin(angles)], axis=-1)
    return (cosine, sine)


def cont_positions(segment_row, gap_row, prompt_length):
    order = jnp.arange(segment_row.shape[0], dtype=jnp.int32)
    same = segment_row[:, None] == segment_row[None, :]
    earlier = order[None, :] < order[:, None]
    offset = jnp.sum((same & earlier).astype(jnp.int32), axis=1)
    labels = jnp.arange(gap_row.shape[0], dtype=jnp.int32)
    shifted = jnp.sum(
        jnp.where(segment_row[:, None] == labels[None, :], gap_row[None, :], 0), axis=1
    )
    return prompt_length + shifted + offset


def dot_nn(left, right):
    return jnp.dot(left, right, preferred_element_type=FULL)


def dot_tn(left, right):
    return lax.dot_general(left, right, (((0,), (0,)), ((), ())), preferred_element_type=FULL)


def dot_nt(left, right):
    return lax.dot_general(left, right, (((1,), (1,)), ((), ())), preferred_element_type=FULL)


def collect_prompt(own, first, second):
    near, far = swap_bit(own, "dp", 1), swap_bit(own, "dp", 2)
    last = swap_bit(near if first == 1 else far, "dp", second)
    stay = jnp.stack([own, near, far, last], axis=0)
    return stay, swap_bit(stay, "dp", 0)


def merge_kernel(even_ref, got_ref, keys_ref, values_ref, far_ref, near_ref):
    near, far, last = 0, 1, 2
    add = lambda j, which: add_low(even_ref[j, which], got_ref[j + 1, which])
    keys_ref[0], keys_ref[1] = add(near, 0), add(last, 0)
    values_ref[0], values_ref[1] = add(far, 1), add(last, 1)
    far_ref[...], near_ref[...] = add(far, 0), add(near, 1)


def return_prompt(odd, even):
    got = swap_bit(odd, "dp", 0)
    one = jax.ShapeDtypeStruct(even.shape[2:], LOW)
    two = jax.ShapeDtypeStruct(even.shape[1:], LOW)
    keys, values, far, near = pl.pallas_call(merge_kernel, out_shape=[two, two, one, one])(even, got)
    keys, values = swap_bit(keys, "dp", 1), swap_bit(values, "dp", 2)
    last_keys = swap_bit(add_low(far, keys[1]), "dp", 2)
    last_values = swap_bit(add_low(near, values[1]), "dp", 1)
    return got, keys, values, last_keys, last_values


def turn(values):
    return pltpu.roll(values, HEAD // 2, 1)


def rope_kernel(pre_ref, gain_ref, scale_ref, cos_ref, sin_ref, out_ref):
    scale, cosine, sine = scale_ref[...], cos_ref[...], sin_ref[...]
    for at in range(0, pre_ref.shape[1], HEAD):
        span = slice(at, at + HEAD)
        normed = pre_ref[:, span] * scale * gain_ref[:, span]
        out_ref[:, span] = (normed * cosine + turn(normed) * sine).astype(LOW)


def rope_pass(flat, gain, scale, cosine, sine):
    rows, width = flat.shape
    part = width // 2
    wide = lambda rows: pl.BlockSpec((rows, part), lambda h: (0, h))
    return pl.pallas_call(
        rope_kernel,
        grid=(2,),
        in_specs=[wide(rows), wide(1)] + [kept_spec(a) for a in (scale, cosine, sine)],
        out_specs=wide(rows),
        out_shape=jax.ShapeDtypeStruct((rows, width), LOW),
    )(flat, gain, scale, cosine, sine)


PAIR = 2


def head_spec(rows):
    return pl.BlockSpec((rows, PAIR * HEAD), lambda h: (0, h))


def kept_spec(array):
    zeros = (0,) * array.ndim
    return pl.BlockSpec(array.shape, lambda h: zeros, pipeline_mode=pl.Buffered(1))


def piece_spec(count):
    return pl.BlockSpec((count, PR_DEV, PAIR * HEAD), lambda h: (0, 0, h))


def all_keys(own_ref, stay_ref, cross_ref, span):
    blocks = []
    for j in range(GROUP // 2):
        blocks += [stay_ref[j, :, span], cross_ref[j, :, span]]
    return jnp.concatenate(blocks + [own_ref[PR_DEV:, span]], axis=0)


def softmax_rows(query, keys, bias):
    scores = dot_nt(query, keys) * HEAD ** (-0.5) + bias
    weights = jnp.exp(scores - jnp.max(scores, axis=1, keepdims=True))
    return weights * (1.0 / jnp.sum(weights, axis=1, keepdims=True))


def attend_kernel(q_ref, k_ref, v_ref, bias_ref, k_stay, k_cross, v_stay, v_cross, out_ref):
    bias = bias_ref[...].astype(FULL)
    for at in range(0, PAIR * HEAD, HEAD):
        span = slice(at, at + HEAD)
        probs = softmax_rows(q_ref[:, span], all_keys(k_ref, k_stay, k_cross, span), bias)
        out_ref[:, span] = dot_nn(
            probs.astype(LOW), all_keys(v_ref, v_stay, v_cross, span)
        ).astype(LOW)


def attend(queries, keys, values, bias, pieces):
    rows, width = queries.shape
    return pl.pallas_call(
        attend_kernel,
        grid=(width // HEAD // PAIR,),
        in_specs=[head_spec(rows)] * 3 + [kept_spec(bias)] + [piece_spec(GROUP // 2)] * 4,
        out_specs=head_spec(rows),
        out_shape=jax.ShapeDtypeStruct((rows, width), LOW),
        compiler_params=pltpu.CompilerParams(vmem_limit_bytes=40 * 1024 * 1024),
    )(queries, keys, values, bias, *pieces)


def norm_parts(step, at, grad, flat_ref, gain_ref, scale_ref, inner_ref, gain_grad_ref):
    span = slice(at, at + HEAD)
    product = flat_ref[:, span] * grad
    inner = jnp.sum(product * gain_ref[:, span], axis=1, keepdims=True)
    gain_grad_ref[:, span] = jnp.sum(product * scale_ref[...], axis=0, keepdims=True)
    if at:
        inner_ref[...] += inner
    else:
        inner_ref[...] = jnp.where(step == 0, 0.0, inner_ref[...]) + inner


def attend_back_kernel(
    q_ref,
    k_ref,
    v_ref,
    bias_ref,
    back_ref,
    flat_ref,
    gain_ref,
    scale_ref,
    cos_ref,
    sin_ref,
    k_stay,
    k_cross,
    v_stay,
    v_cross,
    qg_ref,
    inner_ref,
    gain_grad_ref,
    kg_ref,
    vg_ref,
    odd_ref,
    even_ref,
):
    step = pl.program_id(0)
    bias = bias_ref[...].astype(FULL)
    cosine, sine = cos_ref[...], sin_ref[...]
    prompt = PR_DEV * GROUP
    for at in range(0, PAIR * HEAD, HEAD):
        span = slice(at, at + HEAD)
        query, back = q_ref[:, span], back_ref[:, span]
        keys = all_keys(k_ref, k_stay, k_cross, span)
        values = all_keys(v_ref, v_stay, v_cross, span)
        probs = softmax_rows(query, keys, bias)
        prob_grad = dot_nt(back, values)
        value_grad = dot_tn(probs.astype(LOW), back)
        row_dot = jnp.sum(probs * prob_grad, axis=1, keepdims=True)
        score_grad = (probs * (prob_grad - row_dot)).astype(LOW)
        query_grad = dot_nn(score_grad, keys) * HEAD ** (-0.5)
        key_grad = dot_tn(score_grad, query) * HEAD ** (-0.5)
        query_grad = query_grad * cosine - turn(query_grad) * sine
        qg_ref[:, span] = query_grad
        norm_parts(step, at, query_grad, flat_ref, gain_ref, scale_ref, inner_ref, gain_grad_ref)
        for which, grad, own_ref in ((0, key_grad, kg_ref), (1, value_grad, vg_ref)):
            own_ref[:PR_DEV, span] = grad[:PR_DEV]
            own_ref[PR_DEV:, span] = grad[prompt:]
            for j in range(1, GROUP):
                to = odd_ref if j % 2 else even_ref
                to[(j - 1) // 2, which, :, span] = grad[j * PR_DEV : (j + 1) * PR_DEV].astype(LOW)


def attend_back(queries, keys, values, bias, back, flat, gain, scale, cosine, sine, pieces):
    rows, width = queries.shape
    wide = jax.ShapeDtypeStruct((rows, width), FULL)
    both = lambda count: pl.BlockSpec((count, 2, PR_DEV, PAIR * HEAD), lambda h: (0, 0, 0, h))
    return pl.pallas_call(
        attend_back_kernel,
        grid=(width // HEAD // PAIR,),
        in_specs=[head_spec(rows)] * 3
        + [kept_spec(bias), head_spec(rows), head_spec(rows), head_spec(1)]
        + [kept_spec(a) for a in (scale, cosine, sine)]
        + [piece_spec(GROUP // 2)] * 4,
        out_specs=[
            head_spec(rows),
            pl.BlockSpec((rows, 1), lambda h: (0, 0)),
            head_spec(1),
            head_spec(rows),
            head_spec(rows),
            both(4),
            both(3),
        ],
        out_shape=[
            wide,
            jax.ShapeDtypeStruct((rows, 1), FULL),
            jax.ShapeDtypeStruct((1, width), FULL),
            wide,
            wide,
            jax.ShapeDtypeStruct((4, 2, PR_DEV, width), LOW),
            jax.ShapeDtypeStruct((3, 2, PR_DEV, width), LOW),
        ],
        compiler_params=pltpu.CompilerParams(vmem_limit_bytes=58 * 1024 * 1024),
    )(queries, keys, values, bias, back, flat, gain, scale, cosine, sine, *pieces)


def key_back_kernel(*refs):
    kg_ref, vg_ref, flat_ref, gain_ref, scale_ref, cos_ref, sin_ref = refs[:7]
    got, keys, values, last_keys, last_values = refs[7:12]
    out_ref, inner_ref, gain_grad_ref, value_ref = refs[12:]
    step = pl.program_id(0)
    for at in range(0, PAIR * HEAD, HEAD):
        span = slice(at, at + HEAD)
        grads = []
        for which, own_ref, near, last in ((0, kg_ref, keys, last_keys), (1, vg_ref, values, last_values)):
            first = own_ref[:PR_DEV, span] + got[0, which, :, span].astype(FULL)
            first = first + near[0, :, span].astype(FULL) + last[:, span].astype(FULL)
            grads.append(jnp.concatenate([first, own_ref[PR_DEV:, span]], axis=0))
        key_grad = grads[0] * cos_ref[...] - turn(grads[0]) * sin_ref[...]
        out_ref[:, span] = key_grad
        norm_parts(step, at, key_grad, flat_ref, gain_ref, scale_ref, inner_ref, gain_grad_ref)
        value_ref[:, span] = grads[1].astype(LOW)


def key_back(key_grad, value_grad, flat, gain, scale, cosine, sine, returned):
    rows, width = flat.shape
    columns = PAIR * HEAD
    return pl.pallas_call(
        key_back_kernel,
        grid=(width // columns,),
        in_specs=[head_spec(rows)] * 3
        + [head_spec(1)]
        + [kept_spec(a) for a in (scale, cosine, sine)]
        + [pl.BlockSpec((1, 2, PR_DEV, columns), lambda h: (0, 0, 0, h))]
        + [pl.BlockSpec((1, PR_DEV, columns), lambda h: (0, 0, h))] * 2
        + [head_spec(PR_DEV)] * 2,
        out_specs=[
            head_spec(rows),
            pl.BlockSpec((rows, 1), lambda h: (0, 0)),
            head_spec(1),
            head_spec(rows),
        ],
        out_shape=[
            jax.ShapeDtypeStruct((rows, width), FULL),
            jax.ShapeDtypeStruct((rows, 1), FULL),
            jax.ShapeDtypeStruct((1, width), FULL),
            jax.ShapeDtypeStruct((rows, width), LOW),
        ],
    )(key_grad, value_grad, flat, gain, scale, cosine, sine, *returned)


def pack_kernel(query, key, value, rest, *refs):
    packed = refs[-1]
    at = 0
    for ref in (query, key, value, rest):
        packed[at : at + ref.shape[0]] = ref[...]
        at += ref.shape[0]
    for back in refs[:-1]:
        width = packed.shape[1]
        for start in range(0, back.shape[1], width):
            packed[at : at + back.shape[0]] = back[:, start : start + width].astype(LOW)
            at += back.shape[0]


def pack_weights(w_query, w_key, w_value, rest, back):
    width = w_query.shape[1]
    rows = 3 * w_query.shape[0] + rest.shape[0] + sum(b.size // width for b in back)
    return pl.pallas_call(pack_kernel, out_shape=jax.ShapeDtypeStruct((rows, width), LOW))(
        w_query, w_key, w_value, rest, *back
    )


def unpack_kernel(first, blocks_ref, packed, out, sems):
    width = packed.shape[2]
    parts = out.shape[1] // width
    rows = (packed.shape[1] - first) // parts
    copies = [
        pltpu.make_async_copy(
            packed.at[blocks_ref[i], pl.ds(first + j * rows, rows)],
            out.at[pl.ds(i * rows, rows), pl.ds(j * width, width)],
            sems.at[i * parts + j],
        )
        for i in range(packed.shape[0])
        for j in range(parts)
    ]
    for one in copies:
        one.start()
    for one in copies:
        one.wait()


def unpack_rows(packed, blocks, first, width):
    count = packed.shape[0]
    parts = width // packed.shape[2]
    rows = (packed.shape[1] - first) // parts
    return pl.pallas_call(
        lambda *refs: unpack_kernel(first, *refs),
        in_specs=[pl.BlockSpec(memory_space=pltpu.SMEM), pl.BlockSpec(memory_space=pl.ANY)],
        out_specs=pl.BlockSpec(memory_space=pl.ANY),
        out_shape=jax.ShapeDtypeStruct((count * rows, width), LOW),
        scratch_shapes=[pltpu.SemaphoreType.DMA((count * parts,))],
    )(blocks, packed)


def pack_specs(gathered, places, steps, at):
    count, width = gathered.shape[0] // steps, gathered.shape[2]
    block = at
    return [
        pl.BlockSpec((count, block, width), lambda i, place=place: (i, place, 0))
        for place in places
    ]


def project_kernel(mats, roundings, rows_ref, *refs):
    mat_refs, out_refs, totals = refs[:mats], refs[mats : 2 * mats], refs[2 * mats :]
    step = pl.program_id(0)
    rows = rows_ref[...]
    for mat, out, total, rounding in zip(mat_refs, out_refs, totals, roundings):
        flat = mat[...].reshape(-1, mat.shape[2])
        part = dot_nn(rows, flat)

        @pl.when(step == 0)
        def _():
            total[...] = part

        @pl.when(step > 0)
        def _():
            total[...] += part

        @pl.when(step == pl.num_programs(0) - 1)
        def _():
            out[...] = total[...].astype(rounding)


def project(rows, gathered, block, places, roundings):
    count, width = rows.shape
    columns = gathered.shape[2]
    steps = 4
    outs = [jax.ShapeDtypeStruct((count, columns), rounding) for rounding in roundings]
    return pl.pallas_call(
        lambda *refs: project_kernel(len(places), roundings, *refs),
        grid=(steps,),
        in_specs=[pl.BlockSpec((count, width // steps), lambda i: (0, i))]
        + pack_specs(gathered, places, steps, block),
        out_specs=[pl.BlockSpec((count, columns), lambda i: (0, 0)) for _ in outs],
        out_shape=outs,
        scratch_shapes=[pltpu.VMEM((count, columns), FULL)] * len(outs),
        compiler_params=pltpu.CompilerParams(vmem_limit_bytes=40 * 1024 * 1024),
        cost_estimate=pl.CostEstimate(
            flops=2 * count * width * columns * len(places),
            bytes_accessed=2 * width * columns * len(places) + 8 * count * columns,
            transcendentals=0,
        ),
    )(rows, *[gathered] * len(places))


def project_back_kernel(mats, *refs):
    out = refs[-1]
    total = None
    for rows_ref, mat in zip(refs[:mats], refs[mats:-1]):
        part = dot_nt(rows_ref[...], mat[...].reshape(-1, mat.shape[2]))
        total = part if total is None else total + part
    out[...] = total


def project_back(rows, gathered, block, places):
    count, columns = rows[0].shape
    width = gathered.shape[0] * block
    steps = 4
    fixed = pl.BlockSpec((count, columns), lambda i: (0, 0), pipeline_mode=pl.Buffered(1))
    return pl.pallas_call(
        lambda *refs: project_back_kernel(len(places), *refs),
        grid=(steps,),
        in_specs=[fixed] * len(rows) + pack_specs(gathered, places, steps, block),
        out_specs=pl.BlockSpec((count, width // steps), lambda i: (0, i)),
        out_shape=jax.ShapeDtypeStruct((count, width), FULL),
        compiler_params=pltpu.CompilerParams(vmem_limit_bytes=40 * 1024 * 1024),
        cost_estimate=pl.CostEstimate(
            flops=2 * count * width * columns * len(places),
            bytes_accessed=2 * width * columns * len(places) + 4 * count * width,
            transcendentals=0,
        ),
    )(*rows, *[gathered] * len(places))


def ring_weights(first, second, fillers):
    rows = first.shape[0] // len(RING)
    cut = (first.shape[1] + second.shape[1]) // 2
    chip = lax.axis_index("dp") // 2
    place = jnp.where(chip % 2 == 0, chip // 2, 7 - chip // 2)

    def part(hop):
        there = (place + hop) % len(RING)
        at = jnp.where(there < 4, 2 * there, 2 * (7 - there) + 1) * rows
        return jnp.concatenate(
            [lax.dynamic_slice_in_dim(a, at, rows, axis=0) for a in (first, second)], axis=1
        )

    far = fillers.next(part(4))
    right, left = ahead(far[:, :cut]), behind(far[:, cut:])
    left = fillers.next(left)
    outward, inward = part(3), part(-3)
    right = jnp.concatenate([add_low(outward[:, :cut], right), outward[:, cut:]], axis=1)
    left = jnp.concatenate([inward[:, :cut], add_low(inward[:, cut:], left)], axis=1)
    right, left = ahead(right), behind(left)
    left = fillers.next(left)
    for hop in (2, 1):
        right, left = ahead(add_low(part(hop), right)), behind(add_low(part(-hop), left))
        left = fillers.next(left)
    return part(0).astype(FULL) + right.astype(FULL) + left.astype(FULL)


def expert_kernel(
    rows_ref, back_ref, gate_ref, wg0, wg1, wu0, wu1, wd0, wd1, grad_ref, h0, h1, g0, g1, u0, u1
):
    rows = rows_ref[...]
    back = back_ref[...]
    gate = gate_ref[...]
    total = None
    for wg, wu, wd, h, g, u in ((wg0, wu0, wd0, h0, g0, u0), (wg1, wu1, wd1, h1, g1, u1)):
        gate_pre = dot_nn(rows, wg[...])
        up_pre = dot_nn(rows, wu[...])
        hidden_grad = gate * dot_nt(back, wd[...])
        sig = 1.0 / (1.0 + jnp.exp(-gate_pre))
        act = gate_pre * sig
        h[...] = (gate * (act * up_pre)).astype(LOW)
        gate_grad = (hidden_grad * up_pre * (sig * (1.0 + gate_pre * (1.0 - sig)))).astype(LOW)
        up_grad = (hidden_grad * act).astype(LOW)
        g[...] = gate_grad
        u[...] = up_grad
        part = dot_nt(gate_grad, wg[...]) + dot_nt(up_grad, wu[...])
        total = part if total is None else total + part
    grad_ref[...] = total.astype(LOW)


def expert_pass(rows, back, gate, gate_mats, up_mats, down_mats):
    count, width = rows.shape
    hidden = gate_mats[0].shape[1]
    tile = 256
    whole = lambda array: pl.BlockSpec(
        array.shape, lambda i: (0, 0), pipeline_mode=pl.Buffered(1)
    )
    tall = lambda columns: pl.BlockSpec((tile, columns), lambda i: (i, 0))
    mats = [*gate_mats, *up_mats, *down_mats]
    flops = 2 * 5 * count * width * hidden * 2
    return pl.pallas_call(
        expert_kernel,
        grid=(count // tile,),
        in_specs=[tall(width), tall(width), tall(1)] + [whole(m) for m in mats],
        out_specs=[tall(width)] + [tall(hidden)] * 6,
        out_shape=[jax.ShapeDtypeStruct((count, width), LOW)]
        + [jax.ShapeDtypeStruct((count, hidden), LOW)] * 6,
        compiler_params=pltpu.CompilerParams(vmem_limit_bytes=58 * 1024 * 1024),
        cost_estimate=pl.CostEstimate(
            flops=flops,
            bytes_accessed=2 * (3 * count * width + 6 * count * hidden + 6 * width * hidden),
            transcendentals=2 * count * hidden,
        ),
    )(rows, back, gate, *mats)


def chunk_kernel(pieces, held, at, size, gate_ref, *refs):
    piece_refs, refs = refs[:pieces], refs[pieces:]
    back_ref, mats, refs = refs[0], refs[1:7], refs[7 + held :]
    same_ref, cross_ref, rows_out = refs[:3]
    outs = refs[3:9]
    rows, back, wg, wu, wd, hidden, gate_grad, up_grad, grads, sems = refs[9:]
    count = rows.shape[0]
    part = wg.shape[2]
    slab = wg.shape[1] // 4
    place = pl.ds(at * count, count)
    copy = pltpu.make_async_copy
    load_rows, start = [], 0
    for piece in piece_refs:
        span = pl.ds(start, piece.shape[0])
        load_rows.append(copy(piece, rows.at[span], sems.at[len(load_rows)]))
        start += piece.shape[0]
    load_back = copy(back_ref.at[place], back, sems.at[4])
    loads = [
        [copy(mats[2 * k + half], to.at[half], sems.at[5 + 3 * half + k]) for k, to in enumerate((wg, wu, wd))]
        for half in range(2)
    ]
    for one in load_rows + loads[0][:2] + [load_back] + loads[0][2:] + loads[1]:
        one.start()
    gate = gate_ref[...]
    for one in load_rows:
        one.wait()
    stores = [copy(rows, rows_out.at[place], sems.at[11])]
    stores[0].start()
    for half in range(2):
        columns = pl.ds(half * part, part)
        loads[half][0].wait()
        gate_pre = dot_nn(rows[...], wg[half])
        loads[half][1].wait()
        up_pre = dot_nn(rows[...], wu[half])
        if half == 0:
            load_back.wait()
        loads[half][2].wait()
        hidden_grad = gate * dot_nt(back[...], wd[half])
        sig = 1.0 / (1.0 + jnp.exp(-gate_pre))
        act = gate_pre * sig
        hidden[:, columns] = (gate * (act * up_pre)).astype(LOW)
        gate_grad[:, columns] = (
            hidden_grad * up_pre * (sig * (1.0 + gate_pre * (1.0 - sig)))
        ).astype(LOW)
        up_grad[:, columns] = (hidden_grad * act).astype(LOW)
        for k, held_in in enumerate((hidden, gate_grad, up_grad)):
            stores.append(
                copy(
                    held_in.at[:, columns], outs[2 * k + half].at[place], sems.at[12 + 3 * half + k]
                )
            )
            stores[-1].start()

    @pl.loop(0, 4)
    def _(j):
        span = pl.ds(pl.multiple_of(j * slab, slab), slab)
        total = None
        for grad, mat in ((gate_grad, wg), (up_grad, wu)):
            for half in range(2):
                piece = dot_nt(grad[:, half * part : (half + 1) * part], mat[half, span])
                total = piece if total is None else total + piece
        grads[:, span] = total.astype(LOW)

    for k in range(count // size):
        to = cross_ref if k % 2 else same_ref
        stores.append(
            copy(
                grads.at[pl.ds(k * size, size)],
                to.at[pl.ds(k // 2 * size, size)],
                sems.at[18 + k],
            )
        )
        stores[-1].start()
    for one in stores:
        one.wait()


def expert_chunk(pieces, back, gate, mats, at, held, size):
    all_rows, width = back.shape
    part = mats[0].shape[1]
    hidden = 2 * part
    count = sum(piece.shape[0] for piece in pieces)
    anywhere = pl.BlockSpec(memory_space=pl.ANY)
    held = [] if held is None else list(held)
    args = [gate, *pieces, back, *mats, *held]
    out = pl.pallas_call(
        lambda *refs: chunk_kernel(len(pieces), len(held), at, size, *refs),
        grid=(1,),
        in_specs=[pl.BlockSpec((count, 1), lambda j: (at, 0))] + [anywhere] * (len(args) - 1),
        out_specs=[anywhere] * 9,
        out_shape=[jax.ShapeDtypeStruct((count // 2, width), LOW)] * 2
        + [jax.ShapeDtypeStruct((all_rows, width), LOW)]
        + [jax.ShapeDtypeStruct((all_rows, part), LOW)] * 6,
        scratch_shapes=[
            pltpu.VMEM((count, width), LOW),
            pltpu.VMEM((count, width), LOW),
            pltpu.VMEM((2, width, part), LOW),
            pltpu.VMEM((2, width, part), LOW),
            pltpu.VMEM((2, part, width), LOW),
            pltpu.VMEM((count, hidden), LOW),
            pltpu.VMEM((count, hidden), LOW),
            pltpu.VMEM((count, hidden), LOW),
            pltpu.VMEM((count, width), LOW),
            pltpu.SemaphoreType.DMA((22,)),
        ],
        input_output_aliases={len(args) - len(held) + k: 2 + k for k in range(len(held))},
        compiler_params=pltpu.CompilerParams(vmem_limit_bytes=50 * 1024 * 1024),
        cost_estimate=pl.CostEstimate(
            flops=2 * 5 * count * width * hidden,
            bytes_accessed=2 * (4 * count * width + 3 * count * hidden + 3 * width * hidden),
            transcendentals=count * hidden,
        ),
    )(*args)
    return out[0], out[1], out[2:]


def mixed_kernel(chip_ref, core_ref, h0_ref, h1_ref, first_ref, second_ref, out_ref):
    rows = out_ref.shape[2]
    result = dot_nn(h0_ref[...], first_ref[...]) + dot_nn(h1_ref[...], second_ref[...])
    result = result.astype(LOW)
    out_ref[0, core_ref[0]] = result[:rows]
    out_ref[0, 1 - core_ref[0]] = result[rows:]


def mixed_pass(h0, h1, down_mats, blocks):
    count, columns = h0.shape
    width = down_mats[0].shape[1]
    chips = blocks.shape[0] // 2
    rows = count // chips
    once = pl.Buffered(1)
    fixed = lambda m: pl.BlockSpec(m.shape, lambda i, a, b: (0, 0), pipeline_mode=once)
    out = pl.pallas_call(
        mixed_kernel,
        grid_spec=pltpu.PrefetchScalarGridSpec(
            num_scalar_prefetch=2,
            grid=(chips,),
            in_specs=[pl.BlockSpec((rows, columns), lambda i, a, b: (i, 0))] * 2
            + [fixed(m) for m in down_mats],
            out_specs=pl.BlockSpec(
                (1, 2, rows // 2, width), lambda i, chip, core: (chip[i], 0, 0, 0)
            ),
        ),
        out_shape=jax.ShapeDtypeStruct((chips, 2, rows // 2, width), LOW),
        compiler_params=pltpu.CompilerParams(vmem_limit_bytes=40 * 1024 * 1024),
        cost_estimate=pl.CostEstimate(
            flops=4 * count * columns * width,
            bytes_accessed=2 * (count * (2 * columns + width) + 2 * columns * width),
            transcendentals=0,
        ),
    )(blocks[::2] // 2, blocks[:1] % 2, h0, h1, *down_mats)
    return out.reshape(count, width)


def expert_ring(rows, back, gate, mats, waiting):
    size = rows.shape[0]
    cut = size // 2
    same, cross = {}, {}
    swap = lambda block: swap_bit(block, "dp", 0)
    rows, pair = together(rows, swap(rows))
    left, right = ahead(rows), behind(rows)
    same[0], cross[0], held = expert_chunk([rows, pair], back, gate, mats, 6, None, size)
    for hop in (1, 2, 3):
        pieces = [left, swap(left), right, swap(right)]
        if hop < 3:
            left, right = ahead(left), behind(right)
        else:
            left, right = ahead(left[:cut]), behind(right[cut:])
            pieces[0], waiting = together(pieces[0], waiting)
        same[hop], cross[hop], held = expert_chunk(pieces, back, gate, mats, hop - 1, held, size)
    pieces = [left, right, swap(left), swap(right)]
    same[4], cross[4], held = expert_chunk(pieces, back, gate, mats, 7, held, size)
    return same, cross, held, waiting


def halving_sum(parts):
    bits = parts.shape[0].bit_length() - 1
    index = lax.axis_index("dp")
    for bit in reversed(range(bits)):
        rows = parts.shape[0] // 2
        upper = index >> bit & 1
        kept = lax.dynamic_slice_in_dim(parts, upper * rows, rows, axis=0)
        sent = lax.dynamic_slice_in_dim(parts, (1 - upper) * rows, rows, axis=0)
        parts = kept + swap_bit(sent, "dp", bit)
    return parts[0]


def body(
    inputs,
    attn_gain,
    w_query,
    w_key,
    w_value,
    query_gain,
    key_gain,
    w_out,
    moe_gain,
    w_gate,
    w_up,
    w_down,
    experts,
    gates,
    segments,
    gaps,
    cotangent,
):
    dp_count = lax.axis_size("dp")
    dp_index = lax.axis_index("dp")
    side = lax.axis_index("tensor")
    token_count, model_width = inputs.shape
    half_count = token_count // 2
    top_count = experts.shape[1]
    expert_count = w_gate.shape[0] * dp_count
    capacity = token_count * top_count * dp_count * 9 // (8 * expert_count)
    prompt_length = PR_DEV * GROUP
    column_total = HEADS * HEAD
    block = w_query.shape[0]
    local_width = w_query.shape[1]
    local_heads = local_width // HEAD

    def own_half(array):
        return lax.dynamic_slice_in_dim(array, side * half_count, half_count, axis=0)

    def other_half(array):
        return lax.dynamic_slice_in_dim(array, (1 - side) * half_count, half_count, axis=0)

    def both_halves(own, other):
        first = side == 0
        return jnp.concatenate(
            [jnp.where(first, own, other), jnp.where(first, other, own)], axis=0
        )

    gate_mats = (w_gate[0], swap_tensor(w_gate[0]))
    up_mats = (w_up[0], swap_tensor(w_up[0]))

    ring = dp_count == 2 * len(RING)

    gates_high = gates.astype(LOW)
    gates_low = (gates - gates_high.astype(FULL)).astype(LOW)
    routing = jnp.concatenate([experts.astype(LOW).T, gates_high.T, gates_low.T], axis=1)
    routing = jnp.pad(routing, ((0, 0), (0, local_width - 3 * token_count)))
    gains = jnp.concatenate([attn_gain, moe_gain, query_gain, key_gain])
    gains = jnp.pad(gains[None], ((0, 7), (0, local_width - 4 * block)))
    cotangent_half = own_half(cotangent)
    packed = pack_weights(
        w_query,
        w_key,
        w_value,
        jnp.concatenate([gains, routing], axis=0),
        [cotangent_half] if ring else [],
    )
    gathered = lax.all_gather(packed, "dp", axis=0, tiled=False)
    gathered_out = lax.all_gather(w_out.T, "dp", axis=0, tiled=False)
    gathered, *early = lax.optimization_barrier((gathered, gate_mats[1], up_mats[1]))
    gate_mats, up_mats = (gate_mats[0], early[0]), (up_mats[0], early[1])
    rest = gathered[:, 3 * block : 3 * block + 16]
    gain_rows = rest[:, 0].astype(FULL)
    gain_one, gain_two, gain_q, gain_k = (
        gain_rows[:, j * block : (j + 1) * block].reshape(-1) for j in range(4)
    )
    gain_query_local = lax.dynamic_slice_in_dim(gain_q, side * local_width, local_width)
    gain_key_local = lax.dynamic_slice_in_dim(gain_k, side * local_width, local_width)

    names, *parts = (
        rest[:, 8:, j * token_count : (j + 1) * token_count] for j in range(3)
    )
    weights = parts[0].astype(FULL) + parts[1].astype(FULL)
    named = names == dp_index.astype(LOW)
    picked = jnp.sum(named.astype(FULL), axis=1)
    weight = jnp.sum(jnp.where(named, weights, 0.0), axis=1)
    order = jnp.arange(token_count, dtype=jnp.int32)
    earlier = (order[:, None] < order[None, :]).astype(LOW)
    within = dot_nn(picked.astype(LOW), earlier)
    per_row = jnp.sum(picked, axis=1)
    rows_order = jnp.arange(dp_count, dtype=jnp.int32)
    ahead = jnp.sum(
        jnp.where(rows_order[None, :] < rows_order[:, None], per_row[None, :], 0.0), axis=1
    )
    kept = (picked > 0.0) & (within + ahead[:, None] < capacity)
    weight = jnp.where(kept, weight, 0.0)
    weight = lax.dynamic_slice_in_dim(weight, side * half_count, half_count, axis=1)
    if ring:
        blocks = ring_blocks(dp_index)
        weight = weight[blocks]
    weight = weight.reshape(-1, 1)

    core = dp_index % 2
    tokens_f = inputs.astype(FULL)
    prompt_pos = dp_index % GROUP * PR_DEV + jnp.arange(PR_DEV, dtype=jnp.int32)
    later_pos = cont_positions(segments[0], gaps[0], prompt_length)
    positions = jnp.concatenate([prompt_pos, later_pos], axis=0)
    cosine, sine = rope_tables(positions, HEAD)
    sine = jnp.where(jnp.arange(HEAD) < HEAD // 2, -sine, sine)
    prompt_query = jnp.arange(token_count, dtype=jnp.int32) < PR_DEV
    prompt_at = jnp.arange(prompt_length, dtype=jnp.int32)
    prompt_keypos = ((dp_index % GROUP) ^ (prompt_at // PR_DEV)) * PR_DEV + prompt_at % PR_DEV
    allowed_prompt = (~prompt_query)[:, None] | (prompt_keypos[None, :] <= positions[:, None])
    query_segment = jnp.concatenate([jnp.full((PR_DEV,), -1, jnp.int32), segments[0]], axis=0)
    allowed_cont = (query_segment[:, None] == segments[0][None, :]) & (
        later_pos[None, :] <= positions[:, None]
    )
    allowed = jnp.concatenate([allowed_prompt, allowed_cont], axis=1)
    bias = jnp.where(allowed, 0.0, -1e30).astype(LOW)
    normed_b = rms_norm(tokens_f, gain_one).astype(LOW)
    query_flat, key_flat, values_b = project(
        normed_b, gathered, block, (0, 1, 2), (FULL, FULL, LOW)
    )
    key_sq = jnp.sum(key_flat * key_flat, axis=1)
    key_sq, value_prompt = together(key_sq, values_b[:PR_DEV])
    value_pieces = collect_prompt(value_prompt, 1, 2)
    query_sq, key_sq = lax.psum(
        (jnp.sum(query_flat * query_flat, axis=1), key_sq), "tensor"
    )
    query_sq, down_mat = lax.optimization_barrier((query_sq, w_down[0]))
    down_mats = (down_mat, swap_tensor(down_mat))
    query_scale = lax.rsqrt(query_sq / column_total + EPSILON)[:, None]
    key_scale = lax.rsqrt(key_sq / column_total + EPSILON)[:, None]
    keys_b = rope_pass(key_flat, gain_key_local[None], key_scale, cosine, sine)
    pieces = (*collect_prompt(keys_b[:PR_DEV], 2, 1), *value_pieces)
    queries_b = rope_pass(query_flat, gain_query_local[None], query_scale, cosine, sine)
    context_b = attend(queries_b, keys_b, values_b, bias, pieces)
    attn_part = project_back([context_b], gathered_out, block, (0,))
    attn_part, late, weight = together(attn_part, down_mats[1], weight)
    down_mats = (down_mats[0], late)
    mats = (*gate_mats, *up_mats, *down_mats)
    attn_other = swap_tensor(other_half(attn_part).astype(LOW))
    if ring:
        gathered, attn_part = together(gathered, attn_part)
        back_rows = unpack_rows(gathered, blocks, 3 * block + 16, model_width)
    else:
        back_rows = lax.all_gather(cotangent_half.astype(LOW), "dp", axis=0, tiled=True)
    attn_other, back_rows, weight = together(attn_other, back_rows, weight)
    hidden_state = own_half(tokens_f) + own_half(attn_part) + attn_other.astype(FULL)
    normed_two_b = rms_norm(hidden_state, gain_two).astype(LOW)

    low_tn = lambda left, right: dot_tn(left, right).astype(LOW)
    upper = lambda array: array[: array.shape[0] // 2]
    lower = lambda array: array[array.shape[0] // 2 :]
    hidden_other = swap_tensor(hidden_state)
    if ring:
        same, cross, held, hidden_other = expert_ring(
            normed_two_b, back_rows, weight, mats, hidden_other
        )
        expert_in, h0, h1, g0, g1, u0, u1 = held
        down_got = swap_tensor(low_tn(h1, back_rows))
        fillers = Fillers(
            [
                [(low_tn, expert_in, g1)],
                [(low_tn, expert_in, u1)],
                [(lambda *h: mixed_pass(*h, down_mats, blocks), h0, h1)],
            ]
        )
        normed_two_grad = ring_sum(same, cross, fillers)
        gate_sent, up_sent, mixed_rows = fillers.outs
    else:
        expert_in = lax.all_gather(normed_two_b, "dp", axis=0, tiled=True)
        grad_rows, h0, h1, g0, g1, u0, u1 = expert_pass(
            expert_in, back_rows, weight, gate_mats, up_mats, down_mats
        )
        normed_two_grad = lax.psum_scatter(
            grad_rows, "dp", scatter_dimension=0, tiled=True
        ).astype(FULL)
        mixed_rows = (dot_nn(h0, down_mats[0]) + dot_nn(h1, down_mats[1])).astype(LOW)
        down_got = swap_tensor(low_tn(h1, back_rows))
        gate_sent = low_tn(expert_in, g1)
        up_sent = low_tn(expert_in, u1)
    gate_first = swap_tensor(upper(gate_sent))
    normed_two_grad, down_got, gate_first, mixed_rows = together(
        normed_two_grad, down_got, gate_first, mixed_rows
    )
    mixed = lax.psum_scatter(mixed_rows, "dp", scatter_dimension=0, tiled=True)

    unused_two, norm_two_back = jax.vjp(rms_norm, hidden_state, gain_two)
    state_part, gain_two_grad = norm_two_back(normed_two_grad)
    state_half = cotangent_half + state_part
    attn_grad_half = state_half.astype(LOW)
    attn_grad_b = both_halves(attn_grad_half, swap_tensor(attn_grad_half))
    attn_grad_b, gate_sent = together(attn_grad_b, gate_sent)
    gate_second = swap_tensor(lower(gate_sent))
    (context_grad_b,) = project(attn_grad_b, gathered_out, block, (0,), (LOW,))
    query_normed_grad, query_inner, query_gain_part, key_grad, value_grad, odd, even = attend_back(
        queries_b,
        keys_b,
        values_b,
        bias,
        context_grad_b,
        query_flat,
        gain_query_local[None],
        query_scale,
        cosine,
        sine,
        pieces,
    )
    query_inner, gate_second = together(query_inner, gate_second)
    query_inner = lax.psum(query_inner[:, 0], "tensor")
    query_inner, up_sent = together(query_inner, up_sent)
    up_first = swap_tensor(upper(up_sent))
    query_pre_grad = (
        query_scale * gain_query_local * query_normed_grad
        - query_flat * (query_scale * query_scale * query_scale) * (query_inner / column_total)[:, None]
    ).astype(LOW)
    if ring:
        columns = local_width // 2
        mine = lambda a: lax.dynamic_slice_in_dim(a, core * columns, columns, axis=1)
        theirs = lambda a: lax.dynamic_slice_in_dim(a, (1 - core) * columns, columns, axis=1)
        pair = lambda own, sent: jnp.concatenate([own, swap_bit(sent, "dp", 0)], axis=0)
        half = lambda a: pair(mine(a), theirs(a))
        normed_pair, attn_grad_pair = pair(normed_b, normed_b), pair(attn_grad_b, attn_grad_b)
        normed_pair, attn_grad_pair, context_half = together(
            normed_pair, attn_grad_pair, half(context_b)
        )
        normed_pair, query_half = together(normed_pair, half(query_pre_grad))
        first_halves = ring_weights(
            low_tn(normed_pair, query_half), low_tn(attn_grad_pair, context_half), Fillers([])
        )
    returned = return_prompt(odd, even)
    key_normed_grad, key_inner, key_gain_part, value_pre_grad = key_back(
        key_grad, value_grad, key_flat, gain_key_local[None], key_scale, cosine, sine, returned
    )
    key_inner, up_first = together(key_inner, up_first)
    key_inner = lax.psum(key_inner[:, 0], "tensor")
    key_inner, mixed, up_sent = together(key_inner, mixed, up_sent)
    up_second = swap_tensor(lower(up_sent))
    mixed_other = swap_tensor(mixed)
    key_pre_grad = (
        key_scale * gain_key_local * key_normed_grad
        - key_flat * (key_scale * key_scale * key_scale) * (key_inner / column_total)[:, None]
    ).astype(LOW)
    output = both_halves(
        hidden_state + mixed.astype(FULL), hidden_other + mixed_other.astype(FULL)
    )
    wide = lambda part: lax.dynamic_update_slice_in_dim(
        jnp.zeros((column_total,), FULL), part, side * local_width, 0
    )
    gate_got = jnp.concatenate([gate_first, gate_second], axis=0)
    up_got = jnp.concatenate([up_first, up_second], axis=0)
    pre_grads = (query_pre_grad, key_pre_grad, value_pre_grad)
    grad_sum = lambda left, right, got: dot_tn(left, right) + got.astype(FULL)
    down, gate, up = (h0, back_rows, down_got), (expert_in, g0, gate_got), (expert_in, u0, up_got)
    back_all = lambda *grads: project_back(grads, gathered, block, (0, 1, 2))
    if ring:
        fillers = Fillers(
            [
                [(back_all, *pre_grads)],
                [(grad_sum, *down)],
                [(grad_sum, *gate)],
                [(grad_sum, *up)],
            ]
        )
        second_halves = ring_weights(
            low_tn(normed_pair, half(key_pre_grad)),
            low_tn(normed_pair, half(value_pre_grad)),
            fillers,
        )
        normed_part, down_grad, gate_w_grad, up_w_grad = fillers.outs
        w_half = jnp.concatenate([first_halves, second_halves], axis=1)
        own_w = lax.dynamic_slice_in_dim(w_half, core * block, block, axis=0)
        got_w = swap_bit(
            lax.dynamic_slice_in_dim(w_half, (1 - core) * block, block, axis=0), "dp", 0
        )
        left_w, right_w = jnp.where(core == 0, own_w, got_w), jnp.where(core == 0, got_w, own_w)
        w_sums = [
            jnp.concatenate([w[:, j * columns : (j + 1) * columns] for w in (left_w, right_w)], axis=1)
            for j in (0, 2, 3, 1)
        ]
    else:
        w_grads = jnp.concatenate(
            [low_tn(normed_b, g) for g in pre_grads] + [low_tn(attn_grad_b, context_b)], axis=1
        )
        w_sum = lax.psum_scatter(w_grads, "dp", scatter_dimension=0, tiled=True).astype(FULL)
        w_sums = [w_sum[:, j * local_width : (j + 1) * local_width] for j in range(4)]
        down_grad, gate_w_grad, up_w_grad = grad_sum(*down), grad_sum(*gate), grad_sum(*up)
        normed_part = back_all(*pre_grads)
    normed_other = swap_tensor(other_half(normed_part).astype(LOW))
    normed_grad = own_half(normed_part) + normed_other.astype(FULL)
    unused_one, norm_one_back = jax.vjp(rms_norm, own_half(tokens_f), gain_one)
    input_part, gain_one_grad = norm_one_back(normed_grad)
    input_half = state_half + input_part
    input_grad = both_halves(input_half, swap_tensor(input_half))
    gain_grads = jnp.stack(
        [gain_one_grad, gain_two_grad, wide(query_gain_part[0]), wide(key_gain_part[0])]
    ).reshape(4, dp_count, block)
    gain_sums = halving_sum(jnp.swapaxes(gain_grads, 0, 1))
    gain_sums = gain_sums + swap_tensor(gain_sums)
    return (
        output,
        input_grad,
        gain_sums[0],
        w_sums[0],
        w_sums[1],
        w_sums[2],
        gain_sums[2],
        gain_sums[3],
        w_sums[3].T,
        gain_sums[1],
        gate_w_grad[None],
        up_w_grad[None],
        down_grad[None],
    )


def solution(mesh):
    return jax.shard_map(
        body,
        mesh=mesh,
        in_specs=(
            P("dp", None),
            P("dp"),
            P("dp", "tensor"),
            P("dp", "tensor"),
            P("dp", "tensor"),
            P("dp"),
            P("dp"),
            P("tensor", "dp"),
            P("dp"),
            P("dp", None, "tensor"),
            P("dp", None, "tensor"),
            P("dp", "tensor", None),
            P("dp", None),
            P("dp", None),
            P("dp", None),
            P("dp", None),
            P("dp", None),
        ),
        out_specs=(
            P("dp", None),
            P("dp", None),
            P("dp"),
            P("dp", "tensor"),
            P("dp", "tensor"),
            P("dp", "tensor"),
            P("dp"),
            P("dp"),
            P("tensor", "dp"),
            P("dp"),
            P("dp", None, "tensor"),
            P("dp", None, "tensor"),
            P("dp", "tensor", None),
        ),
        check_vma=False,
    )
```

```python
import jax
import jax.numpy as jnp
from jax import lax
from jax.experimental import pallas as pl
from jax.experimental.pallas import tpu as pltpu
from jax.sharding import PartitionSpec as P

HEADS = 16
HEAD = 128
GROUP = 8
PR_DEV = 128


EPSILON = 1e-05
LOW = jnp.bfloat16
FULL = jnp.float32


def swap_bit(block, axis, bit):
    count = lax.axis_size(axis)
    return lax.ppermute(block, axis, [(i, i ^ (1 << bit)) for i in range(count)])


def swap_tensor(block):
    return lax.ppermute(block, "tensor", [(0, 1), (1, 0)])


RING = (0, 2, 4, 6, 7, 5, 3, 1)
AHEAD = [
    (RING[p] * 2 + c, RING[(p + 1) % len(RING)] * 2 + c) for p in range(len(RING)) for c in range(2)
]
BEHIND = [(to, at) for at, to in AHEAD]
HOPS = (-1, 1, -2, 2, -3, 3, 0, 4)


def ahead(block):
    return lax.ppermute(block, "dp", AHEAD)


def behind(block):
    return lax.ppermute(block, "dp", BEHIND)


def ring_blocks(dp_index):
    chip, core = dp_index // 2, dp_index % 2
    place = jnp.where(chip % 2 == 0, chip // 2, 7 - chip // 2)
    steps, cross = [], []
    for hop in HOPS:
        steps += [hop, hop]
        cross += [0, 1]
    there = (place + jnp.array(steps, jnp.int32)) % 8
    chips = jnp.where(there < 4, 2 * there, 2 * (7 - there) + 1)
    return 2 * chips + (core ^ jnp.array(cross, jnp.int32))


def add_low(*parts):
    total = parts[0].astype(FULL)
    for part in parts[1:]:
        total = total + part.astype(FULL)
    return total.astype(LOW)


def together(value, *others):
    return lax.optimization_barrier((value, *others))


def after(value, token):
    return lax.optimization_barrier((value, token))[0]


class Fillers:
    def __init__(self, stages):
        self.stages = list(stages)
        self.outs = []

    def next(self, token):
        for work, *operands in self.stages.pop(0) if self.stages else ():
            operands = [after(operand, token) for operand in operands]
            self.outs.append(work(*operands))


def ring_sum(same, cross, fillers):
    both = {hop: add_low(same[hop], swap_bit(cross[hop], "dp", 0)) for hop in (4, 3, 2, 1, 0)}
    rows = both[0].shape[0]
    cut = rows // 2
    right, left = ahead(both[4][:cut]), behind(both[4][cut:])
    fillers.next(left)
    outward, inward = both[3][rows:], both[3][:rows]
    right = jnp.concatenate([add_low(outward[:cut], right), outward[cut:]], axis=0)
    left = jnp.concatenate([inward[:cut], add_low(inward[cut:], left)], axis=0)
    right, left = ahead(right), behind(left)
    fillers.next(left)
    for hop in (2, 1):
        right = ahead(add_low(both[hop][rows:], right))
        left = behind(add_low(both[hop][:rows], left))
        fillers.next(left)
    return both[0].astype(FULL) + right.astype(FULL) + left.astype(FULL)


def rms_norm(values, gain):
    return values * lax.rsqrt(jnp.mean(values * values, axis=-1, keepdims=True) + EPSILON) * gain


def rope_tables(positions, head_size):
    half_size = head_size // 2
    inverse = 10000.0 ** (-(jnp.arange(half_size, dtype=FULL) * 2.0) / head_size)
    angles = positions.astype(FULL)[:, None] * inverse[None, :]
    cosine = jnp.concatenate([jnp.cos(angles), jnp.cos(angles)], axis=-1)
    sine = jnp.concatenate([jnp.sin(angles), jnp.sin(angles)], axis=-1)
    return (cosine, sine)


def cont_positions(segment_row, gap_row, prompt_length):
    order = jnp.arange(segment_row.shape[0], dtype=jnp.int32)
    same = segment_row[:, None] == segment_row[None, :]
    earlier = order[None, :] < order[:, None]
    offset = jnp.sum((same & earlier).astype(jnp.int32), axis=1)
    labels = jnp.arange(gap_row.shape[0], dtype=jnp.int32)
    shifted = jnp.sum(
        jnp.where(segment_row[:, None] == labels[None, :], gap_row[None, :], 0), axis=1
    )
    return prompt_length + shifted + offset


def dot_nn(left, right):
    return jnp.dot(left, right, preferred_element_type=FULL)


def dot_tn(left, right):
    return lax.dot_general(left, right, (((0,), (0,)), ((), ())), preferred_element_type=FULL)


def dot_nt(left, right):
    return lax.dot_general(left, right, (((1,), (1,)), ((), ())), preferred_element_type=FULL)


def collect_prompt(own, first, second):
    near, far = swap_bit(own, "dp", 1), swap_bit(own, "dp", 2)
    last = swap_bit(near if first == 1 else far, "dp", second)
    stay = jnp.stack([own, near, far, last], axis=0)
    return stay, swap_bit(stay, "dp", 0)


def merge_kernel(even_ref, got_ref, keys_ref, values_ref, far_ref, near_ref):
    near, far, last = 0, 1, 2
    add = lambda j, which: add_low(even_ref[j, which], got_ref[j + 1, which])
    keys_ref[0], keys_ref[1] = add(near, 0), add(last, 0)
    values_ref[0], values_ref[1] = add(far, 1), add(last, 1)
    far_ref[...], near_ref[...] = add(far, 0), add(near, 1)


def return_prompt(odd, even):
    got = swap_bit(odd, "dp", 0)
    one = jax.ShapeDtypeStruct(even.shape[2:], LOW)
    two = jax.ShapeDtypeStruct(even.shape[1:], LOW)
    keys, values, far, near = pl.pallas_call(merge_kernel, out_shape=[two, two, one, one])(even, got)
    keys, values = swap_bit(keys, "dp", 1), swap_bit(values, "dp", 2)
    last_keys = swap_bit(add_low(far, keys[1]), "dp", 2)
    last_values = swap_bit(add_low(near, values[1]), "dp", 1)
    return got, keys, values, last_keys, last_values


def turn(values):
    return pltpu.roll(values, HEAD // 2, 1)


def rope_kernel(pre_ref, gain_ref, scale_ref, cos_ref, sin_ref, out_ref):
    scale, cosine, sine = scale_ref[...], cos_ref[...], sin_ref[...]
    for at in range(0, pre_ref.shape[1], HEAD):
        span = slice(at, at + HEAD)
        normed = pre_ref[:, span] * scale * gain_ref[:, span]
        out_ref[:, span] = (normed * cosine + turn(normed) * sine).astype(LOW)


def rope_pass(flat, gain, scale, cosine, sine):
    rows, width = flat.shape
    part = width // 2
    wide = lambda rows: pl.BlockSpec((rows, part), lambda h: (0, h))
    return pl.pallas_call(
        rope_kernel,
        grid=(2,),
        in_specs=[wide(rows), wide(1)] + [kept_spec(a) for a in (scale, cosine, sine)],
        out_specs=wide(rows),
        out_shape=jax.ShapeDtypeStruct((rows, width), LOW),
    )(flat, gain, scale, cosine, sine)


PAIR = 2


def head_spec(rows):
    return pl.BlockSpec((rows, PAIR * HEAD), lambda h: (0, h))


def kept_spec(array):
    zeros = (0,) * array.ndim
    return pl.BlockSpec(array.shape, lambda h: zeros, pipeline_mode=pl.Buffered(1))


def piece_spec(count):
    return pl.BlockSpec((count, PR_DEV, PAIR * HEAD), lambda h: (0, 0, h))


def all_keys(own_ref, stay_ref, cross_ref, span):
    blocks = []
    for j in range(GROUP // 2):
        blocks += [stay_ref[j, :, span], cross_ref[j, :, span]]
    return jnp.concatenate(blocks + [own_ref[PR_DEV:, span]], axis=0)


def softmax_rows(query, keys, bias):
    scores = dot_nt(query, keys) * HEAD ** (-0.5) + bias
    weights = jnp.exp(scores - jnp.max(scores, axis=1, keepdims=True))
    return weights * (1.0 / jnp.sum(weights, axis=1, keepdims=True))


def attend_kernel(q_ref, k_ref, v_ref, bias_ref, k_stay, k_cross, v_stay, v_cross, out_ref):
    bias = bias_ref[...].astype(FULL)
    for at in range(0, PAIR * HEAD, HEAD):
        span = slice(at, at + HEAD)
        probs = softmax_rows(q_ref[:, span], all_keys(k_ref, k_stay, k_cross, span), bias)
        out_ref[:, span] = dot_nn(
            probs.astype(LOW), all_keys(v_ref, v_stay, v_cross, span)
        ).astype(LOW)


def attend(queries, keys, values, bias, pieces):
    rows, width = queries.shape
    return pl.pallas_call(
        attend_kernel,
        grid=(width // HEAD // PAIR,),
        in_specs=[head_spec(rows)] * 3 + [kept_spec(bias)] + [piece_spec(GROUP // 2)] * 4,
        out_specs=head_spec(rows),
        out_shape=jax.ShapeDtypeStruct((rows, width), LOW),
        compiler_params=pltpu.CompilerParams(vmem_limit_bytes=40 * 1024 * 1024),
    )(queries, keys, values, bias, *pieces)


def norm_parts(step, at, grad, flat_ref, gain_ref, scale_ref, inner_ref, gain_grad_ref):
    span = slice(at, at + HEAD)
    product = flat_ref[:, span] * grad
    inner = jnp.sum(product * gain_ref[:, span], axis=1, keepdims=True)
    gain_grad_ref[:, span] = jnp.sum(product * scale_ref[...], axis=0, keepdims=True)
    if at:
        inner_ref[...] += inner
    else:
        inner_ref[...] = jnp.where(step == 0, 0.0, inner_ref[...]) + inner


def attend_back_kernel(
    q_ref,
    k_ref,
    v_ref,
    bias_ref,
    back_ref,
    flat_ref,
    gain_ref,
    scale_ref,
    cos_ref,
    sin_ref,
    k_stay,
    k_cross,
    v_stay,
    v_cross,
    qg_ref,
    inner_ref,
    gain_grad_ref,
    kg_ref,
    vg_ref,
    odd_ref,
    even_ref,
):
    step = pl.program_id(0)
    bias = bias_ref[...].astype(FULL)
    cosine, sine = cos_ref[...], sin_ref[...]
    prompt = PR_DEV * GROUP
    for at in range(0, PAIR * HEAD, HEAD):
        span = slice(at, at + HEAD)
        query, back = q_ref[:, span], back_ref[:, span]
        keys = all_keys(k_ref, k_stay, k_cross, span)
        values = all_keys(v_ref, v_stay, v_cross, span)
        probs = softmax_rows(query, keys, bias)
        prob_grad = dot_nt(back, values)
        value_grad = dot_tn(probs.astype(LOW), back)
        row_dot = jnp.sum(probs * prob_grad, axis=1, keepdims=True)
        score_grad = (probs * (prob_grad - row_dot)).astype(LOW)
        query_grad = dot_nn(score_grad, keys) * HEAD ** (-0.5)
        key_grad = dot_tn(score_grad, query) * HEAD ** (-0.5)
        query_grad = query_grad * cosine - turn(query_grad) * sine
        qg_ref[:, span] = query_grad
        norm_parts(step, at, query_grad, flat_ref, gain_ref, scale_ref, inner_ref, gain_grad_ref)
        for which, grad, own_ref in ((0, key_grad, kg_ref), (1, value_grad, vg_ref)):
            own_ref[:PR_DEV, span] = grad[:PR_DEV]
            own_ref[PR_DEV:, span] = grad[prompt:]
            for j in range(1, GROUP):
                to = odd_ref if j % 2 else even_ref
                to[(j - 1) // 2, which, :, span] = grad[j * PR_DEV : (j + 1) * PR_DEV].astype(LOW)


def attend_back(queries, keys, values, bias, back, flat, gain, scale, cosine, sine, pieces):
    rows, width = queries.shape
    wide = jax.ShapeDtypeStruct((rows, width), FULL)
    both = lambda count: pl.BlockSpec((count, 2, PR_DEV, PAIR * HEAD), lambda h: (0, 0, 0, h))
    return pl.pallas_call(
        attend_back_kernel,
        grid=(width // HEAD // PAIR,),
        in_specs=[head_spec(rows)] * 3
        + [kept_spec(bias), head_spec(rows), head_spec(rows), head_spec(1)]
        + [kept_spec(a) for a in (scale, cosine, sine)]
        + [piece_spec(GROUP // 2)] * 4,
        out_specs=[
            head_spec(rows),
            pl.BlockSpec((rows, 1), lambda h: (0, 0)),
            head_spec(1),
            head_spec(rows),
            head_spec(rows),
            both(4),
            both(3),
        ],
        out_shape=[
            wide,
            jax.ShapeDtypeStruct((rows, 1), FULL),
            jax.ShapeDtypeStruct((1, width), FULL),
            wide,
            wide,
            jax.ShapeDtypeStruct((4, 2, PR_DEV, width), LOW),
            jax.ShapeDtypeStruct((3, 2, PR_DEV, width), LOW),
        ],
        compiler_params=pltpu.CompilerParams(vmem_limit_bytes=58 * 1024 * 1024),
    )(queries, keys, values, bias, back, flat, gain, scale, cosine, sine, *pieces)


def key_back_kernel(*refs):
    kg_ref, vg_ref, flat_ref, gain_ref, scale_ref, cos_ref, sin_ref = refs[:7]
    got, keys, values, last_keys, last_values = refs[7:12]
    out_ref, inner_ref, gain_grad_ref, value_ref = refs[12:]
    step = pl.program_id(0)
    for at in range(0, PAIR * HEAD, HEAD):
        span = slice(at, at + HEAD)
        grads = []
        for which, own_ref, near, last in ((0, kg_ref, keys, last_keys), (1, vg_ref, values, last_values)):
            first = own_ref[:PR_DEV, span] + got[0, which, :, span].astype(FULL)
            first = first + near[0, :, span].astype(FULL) + last[:, span].astype(FULL)
            grads.append(jnp.concatenate([first, own_ref[PR_DEV:, span]], axis=0))
        key_grad = grads[0] * cos_ref[...] - turn(grads[0]) * sin_ref[...]
        out_ref[:, span] = key_grad
        norm_parts(step, at, key_grad, flat_ref, gain_ref, scale_ref, inner_ref, gain_grad_ref)
        value_ref[:, span] = grads[1].astype(LOW)


def key_back(key_grad, value_grad, flat, gain, scale, cosine, sine, returned):
    rows, width = flat.shape
    columns = PAIR * HEAD
    return pl.pallas_call(
        key_back_kernel,
        grid=(width // columns,),
        in_specs=[head_spec(rows)] * 3
        + [head_spec(1)]
        + [kept_spec(a) for a in (scale, cosine, sine)]
        + [pl.BlockSpec((1, 2, PR_DEV, columns), lambda h: (0, 0, 0, h))]
        + [pl.BlockSpec((1, PR_DEV, columns), lambda h: (0, 0, h))] * 2
        + [head_spec(PR_DEV)] * 2,
        out_specs=[
            head_spec(rows),
            pl.BlockSpec((rows, 1), lambda h: (0, 0)),
            head_spec(1),
            head_spec(rows),
        ],
        out_shape=[
            jax.ShapeDtypeStruct((rows, width), FULL),
            jax.ShapeDtypeStruct((rows, 1), FULL),
            jax.ShapeDtypeStruct((1, width), FULL),
            jax.ShapeDtypeStruct((rows, width), LOW),
        ],
    )(key_grad, value_grad, flat, gain, scale, cosine, sine, *returned)


def pack_kernel(query, key, value, rest, out, *refs):
    packed, turned = refs[-2:]
    at = 0
    for ref in (query, key, value, rest):
        packed[at : at + ref.shape[0]] = ref[...]
        at += ref.shape[0]
    for back in refs[:-2]:
        width = packed.shape[1]
        for start in range(0, back.shape[1], width):
            packed[at : at + back.shape[0]] = back[:, start : start + width].astype(LOW)
            at += back.shape[0]
    turned[...] = out[...].T


def pack_weights(w_query, w_key, w_value, rest, w_out, back):
    width = w_query.shape[1]
    rows = 3 * w_query.shape[0] + rest.shape[0] + sum(b.size // width for b in back)
    return pl.pallas_call(
        pack_kernel,
        out_shape=[
            jax.ShapeDtypeStruct((rows, width), LOW),
            jax.ShapeDtypeStruct(w_out.shape[::-1], LOW),
        ],
    )(w_query, w_key, w_value, rest, w_out, *back)


def unpack_kernel(first, blocks_ref, packed, out, held, sems):
    width = packed.shape[2]
    parts = out.shape[1] // width
    rows = (packed.shape[1] - first) // parts
    count = packed.shape[0]
    place = lambda i: pl.ds(i * rows, rows)
    loads = [
        pltpu.make_async_copy(
            packed.at[blocks_ref[i], pl.ds(first + j * rows, rows)],
            held.at[place(i), pl.ds(j * width, width)],
            sems.at[i * parts + j],
        )
        for i in range(count)
        for j in range(parts)
    ]
    stores = [
        pltpu.make_async_copy(held.at[place(i)], out.at[place(i)], sems.at[count * parts + i])
        for i in range(count)
    ]
    for one in loads:
        one.start()
    for i, store in enumerate(stores):
        for j in range(parts):
            loads[i * parts + j].wait()
        store.start()
    for store in stores:
        store.wait()


def unpack_rows(packed, blocks, first, width):
    count = packed.shape[0]
    parts = width // packed.shape[2]
    rows = (packed.shape[1] - first) // parts
    return pl.pallas_call(
        lambda *refs: unpack_kernel(first, *refs),
        in_specs=[pl.BlockSpec(memory_space=pltpu.SMEM), pl.BlockSpec(memory_space=pl.ANY)],
        out_specs=pl.BlockSpec(memory_space=pl.ANY),
        out_shape=jax.ShapeDtypeStruct((count * rows, width), LOW),
        scratch_shapes=[
            pltpu.VMEM((count * rows, width), LOW),
            pltpu.SemaphoreType.DMA((count * parts + count,)),
        ],
        compiler_params=pltpu.CompilerParams(vmem_limit_bytes=24 * 1024 * 1024),
    )(blocks, packed)


def pack_specs(gathered, places, steps, at):
    count, width = gathered.shape[0] // steps, gathered.shape[2]
    block = at
    return [
        pl.BlockSpec((count, block, width), lambda i, place=place: (i, place, 0))
        for place in places
    ]


def project_kernel(mats, roundings, rows_ref, *refs):
    mat_refs, out_refs, totals = refs[:mats], refs[mats : 2 * mats], refs[2 * mats :]
    step = pl.program_id(0)
    rows = rows_ref[...]
    for mat, out, total, rounding in zip(mat_refs, out_refs, totals, roundings):
        flat = mat[...].reshape(-1, mat.shape[2])
        part = dot_nn(rows, flat)

        @pl.when(step == 0)
        def _():
            total[...] = part

        @pl.when(step > 0)
        def _():
            total[...] += part

        @pl.when(step == pl.num_programs(0) - 1)
        def _():
            out[...] = total[...].astype(rounding)


def project(rows, gathered, block, places, roundings):
    count, width = rows.shape
    columns = gathered.shape[2]
    steps = 4
    outs = [jax.ShapeDtypeStruct((count, columns), rounding) for rounding in roundings]
    return pl.pallas_call(
        lambda *refs: project_kernel(len(places), roundings, *refs),
        grid=(steps,),
        in_specs=[pl.BlockSpec((count, width // steps), lambda i: (0, i))]
        + pack_specs(gathered, places, steps, block),
        out_specs=[pl.BlockSpec((count, columns), lambda i: (0, 0)) for _ in outs],
        out_shape=outs,
        scratch_shapes=[pltpu.VMEM((count, columns), FULL)] * len(outs),
        compiler_params=pltpu.CompilerParams(vmem_limit_bytes=40 * 1024 * 1024),
        cost_estimate=pl.CostEstimate(
            flops=2 * count * width * columns * len(places),
            bytes_accessed=2 * width * columns * len(places) + 8 * count * columns,
            transcendentals=0,
        ),
    )(rows, *[gathered] * len(places))


def project_back_kernel(mats, *refs):
    out = refs[-1]
    total = None
    for rows_ref, mat in zip(refs[:mats], refs[mats:-1]):
        part = dot_nt(rows_ref[...], mat[...].reshape(-1, mat.shape[2]))
        total = part if total is None else total + part
    out[...] = total


def project_back(rows, gathered, block, places):
    count, columns = rows[0].shape
    width = gathered.shape[0] * block
    steps = 4
    fixed = pl.BlockSpec((count, columns), lambda i: (0, 0), pipeline_mode=pl.Buffered(1))
    return pl.pallas_call(
        lambda *refs: project_back_kernel(len(places), *refs),
        grid=(steps,),
        in_specs=[fixed] * len(rows) + pack_specs(gathered, places, steps, block),
        out_specs=pl.BlockSpec((count, width // steps), lambda i: (0, i)),
        out_shape=jax.ShapeDtypeStruct((count, width), FULL),
        compiler_params=pltpu.CompilerParams(vmem_limit_bytes=40 * 1024 * 1024),
        cost_estimate=pl.CostEstimate(
            flops=2 * count * width * columns * len(places),
            bytes_accessed=2 * width * columns * len(places) + 4 * count * width,
            transcendentals=0,
        ),
    )(*rows, *[gathered] * len(places))


def ring_weights(first, second, fillers):
    rows = first.shape[0] // len(RING)
    cut = (first.shape[1] + second.shape[1]) // 2
    chip = lax.axis_index("dp") // 2
    place = jnp.where(chip % 2 == 0, chip // 2, 7 - chip // 2)

    def part(hop):
        there = (place + hop) % len(RING)
        at = jnp.where(there < 4, 2 * there, 2 * (7 - there) + 1) * rows
        return jnp.concatenate(
            [lax.dynamic_slice_in_dim(a, at, rows, axis=0) for a in (first, second)], axis=1
        )

    far = part(4)
    right, left = ahead(far[:, :cut]), behind(far[:, cut:])
    fillers.next(left)
    outward, inward = part(3), part(-3)
    right = jnp.concatenate([add_low(outward[:, :cut], right), outward[:, cut:]], axis=1)
    left = jnp.concatenate([inward[:, :cut], add_low(inward[:, cut:], left)], axis=1)
    right, left = ahead(right), behind(left)
    fillers.next(left)
    token = left
    for hop in (2, 1):
        right, left = ahead(add_low(part(hop), right)), behind(add_low(part(-hop), left))
        fillers.next(left)
        token = left if hop == 2 else token
    return part(0).astype(FULL) + right.astype(FULL) + left.astype(FULL), token


def expert_kernel(
    rows_ref, back_ref, gate_ref, wg0, wg1, wu0, wu1, wd0, wd1, grad_ref, h0, h1, g0, g1, u0, u1
):
    rows = rows_ref[...]
    back = back_ref[...]
    gate = gate_ref[...]
    total = None
    for wg, wu, wd, h, g, u in ((wg0, wu0, wd0, h0, g0, u0), (wg1, wu1, wd1, h1, g1, u1)):
        gate_pre = dot_nn(rows, wg[...])
        up_pre = dot_nn(rows, wu[...])
        hidden_grad = gate * dot_nt(back, wd[...])
        sig = 1.0 / (1.0 + jnp.exp(-gate_pre))
        act = gate_pre * sig
        h[...] = (gate * (act * up_pre)).astype(LOW)
        gate_grad = (hidden_grad * up_pre * (sig * (1.0 + gate_pre * (1.0 - sig)))).astype(LOW)
        up_grad = (hidden_grad * act).astype(LOW)
        g[...] = gate_grad
        u[...] = up_grad
        part = dot_nt(gate_grad, wg[...]) + dot_nt(up_grad, wu[...])
        total = part if total is None else total + part
    grad_ref[...] = total.astype(LOW)


def expert_pass(rows, back, gate, gate_mats, up_mats, down_mats):
    count, width = rows.shape
    hidden = gate_mats[0].shape[1]
    tile = 256
    whole = lambda array: pl.BlockSpec(
        array.shape, lambda i: (0, 0), pipeline_mode=pl.Buffered(1)
    )
    tall = lambda columns: pl.BlockSpec((tile, columns), lambda i: (i, 0))
    mats = [*gate_mats, *up_mats, *down_mats]
    flops = 2 * 5 * count * width * hidden * 2
    return pl.pallas_call(
        expert_kernel,
        grid=(count // tile,),
        in_specs=[tall(width), tall(width), tall(1)] + [whole(m) for m in mats],
        out_specs=[tall(width)] + [tall(hidden)] * 6,
        out_shape=[jax.ShapeDtypeStruct((count, width), LOW)]
        + [jax.ShapeDtypeStruct((count, hidden), LOW)] * 6,
        compiler_params=pltpu.CompilerParams(vmem_limit_bytes=58 * 1024 * 1024),
        cost_estimate=pl.CostEstimate(
            flops=flops,
            bytes_accessed=2 * (3 * count * width + 6 * count * hidden + 6 * width * hidden),
            transcendentals=2 * count * hidden,
        ),
    )(rows, back, gate, *mats)


def chunk_kernel(pieces, held, at, size, gate_ref, *refs):
    piece_refs, refs = refs[:pieces], refs[pieces:]
    back_ref, mats, refs = refs[0], refs[1:7], refs[7 + held :]
    same_ref, cross_ref, rows_out = refs[:3]
    outs = refs[3:9]
    rows, back, wide, wd, hidden, both_grads, grads, sems = refs[9:]
    count = rows.shape[0]
    part = wd.shape[1]
    slab = wide.shape[0] // 4
    across = lambda k, half: pl.ds((2 * k + half) * part, part)
    place = pl.ds(at * count, count)
    copy = pltpu.make_async_copy
    load_rows, start = [], 0
    for piece in piece_refs:
        span = pl.ds(start, piece.shape[0])
        load_rows.append(copy(piece, rows.at[span], sems.at[len(load_rows)]))
        start += piece.shape[0]
    load_back = copy(back_ref.at[place], back, sems.at[4])
    loads = []
    for half in range(2):
        places = [wide.at[:, across(0, half)], wide.at[:, across(1, half)], wd.at[half]]
        loads.append(
            [copy(mats[2 * k + half], to, sems.at[5 + 3 * half + k]) for k, to in enumerate(places)]
        )
    for one in load_rows + loads[0][:2] + [load_back] + loads[0][2:] + loads[1]:
        one.start()
    gate = gate_ref[...]
    for one in load_rows:
        one.wait()
    stores = [copy(rows, rows_out.at[place], sems.at[11])]
    stores[0].start()
    for half in range(2):
        columns = pl.ds(half * part, part)
        if half == 0:
            loads[0][0].wait()
        gate_pre = dot_nn(rows[...], wide[:, across(0, half)])
        if half == 0:
            loads[0][1].wait()
        up_pre = dot_nn(rows[...], wide[:, across(1, half)])
        if half == 0:
            load_back.wait()
            for one in loads[0][2:] + loads[1]:
                one.wait()
        hidden_grad = gate * dot_nt(back[...], wd[half])
        sig = 1.0 / (1.0 + jnp.exp(-gate_pre))
        act = gate_pre * sig
        hidden[:, columns] = (gate * (act * up_pre)).astype(LOW)
        both_grads[:, across(0, half)] = (
            hidden_grad * up_pre * (sig * (1.0 + gate_pre * (1.0 - sig)))
        ).astype(LOW)
        both_grads[:, across(1, half)] = (hidden_grad * act).astype(LOW)
    for half in range(2):
        held_in = (
            hidden.at[:, pl.ds(half * part, part)],
            both_grads.at[:, across(0, half)],
            both_grads.at[:, across(1, half)],
        )
        for k, source in enumerate(held_in):
            stores.append(copy(source, outs[2 * k + half].at[place], sems.at[12 + 3 * half + k]))
            stores[-1].start()

    @pl.loop(0, 4)
    def _(j):
        span = pl.ds(pl.multiple_of(j * slab, slab), slab)
        grads[:, span] = dot_nt(both_grads[...], wide[span]).astype(LOW)

    for k in range(count // size):
        to = cross_ref if k % 2 else same_ref
        stores.append(
            copy(
                grads.at[pl.ds(k * size, size)],
                to.at[pl.ds(k // 2 * size, size)],
                sems.at[18 + k],
            )
        )
        stores[-1].start()
    for one in stores:
        one.wait()


def expert_chunk(pieces, back, gate, mats, at, held, size):
    all_rows, width = back.shape
    part = mats[0].shape[1]
    hidden = 2 * part
    count = sum(piece.shape[0] for piece in pieces)
    anywhere = pl.BlockSpec(memory_space=pl.ANY)
    held = [] if held is None else list(held)
    args = [gate, *pieces, back, *mats, *held]
    out = pl.pallas_call(
        lambda *refs: chunk_kernel(len(pieces), len(held), at, size, *refs),
        grid=(1,),
        in_specs=[pl.BlockSpec((count, 1), lambda j: (at, 0))] + [anywhere] * (len(args) - 1),
        out_specs=[anywhere] * 9,
        out_shape=[jax.ShapeDtypeStruct((count // 2, width), LOW)] * 2
        + [jax.ShapeDtypeStruct((all_rows, width), LOW)]
        + [jax.ShapeDtypeStruct((all_rows, part), LOW)] * 6,
        scratch_shapes=[
            pltpu.VMEM((count, width), LOW),
            pltpu.VMEM((count, width), LOW),
            pltpu.VMEM((width, 2 * hidden), LOW),
            pltpu.VMEM((2, part, width), LOW),
            pltpu.VMEM((count, hidden), LOW),
            pltpu.VMEM((count, 2 * hidden), LOW),
            pltpu.VMEM((count, width), LOW),
            pltpu.SemaphoreType.DMA((22,)),
        ],
        input_output_aliases={len(args) - len(held) + k: 2 + k for k in range(len(held))},
        compiler_params=pltpu.CompilerParams(vmem_limit_bytes=50 * 1024 * 1024),
        cost_estimate=pl.CostEstimate(
            flops=2 * 5 * count * width * hidden,
            bytes_accessed=2 * (4 * count * width + 3 * count * hidden + 3 * width * hidden),
            transcendentals=count * hidden,
        ),
    )(*args)
    return out[0], out[1], out[2:]


def mixed_kernel(chip_ref, core_ref, h0_ref, h1_ref, first_ref, second_ref, out_ref):
    rows = out_ref.shape[2]
    result = dot_nn(h0_ref[...], first_ref[...]) + dot_nn(h1_ref[...], second_ref[...])
    result = result.astype(LOW)
    out_ref[0, core_ref[0]] = result[:rows]
    out_ref[0, 1 - core_ref[0]] = result[rows:]


def mixed_pass(h0, h1, down_mats, blocks):
    count, columns = h0.shape
    width = down_mats[0].shape[1]
    chips = blocks.shape[0] // 2
    rows = count // chips
    once = pl.Buffered(1)
    fixed = lambda m: pl.BlockSpec(m.shape, lambda i, a, b: (0, 0), pipeline_mode=once)
    out = pl.pallas_call(
        mixed_kernel,
        grid_spec=pltpu.PrefetchScalarGridSpec(
            num_scalar_prefetch=2,
            grid=(chips,),
            in_specs=[pl.BlockSpec((rows, columns), lambda i, a, b: (i, 0))] * 2
            + [fixed(m) for m in down_mats],
            out_specs=pl.BlockSpec(
                (1, 2, rows // 2, width), lambda i, chip, core: (chip[i], 0, 0, 0)
            ),
        ),
        out_shape=jax.ShapeDtypeStruct((chips, 2, rows // 2, width), LOW),
        compiler_params=pltpu.CompilerParams(vmem_limit_bytes=40 * 1024 * 1024),
        cost_estimate=pl.CostEstimate(
            flops=4 * count * columns * width,
            bytes_accessed=2 * (count * (2 * columns + width) + 2 * columns * width),
            transcendentals=0,
        ),
    )(blocks[::2] // 2, blocks[:1] % 2, h0, h1, *down_mats)
    return out.reshape(count, width)


def expert_ring(rows, back, gate, mats, waiting):
    size = rows.shape[0]
    cut = size // 2
    same, cross = {}, {}
    swap = lambda block: swap_bit(block, "dp", 0)
    rows, pair = together(rows, swap(rows))
    left, right = ahead(rows), behind(rows)
    waiting = swap_tensor(after(waiting, pair))
    same[0], cross[0], held = expert_chunk([rows, pair], back, gate, mats, 6, None, size)
    for hop in (1, 2, 3):
        pieces = [left, swap(left), right, swap(right)]
        if hop < 3:
            left, right, same[hop - 1] = together(left, right, same[hop - 1])
            left, right = ahead(left), behind(right)
        else:
            left, right = ahead(left[:cut]), behind(right[cut:])
            pieces[0], waiting = together(pieces[0], waiting)
        same[hop], cross[hop], held = expert_chunk(pieces, back, gate, mats, hop - 1, held, size)
    pieces = [left, right, swap(left), swap(right)]
    same[4], cross[4], held = expert_chunk(pieces, back, gate, mats, 7, held, size)
    return same, cross, held, waiting


def halving_sum(parts):
    bits = parts.shape[0].bit_length() - 1
    index = lax.axis_index("dp")
    for bit in reversed(range(bits)):
        rows = parts.shape[0] // 2
        upper = index >> bit & 1
        kept = lax.dynamic_slice_in_dim(parts, upper * rows, rows, axis=0)
        sent = lax.dynamic_slice_in_dim(parts, (1 - upper) * rows, rows, axis=0)
        parts = kept + swap_bit(sent, "dp", bit)
    return parts[0]


def body(
    inputs,
    attn_gain,
    w_query,
    w_key,
    w_value,
    query_gain,
    key_gain,
    w_out,
    moe_gain,
    w_gate,
    w_up,
    w_down,
    experts,
    gates,
    segments,
    gaps,
    cotangent,
):
    dp_count = lax.axis_size("dp")
    dp_index = lax.axis_index("dp")
    side = lax.axis_index("tensor")
    token_count, model_width = inputs.shape
    half_count = token_count // 2
    top_count = experts.shape[1]
    expert_count = w_gate.shape[0] * dp_count
    capacity = token_count * top_count * dp_count * 9 // (8 * expert_count)
    prompt_length = PR_DEV * GROUP
    column_total = HEADS * HEAD
    block = w_query.shape[0]
    local_width = w_query.shape[1]
    local_heads = local_width // HEAD

    def own_half(array):
        return lax.dynamic_slice_in_dim(array, side * half_count, half_count, axis=0)

    def other_half(array):
        return lax.dynamic_slice_in_dim(array, (1 - side) * half_count, half_count, axis=0)

    def both_halves(own, other):
        first = side == 0
        return jnp.concatenate(
            [jnp.where(first, own, other), jnp.where(first, other, own)], axis=0
        )

    gate_mats = (w_gate[0], swap_tensor(w_gate[0]))
    up_mats = (w_up[0], swap_tensor(w_up[0]))

    ring = dp_count == 2 * len(RING)

    gates_high = gates.astype(LOW)
    gates_low = (gates - gates_high.astype(FULL)).astype(LOW)
    routing = jnp.concatenate([experts.astype(LOW).T, gates_high.T, gates_low.T], axis=1)
    routing = jnp.pad(routing, ((0, 0), (0, local_width - 3 * token_count)))
    gains = jnp.concatenate([attn_gain, moe_gain, query_gain, key_gain])
    gains = jnp.pad(gains[None], ((0, 7), (0, local_width - 4 * block)))
    cotangent_half = own_half(cotangent)
    packed, turned = pack_weights(
        w_query,
        w_key,
        w_value,
        jnp.concatenate([gains, routing], axis=0),
        w_out,
        [cotangent_half] if ring else [],
    )
    gathered = lax.all_gather(packed, "dp", axis=0, tiled=False)
    gathered_out = lax.all_gather(turned, "dp", axis=0, tiled=False)
    gathered, *early = lax.optimization_barrier((gathered, gate_mats[1], up_mats[1]))
    gate_mats, up_mats = (gate_mats[0], early[0]), (up_mats[0], early[1])
    rest = gathered[:, 3 * block : 3 * block + 16]
    gain_rows = rest[:, 0].astype(FULL)
    gain_one, gain_two, gain_q, gain_k = (
        gain_rows[:, j * block : (j + 1) * block].reshape(-1) for j in range(4)
    )
    gain_query_local = lax.dynamic_slice_in_dim(gain_q, side * local_width, local_width)
    gain_key_local = lax.dynamic_slice_in_dim(gain_k, side * local_width, local_width)

    names, *parts = (
        rest[:, 8:, j * token_count : (j + 1) * token_count] for j in range(3)
    )
    weights = parts[0].astype(FULL) + parts[1].astype(FULL)
    named = names == dp_index.astype(LOW)
    picked = jnp.sum(named.astype(FULL), axis=1)
    weight = jnp.sum(jnp.where(named, weights, 0.0), axis=1)
    order = jnp.arange(token_count, dtype=jnp.int32)
    earlier = (order[:, None] < order[None, :]).astype(LOW)
    within = dot_nn(picked.astype(LOW), earlier)
    per_row = jnp.sum(picked, axis=1)
    rows_order = jnp.arange(dp_count, dtype=jnp.int32)
    ahead = jnp.sum(
        jnp.where(rows_order[None, :] < rows_order[:, None], per_row[None, :], 0.0), axis=1
    )
    kept = (picked > 0.0) & (within + ahead[:, None] < capacity)
    weight = jnp.where(kept, weight, 0.0)
    weight = lax.dynamic_slice_in_dim(weight, side * half_count, half_count, axis=1)
    if ring:
        blocks = ring_blocks(dp_index)
        weight = weight[blocks]
    weight = weight.reshape(-1, 1)

    core = dp_index % 2
    tokens_f = inputs.astype(FULL)
    prompt_pos = dp_index % GROUP * PR_DEV + jnp.arange(PR_DEV, dtype=jnp.int32)
    later_pos = cont_positions(segments[0], gaps[0], prompt_length)
    positions = jnp.concatenate([prompt_pos, later_pos], axis=0)
    cosine, sine = rope_tables(positions, HEAD)
    sine = jnp.where(jnp.arange(HEAD) < HEAD // 2, -sine, sine)
    prompt_query = jnp.arange(token_count, dtype=jnp.int32) < PR_DEV
    prompt_at = jnp.arange(prompt_length, dtype=jnp.int32)
    prompt_keypos = ((dp_index % GROUP) ^ (prompt_at // PR_DEV)) * PR_DEV + prompt_at % PR_DEV
    allowed_prompt = (~prompt_query)[:, None] | (prompt_keypos[None, :] <= positions[:, None])
    query_segment = jnp.concatenate([jnp.full((PR_DEV,), -1, jnp.int32), segments[0]], axis=0)
    allowed_cont = (query_segment[:, None] == segments[0][None, :]) & (
        later_pos[None, :] <= positions[:, None]
    )
    allowed = jnp.concatenate([allowed_prompt, allowed_cont], axis=1)
    bias = jnp.where(allowed, 0.0, -1e30).astype(LOW)
    normed_b = rms_norm(tokens_f, gain_one).astype(LOW)
    query_flat, key_flat, values_b = project(
        normed_b, gathered, block, (0, 1, 2), (FULL, FULL, LOW)
    )
    key_sq = jnp.sum(key_flat * key_flat, axis=1)
    key_sq, value_prompt = together(key_sq, values_b[:PR_DEV])
    value_pieces = collect_prompt(value_prompt, 1, 2)
    query_sq, key_sq = lax.psum(
        (jnp.sum(query_flat * query_flat, axis=1), key_sq), "tensor"
    )
    query_sq, down_mat = lax.optimization_barrier((query_sq, w_down[0]))
    down_mats = (down_mat, swap_tensor(down_mat))
    query_scale = lax.rsqrt(query_sq / column_total + EPSILON)[:, None]
    key_scale = lax.rsqrt(key_sq / column_total + EPSILON)[:, None]
    keys_b = rope_pass(key_flat, gain_key_local[None], key_scale, cosine, sine)
    pieces = (*collect_prompt(keys_b[:PR_DEV], 2, 1), *value_pieces)
    queries_b = rope_pass(query_flat, gain_query_local[None], query_scale, cosine, sine)
    context_b = attend(queries_b, keys_b, values_b, bias, pieces)
    gathered_out = after(gathered_out, context_b)
    attn_part = project_back([context_b], gathered_out, block, (0,))
    attn_part, late, weight = together(attn_part, down_mats[1], weight)
    down_mats = (down_mats[0], late)
    mats = (*gate_mats, *up_mats, *down_mats)
    attn_other = swap_tensor(other_half(attn_part).astype(LOW))
    if ring:
        back_rows = unpack_rows(
            after(gathered, attn_part), blocks, 3 * block + 16, model_width
        )
    else:
        back_rows = lax.all_gather(cotangent_half.astype(LOW), "dp", axis=0, tiled=True)
    attn_other, back_rows, weight = together(attn_other, back_rows, weight)
    hidden_state = own_half(tokens_f) + own_half(attn_part) + attn_other.astype(FULL)
    normed_two_b = rms_norm(hidden_state, gain_two).astype(LOW)

    low_tn = lambda left, right: dot_tn(left, right).astype(LOW)
    upper = lambda array: array[: array.shape[0] // 2]
    lower = lambda array: array[array.shape[0] // 2 :]
    if ring:
        same, cross, held, hidden_other = expert_ring(
            normed_two_b, back_rows, weight, mats, hidden_state
        )
        expert_in, h0, h1, g0, g1, u0, u1 = held
        down_got = swap_tensor(low_tn(h1, back_rows))
        fillers = Fillers(
            [
                [(low_tn, expert_in, g1)],
                [(low_tn, expert_in, u1)],
                [(lambda *h: mixed_pass(*h, down_mats, blocks), h0, h1)],
            ]
        )
        normed_two_grad = ring_sum(same, cross, fillers)
        gate_sent, up_sent, mixed_rows = fillers.outs
    else:
        hidden_other = swap_tensor(hidden_state)
        expert_in = lax.all_gather(normed_two_b, "dp", axis=0, tiled=True)
        grad_rows, h0, h1, g0, g1, u0, u1 = expert_pass(
            expert_in, back_rows, weight, gate_mats, up_mats, down_mats
        )
        normed_two_grad = lax.psum_scatter(
            grad_rows, "dp", scatter_dimension=0, tiled=True
        ).astype(FULL)
        mixed_rows = (dot_nn(h0, down_mats[0]) + dot_nn(h1, down_mats[1])).astype(LOW)
        down_got = swap_tensor(low_tn(h1, back_rows))
        gate_sent = low_tn(expert_in, g1)
        up_sent = low_tn(expert_in, u1)
    gate_first = swap_tensor(upper(gate_sent))
    normed_two_grad, down_got, gate_first, mixed_rows, up_sent = together(
        normed_two_grad, down_got, gate_first, mixed_rows, up_sent
    )
    mixed = lax.psum_scatter(mixed_rows, "dp", scatter_dimension=0, tiled=True)

    unused_two, norm_two_back = jax.vjp(rms_norm, hidden_state, gain_two)
    state_part, gain_two_grad = norm_two_back(normed_two_grad)
    state_half = cotangent_half + state_part
    attn_grad_half = state_half.astype(LOW)
    attn_grad_b = both_halves(attn_grad_half, swap_tensor(attn_grad_half))
    attn_grad_b, gate_sent, up_sent = together(attn_grad_b, gate_sent, up_sent)
    gate_second, up_got = swap_tensor(lower(gate_sent)), swap_tensor(up_sent)
    (context_grad_b,) = project(attn_grad_b, gathered_out, block, (0,), (LOW,))
    query_normed_grad, query_inner, query_gain_part, key_grad, value_grad, odd, even = attend_back(
        queries_b,
        keys_b,
        values_b,
        bias,
        context_grad_b,
        query_flat,
        gain_query_local[None],
        query_scale,
        cosine,
        sine,
        pieces,
    )
    returned = return_prompt(odd, even)
    key_normed_grad, key_inner, key_gain_part, value_pre_grad = key_back(
        key_grad, value_grad, key_flat, gain_key_local[None], key_scale, cosine, sine, returned
    )
    query_inner, key_inner, gate_second, up_got = together(
        query_inner, key_inner, gate_second, up_got
    )
    query_inner, key_inner = lax.psum((query_inner[:, 0], key_inner[:, 0]), "tensor")
    pre_grad = lambda scale, gain, grad, flat, inner: (
        scale * gain * grad - flat * (scale * scale * scale) * (inner / column_total)[:, None]
    ).astype(LOW)
    query_pre_grad = pre_grad(
        query_scale, gain_query_local, query_normed_grad, query_flat, query_inner
    )
    key_pre_grad = pre_grad(key_scale, gain_key_local, key_normed_grad, key_flat, key_inner)
    mixed = after(mixed, key_pre_grad)
    gate_got = jnp.concatenate([gate_first, gate_second], axis=0)
    pre_grads = (query_pre_grad, key_pre_grad, value_pre_grad)
    grad_sum = lambda left, right, got: dot_tn(left, right) + got.astype(FULL)
    down, gate, up = (h0, back_rows, down_got), (expert_in, g0, gate_got), (expert_in, u0, up_got)
    back_all = lambda *grads: project_back(grads, gathered, block, (0, 1, 2))

    def share(part):
        return own_half(part), swap_tensor(other_half(part).astype(LOW))

    def input_side(own, other):
        unused_one, norm_one_back = jax.vjp(rms_norm, own_half(tokens_f), gain_one)
        input_part, gain_one_grad = norm_one_back(own + other.astype(FULL))
        input_half = state_half + input_part
        return input_half, swap_tensor(input_half), gain_one_grad

    if ring:
        columns = local_width // 2
        mine = lambda a: lax.dynamic_slice_in_dim(a, core * columns, columns, axis=1)
        theirs = lambda a: lax.dynamic_slice_in_dim(a, (1 - core) * columns, columns, axis=1)
        pair = lambda own, sent: jnp.concatenate([own, swap_bit(sent, "dp", 0)], axis=0)
        half = lambda *a: pair(
            jnp.concatenate([mine(x) for x in a], axis=1),
            jnp.concatenate([theirs(x) for x in a], axis=1),
        )
        normed_pair, attn_grad_pair = pair(normed_b, normed_b), pair(attn_grad_b, attn_grad_b)
        normed_pair, attn_grad_pair, context_half = together(
            normed_pair, attn_grad_pair, half(context_b)
        )
        out_half = low_tn(attn_grad_pair, context_half)
        grads_half, out_half = together(half(*pre_grads), out_half)
        fillers = Fillers(
            [
                [(lambda *grads: share(back_all(*grads)), *pre_grads)],
                [(grad_sum, *down), (swap_tensor, mixed)],
                [(grad_sum, *gate)],
            ]
        )
        w_half, token = ring_weights(low_tn(normed_pair, grads_half), out_half, fillers)
        (own_part, other_part), down_grad, mixed_other, gate_w_grad = fillers.outs
        input_half, input_other, gain_one_grad = input_side(own_part, after(other_part, token))
        up_w_grad = grad_sum(after(up[0], token), *up[1:])
        own_w = lax.dynamic_slice_in_dim(w_half, core * block, block, axis=0)
        got_w = swap_bit(
            lax.dynamic_slice_in_dim(w_half, (1 - core) * block, block, axis=0), "dp", 0
        )
        left_w, right_w = jnp.where(core == 0, own_w, got_w), jnp.where(core == 0, got_w, own_w)
        w_sums = [
            jnp.concatenate([w[:, j * columns : (j + 1) * columns] for w in (left_w, right_w)], axis=1)
            for j in range(4)
        ]
        mixed_other = after(mixed_other, token)
    else:
        w_grads = jnp.concatenate(
            [low_tn(normed_b, g) for g in pre_grads] + [low_tn(attn_grad_b, context_b)], axis=1
        )
        w_sum = lax.psum_scatter(w_grads, "dp", scatter_dimension=0, tiled=True).astype(FULL)
        w_sums = [w_sum[:, j * local_width : (j + 1) * local_width] for j in range(4)]
        down_grad, gate_w_grad, up_w_grad = grad_sum(*down), grad_sum(*gate), grad_sum(*up)
        mixed_other = swap_tensor(mixed)
        input_half, input_other, gain_one_grad = input_side(*share(back_all(*pre_grads)))
    input_grad = both_halves(input_half, input_other)
    output = both_halves(
        hidden_state + mixed.astype(FULL), hidden_other + mixed_other.astype(FULL)
    )
    wide = lambda part: lax.dynamic_update_slice_in_dim(
        jnp.zeros((column_total,), FULL), part, side * local_width, 0
    )
    gain_grads = jnp.stack(
        [gain_one_grad, gain_two_grad, wide(query_gain_part[0]), wide(key_gain_part[0])]
    ).reshape(4, dp_count, block)
    gain_sums = halving_sum(jnp.swapaxes(gain_grads, 0, 1))
    gain_sums = gain_sums + swap_tensor(gain_sums)
    return (
        output,
        input_grad,
        gain_sums[0],
        w_sums[0],
        w_sums[1],
        w_sums[2],
        gain_sums[2],
        gain_sums[3],
        w_sums[3].T,
        gain_sums[1],
        gate_w_grad[None],
        up_w_grad[None],
        down_grad[None],
    )


def solution(mesh):
    return jax.shard_map(
        body,
        mesh=mesh,
        in_specs=(
            P("dp", None),
            P("dp"),
            P("dp", "tensor"),
            P("dp", "tensor"),
            P("dp", "tensor"),
            P("dp"),
            P("dp"),
            P("tensor", "dp"),
            P("dp"),
            P("dp", None, "tensor"),
            P("dp", None, "tensor"),
            P("dp", "tensor", None),
            P("dp", None),
            P("dp", None),
            P("dp", None),
            P("dp", None),
            P("dp", None),
        ),
        out_specs=(
            P("dp", None),
            P("dp", None),
            P("dp"),
            P("dp", "tensor"),
            P("dp", "tensor"),
            P("dp", "tensor"),
            P("dp"),
            P("dp"),
            P("tensor", "dp"),
            P("dp"),
            P("dp", None, "tensor"),
            P("dp", None, "tensor"),
            P("dp", "tensor", None),
        ),
        check_vma=False,
    )
```

```python
import jax
import jax.numpy as jnp
from jax import lax
from jax.experimental import pallas as pl
from jax.experimental.pallas import tpu as pltpu
from jax.sharding import PartitionSpec as P

HEADS = 16
HEAD = 128
GROUP = 8
PR_DEV = 128


EPSILON = 1e-05
LOW = jnp.bfloat16
FULL = jnp.float32


def swap_bit(block, axis, bit):
    count = lax.axis_size(axis)
    return lax.ppermute(block, axis, [(i, i ^ (1 << bit)) for i in range(count)])


def swap_tensor(block):
    return lax.ppermute(block, "tensor", [(0, 1), (1, 0)])


RING = (0, 2, 4, 6, 7, 5, 3, 1)
AHEAD = [
    (RING[p] * 2 + c, RING[(p + 1) % len(RING)] * 2 + c) for p in range(len(RING)) for c in range(2)
]
BEHIND = [(to, at) for at, to in AHEAD]
HOPS = (-1, 1, -2, 2, -3, 3, 0, 4)


def ahead(block):
    return lax.ppermute(block, "dp", AHEAD)


def behind(block):
    return lax.ppermute(block, "dp", BEHIND)


def ring_blocks(dp_index):
    chip, core = dp_index // 2, dp_index % 2
    place = jnp.where(chip % 2 == 0, chip // 2, 7 - chip // 2)
    steps, cross = [], []
    for hop in HOPS:
        steps += [hop, hop]
        cross += [0, 1]
    there = (place + jnp.array(steps, jnp.int32)) % 8
    chips = jnp.where(there < 4, 2 * there, 2 * (7 - there) + 1)
    return 2 * chips + (core ^ jnp.array(cross, jnp.int32))


def add_low(*parts):
    total = parts[0].astype(FULL)
    for part in parts[1:]:
        total = total + part.astype(FULL)
    return total.astype(LOW)


def together(value, *others):
    return lax.optimization_barrier((value, *others))


def after(value, token):
    return lax.optimization_barrier((value, token))[0]


class Fillers:
    def __init__(self, *stages):
        self.stages = list(stages)

    def next(self, token):
        if self.stages:
            self.stages.pop(0)(lambda value: after(value, token))


def ring_sum(same, cross, fillers):
    both = {hop: add_low(same[hop], swap_bit(cross[hop], "dp", 0)) for hop in (4, 3, 2, 1, 0)}
    rows = both[0].shape[0]
    cut = rows // 2
    right, left = ahead(both[4][:cut]), behind(both[4][cut:])
    fillers.next(left)
    outward, inward = both[3][rows:], both[3][:rows]
    right = jnp.concatenate([add_low(outward[:cut], right), outward[cut:]], axis=0)
    left = jnp.concatenate([inward[:cut], add_low(inward[cut:], left)], axis=0)
    right, left = ahead(right), behind(left)
    fillers.next(left)
    for hop in (2, 1):
        right = ahead(add_low(both[hop][rows:], right))
        left = behind(add_low(both[hop][:rows], left))
        fillers.next(left)
    return both[0].astype(FULL) + right.astype(FULL) + left.astype(FULL)


def swap_in_turn(arrays, pieces, token):
    whole = []
    for array in arrays:
        rows, got = array.shape[0] // pieces, []
        for i in range(pieces):
            got.append(swap_tensor(after(array[i * rows : (i + 1) * rows], token)))
            token = got[-1]
        whole.append(jnp.concatenate(got, axis=0))
    return whole


def rms_norm(values, gain):
    return values * lax.rsqrt(jnp.mean(values * values, axis=-1, keepdims=True) + EPSILON) * gain


def rope_tables(positions, head_size):
    half_size = head_size // 2
    inverse = 10000.0 ** (-(jnp.arange(half_size, dtype=FULL) * 2.0) / head_size)
    angles = positions.astype(FULL)[:, None] * inverse[None, :]
    cosine = jnp.concatenate([jnp.cos(angles), jnp.cos(angles)], axis=-1)
    sine = jnp.concatenate([jnp.sin(angles), jnp.sin(angles)], axis=-1)
    return (cosine, sine)


def cont_positions(segment_row, gap_row, prompt_length):
    order = jnp.arange(segment_row.shape[0], dtype=jnp.int32)
    same = segment_row[:, None] == segment_row[None, :]
    earlier = order[None, :] < order[:, None]
    offset = jnp.sum((same & earlier).astype(jnp.int32), axis=1)
    labels = jnp.arange(gap_row.shape[0], dtype=jnp.int32)
    shifted = jnp.sum(
        jnp.where(segment_row[:, None] == labels[None, :], gap_row[None, :], 0), axis=1
    )
    return prompt_length + shifted + offset


def dot_nn(left, right):
    return jnp.dot(left, right, preferred_element_type=FULL)


def dot_tn(left, right):
    return lax.dot_general(left, right, (((0,), (0,)), ((), ())), preferred_element_type=FULL)


def dot_nt(left, right):
    return lax.dot_general(left, right, (((1,), (1,)), ((), ())), preferred_element_type=FULL)


def collect_prompt(own, first, second):
    near, far = swap_bit(own, "dp", 1), swap_bit(own, "dp", 2)
    last = swap_bit(near if first == 1 else far, "dp", second)
    blocks = []
    for block in (own, near, far, last):
        blocks += [block, swap_bit(block, "dp", 0)]
    return blocks[1:]


SMALL = pl.CostEstimate(flops=1, bytes_accessed=1, transcendentals=0)


def merge_kernel(even_ref, *refs):
    got, (keys_ref, values_ref, far_ref, near_ref) = refs[:3], refs[3:]
    near, far, last = 0, 1, 2
    add = lambda j, which: add_low(even_ref[j, which], got[j][which])
    keys_ref[0], keys_ref[1] = add(near, 0), add(last, 0)
    values_ref[0], values_ref[1] = add(far, 1), add(last, 1)
    far_ref[...], near_ref[...] = add(far, 0), add(near, 1)


def return_prompt(odd, even):
    got = [swap_bit(block, "dp", 0) for block in odd]
    one = jax.ShapeDtypeStruct(even.shape[2:], LOW)
    two = jax.ShapeDtypeStruct(even.shape[1:], LOW)
    keys, values, far, near = pl.pallas_call(
        merge_kernel, out_shape=[two, two, one, one], cost_estimate=SMALL
    )(even, *got[1:])
    keys, values = swap_bit(keys, "dp", 1), swap_bit(values, "dp", 2)
    last_keys = swap_bit(add_low(far, keys[1]), "dp", 2)
    last_values = swap_bit(add_low(near, values[1]), "dp", 1)
    return got[0], keys, values, last_keys, last_values


def turn(values):
    return pltpu.roll(values, HEAD // 2, 1)


def rope_kernel(pre_ref, gain_ref, scale_ref, cos_ref, sin_ref, out_ref):
    scale, cosine, sine = scale_ref[...], cos_ref[...], sin_ref[...]
    for at in range(0, pre_ref.shape[1], HEAD):
        span = slice(at, at + HEAD)
        normed = pre_ref[:, span] * scale * gain_ref[:, span]
        out_ref[:, span] = (normed * cosine + turn(normed) * sine).astype(LOW)


def rope_pass(flat, gain, scale, cosine, sine):
    rows, width = flat.shape
    part = width // 2
    wide = lambda rows: pl.BlockSpec((rows, part), lambda h: (0, h))
    return pl.pallas_call(
        rope_kernel,
        grid=(2,),
        in_specs=[wide(rows), wide(1)] + [kept_spec(a) for a in (scale, cosine, sine)],
        out_specs=wide(rows),
        out_shape=jax.ShapeDtypeStruct((rows, width), LOW),
    )(flat, gain, scale, cosine, sine)


PAIR = 2


def head_spec(rows):
    return pl.BlockSpec((rows, PAIR * HEAD), lambda h: (0, h))


def kept_spec(array):
    zeros = (0,) * array.ndim
    return pl.BlockSpec(array.shape, lambda h: zeros, pipeline_mode=pl.Buffered(1))


def all_keys(own_ref, pieces, span):
    return jnp.concatenate(
        [own_ref[:PR_DEV, span]] + [p[:, span] for p in pieces] + [own_ref[PR_DEV:, span]], axis=0
    )


def turned_query(flat_ref, gain_ref, scale, cosine, sine, span):
    normed = flat_ref[:, span] * scale * gain_ref[:, span]
    return (normed * cosine + turn(normed) * sine).astype(LOW)


def softmax_rows(query, keys, bias):
    scores = dot_nt(query, keys) * HEAD ** (-0.5) + bias
    weights = jnp.exp(scores - jnp.max(scores, axis=1, keepdims=True))
    return weights * (1.0 / jnp.sum(weights, axis=1, keepdims=True))


PIECES = GROUP - 1


def attend_kernel(flat_ref, gain_ref, scale_ref, cos_ref, sin_ref, bias_ref, k_ref, v_ref, *refs):
    out_ref = refs[-1]
    bias = bias_ref[...].astype(FULL)
    scale, cosine, sine = scale_ref[...], cos_ref[...], sin_ref[...]
    for at in range(0, PAIR * HEAD, HEAD):
        span = slice(at, at + HEAD)
        query = turned_query(flat_ref, gain_ref, scale, cosine, sine, span)
        probs = softmax_rows(query, all_keys(k_ref, refs[:PIECES], span), bias)
        values = all_keys(v_ref, refs[PIECES : 2 * PIECES], span)
        out_ref[:, span] = dot_nn(probs.astype(LOW), values).astype(LOW)


def attend_specs(rows, scale, cosine, sine, bias):
    return (
        [head_spec(rows), head_spec(1)]
        + [kept_spec(a) for a in (scale, cosine, sine, bias)]
        + [head_spec(rows)] * 2
        + [head_spec(PR_DEV)] * (2 * PIECES)
    )


def attend(flat, gain, scale, cosine, sine, bias, keys, values, pieces):
    rows, width = flat.shape
    return pl.pallas_call(
        attend_kernel,
        grid=(width // HEAD // PAIR,),
        in_specs=attend_specs(rows, scale, cosine, sine, bias),
        out_specs=head_spec(rows),
        out_shape=jax.ShapeDtypeStruct((rows, width), LOW),
        compiler_params=pltpu.CompilerParams(vmem_limit_bytes=40 * 1024 * 1024),
    )(flat, gain, scale, cosine, sine, bias, keys, values, *pieces)


def norm_parts(step, at, grad, flat_ref, gain_ref, scale_ref, inner_ref, gain_grad_ref):
    span = slice(at, at + HEAD)
    product = flat_ref[:, span] * grad
    inner = jnp.sum(product * gain_ref[:, span], axis=1, keepdims=True)
    gain_grad_ref[:, span] = jnp.sum(product * scale_ref[...], axis=0, keepdims=True)
    if at:
        inner_ref[...] += inner
    else:
        inner_ref[...] = jnp.where(step == 0, 0.0, inner_ref[...]) + inner


def attend_back_kernel(
    flat_ref, gain_ref, scale_ref, cos_ref, sin_ref, bias_ref, k_ref, v_ref, *refs
):
    back_ref = refs[2 * PIECES]
    qg_ref, inner_ref, gain_grad_ref, kg_ref, vg_ref, even_ref = refs[2 * PIECES + 1 : -4]
    odd_refs = refs[-4:]
    step = pl.program_id(0)
    bias = bias_ref[...].astype(FULL)
    scale, cosine, sine = scale_ref[...], cos_ref[...], sin_ref[...]
    prompt = PR_DEV * GROUP
    for at in range(0, PAIR * HEAD, HEAD):
        span = slice(at, at + HEAD)
        query = turned_query(flat_ref, gain_ref, scale, cosine, sine, span)
        back = back_ref[:, span]
        keys = all_keys(k_ref, refs[:PIECES], span)
        values = all_keys(v_ref, refs[PIECES : 2 * PIECES], span)
        probs = softmax_rows(query, keys, bias)
        prob_grad = dot_nt(back, values)
        value_grad = dot_tn(probs.astype(LOW), back)
        row_dot = jnp.sum(probs * prob_grad, axis=1, keepdims=True)
        score_grad = (probs * (prob_grad - row_dot)).astype(LOW)
        query_grad = dot_nn(score_grad, keys) * HEAD ** (-0.5)
        key_grad = dot_tn(score_grad, query) * HEAD ** (-0.5)
        query_grad = query_grad * cosine - turn(query_grad) * sine
        qg_ref[:, span] = query_grad
        norm_parts(step, at, query_grad, flat_ref, gain_ref, scale_ref, inner_ref, gain_grad_ref)
        for which, grad, own_ref in ((0, key_grad, kg_ref), (1, value_grad, vg_ref)):
            own_ref[:PR_DEV, span] = grad[:PR_DEV]
            own_ref[PR_DEV:, span] = grad[prompt:]
            for j in range(1, GROUP):
                to = odd_refs[j // 2] if j % 2 else even_ref.at[j // 2 - 1]
                to[which, :, span] = grad[j * PR_DEV : (j + 1) * PR_DEV].astype(LOW)


def attend_back(flat, gain, scale, cosine, sine, bias, keys, values, pieces, back):
    rows, width = flat.shape
    wide = jax.ShapeDtypeStruct((rows, width), FULL)
    both = pl.BlockSpec((3, 2, PR_DEV, PAIR * HEAD), lambda h: (0, 0, 0, h))
    return pl.pallas_call(
        attend_back_kernel,
        grid=(width // HEAD // PAIR,),
        in_specs=attend_specs(rows, scale, cosine, sine, bias) + [head_spec(rows)],
        out_specs=[
            head_spec(rows),
            pl.BlockSpec((rows, 1), lambda h: (0, 0)),
            head_spec(1),
            head_spec(rows),
            head_spec(rows),
            both,
        ]
        + [pl.BlockSpec((2, PR_DEV, PAIR * HEAD), lambda h: (0, 0, h))] * 4,
        out_shape=[
            wide,
            jax.ShapeDtypeStruct((rows, 1), FULL),
            jax.ShapeDtypeStruct((1, width), FULL),
            wide,
            wide,
            jax.ShapeDtypeStruct((3, 2, PR_DEV, width), LOW),
        ]
        + [jax.ShapeDtypeStruct((2, PR_DEV, width), LOW)] * 4,
        compiler_params=pltpu.CompilerParams(vmem_limit_bytes=58 * 1024 * 1024),
        cost_estimate=pl.CostEstimate(
            flops=20 * 10**9, bytes_accessed=40 * 10**6, transcendentals=4 * 10**6
        ),
    )(flat, gain, scale, cosine, sine, bias, keys, values, *pieces, back)


def key_back_kernel(*refs):
    kg_ref, vg_ref, flat_ref, gain_ref, scale_ref, cos_ref, sin_ref = refs[:7]
    got, keys, values, last_keys, last_values = refs[7:12]
    out_ref, inner_ref, gain_grad_ref, value_ref = refs[12:]
    step = pl.program_id(0)
    for at in range(0, PAIR * HEAD, HEAD):
        span = slice(at, at + HEAD)
        grads = []
        for which, own_ref, near, last in ((0, kg_ref, keys, last_keys), (1, vg_ref, values, last_values)):
            first = own_ref[:PR_DEV, span] + got[which, :, span].astype(FULL)
            first = first + near[0, :, span].astype(FULL) + last[:, span].astype(FULL)
            grads.append(jnp.concatenate([first, own_ref[PR_DEV:, span]], axis=0))
        key_grad = grads[0] * cos_ref[...] - turn(grads[0]) * sin_ref[...]
        out_ref[:, span] = key_grad
        norm_parts(step, at, key_grad, flat_ref, gain_ref, scale_ref, inner_ref, gain_grad_ref)
        value_ref[:, span] = grads[1].astype(LOW)


def key_back(key_grad, value_grad, flat, gain, scale, cosine, sine, returned):
    rows, width = flat.shape
    columns = PAIR * HEAD
    return pl.pallas_call(
        key_back_kernel,
        grid=(width // columns,),
        in_specs=[head_spec(rows)] * 3
        + [head_spec(1)]
        + [kept_spec(a) for a in (scale, cosine, sine)]
        + [pl.BlockSpec((2, PR_DEV, columns), lambda h: (0, 0, h))]
        + [pl.BlockSpec((1, PR_DEV, columns), lambda h: (0, 0, h))] * 2
        + [head_spec(PR_DEV)] * 2,
        out_specs=[
            head_spec(rows),
            pl.BlockSpec((rows, 1), lambda h: (0, 0)),
            head_spec(1),
            head_spec(rows),
        ],
        out_shape=[
            jax.ShapeDtypeStruct((rows, width), FULL),
            jax.ShapeDtypeStruct((rows, 1), FULL),
            jax.ShapeDtypeStruct((1, width), FULL),
            jax.ShapeDtypeStruct((rows, width), LOW),
        ],
        cost_estimate=SMALL,
    )(key_grad, value_grad, flat, gain, scale, cosine, sine, *returned)


def pack_kernel(query, key, value, rest, out, *refs):
    packed, turned = refs[-2:]
    at = 0
    for ref in (query, key, value, rest):
        packed[at : at + ref.shape[0]] = ref[...]
        at += ref.shape[0]
    for back in refs[:-2]:
        width = packed.shape[1]
        for start in range(0, back.shape[1], width):
            packed[at : at + back.shape[0]] = back[:, start : start + width].astype(LOW)
            at += back.shape[0]
    turned[...] = out[...].T


def pack_weights(w_query, w_key, w_value, rest, w_out, back):
    width = w_query.shape[1]
    rows = 3 * w_query.shape[0] + rest.shape[0] + sum(b.size // width for b in back)
    return pl.pallas_call(
        pack_kernel,
        out_shape=[
            jax.ShapeDtypeStruct((rows, width), LOW),
            jax.ShapeDtypeStruct(w_out.shape[::-1], LOW),
        ],
    )(w_query, w_key, w_value, rest, w_out, *back)


def unpack_kernel(first, blocks_ref, packed, out, held, sems):
    width = packed.shape[2]
    parts = out.shape[1] // width
    rows = (packed.shape[1] - first) // parts
    count = packed.shape[0]
    place = lambda i: pl.ds(i * rows, rows)
    loads = [
        pltpu.make_async_copy(
            packed.at[blocks_ref[i], pl.ds(first + j * rows, rows)],
            held.at[place(i), pl.ds(j * width, width)],
            sems.at[i * parts + j],
        )
        for i in range(count)
        for j in range(parts)
    ]
    stores = [
        pltpu.make_async_copy(held.at[place(i)], out.at[place(i)], sems.at[count * parts + i])
        for i in range(count)
    ]
    for one in loads:
        one.start()
    for i, store in enumerate(stores):
        for j in range(parts):
            loads[i * parts + j].wait()
        store.start()
    for store in stores:
        store.wait()


def unpack_rows(packed, blocks, first, width):
    count = packed.shape[0]
    parts = width // packed.shape[2]
    rows = (packed.shape[1] - first) // parts
    return pl.pallas_call(
        lambda *refs: unpack_kernel(first, *refs),
        in_specs=[pl.BlockSpec(memory_space=pltpu.SMEM), pl.BlockSpec(memory_space=pl.ANY)],
        out_specs=pl.BlockSpec(memory_space=pl.ANY),
        out_shape=jax.ShapeDtypeStruct((count * rows, width), LOW),
        scratch_shapes=[
            pltpu.VMEM((count * rows, width), LOW),
            pltpu.SemaphoreType.DMA((count * parts + count,)),
        ],
        compiler_params=pltpu.CompilerParams(vmem_limit_bytes=24 * 1024 * 1024),
    )(blocks, packed)


def pack_specs(gathered, places, steps, at):
    count, width = gathered.shape[0] // steps, gathered.shape[2]
    block = at
    return [
        pl.BlockSpec((count, block, width), lambda i, place=place: (i, place, 0))
        for place in places
    ]


def project_kernel(mats, roundings, rows_ref, *refs):
    mat_refs, out_refs, totals = refs[:mats], refs[mats : 2 * mats], refs[2 * mats :]
    step = pl.program_id(0)
    rows = rows_ref[...]
    for mat, out, total, rounding in zip(mat_refs, out_refs, totals, roundings):
        flat = mat[...].reshape(-1, mat.shape[2])
        part = dot_nn(rows, flat)

        @pl.when(step == 0)
        def _():
            total[...] = part

        @pl.when(step > 0)
        def _():
            total[...] += part

        @pl.when(step == pl.num_programs(0) - 1)
        def _():
            out[...] = total[...].astype(rounding)


def project(rows, gathered, block, places, roundings):
    count, width = rows.shape
    columns = gathered.shape[2]
    steps = 4
    outs = [jax.ShapeDtypeStruct((count, columns), rounding) for rounding in roundings]
    return pl.pallas_call(
        lambda *refs: project_kernel(len(places), roundings, *refs),
        grid=(steps,),
        in_specs=[pl.BlockSpec((count, width // steps), lambda i: (0, i))]
        + pack_specs(gathered, places, steps, block),
        out_specs=[pl.BlockSpec((count, columns), lambda i: (0, 0)) for _ in outs],
        out_shape=outs,
        scratch_shapes=[pltpu.VMEM((count, columns), FULL)] * len(outs),
        compiler_params=pltpu.CompilerParams(vmem_limit_bytes=40 * 1024 * 1024),
        cost_estimate=pl.CostEstimate(
            flops=2 * count * width * columns * len(places),
            bytes_accessed=2 * width * columns * len(places) + 8 * count * columns,
            transcendentals=0,
        ),
    )(rows, *[gathered] * len(places))


def project_back_kernel(mats, *refs):
    out = refs[-1]
    total = None
    for rows_ref, mat in zip(refs[:mats], refs[mats:-1]):
        part = dot_nt(rows_ref[...], mat[...].reshape(-1, mat.shape[2]))
        total = part if total is None else total + part
    out[...] = total


def project_back(rows, gathered, block, places):
    count, columns = rows[0].shape
    width = gathered.shape[0] * block
    steps = 4
    fixed = pl.BlockSpec((count, columns), lambda i: (0, 0), pipeline_mode=pl.Buffered(1))
    return pl.pallas_call(
        lambda *refs: project_back_kernel(len(places), *refs),
        grid=(steps,),
        in_specs=[fixed] * len(rows) + pack_specs(gathered, places, steps, block),
        out_specs=pl.BlockSpec((count, width // steps), lambda i: (0, i)),
        out_shape=jax.ShapeDtypeStruct((count, width), FULL),
        compiler_params=pltpu.CompilerParams(vmem_limit_bytes=40 * 1024 * 1024),
        cost_estimate=pl.CostEstimate(
            flops=2 * count * width * columns * len(places),
            bytes_accessed=2 * width * columns * len(places) + 4 * count * width,
            transcendentals=0,
        ),
    )(*rows, *[gathered] * len(places))


def pre_kernel(core_ref, *refs):
    inputs, outs = refs[:11], refs[11:]
    step = pl.program_id(0)
    columns = inputs[0].shape[1]
    parts = []
    for flat, grad, gain, scale, inner in (inputs[:5], inputs[5:10]):
        scaled = scale[...]
        mean = inner[...] * (1.0 / (HEADS * HEAD))
        parts.append(
            (
                scaled * gain[...] * grad[...] - flat[...] * (scaled * scaled * scaled) * mean
            ).astype(LOW)
        )
    outs[0][...], outs[1][...] = parts

    @pl.when(step != core_ref[0])
    def _():
        for j, part in enumerate((*parts, inputs[10][...])):
            outs[2][:, j * columns : (j + 1) * columns] = part


def pre_grads_pass(core, query, key, value):
    rows, width = value.shape
    columns = width // 2
    half = lambda rows: pl.BlockSpec((rows, columns), lambda h: (0, h))
    side = [half(rows), half(rows), half(1)] + [pl.BlockSpec((rows, 1), lambda h: (0, 0))] * 2
    return pl.pallas_call(
        pre_kernel,
        grid=(2,),
        in_specs=[pl.BlockSpec(memory_space=pltpu.SMEM)] + side + side + [half(rows)],
        out_specs=[half(rows), half(rows), pl.BlockSpec((rows, 3 * columns), lambda h: (0, 0))],
        out_shape=[jax.ShapeDtypeStruct((rows, width), LOW)] * 2
        + [jax.ShapeDtypeStruct((rows, 3 * columns), LOW)],
    )(core, *query, *key, value)


def weight_kernel(chip_ref, core_ref, *refs):
    normed, normed_got, back, back_got, query, key, value, got, context, context_got = refs[:10]
    out_ref, pre_both, context_both = refs[10:]
    rows, columns = query.shape

    @pl.when(pl.program_id(0) == 0)
    def _():
        for j, part in enumerate((query, key, value)):
            pre_both[:rows, j * columns : (j + 1) * columns] = part[...]
        pre_both[rows:] = got[...]
        context_both[:rows] = context[...]
        context_both[rows:] = context_got[...]

    left = jnp.concatenate([normed[...], normed_got[...]], axis=0)
    out_ref[0, :, : 3 * columns] = dot_tn(left, pre_both[...]).astype(LOW)
    left = jnp.concatenate([back[...], back_got[...]], axis=0)
    out_ref[0, :, 3 * columns :] = dot_tn(left, context_both[...]).astype(LOW)


def weight_grads(chips, core, normed, back, pre_grads, got, context, context_got):
    rows, width = normed[0].shape
    columns = context_got.shape[1]
    count = chips.shape[0]
    block = width // count
    tall = pl.BlockSpec((rows, block), lambda i, chip, core: (0, chip[i]))
    mine = pl.BlockSpec((rows, columns), lambda i, chip, core: (0, core[0]))
    fixed = lambda a: pl.BlockSpec(a.shape, lambda i, chip, core: (0, 0))
    return pl.pallas_call(
        weight_kernel,
        grid_spec=pltpu.PrefetchScalarGridSpec(
            num_scalar_prefetch=2,
            grid=(count,),
            in_specs=[tall] * 4 + [mine] * 3 + [fixed(got), mine, fixed(context_got)],
            out_specs=pl.BlockSpec((1, block, 4 * columns), lambda i, chip, core: (i, 0, 0)),
            scratch_shapes=[
                pltpu.VMEM((2 * rows, 3 * columns), LOW),
                pltpu.VMEM((2 * rows, columns), LOW),
            ],
        ),
        out_shape=jax.ShapeDtypeStruct((count, block, 4 * columns), LOW),
        compiler_params=pltpu.CompilerParams(vmem_limit_bytes=40 * 1024 * 1024),
        cost_estimate=pl.CostEstimate(
            flops=16 * rows * width * columns,
            bytes_accessed=2 * (4 * rows * width + 8 * rows * columns + 4 * width * columns),
            transcendentals=0,
        ),
    )(chips, core, *normed, *back, *pre_grads, got, context, context_got)


def ring_weights(blocks, fillers):
    part = lambda hop: blocks[HOPS.index(hop)]
    cut = blocks.shape[2] // 2
    right, left = ahead(part(4)[:, :cut]), behind(part(4)[:, cut:])
    fillers.next(left)
    outward, inward = part(3), part(-3)
    right = jnp.concatenate([add_low(outward[:, :cut], right), outward[:, cut:]], axis=1)
    left = jnp.concatenate([inward[:, :cut], add_low(inward[:, cut:], left)], axis=1)
    right, left = ahead(right), behind(left)
    fillers.next(left)
    token = left
    for hop in (2, 1):
        right, left = ahead(add_low(part(hop), right)), behind(add_low(part(-hop), left))
        fillers.next(left)
        token = left if hop == 2 else token
    return part(0).astype(FULL) + right.astype(FULL) + left.astype(FULL), token


def expert_kernel(
    rows_ref, back_ref, gate_ref, wg0, wg1, wu0, wu1, wd0, wd1, grad_ref, h0, h1, g0, g1, u0, u1
):
    rows = rows_ref[...]
    back = back_ref[...]
    gate = gate_ref[...]
    total = None
    for wg, wu, wd, h, g, u in ((wg0, wu0, wd0, h0, g0, u0), (wg1, wu1, wd1, h1, g1, u1)):
        gate_pre = dot_nn(rows, wg[...])
        up_pre = dot_nn(rows, wu[...])
        hidden_grad = gate * dot_nt(back, wd[...])
        sig = 1.0 / (1.0 + jnp.exp(-gate_pre))
        act = gate_pre * sig
        h[...] = (gate * (act * up_pre)).astype(LOW)
        gate_grad = (hidden_grad * up_pre * (sig * (1.0 + gate_pre * (1.0 - sig)))).astype(LOW)
        up_grad = (hidden_grad * act).astype(LOW)
        g[...] = gate_grad
        u[...] = up_grad
        part = dot_nt(gate_grad, wg[...]) + dot_nt(up_grad, wu[...])
        total = part if total is None else total + part
    grad_ref[...] = total.astype(LOW)


def expert_pass(rows, back, gate, gate_mats, up_mats, down_mats):
    count, width = rows.shape
    hidden = gate_mats[0].shape[1]
    tile = 256
    whole = lambda array: pl.BlockSpec(
        array.shape, lambda i: (0, 0), pipeline_mode=pl.Buffered(1)
    )
    tall = lambda columns: pl.BlockSpec((tile, columns), lambda i: (i, 0))
    mats = [*gate_mats, *up_mats, *down_mats]
    flops = 2 * 5 * count * width * hidden * 2
    return pl.pallas_call(
        expert_kernel,
        grid=(count // tile,),
        in_specs=[tall(width), tall(width), tall(1)] + [whole(m) for m in mats],
        out_specs=[tall(width)] + [tall(hidden)] * 6,
        out_shape=[jax.ShapeDtypeStruct((count, width), LOW)]
        + [jax.ShapeDtypeStruct((count, hidden), LOW)] * 6,
        compiler_params=pltpu.CompilerParams(vmem_limit_bytes=58 * 1024 * 1024),
        cost_estimate=pl.CostEstimate(
            flops=flops,
            bytes_accessed=2 * (3 * count * width + 6 * count * hidden + 6 * width * hidden),
            transcendentals=2 * count * hidden,
        ),
    )(rows, back, gate, *mats)


def chunk_kernel(pieces, held, at, size, gate_ref, *refs):
    piece_refs, refs = refs[:pieces], refs[pieces:]
    back_ref, mats, refs = refs[0], refs[1:7], refs[7 + held :]
    same_ref, cross_ref, rows_out = refs[:3]
    outs = refs[3:9]
    rows, back, wide, wd, hidden, both_grads, grads, sems = refs[9:]
    count = rows.shape[0]
    part = wd.shape[1]
    slab = wide.shape[0] // 4
    across = lambda k, half: pl.ds((2 * k + half) * part, part)
    place = pl.ds(at * count, count)
    copy = pltpu.make_async_copy
    load_rows, start = [], 0
    for piece in piece_refs:
        span = pl.ds(start, piece.shape[0])
        load_rows.append(copy(piece, rows.at[span], sems.at[len(load_rows)]))
        start += piece.shape[0]
    load_back = copy(back_ref.at[place], back, sems.at[4])
    loads = []
    for half in range(2):
        places = [wide.at[:, across(0, half)], wide.at[:, across(1, half)], wd.at[half]]
        loads.append(
            [copy(mats[2 * k + half], to, sems.at[5 + 3 * half + k]) for k, to in enumerate(places)]
        )
    for one in load_rows + loads[0][:2] + [load_back] + loads[0][2:] + loads[1]:
        one.start()
    gate = gate_ref[...]
    for one in load_rows:
        one.wait()
    stores = [copy(rows, rows_out.at[place], sems.at[11])]
    stores[0].start()
    for half in range(2):
        columns = pl.ds(half * part, part)
        loads[half][0].wait()
        gate_pre = dot_nn(rows[...], wide[:, across(0, half)])
        loads[half][1].wait()
        up_pre = dot_nn(rows[...], wide[:, across(1, half)])
        if half == 0:
            load_back.wait()
        loads[half][2].wait()
        hidden_grad = gate * dot_nt(back[...], wd[half])
        sig = 1.0 / (1.0 + jnp.exp(-gate_pre))
        act = gate_pre * sig
        hidden[:, columns] = (gate * (act * up_pre)).astype(LOW)
        both_grads[:, across(0, half)] = (
            hidden_grad * up_pre * (sig * (1.0 + gate_pre * (1.0 - sig)))
        ).astype(LOW)
        both_grads[:, across(1, half)] = (hidden_grad * act).astype(LOW)
    for half in range(2):
        held_in = (
            hidden.at[:, pl.ds(half * part, part)],
            both_grads.at[:, across(0, half)],
            both_grads.at[:, across(1, half)],
        )
        for k, source in enumerate(held_in):
            stores.append(copy(source, outs[2 * k + half].at[place], sems.at[12 + 3 * half + k]))
            stores[-1].start()

    @pl.loop(0, 4)
    def _(j):
        span = pl.ds(pl.multiple_of(j * slab, slab), slab)
        grads[:, span] = dot_nt(both_grads[...], wide[span]).astype(LOW)

    for k in range(count // size):
        to = cross_ref if k % 2 else same_ref
        stores.append(
            copy(
                grads.at[pl.ds(k * size, size)],
                to.at[pl.ds(k // 2 * size, size)],
                sems.at[18 + k],
            )
        )
        stores[-1].start()
    for one in stores:
        one.wait()


def expert_chunk(pieces, back, gate, mats, at, held, size):
    all_rows, width = back.shape
    part = mats[0].shape[1]
    hidden = 2 * part
    count = sum(piece.shape[0] for piece in pieces)
    anywhere = pl.BlockSpec(memory_space=pl.ANY)
    held = [] if held is None else list(held)
    args = [gate, *pieces, back, *mats, *held]
    out = pl.pallas_call(
        lambda *refs: chunk_kernel(len(pieces), len(held), at, size, *refs),
        grid=(1,),
        in_specs=[pl.BlockSpec((count, 1), lambda j: (at, 0))] + [anywhere] * (len(args) - 1),
        out_specs=[anywhere] * 9,
        out_shape=[jax.ShapeDtypeStruct((count // 2, width), LOW)] * 2
        + [jax.ShapeDtypeStruct((all_rows, width), LOW)]
        + [jax.ShapeDtypeStruct((all_rows, part), LOW)] * 6,
        scratch_shapes=[
            pltpu.VMEM((count, width), LOW),
            pltpu.VMEM((count, width), LOW),
            pltpu.VMEM((width, 2 * hidden), LOW),
            pltpu.VMEM((2, part, width), LOW),
            pltpu.VMEM((count, hidden), LOW),
            pltpu.VMEM((count, 2 * hidden), LOW),
            pltpu.VMEM((count, width), LOW),
            pltpu.SemaphoreType.DMA((22,)),
        ],
        input_output_aliases={len(args) - len(held) + k: 2 + k for k in range(len(held))},
        compiler_params=pltpu.CompilerParams(vmem_limit_bytes=50 * 1024 * 1024),
        cost_estimate=pl.CostEstimate(
            flops=2 * 5 * count * width * hidden,
            bytes_accessed=2 * (4 * count * width + 3 * count * hidden + 3 * width * hidden),
            transcendentals=count * hidden,
        ),
    )(*args)
    return out[0], out[1], out[2:]


def mixed_kernel(chip_ref, core_ref, h0_ref, h1_ref, first_ref, second_ref, out_ref):
    rows = out_ref.shape[2]
    result = dot_nn(h0_ref[...], first_ref[...]) + dot_nn(h1_ref[...], second_ref[...])
    result = result.astype(LOW)
    out_ref[0, core_ref[0]] = result[:rows]
    out_ref[0, 1 - core_ref[0]] = result[rows:]


def mixed_pass(h0, h1, down_mats, blocks):
    count, columns = h0.shape
    width = down_mats[0].shape[1]
    chips = blocks.shape[0] // 2
    rows = count // chips
    once = pl.Buffered(1)
    fixed = lambda m: pl.BlockSpec(m.shape, lambda i, a, b: (0, 0), pipeline_mode=once)
    out = pl.pallas_call(
        mixed_kernel,
        grid_spec=pltpu.PrefetchScalarGridSpec(
            num_scalar_prefetch=2,
            grid=(chips,),
            in_specs=[pl.BlockSpec((rows, columns), lambda i, a, b: (i, 0))] * 2
            + [fixed(m) for m in down_mats],
            out_specs=pl.BlockSpec(
                (1, 2, rows // 2, width), lambda i, chip, core: (chip[i], 0, 0, 0)
            ),
        ),
        out_shape=jax.ShapeDtypeStruct((chips, 2, rows // 2, width), LOW),
        compiler_params=pltpu.CompilerParams(vmem_limit_bytes=40 * 1024 * 1024),
        cost_estimate=pl.CostEstimate(
            flops=4 * count * columns * width,
            bytes_accessed=2 * (count * (2 * columns + width) + 2 * columns * width),
            transcendentals=0,
        ),
    )(blocks[::2] // 2, blocks[:1] % 2, h0, h1, *down_mats)
    return out.reshape(count, width)


def expert_ring(rows, back, gate, mats, waiting):
    size = rows.shape[0]
    cut = size // 2
    same, cross = {}, {}
    swap = lambda block: swap_bit(block, "dp", 0)
    rows, pair = together(rows, swap(rows))
    left, right = ahead(rows), behind(rows)
    waiting = swap_tensor(after(waiting, pair))
    same[0], cross[0], held = expert_chunk([rows, pair], back, gate, mats, 6, None, size)
    for hop in (1, 2, 3):
        left, right, same[hop - 1] = together(left, right, same[hop - 1])
        pieces = [left, swap(left), right, swap(right)]
        if hop < 3:
            left, right = ahead(left), behind(right)
        else:
            left, right = ahead(left[:cut]), behind(right[cut:])
            pieces[0], waiting = together(pieces[0], waiting)
        same[hop], cross[hop], held = expert_chunk(pieces, back, gate, mats, hop - 1, held, size)
    pieces = [left, right, swap(left), swap(right)]
    same[4], cross[4], held = expert_chunk(pieces, back, gate, mats, 7, held, size)
    return same, cross, held, waiting


def halving_sum(parts):
    bits = parts.shape[0].bit_length() - 1
    index = lax.axis_index("dp")
    for bit in reversed(range(bits)):
        rows = parts.shape[0] // 2
        upper = index >> bit & 1
        kept = lax.dynamic_slice_in_dim(parts, upper * rows, rows, axis=0)
        sent = lax.dynamic_slice_in_dim(parts, (1 - upper) * rows, rows, axis=0)
        parts = kept + swap_bit(sent, "dp", bit)
    return parts[0]


def body(
    inputs,
    attn_gain,
    w_query,
    w_key,
    w_value,
    query_gain,
    key_gain,
    w_out,
    moe_gain,
    w_gate,
    w_up,
    w_down,
    experts,
    gates,
    segments,
    gaps,
    cotangent,
):
    dp_count = lax.axis_size("dp")
    dp_index = lax.axis_index("dp")
    side = lax.axis_index("tensor")
    token_count, model_width = inputs.shape
    half_count = token_count // 2
    top_count = experts.shape[1]
    expert_count = w_gate.shape[0] * dp_count
    capacity = token_count * top_count * dp_count * 9 // (8 * expert_count)
    prompt_length = PR_DEV * GROUP
    column_total = HEADS * HEAD
    block = w_query.shape[0]
    local_width = w_query.shape[1]
    local_heads = local_width // HEAD

    def own_half(array):
        return lax.dynamic_slice_in_dim(array, side * half_count, half_count, axis=0)

    def other_half(array):
        return lax.dynamic_slice_in_dim(array, (1 - side) * half_count, half_count, axis=0)

    def both_halves(own, other):
        first = side == 0
        return jnp.concatenate(
            [jnp.where(first, own, other), jnp.where(first, other, own)], axis=0
        )

    gate_mats = (w_gate[0], swap_tensor(w_gate[0]))
    up_mats = (w_up[0], swap_tensor(w_up[0]))

    ring = dp_count == 2 * len(RING)

    gates_high = gates.astype(LOW)
    gates_low = (gates - gates_high.astype(FULL)).astype(LOW)
    routing = jnp.concatenate([experts.astype(LOW).T, gates_high.T, gates_low.T], axis=1)
    routing = jnp.pad(routing, ((0, 0), (0, local_width - 3 * token_count)))
    gains = jnp.concatenate([attn_gain, moe_gain, query_gain, key_gain])
    gains = jnp.pad(gains[None], ((0, 7), (0, local_width - 4 * block)))
    cotangent_half = own_half(cotangent)
    packed, turned = pack_weights(
        w_query,
        w_key,
        w_value,
        jnp.concatenate([gains, routing], axis=0),
        w_out,
        [cotangent_half] if ring else [],
    )
    gathered = lax.all_gather(packed, "dp", axis=0, tiled=False)
    gathered_out = lax.all_gather(turned, "dp", axis=0, tiled=False)
    gathered, *early = lax.optimization_barrier((gathered, gate_mats[1], up_mats[1]))
    gate_mats, up_mats = (gate_mats[0], early[0]), (up_mats[0], early[1])
    rest = gathered[:, 3 * block : 3 * block + 16]
    gain_rows = rest[:, 0].astype(FULL)
    gain_one, gain_two, gain_q, gain_k = (
        gain_rows[:, j * block : (j + 1) * block].reshape(-1) for j in range(4)
    )
    gain_query_local = lax.dynamic_slice_in_dim(gain_q, side * local_width, local_width)
    gain_key_local = lax.dynamic_slice_in_dim(gain_k, side * local_width, local_width)

    names, *parts = (
        rest[:, 8:, j * token_count : (j + 1) * token_count] for j in range(3)
    )
    weights = parts[0].astype(FULL) + parts[1].astype(FULL)
    named = names == dp_index.astype(LOW)
    picked = jnp.sum(named.astype(FULL), axis=1)
    weight = jnp.sum(jnp.where(named, weights, 0.0), axis=1)
    order = jnp.arange(token_count, dtype=jnp.int32)
    earlier = (order[:, None] < order[None, :]).astype(LOW)
    within = dot_nn(picked.astype(LOW), earlier)
    per_row = jnp.sum(picked, axis=1)
    rows_order = jnp.arange(dp_count, dtype=jnp.int32)
    ahead = jnp.sum(
        jnp.where(rows_order[None, :] < rows_order[:, None], per_row[None, :], 0.0), axis=1
    )
    kept = (picked > 0.0) & (within + ahead[:, None] < capacity)
    weight = jnp.where(kept, weight, 0.0)
    weight = lax.dynamic_slice_in_dim(weight, side * half_count, half_count, axis=1)
    if ring:
        blocks = ring_blocks(dp_index)
        weight = weight[blocks]
    weight = weight.reshape(-1, 1)

    core = dp_index % 2
    tokens_f = inputs.astype(FULL)
    prompt_pos = dp_index % GROUP * PR_DEV + jnp.arange(PR_DEV, dtype=jnp.int32)
    later_pos = cont_positions(segments[0], gaps[0], prompt_length)
    positions = jnp.concatenate([prompt_pos, later_pos], axis=0)
    cosine, sine = rope_tables(positions, HEAD)
    sine = jnp.where(jnp.arange(HEAD) < HEAD // 2, -sine, sine)
    prompt_query = jnp.arange(token_count, dtype=jnp.int32) < PR_DEV
    prompt_at = jnp.arange(prompt_length, dtype=jnp.int32)
    prompt_keypos = ((dp_index % GROUP) ^ (prompt_at // PR_DEV)) * PR_DEV + prompt_at % PR_DEV
    allowed_prompt = (~prompt_query)[:, None] | (prompt_keypos[None, :] <= positions[:, None])
    query_segment = jnp.concatenate([jnp.full((PR_DEV,), -1, jnp.int32), segments[0]], axis=0)
    allowed_cont = (query_segment[:, None] == segments[0][None, :]) & (
        later_pos[None, :] <= positions[:, None]
    )
    allowed = jnp.concatenate([allowed_prompt, allowed_cont], axis=1)
    bias = jnp.where(allowed, 0.0, -1e30).astype(LOW)
    normed_b = rms_norm(tokens_f, gain_one).astype(LOW)
    query_flat, key_flat, values_b = project(
        normed_b, gathered, block, (0, 1, 2), (FULL, FULL, LOW)
    )
    key_sq = jnp.sum(key_flat * key_flat, axis=1)
    key_sq, value_prompt = together(key_sq, values_b[:PR_DEV])
    value_pieces = collect_prompt(value_prompt, 1, 2)
    query_sq, key_sq = lax.psum(
        (jnp.sum(query_flat * query_flat, axis=1), key_sq), "tensor"
    )
    query_sq, down_mat = lax.optimization_barrier((query_sq, w_down[0]))
    down_mats = (down_mat, swap_tensor(down_mat))
    query_scale = lax.rsqrt(query_sq / column_total + EPSILON)[:, None]
    key_scale = lax.rsqrt(key_sq / column_total + EPSILON)[:, None]
    keys_b = rope_pass(key_flat, gain_key_local[None], key_scale, cosine, sine)
    pieces = (*collect_prompt(keys_b[:PR_DEV], 2, 1), *value_pieces)
    turned_by = (gain_query_local[None], query_scale, cosine, sine, bias)
    context_b = attend(query_flat, *turned_by, keys_b, values_b, pieces)
    gathered_out = after(gathered_out, context_b)
    attn_part = project_back([context_b], gathered_out, block, (0,))
    attn_part, late, weight = together(attn_part, down_mats[1], weight)
    down_mats = (down_mats[0], late)
    mats = (*gate_mats, *up_mats, *down_mats)
    attn_other = swap_tensor(other_half(attn_part).astype(LOW))
    if ring:
        back_rows = unpack_rows(
            after(gathered, attn_part), blocks, 3 * block + 16, model_width
        )
    else:
        back_rows = lax.all_gather(cotangent_half.astype(LOW), "dp", axis=0, tiled=True)
    attn_other, back_rows, weight = together(attn_other, back_rows, weight)
    hidden_state = own_half(tokens_f) + own_half(attn_part) + attn_other.astype(FULL)
    normed_two_b = rms_norm(hidden_state, gain_two).astype(LOW)

    low_tn = lambda left, right: dot_tn(left, right).astype(LOW)
    upper = lambda array: array[: array.shape[0] // 2]
    lower = lambda array: array[array.shape[0] // 2 :]
    if ring:
        same, cross, held, hidden_other = expert_ring(
            normed_two_b, back_rows, weight, mats, hidden_state
        )
        expert_in, h0, h1, g0, g1, u0, u1 = held
        down_got = swap_tensor(low_tn(h1, back_rows))
        late = {}

        def gate_stage(gated):
            late["gate"] = low_tn(gated(expert_in), g1)

        def up_stage(gated):
            late["up"] = low_tn(gated(expert_in), u1)

        def mixed_stage(gated):
            late["mixed"] = mixed_pass(gated(h0), h1, down_mats, blocks)

        fillers = Fillers(gate_stage, up_stage, mixed_stage)
        normed_two_grad = ring_sum(same, cross, fillers)
        gate_sent, up_sent, mixed_rows = late["gate"], late["up"], late["mixed"]
    else:
        hidden_other = swap_tensor(hidden_state)
        expert_in = lax.all_gather(normed_two_b, "dp", axis=0, tiled=True)
        grad_rows, h0, h1, g0, g1, u0, u1 = expert_pass(
            expert_in, back_rows, weight, gate_mats, up_mats, down_mats
        )
        normed_two_grad = lax.psum_scatter(
            grad_rows, "dp", scatter_dimension=0, tiled=True
        ).astype(FULL)
        mixed_rows = (dot_nn(h0, down_mats[0]) + dot_nn(h1, down_mats[1])).astype(LOW)
        down_got = swap_tensor(low_tn(h1, back_rows))
        gate_sent = low_tn(expert_in, g1)
        up_sent = low_tn(expert_in, u1)
    gate_first = swap_tensor(upper(gate_sent))
    normed_two_grad, down_got, gate_first, mixed_rows, up_sent = together(
        normed_two_grad, down_got, gate_first, mixed_rows, up_sent
    )
    mixed = lax.psum_scatter(mixed_rows, "dp", scatter_dimension=0, tiled=True)

    unused_two, norm_two_back = jax.vjp(rms_norm, hidden_state, gain_two)
    state_part, gain_two_grad = norm_two_back(normed_two_grad)
    state_half = cotangent_half + state_part
    attn_grad_half = state_half.astype(LOW)
    attn_grad_b = both_halves(attn_grad_half, swap_tensor(attn_grad_half))
    attn_grad_b, gate_sent, up_sent = together(attn_grad_b, gate_sent, up_sent)
    (context_grad_b,) = project(attn_grad_b, gathered_out, block, (0,), (LOW,))
    gate_second, up_first = swap_in_turn([lower(gate_sent), upper(up_sent)], 2, context_grad_b)
    if ring:
        pair = lambda own: (own, swap_bit(own, "dp", 0))
        columns = local_width // 2
        context_sent = lax.dynamic_slice_in_dim(context_b, (1 - core) * columns, columns, axis=1)
        normed_pair, attn_grad_pair = pair(normed_b), pair(attn_grad_b)
        context_got = swap_bit(context_sent, "dp", 0)
    query_normed_grad, query_inner, query_gain_part, key_grad, value_grad, even, *odd = attend_back(
        query_flat, *turned_by, keys_b, values_b, pieces, context_grad_b
    )
    returned = return_prompt(odd, even)
    key_normed_grad, key_inner, key_gain_part, value_pre_grad = key_back(
        key_grad, value_grad, key_flat, gain_key_local[None], key_scale, cosine, sine, returned
    )
    query_inner, gate_second, up_first = together(query_inner, gate_second, up_first)
    query_inner, key_inner = lax.psum((query_inner[:, 0], key_inner[:, 0]), "tensor")
    (up_second,) = swap_in_turn([lower(up_sent)], 2, query_inner)
    query_pre_grad, key_pre_grad, pre_sent = pre_grads_pass(
        core[None],
        (
            query_flat,
            query_normed_grad,
            gain_query_local[None],
            query_scale,
            query_inner[:, None],
        ),
        (key_flat, key_normed_grad, gain_key_local[None], key_scale, key_inner[:, None]),
        value_pre_grad,
    )
    up_got = jnp.concatenate([up_first, up_second], axis=0)
    gate_got = jnp.concatenate([gate_first, gate_second], axis=0)
    pre_grads = (query_pre_grad, key_pre_grad, value_pre_grad)
    grad_sum = lambda left, right, got: dot_tn(left, right) + got.astype(FULL)
    back_all = lambda *grads: project_back(grads, gathered, block, (0, 1, 2))

    def share(part):
        return own_half(part), swap_tensor(other_half(part).astype(LOW))

    def input_side(own, other):
        unused_one, norm_one_back = jax.vjp(rms_norm, own_half(tokens_f), gain_one)
        input_part, gain_one_grad = norm_one_back(own + other.astype(FULL))
        input_half = state_half + input_part
        return input_half, swap_tensor(input_half), gain_one_grad

    if ring:
        pre_got = swap_bit(pre_sent, "dp", 0)
        w_blocks = weight_grads(
            blocks[::2] // 2,
            core[None],
            normed_pair,
            attn_grad_pair,
            pre_grads,
            pre_got,
            context_b,
            context_got,
        )
        w_blocks, mixed = together(w_blocks, mixed)
        mixed_other = swap_tensor(mixed)
        late = {}

        def normed_stage(gated):
            late["normed"] = share(back_all(*[gated(grad) for grad in pre_grads]))

        def expert_stage(gated):
            late["down"] = grad_sum(gated(h0), back_rows, down_got)
            late["up"] = grad_sum(gated(expert_in), u0, up_got)

        def input_stage(gated):
            late["input"] = input_side(late["normed"][0], gated(late["normed"][1]))

        fillers = Fillers(normed_stage, expert_stage, input_stage)
        w_half, token = ring_weights(w_blocks, fillers)
        input_half, input_other, gain_one_grad = late["input"]
        down_grad, up_w_grad = late["down"], late["up"]
        gate_w_grad = grad_sum(after(expert_in, token), g0, gate_got)
        own_w = lax.dynamic_slice_in_dim(w_half, core * block, block, axis=0)
        got_w = swap_bit(
            lax.dynamic_slice_in_dim(w_half, (1 - core) * block, block, axis=0), "dp", 0
        )
        left_w, right_w = jnp.where(core == 0, own_w, got_w), jnp.where(core == 0, got_w, own_w)
        w_sums = [
            jnp.concatenate([w[:, j * columns : (j + 1) * columns] for w in (left_w, right_w)], axis=1)
            for j in range(4)
        ]
        mixed_other = after(mixed_other, token)
    else:
        w_grads = jnp.concatenate(
            [low_tn(normed_b, g) for g in pre_grads] + [low_tn(attn_grad_b, context_b)], axis=1
        )
        w_sum = lax.psum_scatter(w_grads, "dp", scatter_dimension=0, tiled=True).astype(FULL)
        w_sums = [w_sum[:, j * local_width : (j + 1) * local_width] for j in range(4)]
        down_grad = grad_sum(h0, back_rows, down_got)
        gate_w_grad = grad_sum(expert_in, g0, gate_got)
        up_w_grad = grad_sum(expert_in, u0, up_got)
        mixed_other = swap_tensor(mixed)
        input_half, input_other, gain_one_grad = input_side(*share(back_all(*pre_grads)))
    input_grad = both_halves(input_half, input_other)
    output = both_halves(
        hidden_state + mixed.astype(FULL), hidden_other + mixed_other.astype(FULL)
    )
    wide = lambda part: lax.dynamic_update_slice_in_dim(
        jnp.zeros((column_total,), FULL), part, side * local_width, 0
    )
    gain_grads = jnp.stack(
        [gain_one_grad, gain_two_grad, wide(query_gain_part[0]), wide(key_gain_part[0])]
    ).reshape(4, dp_count, block)
    gain_sums = halving_sum(jnp.swapaxes(gain_grads, 0, 1))
    gain_sums = gain_sums + swap_tensor(gain_sums)
    return (
        output,
        input_grad,
        gain_sums[0],
        w_sums[0],
        w_sums[1],
        w_sums[2],
        gain_sums[2],
        gain_sums[3],
        w_sums[3].T,
        gain_sums[1],
        gate_w_grad[None],
        up_w_grad[None],
        down_grad[None],
    )


def solution(mesh):
    return jax.shard_map(
        body,
        mesh=mesh,
        in_specs=(
            P("dp", None),
            P("dp"),
            P("dp", "tensor"),
            P("dp", "tensor"),
            P("dp", "tensor"),
            P("dp"),
            P("dp"),
            P("tensor", "dp"),
            P("dp"),
            P("dp", None, "tensor"),
            P("dp", None, "tensor"),
            P("dp", "tensor", None),
            P("dp", None),
            P("dp", None),
            P("dp", None),
            P("dp", None),
            P("dp", None),
        ),
        out_specs=(
            P("dp", None),
            P("dp", None),
            P("dp"),
            P("dp", "tensor"),
            P("dp", "tensor"),
            P("dp", "tensor"),
            P("dp"),
            P("dp"),
            P("tensor", "dp"),
            P("dp"),
            P("dp", None, "tensor"),
            P("dp", None, "tensor"),
            P("dp", "tensor", None),
        ),
        check_vma=False,
    )
```

```python
import jax
import jax.numpy as jnp
from jax import lax
from jax.experimental import pallas as pl
from jax.experimental.pallas import tpu as pltpu
from jax.sharding import PartitionSpec as P

HEADS = 16
HEAD = 128
GROUP = 8
PR_DEV = 128


EPSILON = 1e-05
VMEM = 60 * 1024 * 1024
LOW = jnp.bfloat16
FULL = jnp.float32


def swap_bit(block, axis, bit):
    count = lax.axis_size(axis)
    return lax.ppermute(block, axis, [(i, i ^ (1 << bit)) for i in range(count)])


def swap_tensor(block):
    return lax.ppermute(block, "tensor", [(0, 1), (1, 0)])


RING = (0, 2, 4, 6, 7, 5, 3, 1)
AHEAD = [
    (RING[p] * 2 + c, RING[(p + 1) % len(RING)] * 2 + c) for p in range(len(RING)) for c in range(2)
]
BEHIND = [(to, at) for at, to in AHEAD]
HOPS = (-1, 1, -2, 2, -3, 3, 0, 4)
LAYOUT = (
    *((-2, 0), (2, 0), (-1, 1), (1, 1)),
    *((-3, 0), (3, 0), (-2, 1), (2, 1)),
    *((4, 0), (4, 1), (-3, 1), (3, 1)),
    *((0, 0), (0, 1)),
    *((-1, 0), (1, 0)),
)


def ahead(block):
    return lax.ppermute(block, "dp", AHEAD)


def behind(block):
    return lax.ppermute(block, "dp", BEHIND)


def ring_chips(dp_index, hops):
    chip = dp_index // 2
    place = jnp.where(chip % 2 == 0, chip // 2, 7 - chip // 2)
    there = (place + jnp.array(hops, jnp.int32)) % len(RING)
    return jnp.where(there < 4, 2 * there, 2 * (7 - there) + 1)


def ring_blocks(dp_index):
    chips = ring_chips(dp_index, [hop for hop, _ in LAYOUT])
    return 2 * chips + (dp_index % 2 ^ jnp.array([cross for _, cross in LAYOUT], jnp.int32))


def add_low(*parts):
    total = parts[0].astype(FULL)
    for part in parts[1:]:
        total = total + part.astype(FULL)
    return total.astype(LOW)


def together(value, *others):
    return lax.optimization_barrier((value, *others))


def after(value, token):
    return lax.optimization_barrier((value, token))[0]


class Fillers:
    def __init__(self, *stages):
        self.stages = list(stages)

    def next(self, token):
        if self.stages:
            return self.stages.pop(0)(lambda value: after(value, token), token)


def ring_sum(same, cross, fillers):
    both = {hop: add_low(same[hop], swap_bit(cross[hop], "dp", 0)) for hop in (4, 3, 2, 1, 0)}
    rows = both[0].shape[0]
    cut = rows // 2
    right, left = ahead(both[4][:cut]), behind(both[4][cut:])
    outward, inward = both[3][rows:], both[3][:rows]
    right = jnp.concatenate([add_low(outward[:cut], right), outward[cut:]], axis=0)
    left = jnp.concatenate([inward[:cut], add_low(inward[cut:], left)], axis=0)
    right, left = together(right, left)
    fillers.next((right, left))
    right, left = ahead(right), behind(left)
    for hop in (2, 1):
        right, left = add_low(both[hop][rows:], right), add_low(both[hop][:rows], left)
        right, left = together(right, left)
        fillers.next((right, left))
        right, left = ahead(right), behind(left)
    return both[0].astype(FULL) + right.astype(FULL) + left.astype(FULL)


def swap_in_turn(pieces, token):
    got = []
    for piece in pieces:
        got.append(swap_tensor(after(piece, token)))
        token = got[-1]
    return got


def cut_rows(array, count):
    rows = array.shape[0] // count
    return [array[i * rows : (i + 1) * rows] for i in range(count)]


def rms_norm(values, gain):
    return values * lax.rsqrt(jnp.mean(values * values, axis=-1, keepdims=True) + EPSILON) * gain


def rope_tables(positions, head_size):
    half_size = head_size // 2
    inverse = 10000.0 ** (-(jnp.arange(half_size, dtype=FULL) * 2.0) / head_size)
    angles = positions.astype(FULL)[:, None] * inverse[None, :]
    cosine = jnp.concatenate([jnp.cos(angles), jnp.cos(angles)], axis=-1)
    sine = jnp.concatenate([jnp.sin(angles), jnp.sin(angles)], axis=-1)
    return (cosine, sine)


def cont_positions(segment_row, gap_row, prompt_length):
    order = jnp.arange(segment_row.shape[0], dtype=jnp.int32)
    same = segment_row[:, None] == segment_row[None, :]
    earlier = order[None, :] < order[:, None]
    offset = jnp.sum((same & earlier).astype(jnp.int32), axis=1)
    labels = jnp.arange(gap_row.shape[0], dtype=jnp.int32)
    shifted = jnp.sum(
        jnp.where(segment_row[:, None] == labels[None, :], gap_row[None, :], 0), axis=1
    )
    return prompt_length + shifted + offset


def dot_nn(left, right):
    return jnp.dot(left, right, preferred_element_type=FULL)


def dot_tn(left, right):
    return lax.dot_general(left, right, (((0,), (0,)), ((), ())), preferred_element_type=FULL)


def dot_nt(left, right):
    return lax.dot_general(left, right, (((1,), (1,)), ((), ())), preferred_element_type=FULL)


def collect_prompt(own, first, second):
    near, far = swap_bit(own, "dp", 1), swap_bit(own, "dp", 2)
    last = swap_bit(near if first == 1 else far, "dp", second)
    blocks = []
    for block in (own, near, far, last):
        blocks += [block, swap_bit(block, "dp", 0)]
    return blocks[1:]


SMALL = pl.CostEstimate(flops=1, bytes_accessed=1, transcendentals=0)


def merge_kernel(even_ref, *refs):
    got, (keys_ref, values_ref, far_ref, near_ref) = refs[:3], refs[3:]
    near, far, last = 0, 1, 2
    add = lambda j, which: add_low(even_ref[j, which], got[j][which])
    keys_ref[0], keys_ref[1] = add(near, 0), add(last, 0)
    values_ref[0], values_ref[1] = add(far, 1), add(last, 1)
    far_ref[...], near_ref[...] = add(far, 0), add(near, 1)


def return_prompt(odd, even):
    got = [swap_bit(block, "dp", 0) for block in odd]
    one = jax.ShapeDtypeStruct(even.shape[2:], LOW)
    two = jax.ShapeDtypeStruct(even.shape[1:], LOW)
    keys, values, far, near = pl.pallas_call(
        merge_kernel, out_shape=[two, two, one, one], cost_estimate=SMALL
    )(even, *got[1:])
    keys, values = swap_bit(keys, "dp", 1), swap_bit(values, "dp", 2)
    last_keys = swap_bit(add_low(far, keys[1]), "dp", 2)
    last_values = swap_bit(add_low(near, values[1]), "dp", 1)
    return got[0], keys, values, last_keys, last_values


def turn(values):
    return pltpu.roll(values, HEAD // 2, 1)


def rope_kernel(pre_ref, gain_ref, scale_ref, cos_ref, sin_ref, out_ref):
    scale, cosine, sine = scale_ref[...], cos_ref[...], sin_ref[...]
    for at in range(0, pre_ref.shape[1], HEAD):
        span = slice(at, at + HEAD)
        normed = pre_ref[:, span] * scale * gain_ref[:, span]
        out_ref[:, span] = (normed * cosine + turn(normed) * sine).astype(LOW)


def rope_pass(flat, gain, scale, cosine, sine):
    rows, width = flat.shape
    part = width // 2
    wide = lambda rows: pl.BlockSpec((rows, part), lambda h: (0, h))
    return pl.pallas_call(
        rope_kernel,
        grid=(2,),
        in_specs=[wide(rows), wide(1)] + [kept_spec(a) for a in (scale, cosine, sine)],
        out_specs=wide(rows),
        out_shape=jax.ShapeDtypeStruct((rows, width), LOW),
    )(flat, gain, scale, cosine, sine)


PAIR = 2


def head_spec(rows):
    return pl.BlockSpec((rows, PAIR * HEAD), lambda h: (0, h))


def kept_spec(array):
    zeros = (0,) * array.ndim
    return pl.BlockSpec(array.shape, lambda h: zeros, pipeline_mode=pl.Buffered(1))


def all_keys(own_ref, pieces, span):
    return jnp.concatenate(
        [own_ref[:PR_DEV, span]] + [p[:, span] for p in pieces] + [own_ref[PR_DEV:, span]], axis=0
    )


def turned_query(flat_ref, gain_ref, scale, cosine, sine, span):
    normed = flat_ref[:, span] * scale * gain_ref[:, span]
    return (normed * cosine + turn(normed) * sine).astype(LOW)


def softmax_rows(query, keys, bias):
    scores = dot_nt(query, keys) * HEAD ** (-0.5) + bias
    weights = jnp.exp(scores - jnp.max(scores, axis=1, keepdims=True))
    return weights * (1.0 / jnp.sum(weights, axis=1, keepdims=True))


PIECES = GROUP - 1


def attend_kernel(flat_ref, gain_ref, scale_ref, cos_ref, sin_ref, bias_ref, k_ref, v_ref, *refs):
    out_ref = refs[-1]
    bias = bias_ref[...].astype(FULL)
    scale, cosine, sine = scale_ref[...], cos_ref[...], sin_ref[...]
    for at in range(0, PAIR * HEAD, HEAD):
        span = slice(at, at + HEAD)
        query = turned_query(flat_ref, gain_ref, scale, cosine, sine, span)
        probs = softmax_rows(query, all_keys(k_ref, refs[:PIECES], span), bias)
        values = all_keys(v_ref, refs[PIECES : 2 * PIECES], span)
        out_ref[:, span] = dot_nn(probs.astype(LOW), values).astype(LOW)


def attend_specs(rows, scale, cosine, sine, bias):
    return (
        [head_spec(rows), head_spec(1)]
        + [kept_spec(a) for a in (scale, cosine, sine, bias)]
        + [head_spec(rows)] * 2
        + [head_spec(PR_DEV)] * (2 * PIECES)
    )


def attend(flat, gain, scale, cosine, sine, bias, keys, values, pieces):
    rows, width = flat.shape
    return pl.pallas_call(
        attend_kernel,
        grid=(width // HEAD // PAIR,),
        in_specs=attend_specs(rows, scale, cosine, sine, bias),
        out_specs=head_spec(rows),
        out_shape=jax.ShapeDtypeStruct((rows, width), LOW),
        compiler_params=pltpu.CompilerParams(vmem_limit_bytes=VMEM),
    )(flat, gain, scale, cosine, sine, bias, keys, values, *pieces)


def norm_parts(step, at, grad, flat_ref, gain_ref, scale_ref, inner_ref, gain_grad_ref):
    span = slice(at, at + HEAD)
    product = flat_ref[:, span] * grad
    inner = jnp.sum(product * gain_ref[:, span], axis=1, keepdims=True)
    gain_grad_ref[:, span] = jnp.sum(product * scale_ref[...], axis=0, keepdims=True)
    if at:
        inner_ref[...] += inner
    else:
        inner_ref[...] = jnp.where(step == 0, 0.0, inner_ref[...]) + inner


def attend_back_kernel(
    flat_ref, gain_ref, scale_ref, cos_ref, sin_ref, bias_ref, k_ref, v_ref, *refs
):
    back_ref = refs[2 * PIECES]
    qg_ref, inner_ref, gain_grad_ref, kg_ref, vg_ref, even_ref = refs[2 * PIECES + 1 : -4]
    odd_refs = refs[-4:]
    step = pl.program_id(0)
    bias = bias_ref[...].astype(FULL)
    scale, cosine, sine = scale_ref[...], cos_ref[...], sin_ref[...]
    prompt = PR_DEV * GROUP
    for at in range(0, PAIR * HEAD, HEAD):
        span = slice(at, at + HEAD)
        query = turned_query(flat_ref, gain_ref, scale, cosine, sine, span)
        back = back_ref[:, span]
        keys = all_keys(k_ref, refs[:PIECES], span)
        values = all_keys(v_ref, refs[PIECES : 2 * PIECES], span)
        probs = softmax_rows(query, keys, bias)
        prob_grad = dot_nt(back, values)
        value_grad = dot_tn(probs.astype(LOW), back)
        row_dot = jnp.sum(probs * prob_grad, axis=1, keepdims=True)
        score_grad = (probs * (prob_grad - row_dot)).astype(LOW)
        query_grad = dot_nn(score_grad, keys) * HEAD ** (-0.5)
        key_grad = dot_tn(score_grad, query) * HEAD ** (-0.5)
        query_grad = query_grad * cosine - turn(query_grad) * sine
        qg_ref[:, span] = query_grad
        norm_parts(step, at, query_grad, flat_ref, gain_ref, scale_ref, inner_ref, gain_grad_ref)
        for which, grad, own_ref in ((0, key_grad, kg_ref), (1, value_grad, vg_ref)):
            own_ref[:PR_DEV, span] = grad[:PR_DEV]
            own_ref[PR_DEV:, span] = grad[prompt:]
            for j in range(1, GROUP):
                to = odd_refs[j // 2] if j % 2 else even_ref.at[j // 2 - 1]
                to[which, :, span] = grad[j * PR_DEV : (j + 1) * PR_DEV].astype(LOW)


def attend_back(flat, gain, scale, cosine, sine, bias, keys, values, pieces, back):
    rows, width = flat.shape
    wide = jax.ShapeDtypeStruct((rows, width), FULL)
    both = pl.BlockSpec((3, 2, PR_DEV, PAIR * HEAD), lambda h: (0, 0, 0, h))
    return pl.pallas_call(
        attend_back_kernel,
        grid=(width // HEAD // PAIR,),
        in_specs=attend_specs(rows, scale, cosine, sine, bias) + [head_spec(rows)],
        out_specs=[
            head_spec(rows),
            pl.BlockSpec((rows, 1), lambda h: (0, 0)),
            head_spec(1),
            head_spec(rows),
            head_spec(rows),
            both,
        ]
        + [pl.BlockSpec((2, PR_DEV, PAIR * HEAD), lambda h: (0, 0, h))] * 4,
        out_shape=[
            wide,
            jax.ShapeDtypeStruct((rows, 1), FULL),
            jax.ShapeDtypeStruct((1, width), FULL),
            wide,
            wide,
            jax.ShapeDtypeStruct((3, 2, PR_DEV, width), LOW),
        ]
        + [jax.ShapeDtypeStruct((2, PR_DEV, width), LOW)] * 4,
        compiler_params=pltpu.CompilerParams(vmem_limit_bytes=VMEM),
        cost_estimate=pl.CostEstimate(
            flops=20 * 10**9, bytes_accessed=40 * 10**6, transcendentals=4 * 10**6
        ),
    )(flat, gain, scale, cosine, sine, bias, keys, values, *pieces, back)


def key_back_kernel(*refs):
    kg_ref, vg_ref, flat_ref, gain_ref, scale_ref, cos_ref, sin_ref = refs[:7]
    got, keys, values, last_keys, last_values = refs[7:12]
    out_ref, inner_ref, gain_grad_ref, value_ref = refs[12:]
    step = pl.program_id(0)
    for at in range(0, PAIR * HEAD, HEAD):
        span = slice(at, at + HEAD)
        grads = []
        for which, own_ref, near, last in ((0, kg_ref, keys, last_keys), (1, vg_ref, values, last_values)):
            first = own_ref[:PR_DEV, span] + got[which, :, span].astype(FULL)
            first = first + near[0, :, span].astype(FULL) + last[:, span].astype(FULL)
            grads.append(jnp.concatenate([first, own_ref[PR_DEV:, span]], axis=0))
        key_grad = grads[0] * cos_ref[...] - turn(grads[0]) * sin_ref[...]
        out_ref[:, span] = key_grad
        norm_parts(step, at, key_grad, flat_ref, gain_ref, scale_ref, inner_ref, gain_grad_ref)
        value_ref[:, span] = grads[1].astype(LOW)


def key_back(key_grad, value_grad, flat, gain, scale, cosine, sine, returned):
    rows, width = flat.shape
    columns = PAIR * HEAD
    return pl.pallas_call(
        key_back_kernel,
        grid=(width // columns,),
        in_specs=[head_spec(rows)] * 3
        + [head_spec(1)]
        + [kept_spec(a) for a in (scale, cosine, sine)]
        + [pl.BlockSpec((2, PR_DEV, columns), lambda h: (0, 0, h))]
        + [pl.BlockSpec((1, PR_DEV, columns), lambda h: (0, 0, h))] * 2
        + [head_spec(PR_DEV)] * 2,
        out_specs=[
            head_spec(rows),
            pl.BlockSpec((rows, 1), lambda h: (0, 0)),
            head_spec(1),
            head_spec(rows),
        ],
        out_shape=[
            jax.ShapeDtypeStruct((rows, width), FULL),
            jax.ShapeDtypeStruct((rows, 1), FULL),
            jax.ShapeDtypeStruct((1, width), FULL),
            jax.ShapeDtypeStruct((rows, width), LOW),
        ],
        cost_estimate=SMALL,
    )(key_grad, value_grad, flat, gain, scale, cosine, sine, *returned)


def pack_kernel(query, key, value, out, rest, packed):
    at = 0
    for ref in (query, key, value):
        packed[at : at + ref.shape[0]] = ref[...]
        at += ref.shape[0]
    packed[at : at + out.shape[1]] = out[...].T
    packed[at + out.shape[1] :] = rest[...]


def pack_weights(w_query, w_key, w_value, w_out, rest):
    rows = 4 * w_query.shape[0] + rest.shape[0]
    return pl.pallas_call(
        pack_kernel, out_shape=jax.ShapeDtypeStruct((rows, w_query.shape[1]), LOW)
    )(w_query, w_key, w_value, w_out, rest)


def unpack_kernel(first, blocks_ref, packed, out, held, sems):
    width = packed.shape[2]
    parts = out.shape[1] // width
    rows = (packed.shape[1] - first) // parts
    count = packed.shape[0]
    place = lambda i: pl.ds(i * rows, rows)
    loads = [
        pltpu.make_async_copy(
            packed.at[blocks_ref[i], pl.ds(first + j * rows, rows)],
            held.at[place(i), pl.ds(j * width, width)],
            sems.at[i * parts + j],
        )
        for i in range(count)
        for j in range(parts)
    ]
    stores = [
        pltpu.make_async_copy(held.at[place(i)], out.at[place(i)], sems.at[count * parts + i])
        for i in range(count)
    ]
    for one in loads:
        one.start()
    for i, store in enumerate(stores):
        for j in range(parts):
            loads[i * parts + j].wait()
        store.start()
    for store in stores:
        store.wait()


def unpack_rows(packed, blocks, first, width):
    count = packed.shape[0]
    parts = width // packed.shape[2]
    rows = (packed.shape[1] - first) // parts
    return pl.pallas_call(
        lambda *refs: unpack_kernel(first, *refs),
        in_specs=[pl.BlockSpec(memory_space=pltpu.SMEM), pl.BlockSpec(memory_space=pl.ANY)],
        out_specs=pl.BlockSpec(memory_space=pl.ANY),
        out_shape=jax.ShapeDtypeStruct((count * rows, width), LOW),
        scratch_shapes=[
            pltpu.VMEM((count * rows, width), LOW),
            pltpu.SemaphoreType.DMA((count * parts + count,)),
        ],
        compiler_params=pltpu.CompilerParams(vmem_limit_bytes=VMEM),
    )(blocks, packed)


def pack_specs(gathered, places, steps, at):
    count, width = gathered.shape[0] // steps, gathered.shape[2]
    block = at
    return [
        pl.BlockSpec((count, block, width), lambda i, place=place: (i, place, 0))
        for place in places
    ]


def project_kernel(mats, roundings, rows_ref, *refs):
    mat_refs, out_refs, totals = refs[:mats], refs[mats : 2 * mats], refs[2 * mats :]
    step = pl.program_id(0)
    rows = rows_ref[...]
    for mat, out, total, rounding in zip(mat_refs, out_refs, totals, roundings):
        flat = mat[...].reshape(-1, mat.shape[2])
        part = dot_nn(rows, flat)

        @pl.when(step == 0)
        def _():
            total[...] = part

        @pl.when(step > 0)
        def _():
            total[...] += part

        @pl.when(step == pl.num_programs(0) - 1)
        def _():
            out[...] = total[...].astype(rounding)


def project(rows, gathered, block, places, roundings):
    count, width = rows.shape
    columns = gathered.shape[2]
    steps = 4
    outs = [jax.ShapeDtypeStruct((count, columns), rounding) for rounding in roundings]
    return pl.pallas_call(
        lambda *refs: project_kernel(len(places), roundings, *refs),
        grid=(steps,),
        in_specs=[pl.BlockSpec((count, width // steps), lambda i: (0, i))]
        + pack_specs(gathered, places, steps, block),
        out_specs=[pl.BlockSpec((count, columns), lambda i: (0, 0)) for _ in outs],
        out_shape=outs,
        scratch_shapes=[pltpu.VMEM((count, columns), FULL)] * len(outs),
        compiler_params=pltpu.CompilerParams(vmem_limit_bytes=VMEM),
        cost_estimate=pl.CostEstimate(
            flops=2 * count * width * columns * len(places),
            bytes_accessed=2 * width * columns * len(places) + 8 * count * columns,
            transcendentals=0,
        ),
    )(rows, *[gathered] * len(places))


def project_back_kernel(mats, *refs):
    out = refs[-1]
    total = None
    for rows_ref, mat in zip(refs[:mats], refs[mats:-1]):
        part = dot_nt(rows_ref[...], mat[...].reshape(-1, mat.shape[2]))
        total = part if total is None else total + part
    out[...] = total


def project_back(rows, gathered, block, places):
    count, columns = rows[0].shape
    width = gathered.shape[0] * block
    steps = 4
    fixed = pl.BlockSpec((count, columns), lambda i: (0, 0), pipeline_mode=pl.Buffered(1))
    return pl.pallas_call(
        lambda *refs: project_back_kernel(len(places), *refs),
        grid=(steps,),
        in_specs=[fixed] * len(rows) + pack_specs(gathered, places, steps, block),
        out_specs=pl.BlockSpec((count, width // steps), lambda i: (0, i)),
        out_shape=jax.ShapeDtypeStruct((count, width), FULL),
        compiler_params=pltpu.CompilerParams(vmem_limit_bytes=VMEM),
        cost_estimate=pl.CostEstimate(
            flops=2 * count * width * columns * len(places),
            bytes_accessed=2 * width * columns * len(places) + 4 * count * width,
            transcendentals=0,
        ),
    )(*rows, *[gathered] * len(places))


def pre_kernel(core_ref, *refs):
    inputs, outs = refs[:11], refs[11:]
    step = pl.program_id(0)
    columns = inputs[0].shape[1]
    parts = []
    for flat, grad, gain, scale, inner in (inputs[:5], inputs[5:10]):
        scaled = scale[...]
        mean = inner[...] * (1.0 / (HEADS * HEAD))
        parts.append(
            (
                scaled * gain[...] * grad[...] - flat[...] * (scaled * scaled * scaled) * mean
            ).astype(LOW)
        )
    outs[0][...], outs[1][...] = parts

    @pl.when(step != core_ref[0])
    def _():
        for j, part in enumerate((*parts, inputs[10][...])):
            outs[2][:, j * columns : (j + 1) * columns] = part


def pre_grads_pass(core, query, key, value):
    rows, width = value.shape
    columns = width // 2
    half = lambda rows: pl.BlockSpec((rows, columns), lambda h: (0, h))
    side = [half(rows), half(rows), half(1)] + [pl.BlockSpec((rows, 1), lambda h: (0, 0))] * 2
    return pl.pallas_call(
        pre_kernel,
        grid=(2,),
        in_specs=[pl.BlockSpec(memory_space=pltpu.SMEM)] + side + side + [half(rows)],
        out_specs=[half(rows), half(rows), pl.BlockSpec((rows, 3 * columns), lambda h: (0, 0))],
        out_shape=[jax.ShapeDtypeStruct((rows, width), LOW)] * 2
        + [jax.ShapeDtypeStruct((rows, 3 * columns), LOW)],
    )(core, *query, *key, value)


def weight_kernel(chip_ref, core_ref, *refs):
    normed, normed_got, back, back_got, query, key, value, got, context, context_got = refs[:10]
    out_ref, right_ref, left_ref, pre_both, context_both = refs[10:]
    rows, columns = query.shape

    @pl.when(pl.program_id(0) == 0)
    def _():
        for j, part in enumerate((query, key, value)):
            pre_both[:rows, j * columns : (j + 1) * columns] = part[...]
        pre_both[rows:] = got[...]
        context_both[:rows] = context[...]
        context_both[rows:] = context_got[...]

    left = jnp.concatenate([normed[...], normed_got[...]], axis=0)
    out_ref[0, :, : 3 * columns] = dot_tn(left, pre_both[...]).astype(LOW)
    left = jnp.concatenate([back[...], back_got[...]], axis=0)
    out_ref[0, :, 3 * columns :] = dot_tn(left, context_both[...]).astype(LOW)

    @pl.when(pl.program_id(0) == HOPS.index(4))
    def _():
        right_ref[...] = out_ref[0, :, : 2 * columns]
        left_ref[...] = out_ref[0, :, 2 * columns :]


def weight_grads(chips, core, normed, back, pre_grads, got, context, context_got):
    rows, width = normed[0].shape
    columns = context_got.shape[1]
    count = chips.shape[0]
    block = width // count
    tall = pl.BlockSpec((rows, block), lambda i, chip, core: (0, chip[i]))
    mine = pl.BlockSpec((rows, columns), lambda i, chip, core: (0, core[0]))
    fixed = lambda a: pl.BlockSpec(a.shape, lambda i, chip, core: (0, 0))
    return pl.pallas_call(
        weight_kernel,
        grid_spec=pltpu.PrefetchScalarGridSpec(
            num_scalar_prefetch=2,
            grid=(count,),
            in_specs=[tall] * 4 + [mine] * 3 + [fixed(got), mine, fixed(context_got)],
            out_specs=[pl.BlockSpec((1, block, 4 * columns), lambda i, chip, core: (i, 0, 0))]
            + [pl.BlockSpec((block, 2 * columns), lambda i, chip, core: (0, 0))] * 2,
            scratch_shapes=[
                pltpu.VMEM((2 * rows, 3 * columns), LOW),
                pltpu.VMEM((2 * rows, columns), LOW),
            ],
        ),
        out_shape=[jax.ShapeDtypeStruct((count, block, 4 * columns), LOW)]
        + [jax.ShapeDtypeStruct((block, 2 * columns), LOW)] * 2,
        compiler_params=pltpu.CompilerParams(vmem_limit_bytes=VMEM),
        cost_estimate=pl.CostEstimate(
            flops=16 * rows * width * columns,
            bytes_accessed=2 * (4 * rows * width + 8 * rows * columns + 4 * width * columns),
            transcendentals=0,
        ),
    )(chips, core, *normed, *back, *pre_grads, got, context, context_got)


def ring_weights(blocks, right, left, fillers):
    part = lambda hop: blocks[HOPS.index(hop)]
    cut = blocks.shape[2] // 2
    right, left = ahead(right), behind(left)
    outward, inward = part(3), part(-3)
    right = jnp.concatenate([add_low(outward[:, :cut], right), outward[:, cut:]], axis=1)
    left = jnp.concatenate([inward[:, :cut], add_low(inward[:, cut:], left)], axis=1)
    right, left = together(right, left)
    fillers.next((right, left))
    right, left = ahead(right), behind(left)
    for hop in (2, 1):
        right, left = add_low(part(hop), right), add_low(part(-hop), left)
        right, left = together(right, left)
        right, left = fillers.next((right, left)) or (right, left)
        token = right
        right, left = ahead(right), behind(left)
    return part(0).astype(FULL) + right.astype(FULL) + left.astype(FULL), token


def expert_kernel(
    rows_ref, back_ref, gate_ref, wg0, wg1, wu0, wu1, wd0, wd1, grad_ref, h0, h1, g0, g1, u0, u1
):
    rows = rows_ref[...]
    back = back_ref[...]
    gate = gate_ref[...]
    total = None
    for wg, wu, wd, h, g, u in ((wg0, wu0, wd0, h0, g0, u0), (wg1, wu1, wd1, h1, g1, u1)):
        gate_pre = dot_nn(rows, wg[...])
        up_pre = dot_nn(rows, wu[...])
        hidden_grad = gate * dot_nt(back, wd[...])
        sig = 1.0 / (1.0 + jnp.exp(-gate_pre))
        act = gate_pre * sig
        h[...] = (gate * (act * up_pre)).astype(LOW)
        gate_grad = (hidden_grad * up_pre * (sig * (1.0 + gate_pre * (1.0 - sig)))).astype(LOW)
        up_grad = (hidden_grad * act).astype(LOW)
        g[...] = gate_grad
        u[...] = up_grad
        part = dot_nt(gate_grad, wg[...]) + dot_nt(up_grad, wu[...])
        total = part if total is None else total + part
    grad_ref[...] = total.astype(LOW)


def expert_pass(rows, back, gate, gate_mats, up_mats, down_mats):
    count, width = rows.shape
    hidden = gate_mats[0].shape[1]
    tile = 256
    whole = lambda array: pl.BlockSpec(
        array.shape, lambda i: (0, 0), pipeline_mode=pl.Buffered(1)
    )
    tall = lambda columns: pl.BlockSpec((tile, columns), lambda i: (i, 0))
    mats = [*gate_mats, *up_mats, *down_mats]
    flops = 2 * 5 * count * width * hidden * 2
    return pl.pallas_call(
        expert_kernel,
        grid=(count // tile,),
        in_specs=[tall(width), tall(width), tall(1)] + [whole(m) for m in mats],
        out_specs=[tall(width)] + [tall(hidden)] * 6,
        out_shape=[jax.ShapeDtypeStruct((count, width), LOW)]
        + [jax.ShapeDtypeStruct((count, hidden), LOW)] * 6,
        compiler_params=pltpu.CompilerParams(vmem_limit_bytes=VMEM),
        cost_estimate=pl.CostEstimate(
            flops=flops,
            bytes_accessed=2 * (3 * count * width + 6 * count * hidden + 6 * width * hidden),
            transcendentals=2 * count * hidden,
        ),
    )(rows, back, gate, *mats)


def chunk_kernel(pieces, held, at, splits, gate_ref, *refs):
    piece_refs, refs = refs[:pieces], refs[pieces:]
    back_ref, mats, refs = refs[0], refs[1:7], refs[7 + held :]
    grad_outs, refs = refs[: len(splits)], refs[len(splits) :]
    rows_out, outs = refs[0], refs[1:7]
    rows, back, wide, wd, hidden, both_grads, grads, sems = refs[7:]
    count = rows.shape[0]
    part = wd.shape[1]
    slab = wide.shape[0] // 4
    across = lambda k, half: pl.ds((2 * k + half) * part, part)
    place = pl.ds(at * count, count)
    copy = pltpu.make_async_copy
    load_rows, start = [], 0
    for piece in piece_refs:
        span = pl.ds(start, piece.shape[0])
        load_rows.append(copy(piece, rows.at[span], sems.at[len(load_rows)]))
        start += piece.shape[0]
    load_back = copy(back_ref.at[place], back, sems.at[6])
    loads = []
    for half in range(2):
        places = [wide.at[:, across(0, half)], wide.at[:, across(1, half)], wd.at[half]]
        loads.append(
            [copy(mats[2 * k + half], to, sems.at[7 + 3 * half + k]) for k, to in enumerate(places)]
        )
    for one in load_rows + loads[0][:2] + [load_back] + loads[0][2:] + loads[1]:
        one.start()
    gate = gate_ref[...]
    for one in load_rows:
        one.wait()
    stores = [copy(rows, rows_out.at[place], sems.at[13])]
    stores[0].start()
    for half in range(2):
        columns = pl.ds(half * part, part)
        loads[half][0].wait()
        gate_pre = dot_nn(rows[...], wide[:, across(0, half)])
        loads[half][1].wait()
        up_pre = dot_nn(rows[...], wide[:, across(1, half)])
        if half == 0:
            load_back.wait()
        loads[half][2].wait()
        hidden_grad = gate * dot_nt(back[...], wd[half])
        sig = 1.0 / (1.0 + jnp.exp(-gate_pre))
        act = gate_pre * sig
        hidden[:, columns] = (gate * (act * up_pre)).astype(LOW)
        both_grads[:, across(0, half)] = (
            hidden_grad * up_pre * (sig * (1.0 + gate_pre * (1.0 - sig)))
        ).astype(LOW)
        both_grads[:, across(1, half)] = (hidden_grad * act).astype(LOW)
    for half in range(2):
        held_in = (
            hidden.at[:, pl.ds(half * part, part)],
            both_grads.at[:, across(0, half)],
            both_grads.at[:, across(1, half)],
        )
        for k, source in enumerate(held_in):
            stores.append(copy(source, outs[2 * k + half].at[place], sems.at[14 + 3 * half + k]))
            stores[-1].start()

    @pl.loop(0, 4)
    def _(j):
        span = pl.ds(pl.multiple_of(j * slab, slab), slab)
        grads[:, span] = dot_nt(both_grads[...], wide[span]).astype(LOW)

    start = 0
    for k, (split, to) in enumerate(zip(splits, grad_outs)):
        stores.append(copy(grads.at[pl.ds(start, split)], to, sems.at[20 + k]))
        stores[-1].start()
        start += split
    for one in stores:
        one.wait()


def expert_chunk(pieces, back, gate, mats, at, held, splits):
    all_rows, width = back.shape
    part = mats[0].shape[1]
    hidden = 2 * part
    count = sum(piece.shape[0] for piece in pieces)
    anywhere = pl.BlockSpec(memory_space=pl.ANY)
    held = [] if held is None else list(held)
    args = [gate, *pieces, back, *mats, *held]
    out = pl.pallas_call(
        lambda *refs: chunk_kernel(len(pieces), len(held), at, splits, *refs),
        grid=(1,),
        in_specs=[pl.BlockSpec((count, 1), lambda j: (at, 0))] + [anywhere] * (len(args) - 1),
        out_specs=[anywhere] * (len(splits) + 7),
        out_shape=[jax.ShapeDtypeStruct((split, width), LOW) for split in splits]
        + [jax.ShapeDtypeStruct((all_rows, width), LOW)]
        + [jax.ShapeDtypeStruct((all_rows, part), LOW)] * 6,
        scratch_shapes=[
            pltpu.VMEM((count, width), LOW),
            pltpu.VMEM((count, width), LOW),
            pltpu.VMEM((width, 2 * hidden), LOW),
            pltpu.VMEM((2, part, width), LOW),
            pltpu.VMEM((count, hidden), LOW),
            pltpu.VMEM((count, 2 * hidden), LOW),
            pltpu.VMEM((count, width), LOW),
            pltpu.SemaphoreType.DMA((23,)),
        ],
        input_output_aliases={
            len(args) - len(held) + k: len(splits) + k for k in range(len(held))
        },
        compiler_params=pltpu.CompilerParams(vmem_limit_bytes=VMEM),
        cost_estimate=pl.CostEstimate(
            flops=2 * 5 * count * width * hidden,
            bytes_accessed=2 * (4 * count * width + 3 * count * hidden + 3 * width * hidden),
            transcendentals=count * hidden,
        ),
    )(*args)
    return out[: len(splits)], out[len(splits) :]


def mixed_kernel(chip_ref, same_ref, cross_ref, core_ref, *refs):
    first_ref, second_ref, out_ref = refs[4:]
    rows = out_ref.shape[2]
    first, second = (
        jnp.concatenate([refs[k][...], refs[k + 1][...]], axis=0) for k in (0, 2)
    )
    result = (dot_nn(first, first_ref[...]) + dot_nn(second, second_ref[...])).astype(LOW)
    out_ref[0, core_ref[0]] = result[:rows]
    out_ref[0, 1 - core_ref[0]] = result[rows:]


def mixed_pass(h0, h1, down_mats, chips, core):
    count, columns = h0.shape
    width = down_mats[0].shape[1]
    rows = count // len(LAYOUT)
    places = [
        jnp.array([LAYOUT.index((hop, cross)) for hop in HOPS], jnp.int32) for cross in (0, 1)
    ]
    once = pl.Buffered(1)
    fixed = lambda m: pl.BlockSpec(m.shape, lambda i, *tables: (0, 0), pipeline_mode=once)
    block = lambda k: pl.BlockSpec((rows, columns), lambda i, *tables: (tables[k][i], 0))
    out = pl.pallas_call(
        mixed_kernel,
        grid_spec=pltpu.PrefetchScalarGridSpec(
            num_scalar_prefetch=4,
            grid=(len(HOPS),),
            in_specs=[block(1), block(2), block(1), block(2)] + [fixed(m) for m in down_mats],
            out_specs=pl.BlockSpec(
                (1, 2, rows, width), lambda i, chip, *tables: (chip[i], 0, 0, 0)
            ),
        ),
        out_shape=jax.ShapeDtypeStruct((len(HOPS), 2, rows, width), LOW),
        compiler_params=pltpu.CompilerParams(vmem_limit_bytes=VMEM),
        cost_estimate=pl.CostEstimate(
            flops=4 * count * columns * width,
            bytes_accessed=2 * (count * (2 * columns + width) + 2 * columns * width),
            transcendentals=0,
        ),
    )(chips, *places, core, h0, h0, h1, h1, *down_mats)
    return out.reshape(count, width)


def expert_ring(rows, back, gate, mats, waiting):
    size = rows.shape[0]
    cut = size // 2
    swap = lambda block: swap_bit(block, "dp", 0)
    chunk = lambda pieces, at, held, *splits: expert_chunk(
        pieces, back, gate, mats, at, held, splits
    )
    rows, pair = together(rows, swap(rows))
    left, right = ahead(rows), behind(rows)
    waiting = swap_tensor(after(waiting, pair))
    same, cross = {}, {}
    (same[0], cross[0]), held = chunk([rows, pair], 6, None, size, size)
    left, right, same[0] = together(left, right, same[0])
    pieces, crossed = [left, right], [swap(left), swap(right)]
    left, right = ahead(left), behind(right)
    (same[1],), held = chunk(pieces, 7, held, 2 * size)
    left, right, same[1] = together(left, right, same[1])
    pieces, crossed = [left, right, *crossed], [swap(left), swap(right)]
    left, right = ahead(left), behind(right)
    (same[2], cross[1]), held = chunk(pieces, 0, held, 2 * size, 2 * size)
    left, right, waiting, same[2] = together(left, right, waiting, same[2])
    pieces, crossed = [left, right, *crossed], [swap(left), swap(right)]
    left, right = ahead(left[:cut]), behind(right[cut:])
    (same[3], cross[2]), held = chunk(pieces, 1, held, 2 * size, 2 * size)
    left, right, same[3] = together(left, right, same[3])
    pieces = [left, right, swap(left), swap(right), *crossed]
    (same[4], cross[4], cross[3]), held = chunk(pieces, 2, held, size, size, 2 * size)
    return same, cross, held, waiting


def halving_sum(parts):
    bits = parts.shape[0].bit_length() - 1
    index = lax.axis_index("dp")
    for bit in reversed(range(bits)):
        rows = parts.shape[0] // 2
        upper = index >> bit & 1
        kept = lax.dynamic_slice_in_dim(parts, upper * rows, rows, axis=0)
        sent = lax.dynamic_slice_in_dim(parts, (1 - upper) * rows, rows, axis=0)
        parts = kept + swap_bit(sent, "dp", bit)
    return parts[0]


def body(
    inputs,
    attn_gain,
    w_query,
    w_key,
    w_value,
    query_gain,
    key_gain,
    w_out,
    moe_gain,
    w_gate,
    w_up,
    w_down,
    experts,
    gates,
    segments,
    gaps,
    cotangent,
):
    dp_count = lax.axis_size("dp")
    dp_index = lax.axis_index("dp")
    side = lax.axis_index("tensor")
    token_count, model_width = inputs.shape
    half_count = token_count // 2
    top_count = experts.shape[1]
    expert_count = w_gate.shape[0] * dp_count
    capacity = token_count * top_count * dp_count * 9 // (8 * expert_count)
    prompt_length = PR_DEV * GROUP
    column_total = HEADS * HEAD
    block = w_query.shape[0]
    local_width = w_query.shape[1]
    local_heads = local_width // HEAD

    def own_half(array):
        return lax.dynamic_slice_in_dim(array, side * half_count, half_count, axis=0)

    def other_half(array):
        return lax.dynamic_slice_in_dim(array, (1 - side) * half_count, half_count, axis=0)

    def both_halves(own, other):
        first = side == 0
        return jnp.concatenate(
            [jnp.where(first, own, other), jnp.where(first, other, own)], axis=0
        )

    gate_mats = (w_gate[0], swap_tensor(w_gate[0]))
    up_mats = (w_up[0], swap_tensor(w_up[0]))

    ring = dp_count == 2 * len(RING)

    gates_high = gates.astype(LOW)
    gates_low = (gates - gates_high.astype(FULL)).astype(LOW)
    routing = jnp.concatenate([experts.astype(LOW).T, gates_high.T, gates_low.T], axis=1)
    routing = jnp.pad(routing, ((0, 0), (0, local_width - 3 * token_count)))
    gains = jnp.concatenate([attn_gain, moe_gain, query_gain, key_gain])
    gains = jnp.pad(gains[None], ((0, 7), (0, local_width - 4 * block)))
    packed = pack_weights(
        w_query, w_key, w_value, w_out, jnp.concatenate([gains, routing], axis=0)
    )
    gathered = lax.all_gather(packed, "dp", axis=0, tiled=False)
    cotangent_half = own_half(cotangent)
    gathered_back = lax.all_gather(cotangent_half.astype(LOW), "dp", axis=0, tiled=False)
    gathered, *early = lax.optimization_barrier((gathered, gate_mats[1], up_mats[1]))
    gate_mats, up_mats = (gate_mats[0], early[0]), (up_mats[0], early[1])
    rest = gathered[:, 4 * block : 4 * block + 16]
    gain_rows = rest[:, 0].astype(FULL)
    gain_one, gain_two, gain_q, gain_k = (
        gain_rows[:, j * block : (j + 1) * block].reshape(-1) for j in range(4)
    )
    gain_query_local = lax.dynamic_slice_in_dim(gain_q, side * local_width, local_width)
    gain_key_local = lax.dynamic_slice_in_dim(gain_k, side * local_width, local_width)

    names, *parts = (
        rest[:, 8:, j * token_count : (j + 1) * token_count] for j in range(3)
    )
    weights = parts[0].astype(FULL) + parts[1].astype(FULL)
    named = names == dp_index.astype(LOW)
    picked = jnp.sum(named.astype(FULL), axis=1)
    weight = jnp.sum(jnp.where(named, weights, 0.0), axis=1)
    order = jnp.arange(token_count, dtype=jnp.int32)
    earlier = (order[:, None] < order[None, :]).astype(LOW)
    within = dot_nn(picked.astype(LOW), earlier)
    per_row = jnp.sum(picked, axis=1)
    rows_order = jnp.arange(dp_count, dtype=jnp.int32)
    ahead = jnp.sum(
        jnp.where(rows_order[None, :] < rows_order[:, None], per_row[None, :], 0.0), axis=1
    )
    kept = (picked > 0.0) & (within + ahead[:, None] < capacity)
    weight = jnp.where(kept, weight, 0.0)
    weight = lax.dynamic_slice_in_dim(weight, side * half_count, half_count, axis=1)
    if ring:
        blocks, chips = ring_blocks(dp_index), ring_chips(dp_index, HOPS)
        weight = weight[blocks]
    weight = weight.reshape(-1, 1)

    core = dp_index % 2
    tokens_f = inputs.astype(FULL)
    prompt_pos = dp_index % GROUP * PR_DEV + jnp.arange(PR_DEV, dtype=jnp.int32)
    later_pos = cont_positions(segments[0], gaps[0], prompt_length)
    positions = jnp.concatenate([prompt_pos, later_pos], axis=0)
    cosine, sine = rope_tables(positions, HEAD)
    sine = jnp.where(jnp.arange(HEAD) < HEAD // 2, -sine, sine)
    prompt_query = jnp.arange(token_count, dtype=jnp.int32) < PR_DEV
    prompt_at = jnp.arange(prompt_length, dtype=jnp.int32)
    prompt_keypos = ((dp_index % GROUP) ^ (prompt_at // PR_DEV)) * PR_DEV + prompt_at % PR_DEV
    allowed_prompt = (~prompt_query)[:, None] | (prompt_keypos[None, :] <= positions[:, None])
    query_segment = jnp.concatenate([jnp.full((PR_DEV,), -1, jnp.int32), segments[0]], axis=0)
    allowed_cont = (query_segment[:, None] == segments[0][None, :]) & (
        later_pos[None, :] <= positions[:, None]
    )
    allowed = jnp.concatenate([allowed_prompt, allowed_cont], axis=1)
    bias = jnp.where(allowed, 0.0, -1e30).astype(LOW)
    normed_b = rms_norm(tokens_f, gain_one).astype(LOW)
    query_flat, key_flat, values_b = project(
        normed_b, gathered, block, (0, 1, 2), (FULL, FULL, LOW)
    )
    key_sq = jnp.sum(key_flat * key_flat, axis=1)
    key_sq, value_prompt = together(key_sq, values_b[:PR_DEV])
    value_pieces = collect_prompt(value_prompt, 1, 2)
    query_sq, key_sq = lax.psum(
        (jnp.sum(query_flat * query_flat, axis=1), key_sq), "tensor"
    )
    query_sq, down_mat = lax.optimization_barrier((query_sq, w_down[0]))
    down_mats = (down_mat, swap_tensor(down_mat))
    query_scale = lax.rsqrt(query_sq / column_total + EPSILON)[:, None]
    key_scale = lax.rsqrt(key_sq / column_total + EPSILON)[:, None]
    keys_b = rope_pass(key_flat, gain_key_local[None], key_scale, cosine, sine)
    pieces = (*collect_prompt(keys_b[:PR_DEV], 2, 1), *value_pieces)
    turned_by = (gain_query_local[None], query_scale, cosine, sine, bias)
    context_b = attend(query_flat, *turned_by, keys_b, values_b, pieces)
    attn_part = project_back([context_b], gathered, block, (3,))
    attn_part, late, weight = together(attn_part, down_mats[1], weight)
    down_mats = (down_mats[0], late)
    mats = (*gate_mats, *up_mats, *down_mats)
    attn_other = swap_tensor(other_half(attn_part).astype(LOW))
    gathered_back = after(gathered_back, attn_part)
    if ring:
        back_rows = unpack_rows(gathered_back, blocks, 0, model_width)
    else:
        back_rows = gathered_back.reshape(-1, model_width)
    attn_other, back_rows, weight = together(attn_other, back_rows, weight)
    hidden_state = own_half(tokens_f) + own_half(attn_part) + attn_other.astype(FULL)
    normed_two_b = rms_norm(hidden_state, gain_two).astype(LOW)

    low_tn = lambda left, right: dot_tn(left, right).astype(LOW)
    upper = lambda array: array[: array.shape[0] // 2]
    lower = lambda array: array[array.shape[0] // 2 :]
    if ring:
        same, cross, held, hidden_other = expert_ring(
            normed_two_b, back_rows, weight, mats, hidden_state
        )
        expert_in, h0, h1, g0, g1, u0, u1 = held
        down_got = swap_tensor(low_tn(h1, back_rows))
        late = {}

        def gate_stage(gated, token):
            late["gate"] = low_tn(gated(expert_in), g1)

        def up_stage(gated, token):
            late["up"] = low_tn(gated(expert_in), u1)

        def mixed_stage(gated, token):
            late["mixed"] = mixed_pass(gated(h0), h1, down_mats, chips, core[None])

        fillers = Fillers(gate_stage, up_stage, mixed_stage)
        normed_two_grad = ring_sum(same, cross, fillers)
        gate_sent, up_sent, mixed_rows = late["gate"], late["up"], late["mixed"]
    else:
        hidden_other = swap_tensor(hidden_state)
        expert_in = lax.all_gather(normed_two_b, "dp", axis=0, tiled=True)
        grad_rows, h0, h1, g0, g1, u0, u1 = expert_pass(
            expert_in, back_rows, weight, gate_mats, up_mats, down_mats
        )
        normed_two_grad = lax.psum_scatter(
            grad_rows, "dp", scatter_dimension=0, tiled=True
        ).astype(FULL)
        mixed_rows = (dot_nn(h0, down_mats[0]) + dot_nn(h1, down_mats[1])).astype(LOW)
        down_got = swap_tensor(low_tn(h1, back_rows))
        gate_sent = low_tn(expert_in, g1)
        up_sent = low_tn(expert_in, u1)
    gate_first = swap_tensor(upper(gate_sent))
    normed_two_grad, down_got, gate_first, mixed_rows, up_sent = together(
        normed_two_grad, down_got, gate_first, mixed_rows, up_sent
    )
    mixed = lax.psum_scatter(mixed_rows, "dp", scatter_dimension=0, tiled=True)

    unused_two, norm_two_back = jax.vjp(rms_norm, hidden_state, gain_two)
    state_part, gain_two_grad = norm_two_back(normed_two_grad)
    state_half = cotangent_half + state_part
    attn_grad_half = state_half.astype(LOW)
    attn_grad_b = both_halves(attn_grad_half, swap_tensor(attn_grad_half))
    attn_grad_b, gate_sent, up_sent = together(attn_grad_b, gate_sent, up_sent)
    (context_grad_b,) = project(attn_grad_b, gathered, block, (3,), (LOW,))
    gate_pieces, up_pieces = cut_rows(gate_sent, 4), cut_rows(up_sent, 4)
    soon = swap_in_turn([*gate_pieces[2:], up_pieces[0]], context_grad_b)
    if ring:
        pair = lambda own: (own, swap_bit(own, "dp", 0))
        columns = local_width // 2
        context_sent = lax.dynamic_slice_in_dim(context_b, (1 - core) * columns, columns, axis=1)
        normed_pair, attn_grad_pair = pair(normed_b), pair(attn_grad_b)
        context_got = swap_bit(context_sent, "dp", 0)
    query_normed_grad, query_inner, query_gain_part, key_grad, value_grad, even, *odd = attend_back(
        query_flat, *turned_by, keys_b, values_b, pieces, context_grad_b
    )
    returned = return_prompt(odd, even)
    if ring:
        key_grad, context_got, *pairs = together(
            key_grad, context_got, normed_pair[1], attn_grad_pair[1]
        )
        normed_pair, attn_grad_pair = (normed_b, pairs[0]), (attn_grad_b, pairs[1])
    key_normed_grad, key_inner, key_gain_part, value_pre_grad = key_back(
        key_grad, value_grad, key_flat, gain_key_local[None], key_scale, cosine, sine, returned
    )
    query_inner, *soon = together(query_inner, *soon)
    query_inner, key_inner = lax.psum((query_inner[:, 0], key_inner[:, 0]), "tensor")
    query_pre_grad, key_pre_grad, pre_sent = pre_grads_pass(
        core[None],
        (
            query_flat,
            query_normed_grad,
            gain_query_local[None],
            query_scale,
            query_inner[:, None],
        ),
        (key_flat, key_normed_grad, gain_key_local[None], key_scale, key_inner[:, None]),
        value_pre_grad,
    )
    gate_got = jnp.concatenate([gate_first, *soon[:2]], axis=0)
    pre_grads = (query_pre_grad, key_pre_grad, value_pre_grad)
    grad_sum = lambda left, right, got: dot_tn(left, right) + got.astype(FULL)
    back_all = lambda *grads: project_back(grads, gathered, block, (0, 1, 2))

    wide = lambda part: lax.dynamic_update_slice_in_dim(
        jnp.zeros((column_total,), FULL), part, side * local_width, 0
    )

    def share(part):
        return own_half(part), swap_tensor(other_half(part).astype(LOW)), gain_part(part)

    def input_side(own, other):
        unused_one, norm_one_back = jax.vjp(
            lambda values: rms_norm(values, gain_one), own_half(tokens_f)
        )
        input_half = state_half + norm_one_back(own + other.astype(FULL))[0]
        return input_half, swap_tensor(input_half)

    def gain_part(part):
        return jnp.sum(part * rms_norm(tokens_f, 1.0), axis=0)

    def gain_side(gain_one_grad):
        grads = jnp.stack(
            [gain_one_grad, gain_two_grad, wide(query_gain_part[0]), wide(key_gain_part[0])]
        ).reshape(4, dp_count, block)
        sums = halving_sum(jnp.swapaxes(grads, 0, 1))
        return sums + swap_tensor(sums)

    if ring:
        pre_got = swap_bit(pre_sent, "dp", 0)
        w_blocks, *far = weight_grads(
            chips,
            core[None],
            normed_pair,
            attn_grad_pair,
            pre_grads,
            pre_got,
            context_b,
            context_got,
        )
        w_blocks, mixed, *far = together(w_blocks, mixed, *far)
        up_got = jnp.concatenate([soon[2], *swap_in_turn(up_pieces[1:], far[0])], axis=0)
        mixed_other = swap_tensor(mixed)
        late = {}

        def normed_stage(gated, token):
            late["normed"] = share(back_all(*[gated(grad) for grad in pre_grads]))

        def expert_stage(gated, token):
            late["down"] = grad_sum(gated(h0), back_rows, down_got)
            late["gate"] = grad_sum(gated(expert_in), g0, gate_got)

        def input_stage(gated, token):
            late["down"], late["gate"], *token = together(late["down"], late["gate"], *token)
            late["input"] = input_side(late["normed"][0], gated(late["normed"][1]))
            late["gains"] = gain_side(gated(late["normed"][2]))
            return token

        fillers = Fillers(normed_stage, expert_stage, input_stage)
        w_half, token = ring_weights(w_blocks, *far, fillers)
        input_half, input_other = late["input"]
        gain_sums, token = together(late["gains"], token)
        down_grad, gate_w_grad = late["down"], late["gate"]
        up_w_grad = grad_sum(after(expert_in, token), u0, up_got)
        own_w = lax.dynamic_slice_in_dim(w_half, core * block, block, axis=0)
        got_w = swap_bit(
            lax.dynamic_slice_in_dim(w_half, (1 - core) * block, block, axis=0), "dp", 0
        )
        left_w, right_w = jnp.where(core == 0, own_w, got_w), jnp.where(core == 0, got_w, own_w)
        w_sums = [
            jnp.concatenate([w[:, j * columns : (j + 1) * columns] for w in (left_w, right_w)], axis=1)
            for j in range(4)
        ]
        mixed_other = after(mixed_other, token)
    else:
        w_grads = jnp.concatenate(
            [low_tn(normed_b, g) for g in pre_grads] + [low_tn(attn_grad_b, context_b)], axis=1
        )
        w_sum = lax.psum_scatter(w_grads, "dp", scatter_dimension=0, tiled=True).astype(FULL)
        w_sums = [w_sum[:, j * local_width : (j + 1) * local_width] for j in range(4)]
        down_grad = grad_sum(h0, back_rows, down_got)
        gate_w_grad = grad_sum(expert_in, g0, gate_got)
        up_got = jnp.concatenate([soon[2], *map(swap_tensor, up_pieces[1:])], axis=0)
        up_w_grad = grad_sum(expert_in, u0, up_got)
        mixed_other = swap_tensor(mixed)
        *normed_parts, gain_one_grad = share(back_all(*pre_grads))
        gain_sums = gain_side(gain_one_grad)
        input_half, input_other = input_side(*normed_parts)
    input_grad = both_halves(input_half, input_other)
    output = both_halves(
        hidden_state + mixed.astype(FULL), hidden_other + mixed_other.astype(FULL)
    )
    return (
        output,
        input_grad,
        gain_sums[0],
        w_sums[0],
        w_sums[1],
        w_sums[2],
        gain_sums[2],
        gain_sums[3],
        w_sums[3].T,
        gain_sums[1],
        gate_w_grad[None],
        up_w_grad[None],
        down_grad[None],
    )


def solution(mesh):
    return jax.shard_map(
        body,
        mesh=mesh,
        in_specs=(
            P("dp", None),
            P("dp"),
            P("dp", "tensor"),
            P("dp", "tensor"),
            P("dp", "tensor"),
            P("dp"),
            P("dp"),
            P("tensor", "dp"),
            P("dp"),
            P("dp", None, "tensor"),
            P("dp", None, "tensor"),
            P("dp", "tensor", None),
            P("dp", None),
            P("dp", None),
            P("dp", None),
            P("dp", None),
            P("dp", None),
        ),
        out_specs=(
            P("dp", None),
            P("dp", None),
            P("dp"),
            P("dp", "tensor"),
            P("dp", "tensor"),
            P("dp", "tensor"),
            P("dp"),
            P("dp"),
            P("tensor", "dp"),
            P("dp"),
            P("dp", None, "tensor"),
            P("dp", None, "tensor"),
            P("dp", "tensor", None),
        ),
        check_vma=False,
    )
```

```python
import jax
import jax.numpy as jnp
from jax import lax
from jax.experimental import pallas as pl
from jax.experimental.pallas import tpu as pltpu
from jax.sharding import PartitionSpec as P

HEADS = 16
HEAD = 128
GROUP = 8
PR_DEV = 128


EPSILON = 1e-05
VMEM = 60 * 1024 * 1024
SOME = 32 * 1024 * 1024
LOW = jnp.bfloat16
FULL = jnp.float32


def swap_bit(block, axis, bit):
    count = lax.axis_size(axis)
    return lax.ppermute(block, axis, [(i, i ^ (1 << bit)) for i in range(count)])


def swap_tensor(block):
    return lax.ppermute(block, "tensor", [(0, 1), (1, 0)])


RING = (0, 2, 4, 6, 7, 5, 3, 1)
AHEAD = [
    (RING[p] * 2 + c, RING[(p + 1) % len(RING)] * 2 + c) for p in range(len(RING)) for c in range(2)
]
BEHIND = [(to, at) for at, to in AHEAD]
HOPS = (-1, 1, -2, 2, -3, 3, 0, 4)
LAYOUT = (
    *((-2, 0), (2, 0), (-1, 1), (1, 1)),
    *((-3, 0), (3, 0), (-2, 1), (2, 1)),
    *((4, 0), (4, 1), (-3, 1), (3, 1)),
    *((0, 0), (0, 1)),
    *((-1, 0), (1, 0)),
)


def ahead(block):
    return lax.ppermute(block, "dp", AHEAD)


def behind(block):
    return lax.ppermute(block, "dp", BEHIND)


def ring_chips(dp_index, hops):
    chip = dp_index // 2
    place = jnp.where(chip % 2 == 0, chip // 2, 7 - chip // 2)
    there = (place + jnp.array(hops, jnp.int32)) % len(RING)
    return jnp.where(there < 4, 2 * there, 2 * (7 - there) + 1)


def ring_blocks(dp_index):
    chips = ring_chips(dp_index, [hop for hop, _ in LAYOUT])
    return 2 * chips + (dp_index % 2 ^ jnp.array([cross for _, cross in LAYOUT], jnp.int32))


def add_low(*parts):
    total = parts[0].astype(FULL)
    for part in parts[1:]:
        total = total + part.astype(FULL)
    return total.astype(LOW)


def together(value, *others):
    return lax.optimization_barrier((value, *others))


def after(value, token):
    return lax.optimization_barrier((value, token))[0]


class Fillers:
    def __init__(self, *stages):
        self.stages = list(stages)

    def next(self, token):
        if self.stages:
            self.stages.pop(0)(lambda value: after(value, token))


def ring_sum(same, cross, fillers):
    both = {hop: add_low(same[hop], swap_bit(cross[hop], "dp", 0)) for hop in (4, 3, 2, 1, 0)}
    rows = both[0].shape[0]
    cut = rows // 2
    right, left = ahead(both[4][:cut]), behind(both[4][cut:])
    fillers.next(left)
    outward, inward = both[3][rows:], both[3][:rows]
    right = jnp.concatenate([add_low(outward[:cut], right), outward[cut:]], axis=0)
    left = jnp.concatenate([inward[:cut], add_low(inward[cut:], left)], axis=0)
    right, left = ahead(right), behind(left)
    fillers.next(left)
    for hop in (2, 1):
        right = ahead(add_low(both[hop][rows:], right))
        left = behind(add_low(both[hop][:rows], left))
        fillers.next(left)
    return both[0].astype(FULL) + right.astype(FULL) + left.astype(FULL)


def swap_in_turn(pieces, token):
    got = []
    for piece in pieces:
        got.append(swap_tensor(after(piece, token)))
        token = got[-1]
    return got


def cut_rows(array, count):
    rows = array.shape[0] // count
    return [array[i * rows : (i + 1) * rows] for i in range(count)]


def rms_norm(values, gain):
    return values * lax.rsqrt(jnp.mean(values * values, axis=-1, keepdims=True) + EPSILON) * gain


def rope_tables(positions, head_size):
    half_size = head_size // 2
    inverse = 10000.0 ** (-(jnp.arange(half_size, dtype=FULL) * 2.0) / head_size)
    angles = positions.astype(FULL)[:, None] * inverse[None, :]
    cosine = jnp.concatenate([jnp.cos(angles), jnp.cos(angles)], axis=-1)
    sine = jnp.concatenate([jnp.sin(angles), jnp.sin(angles)], axis=-1)
    return (cosine, sine)


def cont_positions(segment_row, gap_row, prompt_length):
    order = jnp.arange(segment_row.shape[0], dtype=jnp.int32)
    same = segment_row[:, None] == segment_row[None, :]
    earlier = order[None, :] < order[:, None]
    offset = jnp.sum((same & earlier).astype(jnp.int32), axis=1)
    labels = jnp.arange(gap_row.shape[0], dtype=jnp.int32)
    shifted = jnp.sum(
        jnp.where(segment_row[:, None] == labels[None, :], gap_row[None, :], 0), axis=1
    )
    return prompt_length + shifted + offset


def dot_nn(left, right):
    return jnp.dot(left, right, preferred_element_type=FULL)


def dot_tn(left, right):
    return lax.dot_general(left, right, (((0,), (0,)), ((), ())), preferred_element_type=FULL)


def dot_nt(left, right):
    return lax.dot_general(left, right, (((1,), (1,)), ((), ())), preferred_element_type=FULL)


def collect_prompt(own, first, second):
    near, far = swap_bit(own, "dp", 1), swap_bit(own, "dp", 2)
    last = swap_bit(near if first == 1 else far, "dp", second)
    blocks = []
    for block in (own, near, far, last):
        blocks += [block, swap_bit(block, "dp", 0)]
    return blocks[1:]


SMALL = pl.CostEstimate(flops=1, bytes_accessed=1, transcendentals=0)


def merge_kernel(even_ref, *refs):
    got, (keys_ref, values_ref, far_ref, near_ref) = refs[:3], refs[3:]
    near, far, last = 0, 1, 2
    add = lambda j, which: add_low(even_ref[j, which], got[j][which])
    keys_ref[0], keys_ref[1] = add(near, 0), add(last, 0)
    values_ref[0], values_ref[1] = add(far, 1), add(last, 1)
    far_ref[...], near_ref[...] = add(far, 0), add(near, 1)


def return_prompt(odd, even):
    got = [swap_bit(block, "dp", 0) for block in odd]
    one = jax.ShapeDtypeStruct(even.shape[2:], LOW)
    two = jax.ShapeDtypeStruct(even.shape[1:], LOW)
    keys, values, far, near = pl.pallas_call(
        merge_kernel, out_shape=[two, two, one, one], cost_estimate=SMALL
    )(even, *got[1:])
    keys, values = swap_bit(keys, "dp", 1), swap_bit(values, "dp", 2)
    last_keys = swap_bit(add_low(far, keys[1]), "dp", 2)
    last_values = swap_bit(add_low(near, values[1]), "dp", 1)
    return got[0], keys, values, last_keys, last_values


def turn(values):
    return pltpu.roll(values, HEAD // 2, 1)


def rope_kernel(pre_ref, gain_ref, scale_ref, cos_ref, sin_ref, out_ref):
    scale, cosine, sine = scale_ref[...], cos_ref[...], sin_ref[...]
    for at in range(0, pre_ref.shape[1], HEAD):
        span = slice(at, at + HEAD)
        normed = pre_ref[:, span] * scale * gain_ref[:, span]
        out_ref[:, span] = (normed * cosine + turn(normed) * sine).astype(LOW)


def rope_pass(flat, gain, scale, cosine, sine):
    rows, width = flat.shape
    part = width // 2
    wide = lambda rows: pl.BlockSpec((rows, part), lambda h: (0, h))
    return pl.pallas_call(
        rope_kernel,
        grid=(2,),
        in_specs=[wide(rows), wide(1)] + [kept_spec(a) for a in (scale, cosine, sine)],
        out_specs=wide(rows),
        out_shape=jax.ShapeDtypeStruct((rows, width), LOW),
    )(flat, gain, scale, cosine, sine)


PAIR = 2


def head_spec(rows):
    return pl.BlockSpec((rows, PAIR * HEAD), lambda h: (0, h))


def kept_spec(array):
    zeros = (0,) * array.ndim
    return pl.BlockSpec(array.shape, lambda h: zeros, pipeline_mode=pl.Buffered(1))


def all_keys(own_ref, pieces, span):
    return jnp.concatenate(
        [own_ref[:PR_DEV, span]] + [p[:, span] for p in pieces] + [own_ref[PR_DEV:, span]], axis=0
    )


def turned_query(flat_ref, gain_ref, scale, cosine, sine, span):
    normed = flat_ref[:, span] * scale * gain_ref[:, span]
    return (normed * cosine + turn(normed) * sine).astype(LOW)


def softmax_rows(query, keys, bias):
    scores = dot_nt(query, keys) * HEAD ** (-0.5) + bias
    weights = jnp.exp(scores - jnp.max(scores, axis=1, keepdims=True))
    return weights * (1.0 / jnp.sum(weights, axis=1, keepdims=True))


PIECES = GROUP - 1


def attend_kernel(flat_ref, gain_ref, scale_ref, cos_ref, sin_ref, bias_ref, k_ref, v_ref, *refs):
    out_ref = refs[-1]
    bias = bias_ref[...].astype(FULL)
    scale, cosine, sine = scale_ref[...], cos_ref[...], sin_ref[...]
    for at in range(0, PAIR * HEAD, HEAD):
        span = slice(at, at + HEAD)
        query = turned_query(flat_ref, gain_ref, scale, cosine, sine, span)
        probs = softmax_rows(query, all_keys(k_ref, refs[:PIECES], span), bias)
        values = all_keys(v_ref, refs[PIECES : 2 * PIECES], span)
        out_ref[:, span] = dot_nn(probs.astype(LOW), values).astype(LOW)


def attend_specs(rows, scale, cosine, sine, bias):
    return (
        [head_spec(rows), head_spec(1)]
        + [kept_spec(a) for a in (scale, cosine, sine, bias)]
        + [head_spec(rows)] * 2
        + [head_spec(PR_DEV)] * (2 * PIECES)
    )


def attend(flat, gain, scale, cosine, sine, bias, keys, values, pieces):
    rows, width = flat.shape
    return pl.pallas_call(
        attend_kernel,
        grid=(width // HEAD // PAIR,),
        in_specs=attend_specs(rows, scale, cosine, sine, bias),
        out_specs=head_spec(rows),
        out_shape=jax.ShapeDtypeStruct((rows, width), LOW),
        compiler_params=pltpu.CompilerParams(vmem_limit_bytes=VMEM),
    )(flat, gain, scale, cosine, sine, bias, keys, values, *pieces)


def norm_parts(step, at, grad, flat_ref, gain_ref, scale_ref, inner_ref, gain_grad_ref):
    span = slice(at, at + HEAD)
    product = flat_ref[:, span] * grad
    inner = jnp.sum(product * gain_ref[:, span], axis=1, keepdims=True)
    gain_grad_ref[:, span] = jnp.sum(product * scale_ref[...], axis=0, keepdims=True)
    if at:
        inner_ref[...] += inner
    else:
        inner_ref[...] = jnp.where(step == 0, 0.0, inner_ref[...]) + inner


def attend_back_kernel(
    flat_ref, gain_ref, scale_ref, cos_ref, sin_ref, bias_ref, k_ref, v_ref, *refs
):
    back_ref = refs[2 * PIECES]
    qg_ref, inner_ref, gain_grad_ref, kg_ref, vg_ref, even_ref = refs[2 * PIECES + 1 : -4]
    odd_refs = refs[-4:]
    step = pl.program_id(0)
    bias = bias_ref[...].astype(FULL)
    scale, cosine, sine = scale_ref[...], cos_ref[...], sin_ref[...]
    prompt = PR_DEV * GROUP
    for at in range(0, PAIR * HEAD, HEAD):
        span = slice(at, at + HEAD)
        query = turned_query(flat_ref, gain_ref, scale, cosine, sine, span)
        back = back_ref[:, span]
        keys = all_keys(k_ref, refs[:PIECES], span)
        values = all_keys(v_ref, refs[PIECES : 2 * PIECES], span)
        probs = softmax_rows(query, keys, bias)
        prob_grad = dot_nt(back, values)
        value_grad = dot_tn(probs.astype(LOW), back)
        row_dot = jnp.sum(probs * prob_grad, axis=1, keepdims=True)
        score_grad = (probs * (prob_grad - row_dot)).astype(LOW)
        query_grad = dot_nn(score_grad, keys) * HEAD ** (-0.5)
        key_grad = dot_tn(score_grad, query) * HEAD ** (-0.5)
        query_grad = query_grad * cosine - turn(query_grad) * sine
        qg_ref[:, span] = query_grad
        norm_parts(step, at, query_grad, flat_ref, gain_ref, scale_ref, inner_ref, gain_grad_ref)
        for which, grad, own_ref in ((0, key_grad, kg_ref), (1, value_grad, vg_ref)):
            own_ref[:PR_DEV, span] = grad[:PR_DEV]
            own_ref[PR_DEV:, span] = grad[prompt:]
            for j in range(1, GROUP):
                to = odd_refs[j // 2] if j % 2 else even_ref.at[j // 2 - 1]
                to[which, :, span] = grad[j * PR_DEV : (j + 1) * PR_DEV].astype(LOW)


def attend_back(flat, gain, scale, cosine, sine, bias, keys, values, pieces, back):
    rows, width = flat.shape
    wide = jax.ShapeDtypeStruct((rows, width), FULL)
    both = pl.BlockSpec((3, 2, PR_DEV, PAIR * HEAD), lambda h: (0, 0, 0, h))
    return pl.pallas_call(
        attend_back_kernel,
        grid=(width // HEAD // PAIR,),
        in_specs=attend_specs(rows, scale, cosine, sine, bias) + [head_spec(rows)],
        out_specs=[
            head_spec(rows),
            pl.BlockSpec((rows, 1), lambda h: (0, 0)),
            head_spec(1),
            head_spec(rows),
            head_spec(rows),
            both,
        ]
        + [pl.BlockSpec((2, PR_DEV, PAIR * HEAD), lambda h: (0, 0, h))] * 4,
        out_shape=[
            wide,
            jax.ShapeDtypeStruct((rows, 1), FULL),
            jax.ShapeDtypeStruct((1, width), FULL),
            wide,
            wide,
            jax.ShapeDtypeStruct((3, 2, PR_DEV, width), LOW),
        ]
        + [jax.ShapeDtypeStruct((2, PR_DEV, width), LOW)] * 4,
        compiler_params=pltpu.CompilerParams(vmem_limit_bytes=VMEM),
        cost_estimate=pl.CostEstimate(
            flops=20 * 10**9, bytes_accessed=40 * 10**6, transcendentals=4 * 10**6
        ),
    )(flat, gain, scale, cosine, sine, bias, keys, values, *pieces, back)


def key_back_kernel(*refs):
    kg_ref, vg_ref, flat_ref, gain_ref, scale_ref, cos_ref, sin_ref = refs[:7]
    got, keys, values, last_keys, last_values = refs[7:12]
    out_ref, inner_ref, gain_grad_ref, value_ref = refs[12:]
    step = pl.program_id(0)
    for at in range(0, PAIR * HEAD, HEAD):
        span = slice(at, at + HEAD)
        grads = []
        for which, own_ref, near, last in ((0, kg_ref, keys, last_keys), (1, vg_ref, values, last_values)):
            first = own_ref[:PR_DEV, span] + got[which, :, span].astype(FULL)
            first = first + near[0, :, span].astype(FULL) + last[:, span].astype(FULL)
            grads.append(jnp.concatenate([first, own_ref[PR_DEV:, span]], axis=0))
        key_grad = grads[0] * cos_ref[...] - turn(grads[0]) * sin_ref[...]
        out_ref[:, span] = key_grad
        norm_parts(step, at, key_grad, flat_ref, gain_ref, scale_ref, inner_ref, gain_grad_ref)
        value_ref[:, span] = grads[1].astype(LOW)


def key_back(key_grad, value_grad, flat, gain, scale, cosine, sine, returned):
    rows, width = flat.shape
    columns = PAIR * HEAD
    return pl.pallas_call(
        key_back_kernel,
        grid=(width // columns,),
        in_specs=[head_spec(rows)] * 3
        + [head_spec(1)]
        + [kept_spec(a) for a in (scale, cosine, sine)]
        + [pl.BlockSpec((2, PR_DEV, columns), lambda h: (0, 0, h))]
        + [pl.BlockSpec((1, PR_DEV, columns), lambda h: (0, 0, h))] * 2
        + [head_spec(PR_DEV)] * 2,
        out_specs=[
            head_spec(rows),
            pl.BlockSpec((rows, 1), lambda h: (0, 0)),
            head_spec(1),
            head_spec(rows),
        ],
        out_shape=[
            jax.ShapeDtypeStruct((rows, width), FULL),
            jax.ShapeDtypeStruct((rows, 1), FULL),
            jax.ShapeDtypeStruct((1, width), FULL),
            jax.ShapeDtypeStruct((rows, width), LOW),
        ],
        cost_estimate=SMALL,
    )(key_grad, value_grad, flat, gain, scale, cosine, sine, *returned)


def pack_kernel(query, key, value, out, rest, packed):
    at = 0
    for ref in (query, key, value):
        packed[at : at + ref.shape[0]] = ref[...]
        at += ref.shape[0]
    packed[at : at + out.shape[1]] = out[...].T
    packed[at + out.shape[1] :] = rest[...]


def pack_weights(w_query, w_key, w_value, w_out, rest):
    rows = 4 * w_query.shape[0] + rest.shape[0]
    return pl.pallas_call(
        pack_kernel, out_shape=jax.ShapeDtypeStruct((rows, w_query.shape[1]), LOW)
    )(w_query, w_key, w_value, w_out, rest)


def unpack_kernel(first, blocks_ref, packed, out, held, sems):
    width = packed.shape[2]
    parts = out.shape[1] // width
    rows = (packed.shape[1] - first) // parts
    count = packed.shape[0]
    place = lambda i: pl.ds(i * rows, rows)
    loads = [
        pltpu.make_async_copy(
            packed.at[blocks_ref[i], pl.ds(first + j * rows, rows)],
            held.at[place(i), pl.ds(j * width, width)],
            sems.at[i * parts + j],
        )
        for i in range(count)
        for j in range(parts)
    ]
    stores = [
        pltpu.make_async_copy(held.at[place(i)], out.at[place(i)], sems.at[count * parts + i])
        for i in range(count)
    ]
    for one in loads:
        one.start()
    for i, store in enumerate(stores):
        for j in range(parts):
            loads[i * parts + j].wait()
        store.start()
    for store in stores:
        store.wait()


def unpack_rows(packed, blocks, first, width):
    count = packed.shape[0]
    parts = width // packed.shape[2]
    rows = (packed.shape[1] - first) // parts
    return pl.pallas_call(
        lambda *refs: unpack_kernel(first, *refs),
        in_specs=[pl.BlockSpec(memory_space=pltpu.SMEM), pl.BlockSpec(memory_space=pl.ANY)],
        out_specs=pl.BlockSpec(memory_space=pl.ANY),
        out_shape=jax.ShapeDtypeStruct((count * rows, width), LOW),
        scratch_shapes=[
            pltpu.VMEM((count * rows, width), LOW),
            pltpu.SemaphoreType.DMA((count * parts + count,)),
        ],
        compiler_params=pltpu.CompilerParams(vmem_limit_bytes=SOME),
    )(blocks, packed)


def pack_specs(gathered, places, steps, at):
    count, width = gathered.shape[0] // steps, gathered.shape[2]
    block = at
    return [
        pl.BlockSpec((count, block, width), lambda i, place=place: (i, place, 0))
        for place in places
    ]


def project_kernel(mats, roundings, rows_ref, *refs):
    mat_refs, out_refs, totals = refs[:mats], refs[mats : 2 * mats], refs[2 * mats :]
    step = pl.program_id(0)
    rows = rows_ref[...]
    for mat, out, total, rounding in zip(mat_refs, out_refs, totals, roundings):
        flat = mat[...].reshape(-1, mat.shape[2])
        part = dot_nn(rows, flat)

        @pl.when(step == 0)
        def _():
            total[...] = part

        @pl.when(step > 0)
        def _():
            total[...] += part

        @pl.when(step == pl.num_programs(0) - 1)
        def _():
            out[...] = total[...].astype(rounding)


def project(rows, gathered, block, places, roundings):
    count, width = rows.shape
    columns = gathered.shape[2]
    steps = 4
    outs = [jax.ShapeDtypeStruct((count, columns), rounding) for rounding in roundings]
    return pl.pallas_call(
        lambda *refs: project_kernel(len(places), roundings, *refs),
        grid=(steps,),
        in_specs=[pl.BlockSpec((count, width // steps), lambda i: (0, i))]
        + pack_specs(gathered, places, steps, block),
        out_specs=[pl.BlockSpec((count, columns), lambda i: (0, 0)) for _ in outs],
        out_shape=outs,
        scratch_shapes=[pltpu.VMEM((count, columns), FULL)] * len(outs),
        compiler_params=pltpu.CompilerParams(vmem_limit_bytes=SOME),
        cost_estimate=pl.CostEstimate(
            flops=2 * count * width * columns * len(places),
            bytes_accessed=2 * width * columns * len(places) + 8 * count * columns,
            transcendentals=0,
        ),
    )(rows, *[gathered] * len(places))


def project_back_kernel(mats, *refs):
    out = refs[-1]
    total = None
    for rows_ref, mat in zip(refs[:mats], refs[mats:-1]):
        part = dot_nt(rows_ref[...], mat[...].reshape(-1, mat.shape[2]))
        total = part if total is None else total + part
    out[...] = total


def project_back(rows, gathered, block, places):
    count, columns = rows[0].shape
    width = gathered.shape[0] * block
    steps = 4
    fixed = pl.BlockSpec((count, columns), lambda i: (0, 0), pipeline_mode=pl.Buffered(1))
    return pl.pallas_call(
        lambda *refs: project_back_kernel(len(places), *refs),
        grid=(steps,),
        in_specs=[fixed] * len(rows) + pack_specs(gathered, places, steps, block),
        out_specs=pl.BlockSpec((count, width // steps), lambda i: (0, i)),
        out_shape=jax.ShapeDtypeStruct((count, width), FULL),
        compiler_params=pltpu.CompilerParams(vmem_limit_bytes=SOME),
        cost_estimate=pl.CostEstimate(
            flops=2 * count * width * columns * len(places),
            bytes_accessed=2 * width * columns * len(places) + 4 * count * width,
            transcendentals=0,
        ),
    )(*rows, *[gathered] * len(places))


def pre_kernel(core_ref, *refs):
    inputs, outs = refs[:11], refs[11:]
    step = pl.program_id(0)
    columns = inputs[0].shape[1]
    parts = []
    for flat, grad, gain, scale, inner in (inputs[:5], inputs[5:10]):
        scaled = scale[...]
        mean = inner[...] * (1.0 / (HEADS * HEAD))
        parts.append(
            (
                scaled * gain[...] * grad[...] - flat[...] * (scaled * scaled * scaled) * mean
            ).astype(LOW)
        )
    outs[0][...], outs[1][...] = parts

    @pl.when(step != core_ref[0])
    def _():
        for j, part in enumerate((*parts, inputs[10][...])):
            outs[2][:, j * columns : (j + 1) * columns] = part


def pre_grads_pass(core, query, key, value):
    rows, width = value.shape
    columns = width // 2
    half = lambda rows: pl.BlockSpec((rows, columns), lambda h: (0, h))
    side = [half(rows), half(rows), half(1)] + [pl.BlockSpec((rows, 1), lambda h: (0, 0))] * 2
    return pl.pallas_call(
        pre_kernel,
        grid=(2,),
        in_specs=[pl.BlockSpec(memory_space=pltpu.SMEM)] + side + side + [half(rows)],
        out_specs=[half(rows), half(rows), pl.BlockSpec((rows, 3 * columns), lambda h: (0, 0))],
        out_shape=[jax.ShapeDtypeStruct((rows, width), LOW)] * 2
        + [jax.ShapeDtypeStruct((rows, 3 * columns), LOW)],
    )(core, *query, *key, value)


def weight_kernel(chip_ref, core_ref, *refs):
    normed, normed_got, back, back_got, query, key, value, got, context, context_got = refs[:10]
    out_ref, right_ref, left_ref, pre_both, context_both = refs[10:]
    rows, columns = query.shape

    @pl.when(pl.program_id(0) == 0)
    def _():
        for j, part in enumerate((query, key, value)):
            pre_both[:rows, j * columns : (j + 1) * columns] = part[...]
        pre_both[rows:] = got[...]
        context_both[:rows] = context[...]
        context_both[rows:] = context_got[...]

    left = jnp.concatenate([normed[...], normed_got[...]], axis=0)
    out_ref[0, :, : 3 * columns] = dot_tn(left, pre_both[...]).astype(LOW)
    left = jnp.concatenate([back[...], back_got[...]], axis=0)
    out_ref[0, :, 3 * columns :] = dot_tn(left, context_both[...]).astype(LOW)

    @pl.when(pl.program_id(0) == HOPS.index(4))
    def _():
        right_ref[...] = out_ref[0, :, : 2 * columns]
        left_ref[...] = out_ref[0, :, 2 * columns :]


def weight_grads(chips, core, normed, back, pre_grads, got, context, context_got):
    rows, width = normed[0].shape
    columns = context_got.shape[1]
    count = chips.shape[0]
    block = width // count
    tall = pl.BlockSpec((rows, block), lambda i, chip, core: (0, chip[i]))
    mine = pl.BlockSpec((rows, columns), lambda i, chip, core: (0, core[0]))
    fixed = lambda a: pl.BlockSpec(a.shape, lambda i, chip, core: (0, 0))
    return pl.pallas_call(
        weight_kernel,
        grid_spec=pltpu.PrefetchScalarGridSpec(
            num_scalar_prefetch=2,
            grid=(count,),
            in_specs=[tall] * 4 + [mine] * 3 + [fixed(got), mine, fixed(context_got)],
            out_specs=[pl.BlockSpec((1, block, 4 * columns), lambda i, chip, core: (i, 0, 0))]
            + [pl.BlockSpec((block, 2 * columns), lambda i, chip, core: (0, 0))] * 2,
            scratch_shapes=[
                pltpu.VMEM((2 * rows, 3 * columns), LOW),
                pltpu.VMEM((2 * rows, columns), LOW),
            ],
        ),
        out_shape=[jax.ShapeDtypeStruct((count, block, 4 * columns), LOW)]
        + [jax.ShapeDtypeStruct((block, 2 * columns), LOW)] * 2,
        compiler_params=pltpu.CompilerParams(vmem_limit_bytes=VMEM),
        cost_estimate=pl.CostEstimate(
            flops=16 * rows * width * columns,
            bytes_accessed=2 * (4 * rows * width + 8 * rows * columns + 4 * width * columns),
            transcendentals=0,
        ),
    )(chips, core, *normed, *back, *pre_grads, got, context, context_got)


def ring_weights(blocks, right, left, fillers):
    part = lambda hop: blocks[HOPS.index(hop)]
    cut = blocks.shape[2] // 2
    right, left = ahead(right), behind(left)
    fillers.next(left)
    outward, inward = part(3), part(-3)
    right = jnp.concatenate([add_low(outward[:, :cut], right), outward[:, cut:]], axis=1)
    left = jnp.concatenate([inward[:, :cut], add_low(inward[:, cut:], left)], axis=1)
    right, left = ahead(right), behind(left)
    fillers.next(left)
    token = left
    for hop in (2, 1):
        right, left = ahead(add_low(part(hop), right)), behind(add_low(part(-hop), left))
        fillers.next(left)
        token = left if hop == 2 else token
    return part(0).astype(FULL) + right.astype(FULL) + left.astype(FULL), token


def expert_kernel(
    rows_ref, back_ref, gate_ref, wg0, wg1, wu0, wu1, wd0, wd1, grad_ref, h0, h1, g0, g1, u0, u1
):
    rows = rows_ref[...]
    back = back_ref[...]
    gate = gate_ref[...]
    total = None
    for wg, wu, wd, h, g, u in ((wg0, wu0, wd0, h0, g0, u0), (wg1, wu1, wd1, h1, g1, u1)):
        gate_pre = dot_nn(rows, wg[...])
        up_pre = dot_nn(rows, wu[...])
        hidden_grad = gate * dot_nt(back, wd[...])
        sig = 1.0 / (1.0 + jnp.exp(-gate_pre))
        act = gate_pre * sig
        h[...] = (gate * (act * up_pre)).astype(LOW)
        gate_grad = (hidden_grad * up_pre * (sig * (1.0 + gate_pre * (1.0 - sig)))).astype(LOW)
        up_grad = (hidden_grad * act).astype(LOW)
        g[...] = gate_grad
        u[...] = up_grad
        part = dot_nt(gate_grad, wg[...]) + dot_nt(up_grad, wu[...])
        total = part if total is None else total + part
    grad_ref[...] = total.astype(LOW)


def expert_pass(rows, back, gate, gate_mats, up_mats, down_mats):
    count, width = rows.shape
    hidden = gate_mats[0].shape[1]
    tile = 256
    whole = lambda array: pl.BlockSpec(
        array.shape, lambda i: (0, 0), pipeline_mode=pl.Buffered(1)
    )
    tall = lambda columns: pl.BlockSpec((tile, columns), lambda i: (i, 0))
    mats = [*gate_mats, *up_mats, *down_mats]
    flops = 2 * 5 * count * width * hidden * 2
    return pl.pallas_call(
        expert_kernel,
        grid=(count // tile,),
        in_specs=[tall(width), tall(width), tall(1)] + [whole(m) for m in mats],
        out_specs=[tall(width)] + [tall(hidden)] * 6,
        out_shape=[jax.ShapeDtypeStruct((count, width), LOW)]
        + [jax.ShapeDtypeStruct((count, hidden), LOW)] * 6,
        compiler_params=pltpu.CompilerParams(vmem_limit_bytes=VMEM),
        cost_estimate=pl.CostEstimate(
            flops=flops,
            bytes_accessed=2 * (3 * count * width + 6 * count * hidden + 6 * width * hidden),
            transcendentals=2 * count * hidden,
        ),
    )(rows, back, gate, *mats)


def chunk_kernel(pieces, held, at, splits, gate_ref, *refs):
    piece_refs, refs = refs[:pieces], refs[pieces:]
    back_ref, mats, refs = refs[0], refs[1:7], refs[7 + held :]
    grad_outs, refs = refs[: len(splits)], refs[len(splits) :]
    rows_out, outs = refs[0], refs[1:7]
    rows, back, wide, wd, hidden, both_grads, grads, sems = refs[7:]
    count = rows.shape[0]
    part = wd.shape[1]
    slab = wide.shape[0] // 4
    across = lambda k, half: pl.ds((2 * k + half) * part, part)
    place = pl.ds(at * count, count)
    copy = pltpu.make_async_copy
    load_rows, start = [], 0
    for piece in piece_refs:
        span = pl.ds(start, piece.shape[0])
        load_rows.append(copy(piece, rows.at[span], sems.at[len(load_rows)]))
        start += piece.shape[0]
    load_back = copy(back_ref.at[place], back, sems.at[6])
    loads = []
    for half in range(2):
        places = [wide.at[:, across(0, half)], wide.at[:, across(1, half)], wd.at[half]]
        loads.append(
            [copy(mats[2 * k + half], to, sems.at[7 + 3 * half + k]) for k, to in enumerate(places)]
        )
    for one in load_rows + loads[0][:2] + [load_back] + loads[0][2:] + loads[1]:
        one.start()
    gate = gate_ref[...]
    for one in load_rows:
        one.wait()
    stores = [copy(rows, rows_out.at[place], sems.at[13])]
    stores[0].start()
    for half in range(2):
        columns = pl.ds(half * part, part)
        loads[half][0].wait()
        gate_pre = dot_nn(rows[...], wide[:, across(0, half)])
        loads[half][1].wait()
        up_pre = dot_nn(rows[...], wide[:, across(1, half)])
        if half == 0:
            load_back.wait()
        loads[half][2].wait()
        hidden_grad = gate * dot_nt(back[...], wd[half])
        sig = 1.0 / (1.0 + jnp.exp(-gate_pre))
        act = gate_pre * sig
        hidden[:, columns] = (gate * (act * up_pre)).astype(LOW)
        both_grads[:, across(0, half)] = (
            hidden_grad * up_pre * (sig * (1.0 + gate_pre * (1.0 - sig)))
        ).astype(LOW)
        both_grads[:, across(1, half)] = (hidden_grad * act).astype(LOW)
    for half in range(2):
        held_in = (
            hidden.at[:, pl.ds(half * part, part)],
            both_grads.at[:, across(0, half)],
            both_grads.at[:, across(1, half)],
        )
        for k, source in enumerate(held_in):
            stores.append(copy(source, outs[2 * k + half].at[place], sems.at[14 + 3 * half + k]))
            stores[-1].start()

    @pl.loop(0, 4)
    def _(j):
        span = pl.ds(pl.multiple_of(j * slab, slab), slab)
        grads[:, span] = dot_nt(both_grads[...], wide[span]).astype(LOW)

    start = 0
    for k, (split, to) in enumerate(zip(splits, grad_outs)):
        stores.append(copy(grads.at[pl.ds(start, split)], to, sems.at[20 + k]))
        stores[-1].start()
        start += split
    for one in stores:
        one.wait()


def expert_chunk(pieces, back, gate, mats, at, held, splits):
    all_rows, width = back.shape
    part = mats[0].shape[1]
    hidden = 2 * part
    count = sum(piece.shape[0] for piece in pieces)
    anywhere = pl.BlockSpec(memory_space=pl.ANY)
    held = [] if held is None else list(held)
    args = [gate, *pieces, back, *mats, *held]
    out = pl.pallas_call(
        lambda *refs: chunk_kernel(len(pieces), len(held), at, splits, *refs),
        grid=(1,),
        in_specs=[pl.BlockSpec((count, 1), lambda j: (at, 0))] + [anywhere] * (len(args) - 1),
        out_specs=[anywhere] * (len(splits) + 7),
        out_shape=[jax.ShapeDtypeStruct((split, width), LOW) for split in splits]
        + [jax.ShapeDtypeStruct((all_rows, width), LOW)]
        + [jax.ShapeDtypeStruct((all_rows, part), LOW)] * 6,
        scratch_shapes=[
            pltpu.VMEM((count, width), LOW),
            pltpu.VMEM((count, width), LOW),
            pltpu.VMEM((width, 2 * hidden), LOW),
            pltpu.VMEM((2, part, width), LOW),
            pltpu.VMEM((count, hidden), LOW),
            pltpu.VMEM((count, 2 * hidden), LOW),
            pltpu.VMEM((count, width), LOW),
            pltpu.SemaphoreType.DMA((23,)),
        ],
        input_output_aliases={
            len(args) - len(held) + k: len(splits) + k for k in range(len(held))
        },
        compiler_params=pltpu.CompilerParams(vmem_limit_bytes=VMEM),
        cost_estimate=pl.CostEstimate(
            flops=2 * 5 * count * width * hidden,
            bytes_accessed=2 * (4 * count * width + 3 * count * hidden + 3 * width * hidden),
            transcendentals=count * hidden,
        ),
    )(*args)
    return out[: len(splits)], out[len(splits) :]


def mixed_kernel(chip_ref, same_ref, cross_ref, core_ref, *refs):
    first_ref, second_ref, out_ref = refs[4:]
    rows = out_ref.shape[2]
    first, second = (
        jnp.concatenate([refs[k][...], refs[k + 1][...]], axis=0) for k in (0, 2)
    )
    result = (dot_nn(first, first_ref[...]) + dot_nn(second, second_ref[...])).astype(LOW)
    out_ref[0, core_ref[0]] = result[:rows]
    out_ref[0, 1 - core_ref[0]] = result[rows:]


def mixed_pass(h0, h1, down_mats, chips, core):
    count, columns = h0.shape
    width = down_mats[0].shape[1]
    rows = count // len(LAYOUT)
    places = [
        jnp.array([LAYOUT.index((hop, cross)) for hop in HOPS], jnp.int32) for cross in (0, 1)
    ]
    once = pl.Buffered(1)
    fixed = lambda m: pl.BlockSpec(m.shape, lambda i, *tables: (0, 0), pipeline_mode=once)
    block = lambda k: pl.BlockSpec((rows, columns), lambda i, *tables: (tables[k][i], 0))
    out = pl.pallas_call(
        mixed_kernel,
        grid_spec=pltpu.PrefetchScalarGridSpec(
            num_scalar_prefetch=4,
            grid=(len(HOPS),),
            in_specs=[block(1), block(2), block(1), block(2)] + [fixed(m) for m in down_mats],
            out_specs=pl.BlockSpec(
                (1, 2, rows, width), lambda i, chip, *tables: (chip[i], 0, 0, 0)
            ),
        ),
        out_shape=jax.ShapeDtypeStruct((len(HOPS), 2, rows, width), LOW),
        compiler_params=pltpu.CompilerParams(vmem_limit_bytes=SOME),
        cost_estimate=pl.CostEstimate(
            flops=4 * count * columns * width,
            bytes_accessed=2 * (count * (2 * columns + width) + 2 * columns * width),
            transcendentals=0,
        ),
    )(chips, *places, core, h0, h0, h1, h1, *down_mats)
    return out.reshape(count, width)


def expert_ring(rows, back, gate, mats, waiting):
    size = rows.shape[0]
    cut = size // 2
    swap = lambda block: swap_bit(block, "dp", 0)
    chunk = lambda pieces, at, held, *splits: expert_chunk(
        pieces, back, gate, mats, at, held, splits
    )
    rows, pair = together(rows, swap(rows))
    left, right = ahead(rows), behind(rows)
    parts, crossed = cut_rows(waiting, 4), []
    same, cross = {}, {}
    cross_over = lambda token: crossed.append(swap_tensor(after(parts[len(crossed)], token)))
    cross_over(pair)
    (same[0], cross[0]), held = chunk([rows, pair], 6, None, size, size)
    left, right, same[0] = together(left, right, same[0])
    pieces, got = [left, right], [swap(left), swap(right)]
    left, right = ahead(left), behind(right)
    pieces[0], crossed[0] = together(pieces[0], crossed[0])
    cross_over(pieces[0])
    (same[1],), held = chunk(pieces, 7, held, 2 * size)
    left, right, same[1] = together(left, right, same[1])
    pieces, got = [left, right, *got], [swap(left), swap(right)]
    left, right = ahead(left), behind(right)
    pieces[0], crossed[1] = together(pieces[0], crossed[1])
    cross_over(pieces[0])
    (same[2], cross[1]), held = chunk(pieces, 0, held, 2 * size, 2 * size)
    left, right, same[2] = together(left, right, same[2])
    pieces, got = [left, right, *got], [swap(left), swap(right)]
    left, right = ahead(left[:cut]), behind(right[cut:])
    pieces[0], crossed[2] = together(pieces[0], crossed[2])
    cross_over(pieces[0])
    (same[3], cross[2]), held = chunk(pieces, 1, held, 2 * size, 2 * size)
    left, right, crossed[3], same[3] = together(left, right, crossed[3], same[3])
    pieces = [left, right, swap(left), swap(right), *got]
    (same[4], cross[4], cross[3]), held = chunk(pieces, 2, held, size, size, 2 * size)
    waiting = jnp.concatenate(crossed, axis=0)
    return same, cross, held, waiting


def body(
    inputs,
    attn_gain,
    w_query,
    w_key,
    w_value,
    query_gain,
    key_gain,
    w_out,
    moe_gain,
    w_gate,
    w_up,
    w_down,
    experts,
    gates,
    segments,
    gaps,
    cotangent,
):
    dp_count = lax.axis_size("dp")
    dp_index = lax.axis_index("dp")
    side = lax.axis_index("tensor")
    token_count, model_width = inputs.shape
    half_count = token_count // 2
    top_count = experts.shape[1]
    expert_count = w_gate.shape[0] * dp_count
    capacity = token_count * top_count * dp_count * 9 // (8 * expert_count)
    prompt_length = PR_DEV * GROUP
    column_total = HEADS * HEAD
    block = w_query.shape[0]
    local_width = w_query.shape[1]
    local_heads = local_width // HEAD

    def own_half(array):
        return lax.dynamic_slice_in_dim(array, side * half_count, half_count, axis=0)

    def other_half(array):
        return lax.dynamic_slice_in_dim(array, (1 - side) * half_count, half_count, axis=0)

    def both_halves(own, other):
        first = side == 0
        return jnp.concatenate(
            [jnp.where(first, own, other), jnp.where(first, other, own)], axis=0
        )

    gate_mats = (w_gate[0], swap_tensor(w_gate[0]))
    up_mats = (w_up[0], swap_tensor(w_up[0]))

    ring = dp_count == 2 * len(RING)

    gates_high = gates.astype(LOW)
    gates_low = (gates - gates_high.astype(FULL)).astype(LOW)
    routing = jnp.concatenate([experts.astype(LOW).T, gates_high.T, gates_low.T], axis=1)
    routing = jnp.pad(routing, ((0, 0), (0, local_width - 3 * token_count)))
    gains = jnp.concatenate([attn_gain, moe_gain, query_gain, key_gain])
    gains = jnp.pad(gains[None], ((0, 7), (0, local_width - 4 * block)))
    packed = pack_weights(
        w_query, w_key, w_value, w_out, jnp.concatenate([gains, routing], axis=0)
    )
    gathered = lax.all_gather(packed, "dp", axis=0, tiled=False)
    cotangent_half = own_half(cotangent)
    gathered_back = lax.all_gather(cotangent_half.astype(LOW), "dp", axis=0, tiled=False)
    core = dp_index % 2
    tokens_f = inputs.astype(FULL)
    prompt_pos = dp_index % GROUP * PR_DEV + jnp.arange(PR_DEV, dtype=jnp.int32)
    later_pos = cont_positions(segments[0], gaps[0], prompt_length)
    positions = jnp.concatenate([prompt_pos, later_pos], axis=0)
    cosine, sine = rope_tables(positions, HEAD)
    sine = jnp.where(jnp.arange(HEAD) < HEAD // 2, -sine, sine)
    prompt_query = jnp.arange(token_count, dtype=jnp.int32) < PR_DEV
    prompt_at = jnp.arange(prompt_length, dtype=jnp.int32)
    prompt_keypos = ((dp_index % GROUP) ^ (prompt_at // PR_DEV)) * PR_DEV + prompt_at % PR_DEV
    allowed_prompt = (~prompt_query)[:, None] | (prompt_keypos[None, :] <= positions[:, None])
    query_segment = jnp.concatenate([jnp.full((PR_DEV,), -1, jnp.int32), segments[0]], axis=0)
    allowed_cont = (query_segment[:, None] == segments[0][None, :]) & (
        later_pos[None, :] <= positions[:, None]
    )
    allowed = jnp.concatenate([allowed_prompt, allowed_cont], axis=1)
    bias = jnp.where(allowed, 0.0, -1e30).astype(LOW)
    gathered, cosine, sine, bias, *early = together(
        gathered, cosine, sine, bias, gate_mats[1], up_mats[1]
    )
    gate_mats, up_mats = (gate_mats[0], early[0]), (up_mats[0], early[1])
    rest = gathered[:, 4 * block : 4 * block + 16]
    gain_rows = rest[:, 0].astype(FULL)
    gain_one, gain_two, gain_q, gain_k = (
        gain_rows[:, j * block : (j + 1) * block].reshape(-1) for j in range(4)
    )
    gain_query_local = lax.dynamic_slice_in_dim(gain_q, side * local_width, local_width)
    gain_key_local = lax.dynamic_slice_in_dim(gain_k, side * local_width, local_width)

    names, *parts = (
        rest[:, 8:, j * token_count : (j + 1) * token_count] for j in range(3)
    )
    weights = parts[0].astype(FULL) + parts[1].astype(FULL)
    named = names == dp_index.astype(LOW)
    picked = jnp.sum(named.astype(FULL), axis=1)
    weight = jnp.sum(jnp.where(named, weights, 0.0), axis=1)
    order = jnp.arange(token_count, dtype=jnp.int32)
    earlier = (order[:, None] < order[None, :]).astype(LOW)
    within = dot_nn(picked.astype(LOW), earlier)
    per_row = jnp.sum(picked, axis=1)
    rows_order = jnp.arange(dp_count, dtype=jnp.int32)
    ahead = jnp.sum(
        jnp.where(rows_order[None, :] < rows_order[:, None], per_row[None, :], 0.0), axis=1
    )
    kept = (picked > 0.0) & (within + ahead[:, None] < capacity)
    weight = jnp.where(kept, weight, 0.0)
    weight = lax.dynamic_slice_in_dim(weight, side * half_count, half_count, axis=1)
    if ring:
        blocks, chips = ring_blocks(dp_index), ring_chips(dp_index, HOPS)
        weight = weight[blocks]
    weight = weight.reshape(-1, 1)

    normed_b = rms_norm(tokens_f, gain_one).astype(LOW)
    query_flat, key_flat, values_b = project(
        normed_b, gathered, block, (0, 1, 2), (FULL, FULL, LOW)
    )
    key_sq = jnp.sum(key_flat * key_flat, axis=1)
    key_sq, value_prompt = together(key_sq, values_b[:PR_DEV])
    value_pieces = collect_prompt(value_prompt, 1, 2)
    query_sq, key_sq = lax.psum(
        (jnp.sum(query_flat * query_flat, axis=1), key_sq), "tensor"
    )
    query_sq, down_mat = lax.optimization_barrier((query_sq, w_down[0]))
    down_mats = (down_mat, swap_tensor(down_mat))
    query_scale = lax.rsqrt(query_sq / column_total + EPSILON)[:, None]
    key_scale = lax.rsqrt(key_sq / column_total + EPSILON)[:, None]
    keys_b = rope_pass(key_flat, gain_key_local[None], key_scale, cosine, sine)
    pieces = (*collect_prompt(keys_b[:PR_DEV], 2, 1), *value_pieces)
    turned_by = (gain_query_local[None], query_scale, cosine, sine, bias)
    context_b = attend(query_flat, *turned_by, keys_b, values_b, pieces)
    attn_part = project_back([context_b], gathered, block, (3,))
    attn_part, late, weight = together(attn_part, down_mats[1], weight)
    down_mats = (down_mats[0], late)
    mats = (*gate_mats, *up_mats, *down_mats)
    attn_other = swap_tensor(other_half(attn_part).astype(LOW))
    gathered_back = after(gathered_back, attn_part)
    if ring:
        back_rows = unpack_rows(gathered_back, blocks, 0, model_width)
    else:
        back_rows = gathered_back.reshape(-1, model_width)
    attn_other, back_rows, weight = together(attn_other, back_rows, weight)
    hidden_state = own_half(tokens_f) + own_half(attn_part) + attn_other.astype(FULL)
    normed_two_b = rms_norm(hidden_state, gain_two).astype(LOW)

    low_tn = lambda left, right: dot_tn(left, right).astype(LOW)
    upper = lambda array: array[: array.shape[0] // 2]
    lower = lambda array: array[array.shape[0] // 2 :]
    if ring:
        same, cross, held, hidden_other = expert_ring(
            normed_two_b, back_rows, weight, mats, hidden_state
        )
        expert_in, h0, h1, g0, g1, u0, u1 = held
        down_got = swap_tensor(low_tn(h1, back_rows))
        late = {}

        def gate_stage(gated):
            late["gate"] = low_tn(gated(expert_in), g1)

        def up_stage(gated):
            late["up"] = low_tn(gated(expert_in), u1)

        def mixed_stage(gated):
            late["mixed"] = mixed_pass(gated(h0), h1, down_mats, chips, core[None])

        fillers = Fillers(gate_stage, up_stage, mixed_stage)
        normed_two_grad = ring_sum(same, cross, fillers)
        gate_sent, up_sent, mixed_rows = late["gate"], late["up"], late["mixed"]
    else:
        hidden_other = swap_tensor(hidden_state)
        expert_in = lax.all_gather(normed_two_b, "dp", axis=0, tiled=True)
        grad_rows, h0, h1, g0, g1, u0, u1 = expert_pass(
            expert_in, back_rows, weight, gate_mats, up_mats, down_mats
        )
        normed_two_grad = lax.psum_scatter(
            grad_rows, "dp", scatter_dimension=0, tiled=True
        ).astype(FULL)
        mixed_rows = (dot_nn(h0, down_mats[0]) + dot_nn(h1, down_mats[1])).astype(LOW)
        down_got = swap_tensor(low_tn(h1, back_rows))
        gate_sent = low_tn(expert_in, g1)
        up_sent = low_tn(expert_in, u1)
    gate_first = swap_tensor(upper(gate_sent))
    normed_two_grad, down_got, gate_first, mixed_rows, up_sent = together(
        normed_two_grad, down_got, gate_first, mixed_rows, up_sent
    )
    mixed = lax.psum_scatter(mixed_rows, "dp", scatter_dimension=0, tiled=True)

    unused_two, norm_two_back = jax.vjp(rms_norm, hidden_state, gain_two)
    state_part, gain_two_grad = norm_two_back(normed_two_grad)
    state_half = cotangent_half + state_part
    attn_grad_half = state_half.astype(LOW)
    attn_grad_b = both_halves(attn_grad_half, swap_tensor(attn_grad_half))
    attn_grad_b, gate_sent, up_sent = together(attn_grad_b, gate_sent, up_sent)
    (context_grad_b,) = project(attn_grad_b, gathered, block, (3,), (LOW,))
    soon = swap_in_turn([lower(gate_sent), upper(up_sent)], context_grad_b)
    if ring:
        pair = lambda own: (own, swap_bit(own, "dp", 0))
        columns = local_width // 2
        context_sent = lax.dynamic_slice_in_dim(context_b, (1 - core) * columns, columns, axis=1)
        normed_pair, attn_grad_pair = pair(normed_b), pair(attn_grad_b)
        context_got = swap_bit(context_sent, "dp", 0)
    query_normed_grad, query_inner, query_gain_part, key_grad, value_grad, even, *odd = attend_back(
        query_flat, *turned_by, keys_b, values_b, pieces, context_grad_b
    )
    returned = return_prompt(odd, even)
    if ring:
        key_grad, context_got, *pairs = together(
            key_grad, context_got, normed_pair[1], attn_grad_pair[1]
        )
        normed_pair, attn_grad_pair = (normed_b, pairs[0]), (attn_grad_b, pairs[1])
    key_normed_grad, key_inner, key_gain_part, value_pre_grad = key_back(
        key_grad, value_grad, key_flat, gain_key_local[None], key_scale, cosine, sine, returned
    )
    query_inner, *soon = together(query_inner, *soon)
    query_inner, key_inner = lax.psum((query_inner[:, 0], key_inner[:, 0]), "tensor")
    query_pre_grad, key_pre_grad, pre_sent = pre_grads_pass(
        core[None],
        (
            query_flat,
            query_normed_grad,
            gain_query_local[None],
            query_scale,
            query_inner[:, None],
        ),
        (key_flat, key_normed_grad, gain_key_local[None], key_scale, key_inner[:, None]),
        value_pre_grad,
    )
    gate_got = jnp.concatenate([gate_first, soon[0]], axis=0)
    pre_grads = (query_pre_grad, key_pre_grad, value_pre_grad)
    grad_sum = lambda left, right, got: dot_tn(left, right) + got.astype(FULL)
    back_all = lambda *grads: project_back(grads, gathered, block, (0, 1, 2))

    wide = lambda part: lax.dynamic_update_slice_in_dim(
        jnp.zeros((column_total,), FULL), part, side * local_width, 0
    )

    def share(part):
        return own_half(part), swap_tensor(other_half(part).astype(LOW)), gain_part(part)

    def input_side(own, other):
        unused_one, norm_one_back = jax.vjp(
            lambda values: rms_norm(values, gain_one), own_half(tokens_f)
        )
        input_half = state_half + norm_one_back(own + other.astype(FULL))[0]
        return input_half, swap_tensor(input_half)

    def gain_part(part):
        return jnp.sum(part * rms_norm(tokens_f, 1.0), axis=0)

    def gain_side(gain_one_grad):
        grads = jnp.stack(
            [gain_one_grad, gain_two_grad, wide(query_gain_part[0]), wide(key_gain_part[0])]
        ).reshape(4, dp_count, block)
        grads = jnp.swapaxes(grads, 0, 1).reshape(dp_count, 4 * block)
        sums = jnp.sum(lax.all_to_all(grads, "dp", 0, 0, tiled=True), axis=0)
        return (sums + swap_tensor(sums)).reshape(4, block)

    if ring:
        pre_got = swap_bit(pre_sent, "dp", 0)
        w_blocks, *far = weight_grads(
            chips,
            core[None],
            normed_pair,
            attn_grad_pair,
            pre_grads,
            pre_got,
            context_b,
            context_got,
        )
        w_blocks, mixed, *far = together(w_blocks, mixed, *far)
        up_got = jnp.concatenate(
            [soon[1], *swap_in_turn(cut_rows(lower(up_sent), 2), far[0])], axis=0
        )
        mixed_other = swap_tensor(mixed)
        late = {}

        def normed_stage(gated):
            late["normed"] = share(back_all(*[gated(grad) for grad in pre_grads]))

        def expert_stage(gated):
            late["down"] = grad_sum(gated(h0), back_rows, down_got)
            late["gate"] = grad_sum(gated(expert_in), g0, gate_got)

        def input_stage(gated):
            late["input"] = input_side(late["normed"][0], gated(late["normed"][1]))
            late["gains"] = gain_side(gated(late["normed"][2]))

        fillers = Fillers(normed_stage, expert_stage, input_stage)
        w_half, token = ring_weights(w_blocks, *far, fillers)
        input_half, input_other = late["input"]
        gain_sums = late["gains"]
        down_grad, gate_w_grad = late["down"], late["gate"]
        up_w_grad = grad_sum(after(expert_in, token), u0, up_got)
        own_w = lax.dynamic_slice_in_dim(w_half, core * block, block, axis=0)
        got_w = swap_bit(
            lax.dynamic_slice_in_dim(w_half, (1 - core) * block, block, axis=0), "dp", 0
        )
        left_w, right_w = jnp.where(core == 0, own_w, got_w), jnp.where(core == 0, got_w, own_w)
        w_sums = [
            jnp.concatenate([w[:, j * columns : (j + 1) * columns] for w in (left_w, right_w)], axis=1)
            for j in range(4)
        ]
        mixed_other = after(mixed_other, token)
    else:
        w_grads = jnp.concatenate(
            [low_tn(normed_b, g) for g in pre_grads] + [low_tn(attn_grad_b, context_b)], axis=1
        )
        w_sum = lax.psum_scatter(w_grads, "dp", scatter_dimension=0, tiled=True).astype(FULL)
        w_sums = [w_sum[:, j * local_width : (j + 1) * local_width] for j in range(4)]
        down_grad = grad_sum(h0, back_rows, down_got)
        gate_w_grad = grad_sum(expert_in, g0, gate_got)
        up_got = jnp.concatenate([soon[1], swap_tensor(lower(up_sent))], axis=0)
        up_w_grad = grad_sum(expert_in, u0, up_got)
        mixed_other = swap_tensor(mixed)
        *normed_parts, gain_one_grad = share(back_all(*pre_grads))
        gain_sums = gain_side(gain_one_grad)
        input_half, input_other = input_side(*normed_parts)
    input_grad = both_halves(input_half, input_other)
    output = both_halves(
        hidden_state + mixed.astype(FULL), hidden_other + mixed_other.astype(FULL)
    )
    return (
        output,
        input_grad,
        gain_sums[0],
        w_sums[0],
        w_sums[1],
        w_sums[2],
        gain_sums[2],
        gain_sums[3],
        w_sums[3].T,
        gain_sums[1],
        gate_w_grad[None],
        up_w_grad[None],
        down_grad[None],
    )


def solution(mesh):
    return jax.shard_map(
        body,
        mesh=mesh,
        in_specs=(
            P("dp", None),
            P("dp"),
            P("dp", "tensor"),
            P("dp", "tensor"),
            P("dp", "tensor"),
            P("dp"),
            P("dp"),
            P("tensor", "dp"),
            P("dp"),
            P("dp", None, "tensor"),
            P("dp", None, "tensor"),
            P("dp", "tensor", None),
            P("dp", None),
            P("dp", None),
            P("dp", None),
            P("dp", None),
            P("dp", None),
        ),
        out_specs=(
            P("dp", None),
            P("dp", None),
            P("dp"),
            P("dp", "tensor"),
            P("dp", "tensor"),
            P("dp", "tensor"),
            P("dp"),
            P("dp"),
            P("tensor", "dp"),
            P("dp"),
            P("dp", None, "tensor"),
            P("dp", None, "tensor"),
            P("dp", "tensor", None),
        ),
        check_vma=False,
    )
```

```python
import jax
import jax.numpy as jnp
from jax import lax
from jax.experimental import pallas as pl
from jax.experimental.pallas import tpu as pltpu
from jax.sharding import PartitionSpec as P

HEADS = 16
HEAD = 128
GROUP = 8
PR_DEV = 128


EPSILON = 1e-05
VMEM = 60 * 1024 * 1024
LOW = jnp.bfloat16
FULL = jnp.float32


def swap_bit(block, axis, bit):
    count = lax.axis_size(axis)
    return lax.ppermute(block, axis, [(i, i ^ (1 << bit)) for i in range(count)])


def swap_tensor(block):
    return lax.ppermute(block, "tensor", [(0, 1), (1, 0)])


RING = (0, 2, 4, 6, 7, 5, 3, 1)
AHEAD = [
    (RING[p] * 2 + c, RING[(p + 1) % len(RING)] * 2 + c) for p in range(len(RING)) for c in range(2)
]
BEHIND = [(to, at) for at, to in AHEAD]
HOPS = (-1, 1, -2, 2, -3, 3, 0, 4)
LAYOUT = (
    *((-2, 0), (2, 0), (-1, 1), (1, 1)),
    *((-3, 0), (3, 0), (-2, 1), (2, 1)),
    *((4, 0), (4, 1), (-3, 1), (3, 1)),
    *((0, 0), (0, 1)),
    *((-1, 0), (1, 0)),
)


def ahead(block):
    return lax.ppermute(block, "dp", AHEAD)


def behind(block):
    return lax.ppermute(block, "dp", BEHIND)


def ring_chips(dp_index, hops):
    chip = dp_index // 2
    place = jnp.where(chip % 2 == 0, chip // 2, 7 - chip // 2)
    there = (place + jnp.array(hops, jnp.int32)) % len(RING)
    return jnp.where(there < 4, 2 * there, 2 * (7 - there) + 1)


def ring_blocks(dp_index):
    chips = ring_chips(dp_index, [hop for hop, _ in LAYOUT])
    return 2 * chips + (dp_index % 2 ^ jnp.array([cross for _, cross in LAYOUT], jnp.int32))


def add_low(*parts):
    total = parts[0].astype(FULL)
    for part in parts[1:]:
        total = total + part.astype(FULL)
    return total.astype(LOW)


def together(value, *others):
    return lax.optimization_barrier((value, *others))


def after(value, token):
    return lax.optimization_barrier((value, token))[0]


class Fillers:
    def __init__(self, *stages):
        self.stages = list(stages)

    def next(self, token):
        if self.stages:
            self.stages.pop(0)(lambda value: after(value, token))


def ring_sum(same, cross, fillers):
    both = {hop: add_low(same[hop], swap_bit(cross[hop], "dp", 0)) for hop in (4, 3, 2, 1, 0)}
    rows = both[0].shape[0]
    cut = rows // 2
    fillers.next(both[4])
    right, left = ahead(both[4][:cut]), behind(both[4][cut:])
    fillers.next(left)
    outward, inward = both[3][rows:], both[3][:rows]
    right = jnp.concatenate([add_low(outward[:cut], right), outward[cut:]], axis=0)
    left = jnp.concatenate([inward[:cut], add_low(inward[cut:], left)], axis=0)
    right, left = ahead(right), behind(left)
    fillers.next(left)
    for hop in (2, 1):
        right = ahead(add_low(both[hop][rows:], right))
        left = behind(add_low(both[hop][:rows], left))
        fillers.next(left)
    return both[0].astype(FULL) + right.astype(FULL) + left.astype(FULL)


def swap_in_turn(pieces, token):
    got = []
    for piece in pieces:
        got.append(swap_tensor(after(piece, token)))
        token = got[-1]
    return got


def cut_rows(array, count):
    rows = array.shape[0] // count
    return [array[i * rows : (i + 1) * rows] for i in range(count)]


def rms_norm(values, gain):
    return values * lax.rsqrt(jnp.mean(values * values, axis=-1, keepdims=True) + EPSILON) * gain


def rope_tables(positions, head_size):
    half_size = head_size // 2
    inverse = 10000.0 ** (-(jnp.arange(half_size, dtype=FULL) * 2.0) / head_size)
    angles = positions.astype(FULL)[:, None] * inverse[None, :]
    cosine = jnp.concatenate([jnp.cos(angles), jnp.cos(angles)], axis=-1)
    sine = jnp.concatenate([jnp.sin(angles), jnp.sin(angles)], axis=-1)
    return (cosine, sine)


def cont_positions(segment_row, gap_row, prompt_length):
    order = jnp.arange(segment_row.shape[0], dtype=jnp.int32)
    same = segment_row[:, None] == segment_row[None, :]
    earlier = order[None, :] < order[:, None]
    offset = jnp.sum((same & earlier).astype(jnp.int32), axis=1)
    labels = jnp.arange(gap_row.shape[0], dtype=jnp.int32)
    shifted = jnp.sum(
        jnp.where(segment_row[:, None] == labels[None, :], gap_row[None, :], 0), axis=1
    )
    return prompt_length + shifted + offset


def dot_nn(left, right):
    return jnp.dot(left, right, preferred_element_type=FULL)


def dot_tn(left, right):
    return lax.dot_general(left, right, (((0,), (0,)), ((), ())), preferred_element_type=FULL)


def dot_nt(left, right):
    return lax.dot_general(left, right, (((1,), (1,)), ((), ())), preferred_element_type=FULL)


def collect_prompt(own, first, second):
    near, far = swap_bit(own, "dp", 1), swap_bit(own, "dp", 2)
    last = swap_bit(near if first == 1 else far, "dp", second)
    blocks = []
    for block in (own, near, far, last):
        blocks += [block, swap_bit(block, "dp", 0)]
    return blocks[1:]


SMALL = pl.CostEstimate(flops=1, bytes_accessed=1, transcendentals=0)


def merge_kernel(even_ref, *refs):
    got, (keys_ref, values_ref, far_ref, near_ref) = refs[:3], refs[3:]
    near, far, last = 0, 1, 2
    add = lambda j, which: add_low(even_ref[j, which], got[j][which])
    keys_ref[0], keys_ref[1] = add(near, 0), add(last, 0)
    values_ref[0], values_ref[1] = add(far, 1), add(last, 1)
    far_ref[...], near_ref[...] = add(far, 0), add(near, 1)


def return_prompt(odd, even):
    got = [swap_bit(block, "dp", 0) for block in odd]
    one = jax.ShapeDtypeStruct(even.shape[2:], LOW)
    two = jax.ShapeDtypeStruct(even.shape[1:], LOW)
    keys, values, far, near = pl.pallas_call(
        merge_kernel, out_shape=[two, two, one, one], cost_estimate=SMALL
    )(even, *got[1:])
    keys, values = swap_bit(keys, "dp", 1), swap_bit(values, "dp", 2)
    last_keys = swap_bit(add_low(far, keys[1]), "dp", 2)
    last_values = swap_bit(add_low(near, values[1]), "dp", 1)
    return got[0], keys, values, last_keys, last_values


def turn(values):
    return pltpu.roll(values, HEAD // 2, 1)


def rope_kernel(pre_ref, gain_ref, scale_ref, cos_ref, sin_ref, out_ref):
    scale, cosine, sine = scale_ref[...], cos_ref[...], sin_ref[...]
    for at in range(0, pre_ref.shape[1], HEAD):
        span = slice(at, at + HEAD)
        normed = pre_ref[:, span] * scale * gain_ref[:, span]
        out_ref[:, span] = (normed * cosine + turn(normed) * sine).astype(LOW)


def rope_pass(flat, gain, scale, cosine, sine):
    rows, width = flat.shape
    part = width // 2
    wide = lambda rows: pl.BlockSpec((rows, part), lambda h: (0, h))
    return pl.pallas_call(
        rope_kernel,
        grid=(2,),
        in_specs=[wide(rows), wide(1)] + [kept_spec(a) for a in (scale, cosine, sine)],
        out_specs=wide(rows),
        out_shape=jax.ShapeDtypeStruct((rows, width), LOW),
    )(flat, gain, scale, cosine, sine)


PAIR = 2


def head_spec(rows):
    return pl.BlockSpec((rows, PAIR * HEAD), lambda h: (0, h))


def kept_spec(array):
    zeros = (0,) * array.ndim
    return pl.BlockSpec(array.shape, lambda h: zeros, pipeline_mode=pl.Buffered(1))


def all_keys(own_ref, pieces, span):
    return jnp.concatenate(
        [own_ref[:PR_DEV, span]] + [p[:, span] for p in pieces] + [own_ref[PR_DEV:, span]], axis=0
    )


def turned_query(flat_ref, gain_ref, scale, cosine, sine, span):
    normed = flat_ref[:, span] * scale * gain_ref[:, span]
    return (normed * cosine + turn(normed) * sine).astype(LOW)


def softmax_rows(query, keys, bias):
    scores = dot_nt(query, keys) * HEAD ** (-0.5) + bias
    weights = jnp.exp(scores - jnp.max(scores, axis=1, keepdims=True))
    return weights * (1.0 / jnp.sum(weights, axis=1, keepdims=True))


PIECES = GROUP - 1


def attend_kernel(flat_ref, gain_ref, scale_ref, cos_ref, sin_ref, bias_ref, k_ref, v_ref, *refs):
    out_ref = refs[-1]
    bias = bias_ref[...].astype(FULL)
    scale, cosine, sine = scale_ref[...], cos_ref[...], sin_ref[...]
    for at in range(0, PAIR * HEAD, HEAD):
        span = slice(at, at + HEAD)
        query = turned_query(flat_ref, gain_ref, scale, cosine, sine, span)
        probs = softmax_rows(query, all_keys(k_ref, refs[:PIECES], span), bias)
        values = all_keys(v_ref, refs[PIECES : 2 * PIECES], span)
        out_ref[:, span] = dot_nn(probs.astype(LOW), values).astype(LOW)


def attend_specs(rows, scale, cosine, sine, bias):
    return (
        [head_spec(rows), head_spec(1)]
        + [kept_spec(a) for a in (scale, cosine, sine, bias)]
        + [head_spec(rows)] * 2
        + [head_spec(PR_DEV)] * (2 * PIECES)
    )


def attend(flat, gain, scale, cosine, sine, bias, keys, values, pieces):
    rows, width = flat.shape
    return pl.pallas_call(
        attend_kernel,
        grid=(width // HEAD // PAIR,),
        in_specs=attend_specs(rows, scale, cosine, sine, bias),
        out_specs=head_spec(rows),
        out_shape=jax.ShapeDtypeStruct((rows, width), LOW),
        compiler_params=pltpu.CompilerParams(vmem_limit_bytes=VMEM),
    )(flat, gain, scale, cosine, sine, bias, keys, values, *pieces)


def norm_parts(step, at, grad, flat_ref, gain_ref, scale_ref, inner_ref, gain_grad_ref):
    span = slice(at, at + HEAD)
    product = flat_ref[:, span] * grad
    inner = jnp.sum(product * gain_ref[:, span], axis=1, keepdims=True)
    gain_grad_ref[:, span] = jnp.sum(product * scale_ref[...], axis=0, keepdims=True)
    if at:
        inner_ref[...] += inner
    else:
        inner_ref[...] = jnp.where(step == 0, 0.0, inner_ref[...]) + inner


def attend_back_kernel(
    flat_ref, gain_ref, scale_ref, cos_ref, sin_ref, bias_ref, k_ref, v_ref, *refs
):
    back_ref = refs[2 * PIECES]
    qg_ref, inner_ref, gain_grad_ref, kg_ref, vg_ref, even_ref = refs[2 * PIECES + 1 : -4]
    odd_refs = refs[-4:]
    step = pl.program_id(0)
    bias = bias_ref[...].astype(FULL)
    scale, cosine, sine = scale_ref[...], cos_ref[...], sin_ref[...]
    prompt = PR_DEV * GROUP
    for at in range(0, PAIR * HEAD, HEAD):
        span = slice(at, at + HEAD)
        query = turned_query(flat_ref, gain_ref, scale, cosine, sine, span)
        back = back_ref[:, span]
        keys = all_keys(k_ref, refs[:PIECES], span)
        values = all_keys(v_ref, refs[PIECES : 2 * PIECES], span)
        probs = softmax_rows(query, keys, bias)
        prob_grad = dot_nt(back, values)
        value_grad = dot_tn(probs.astype(LOW), back)
        row_dot = jnp.sum(probs * prob_grad, axis=1, keepdims=True)
        score_grad = (probs * (prob_grad - row_dot)).astype(LOW)
        query_grad = dot_nn(score_grad, keys) * HEAD ** (-0.5)
        key_grad = dot_tn(score_grad, query) * HEAD ** (-0.5)
        query_grad = query_grad * cosine - turn(query_grad) * sine
        qg_ref[:, span] = query_grad
        norm_parts(step, at, query_grad, flat_ref, gain_ref, scale_ref, inner_ref, gain_grad_ref)
        for which, grad, own_ref in ((0, key_grad, kg_ref), (1, value_grad, vg_ref)):
            own_ref[:PR_DEV, span] = grad[:PR_DEV]
            own_ref[PR_DEV:, span] = grad[prompt:]
            for j in range(1, GROUP):
                to = odd_refs[j // 2] if j % 2 else even_ref.at[j // 2 - 1]
                to[which, :, span] = grad[j * PR_DEV : (j + 1) * PR_DEV].astype(LOW)


def attend_back(flat, gain, scale, cosine, sine, bias, keys, values, pieces, back):
    rows, width = flat.shape
    wide = jax.ShapeDtypeStruct((rows, width), FULL)
    both = pl.BlockSpec((3, 2, PR_DEV, PAIR * HEAD), lambda h: (0, 0, 0, h))
    return pl.pallas_call(
        attend_back_kernel,
        grid=(width // HEAD // PAIR,),
        in_specs=attend_specs(rows, scale, cosine, sine, bias) + [head_spec(rows)],
        out_specs=[
            head_spec(rows),
            pl.BlockSpec((rows, 1), lambda h: (0, 0)),
            head_spec(1),
            head_spec(rows),
            head_spec(rows),
            both,
        ]
        + [pl.BlockSpec((2, PR_DEV, PAIR * HEAD), lambda h: (0, 0, h))] * 4,
        out_shape=[
            wide,
            jax.ShapeDtypeStruct((rows, 1), FULL),
            jax.ShapeDtypeStruct((1, width), FULL),
            wide,
            wide,
            jax.ShapeDtypeStruct((3, 2, PR_DEV, width), LOW),
        ]
        + [jax.ShapeDtypeStruct((2, PR_DEV, width), LOW)] * 4,
        compiler_params=pltpu.CompilerParams(vmem_limit_bytes=VMEM),
        cost_estimate=pl.CostEstimate(
            flops=20 * 10**9, bytes_accessed=40 * 10**6, transcendentals=4 * 10**6
        ),
    )(flat, gain, scale, cosine, sine, bias, keys, values, *pieces, back)


def key_back_kernel(*refs):
    kg_ref, vg_ref, flat_ref, gain_ref, scale_ref, cos_ref, sin_ref = refs[:7]
    got, keys, values, last_keys, last_values = refs[7:12]
    out_ref, inner_ref, gain_grad_ref, value_ref = refs[12:]
    step = pl.program_id(0)
    for at in range(0, PAIR * HEAD, HEAD):
        span = slice(at, at + HEAD)
        grads = []
        for which, own_ref, near, last in ((0, kg_ref, keys, last_keys), (1, vg_ref, values, last_values)):
            first = own_ref[:PR_DEV, span] + got[which, :, span].astype(FULL)
            first = first + near[0, :, span].astype(FULL) + last[:, span].astype(FULL)
            grads.append(jnp.concatenate([first, own_ref[PR_DEV:, span]], axis=0))
        key_grad = grads[0] * cos_ref[...] - turn(grads[0]) * sin_ref[...]
        out_ref[:, span] = key_grad
        norm_parts(step, at, key_grad, flat_ref, gain_ref, scale_ref, inner_ref, gain_grad_ref)
        value_ref[:, span] = grads[1].astype(LOW)


def key_back(key_grad, value_grad, flat, gain, scale, cosine, sine, returned):
    rows, width = flat.shape
    columns = PAIR * HEAD
    return pl.pallas_call(
        key_back_kernel,
        grid=(width // columns,),
        in_specs=[head_spec(rows)] * 3
        + [head_spec(1)]
        + [kept_spec(a) for a in (scale, cosine, sine)]
        + [pl.BlockSpec((2, PR_DEV, columns), lambda h: (0, 0, h))]
        + [pl.BlockSpec((1, PR_DEV, columns), lambda h: (0, 0, h))] * 2
        + [head_spec(PR_DEV)] * 2,
        out_specs=[
            head_spec(rows),
            pl.BlockSpec((rows, 1), lambda h: (0, 0)),
            head_spec(1),
            head_spec(rows),
        ],
        out_shape=[
            jax.ShapeDtypeStruct((rows, width), FULL),
            jax.ShapeDtypeStruct((rows, 1), FULL),
            jax.ShapeDtypeStruct((1, width), FULL),
            jax.ShapeDtypeStruct((rows, width), LOW),
        ],
        cost_estimate=SMALL,
    )(key_grad, value_grad, flat, gain, scale, cosine, sine, *returned)


def pack_kernel(query, key, value, out, rest, packed):
    at = 0
    for ref in (query, key, value):
        packed[at : at + ref.shape[0]] = ref[...]
        at += ref.shape[0]
    packed[at : at + out.shape[1]] = out[...].T
    packed[at + out.shape[1] :] = rest[...]


def pack_weights(w_query, w_key, w_value, w_out, rest):
    rows = 4 * w_query.shape[0] + rest.shape[0]
    return pl.pallas_call(
        pack_kernel, out_shape=jax.ShapeDtypeStruct((rows, w_query.shape[1]), LOW)
    )(w_query, w_key, w_value, w_out, rest)


def unpack_kernel(first, blocks_ref, packed, out, held, sems):
    width = packed.shape[2]
    parts = out.shape[1] // width
    rows = (packed.shape[1] - first) // parts
    count = packed.shape[0]
    place = lambda i: pl.ds(i * rows, rows)
    loads = [
        pltpu.make_async_copy(
            packed.at[blocks_ref[i], pl.ds(first + j * rows, rows)],
            held.at[place(i), pl.ds(j * width, width)],
            sems.at[i * parts + j],
        )
        for i in range(count)
        for j in range(parts)
    ]
    stores = [
        pltpu.make_async_copy(held.at[place(i)], out.at[place(i)], sems.at[count * parts + i])
        for i in range(count)
    ]
    for one in loads:
        one.start()
    for i, store in enumerate(stores):
        for j in range(parts):
            loads[i * parts + j].wait()
        store.start()
    for store in stores:
        store.wait()


def unpack_rows(packed, blocks, first, width):
    count = packed.shape[0]
    parts = width // packed.shape[2]
    rows = (packed.shape[1] - first) // parts
    return pl.pallas_call(
        lambda *refs: unpack_kernel(first, *refs),
        in_specs=[pl.BlockSpec(memory_space=pltpu.SMEM), pl.BlockSpec(memory_space=pl.ANY)],
        out_specs=pl.BlockSpec(memory_space=pl.ANY),
        out_shape=jax.ShapeDtypeStruct((count * rows, width), LOW),
        scratch_shapes=[
            pltpu.VMEM((count * rows, width), LOW),
            pltpu.SemaphoreType.DMA((count * parts + count,)),
        ],
        compiler_params=pltpu.CompilerParams(vmem_limit_bytes=VMEM),
    )(blocks, packed)


def pack_specs(gathered, places, steps, at):
    count, width = gathered.shape[0] // steps, gathered.shape[2]
    block = at
    return [
        pl.BlockSpec((count, block, width), lambda i, place=place: (i, place, 0))
        for place in places
    ]


def project_kernel(mats, roundings, rows_ref, *refs):
    mat_refs, out_refs, totals = refs[:mats], refs[mats : 2 * mats], refs[2 * mats :]
    step = pl.program_id(0)
    rows = rows_ref[...]
    for mat, out, total, rounding in zip(mat_refs, out_refs, totals, roundings):
        flat = mat[...].reshape(-1, mat.shape[2])
        part = dot_nn(rows, flat)

        @pl.when(step == 0)
        def _():
            total[...] = part

        @pl.when(step > 0)
        def _():
            total[...] += part

        @pl.when(step == pl.num_programs(0) - 1)
        def _():
            out[...] = total[...].astype(rounding)


def project(rows, gathered, block, places, roundings):
    count, width = rows.shape
    columns = gathered.shape[2]
    steps = 4
    outs = [jax.ShapeDtypeStruct((count, columns), rounding) for rounding in roundings]
    return pl.pallas_call(
        lambda *refs: project_kernel(len(places), roundings, *refs),
        grid=(steps,),
        in_specs=[pl.BlockSpec((count, width // steps), lambda i: (0, i))]
        + pack_specs(gathered, places, steps, block),
        out_specs=[pl.BlockSpec((count, columns), lambda i: (0, 0)) for _ in outs],
        out_shape=outs,
        scratch_shapes=[pltpu.VMEM((count, columns), FULL)] * len(outs),
        compiler_params=pltpu.CompilerParams(vmem_limit_bytes=VMEM),
        cost_estimate=pl.CostEstimate(
            flops=2 * count * width * columns * len(places),
            bytes_accessed=2 * width * columns * len(places) + 8 * count * columns,
            transcendentals=0,
        ),
    )(rows, *[gathered] * len(places))


def project_back_kernel(mats, *refs):
    out = refs[-1]
    total = None
    for rows_ref, mat in zip(refs[:mats], refs[mats:-1]):
        part = dot_nt(rows_ref[...], mat[...].reshape(-1, mat.shape[2]))
        total = part if total is None else total + part
    out[...] = total


def project_back(rows, gathered, block, places):
    count, columns = rows[0].shape
    width = gathered.shape[0] * block
    steps = 4
    fixed = pl.BlockSpec((count, columns), lambda i: (0, 0), pipeline_mode=pl.Buffered(1))
    return pl.pallas_call(
        lambda *refs: project_back_kernel(len(places), *refs),
        grid=(steps,),
        in_specs=[fixed] * len(rows) + pack_specs(gathered, places, steps, block),
        out_specs=pl.BlockSpec((count, width // steps), lambda i: (0, i)),
        out_shape=jax.ShapeDtypeStruct((count, width), FULL),
        compiler_params=pltpu.CompilerParams(vmem_limit_bytes=VMEM),
        cost_estimate=pl.CostEstimate(
            flops=2 * count * width * columns * len(places),
            bytes_accessed=2 * width * columns * len(places) + 4 * count * width,
            transcendentals=0,
        ),
    )(*rows, *[gathered] * len(places))


def pre_kernel(core_ref, *refs):
    inputs, outs = refs[:11], refs[11:]
    step = pl.program_id(0)
    columns = inputs[0].shape[1]
    parts = []
    for flat, grad, gain, scale, inner in (inputs[:5], inputs[5:10]):
        scaled = scale[...]
        mean = inner[...] * (1.0 / (HEADS * HEAD))
        parts.append(
            (
                scaled * gain[...] * grad[...] - flat[...] * (scaled * scaled * scaled) * mean
            ).astype(LOW)
        )
    outs[0][...], outs[1][...] = parts

    @pl.when(step != core_ref[0])
    def _():
        for j, part in enumerate((*parts, inputs[10][...])):
            outs[2][:, j * columns : (j + 1) * columns] = part


def pre_grads_pass(core, query, key, value):
    rows, width = value.shape
    columns = width // 2
    half = lambda rows: pl.BlockSpec((rows, columns), lambda h: (0, h))
    side = [half(rows), half(rows), half(1)] + [pl.BlockSpec((rows, 1), lambda h: (0, 0))] * 2
    return pl.pallas_call(
        pre_kernel,
        grid=(2,),
        in_specs=[pl.BlockSpec(memory_space=pltpu.SMEM)] + side + side + [half(rows)],
        out_specs=[half(rows), half(rows), pl.BlockSpec((rows, 3 * columns), lambda h: (0, 0))],
        out_shape=[jax.ShapeDtypeStruct((rows, width), LOW)] * 2
        + [jax.ShapeDtypeStruct((rows, 3 * columns), LOW)],
    )(core, *query, *key, value)


def weight_kernel(chip_ref, core_ref, *refs):
    normed, normed_got, back, back_got, query, key, value, got, context, context_got = refs[:10]
    out_ref, right_ref, left_ref, pre_both, context_both = refs[10:]
    rows, columns = query.shape

    @pl.when(pl.program_id(0) == 0)
    def _():
        for j, part in enumerate((query, key, value)):
            pre_both[:rows, j * columns : (j + 1) * columns] = part[...]
        pre_both[rows:] = got[...]
        context_both[:rows] = context[...]
        context_both[rows:] = context_got[...]

    left = jnp.concatenate([normed[...], normed_got[...]], axis=0)
    out_ref[0, :, : 3 * columns] = dot_tn(left, pre_both[...]).astype(LOW)
    left = jnp.concatenate([back[...], back_got[...]], axis=0)
    out_ref[0, :, 3 * columns :] = dot_tn(left, context_both[...]).astype(LOW)

    @pl.when(pl.program_id(0) == HOPS.index(4))
    def _():
        right_ref[...] = out_ref[0, :, : 2 * columns]
        left_ref[...] = out_ref[0, :, 2 * columns :]


def weight_grads(chips, core, normed, back, pre_grads, got, context, context_got):
    rows, width = normed[0].shape
    columns = context_got.shape[1]
    count = chips.shape[0]
    block = width // count
    tall = pl.BlockSpec((rows, block), lambda i, chip, core: (0, chip[i]))
    mine = pl.BlockSpec((rows, columns), lambda i, chip, core: (0, core[0]))
    fixed = lambda a: pl.BlockSpec(a.shape, lambda i, chip, core: (0, 0))
    return pl.pallas_call(
        weight_kernel,
        grid_spec=pltpu.PrefetchScalarGridSpec(
            num_scalar_prefetch=2,
            grid=(count,),
            in_specs=[tall] * 4 + [mine] * 3 + [fixed(got), mine, fixed(context_got)],
            out_specs=[pl.BlockSpec((1, block, 4 * columns), lambda i, chip, core: (i, 0, 0))]
            + [pl.BlockSpec((block, 2 * columns), lambda i, chip, core: (0, 0))] * 2,
            scratch_shapes=[
                pltpu.VMEM((2 * rows, 3 * columns), LOW),
                pltpu.VMEM((2 * rows, columns), LOW),
            ],
        ),
        out_shape=[jax.ShapeDtypeStruct((count, block, 4 * columns), LOW)]
        + [jax.ShapeDtypeStruct((block, 2 * columns), LOW)] * 2,
        compiler_params=pltpu.CompilerParams(vmem_limit_bytes=VMEM),
        cost_estimate=pl.CostEstimate(
            flops=16 * rows * width * columns,
            bytes_accessed=2 * (4 * rows * width + 8 * rows * columns + 4 * width * columns),
            transcendentals=0,
        ),
    )(chips, core, *normed, *back, *pre_grads, got, context, context_got)


def ring_weights(blocks, right, left, fillers):
    part = lambda hop: blocks[HOPS.index(hop)]
    cut = blocks.shape[2] // 2
    right, left = ahead(right), behind(left)
    fillers.next(left)
    outward, inward = part(3), part(-3)
    right = jnp.concatenate([add_low(outward[:, :cut], right), outward[:, cut:]], axis=1)
    left = jnp.concatenate([inward[:, :cut], add_low(inward[:, cut:], left)], axis=1)
    right, left = ahead(right), behind(left)
    fillers.next(left)
    token = left
    for hop in (2, 1):
        right, left = ahead(add_low(part(hop), right)), behind(add_low(part(-hop), left))
        fillers.next(left)
        token = left if hop == 2 else token
    return part(0).astype(FULL) + right.astype(FULL) + left.astype(FULL), token


def expert_kernel(
    rows_ref, back_ref, gate_ref, wg0, wg1, wu0, wu1, wd0, wd1, grad_ref, h0, h1, g0, g1, u0, u1
):
    rows = rows_ref[...]
    back = back_ref[...]
    gate = gate_ref[...]
    total = None
    for wg, wu, wd, h, g, u in ((wg0, wu0, wd0, h0, g0, u0), (wg1, wu1, wd1, h1, g1, u1)):
        gate_pre = dot_nn(rows, wg[...])
        up_pre = dot_nn(rows, wu[...])
        hidden_grad = gate * dot_nt(back, wd[...])
        sig = 1.0 / (1.0 + jnp.exp(-gate_pre))
        act = gate_pre * sig
        h[...] = (gate * (act * up_pre)).astype(LOW)
        gate_grad = (hidden_grad * up_pre * (sig * (1.0 + gate_pre * (1.0 - sig)))).astype(LOW)
        up_grad = (hidden_grad * act).astype(LOW)
        g[...] = gate_grad
        u[...] = up_grad
        part = dot_nt(gate_grad, wg[...]) + dot_nt(up_grad, wu[...])
        total = part if total is None else total + part
    grad_ref[...] = total.astype(LOW)


def expert_pass(rows, back, gate, gate_mats, up_mats, down_mats):
    count, width = rows.shape
    hidden = gate_mats[0].shape[1]
    tile = 256
    whole = lambda array: pl.BlockSpec(
        array.shape, lambda i: (0, 0), pipeline_mode=pl.Buffered(1)
    )
    tall = lambda columns: pl.BlockSpec((tile, columns), lambda i: (i, 0))
    mats = [*gate_mats, *up_mats, *down_mats]
    flops = 2 * 5 * count * width * hidden * 2
    return pl.pallas_call(
        expert_kernel,
        grid=(count // tile,),
        in_specs=[tall(width), tall(width), tall(1)] + [whole(m) for m in mats],
        out_specs=[tall(width)] + [tall(hidden)] * 6,
        out_shape=[jax.ShapeDtypeStruct((count, width), LOW)]
        + [jax.ShapeDtypeStruct((count, hidden), LOW)] * 6,
        compiler_params=pltpu.CompilerParams(vmem_limit_bytes=VMEM),
        cost_estimate=pl.CostEstimate(
            flops=flops,
            bytes_accessed=2 * (3 * count * width + 6 * count * hidden + 6 * width * hidden),
            transcendentals=2 * count * hidden,
        ),
    )(rows, back, gate, *mats)


def chunk_kernel(pieces, held, at, splits, gate_ref, *refs):
    piece_refs, refs = refs[:pieces], refs[pieces:]
    back_ref, mats, refs = refs[0], refs[1:7], refs[7 + held :]
    grad_outs, refs = refs[: len(splits)], refs[len(splits) :]
    rows_out, outs = refs[0], refs[1:7]
    rows, back, wide, wd, hidden, both_grads, grads, sems = refs[7:]
    count = rows.shape[0]
    part = wd.shape[1]
    slab = wide.shape[0] // 4
    across = lambda k, half: pl.ds((2 * k + half) * part, part)
    place = pl.ds(at * count, count)
    copy = pltpu.make_async_copy
    load_rows, start = [], 0
    for piece in piece_refs:
        span = pl.ds(start, piece.shape[0])
        load_rows.append(copy(piece, rows.at[span], sems.at[len(load_rows)]))
        start += piece.shape[0]
    load_back = copy(back_ref.at[place], back, sems.at[6])
    loads = []
    for half in range(2):
        places = [wide.at[:, across(0, half)], wide.at[:, across(1, half)], wd.at[half]]
        loads.append(
            [copy(mats[2 * k + half], to, sems.at[7 + 3 * half + k]) for k, to in enumerate(places)]
        )
    for one in load_rows + loads[0][:2] + [load_back] + loads[0][2:] + loads[1]:
        one.start()
    gate = gate_ref[...]
    for one in load_rows:
        one.wait()
    stores = [copy(rows, rows_out.at[place], sems.at[13])]
    stores[0].start()
    for half in range(2):
        columns = pl.ds(half * part, part)
        loads[half][0].wait()
        gate_pre = dot_nn(rows[...], wide[:, across(0, half)])
        loads[half][1].wait()
        up_pre = dot_nn(rows[...], wide[:, across(1, half)])
        if half == 0:
            load_back.wait()
        loads[half][2].wait()
        hidden_grad = gate * dot_nt(back[...], wd[half])
        sig = 1.0 / (1.0 + jnp.exp(-gate_pre))
        act = gate_pre * sig
        hidden[:, columns] = (gate * (act * up_pre)).astype(LOW)
        both_grads[:, across(0, half)] = (
            hidden_grad * up_pre * (sig * (1.0 + gate_pre * (1.0 - sig)))
        ).astype(LOW)
        both_grads[:, across(1, half)] = (hidden_grad * act).astype(LOW)
    for half in range(2):
        held_in = (
            hidden.at[:, pl.ds(half * part, part)],
            both_grads.at[:, across(0, half)],
            both_grads.at[:, across(1, half)],
        )
        for k, source in enumerate(held_in):
            stores.append(copy(source, outs[2 * k + half].at[place], sems.at[14 + 3 * half + k]))
            stores[-1].start()

    @pl.loop(0, 4)
    def _(j):
        span = pl.ds(pl.multiple_of(j * slab, slab), slab)
        grads[:, span] = dot_nt(both_grads[...], wide[span]).astype(LOW)

    start = 0
    for k, (split, to) in enumerate(zip(splits, grad_outs)):
        stores.append(copy(grads.at[pl.ds(start, split)], to, sems.at[20 + k]))
        stores[-1].start()
        start += split
    for one in stores:
        one.wait()


def expert_chunk(pieces, back, gate, mats, at, held, splits):
    all_rows, width = back.shape
    part = mats[0].shape[1]
    hidden = 2 * part
    count = sum(piece.shape[0] for piece in pieces)
    anywhere = pl.BlockSpec(memory_space=pl.ANY)
    held = [] if held is None else list(held)
    args = [gate, *pieces, back, *mats, *held]
    out = pl.pallas_call(
        lambda *refs: chunk_kernel(len(pieces), len(held), at, splits, *refs),
        grid=(1,),
        in_specs=[pl.BlockSpec((count, 1), lambda j: (at, 0))] + [anywhere] * (len(args) - 1),
        out_specs=[anywhere] * (len(splits) + 7),
        out_shape=[jax.ShapeDtypeStruct((split, width), LOW) for split in splits]
        + [jax.ShapeDtypeStruct((all_rows, width), LOW)]
        + [jax.ShapeDtypeStruct((all_rows, part), LOW)] * 6,
        scratch_shapes=[
            pltpu.VMEM((count, width), LOW),
            pltpu.VMEM((count, width), LOW),
            pltpu.VMEM((width, 2 * hidden), LOW),
            pltpu.VMEM((2, part, width), LOW),
            pltpu.VMEM((count, hidden), LOW),
            pltpu.VMEM((count, 2 * hidden), LOW),
            pltpu.VMEM((count, width), LOW),
            pltpu.SemaphoreType.DMA((23,)),
        ],
        input_output_aliases={
            len(args) - len(held) + k: len(splits) + k for k in range(len(held))
        },
        compiler_params=pltpu.CompilerParams(vmem_limit_bytes=VMEM),
        cost_estimate=pl.CostEstimate(
            flops=2 * 5 * count * width * hidden,
            bytes_accessed=2 * (4 * count * width + 3 * count * hidden + 3 * width * hidden),
            transcendentals=count * hidden,
        ),
    )(*args)
    return out[: len(splits)], out[len(splits) :]


def mixed_kernel(chip_ref, same_ref, cross_ref, core_ref, *refs):
    first_ref, second_ref, out_ref = refs[4:]
    rows = out_ref.shape[2]
    first, second = (
        jnp.concatenate([refs[k][...], refs[k + 1][...]], axis=0) for k in (0, 2)
    )
    result = (dot_nn(first, first_ref[...]) + dot_nn(second, second_ref[...])).astype(LOW)
    out_ref[0, core_ref[0]] = result[:rows]
    out_ref[0, 1 - core_ref[0]] = result[rows:]


def mixed_pass(h0, h1, down_mats, chips, core):
    count, columns = h0.shape
    width = down_mats[0].shape[1]
    rows = count // len(LAYOUT)
    places = [
        jnp.array([LAYOUT.index((hop, cross)) for hop in HOPS], jnp.int32) for cross in (0, 1)
    ]
    once = pl.Buffered(1)
    fixed = lambda m: pl.BlockSpec(m.shape, lambda i, *tables: (0, 0), pipeline_mode=once)
    block = lambda k: pl.BlockSpec((rows, columns), lambda i, *tables: (tables[k][i], 0))
    out = pl.pallas_call(
        mixed_kernel,
        grid_spec=pltpu.PrefetchScalarGridSpec(
            num_scalar_prefetch=4,
            grid=(len(HOPS),),
            in_specs=[block(1), block(2), block(1), block(2)] + [fixed(m) for m in down_mats],
            out_specs=pl.BlockSpec(
                (1, 2, rows, width), lambda i, chip, *tables: (chip[i], 0, 0, 0)
            ),
        ),
        out_shape=jax.ShapeDtypeStruct((len(HOPS), 2, rows, width), LOW),
        compiler_params=pltpu.CompilerParams(vmem_limit_bytes=VMEM),
        cost_estimate=pl.CostEstimate(
            flops=4 * count * columns * width,
            bytes_accessed=2 * (count * (2 * columns + width) + 2 * columns * width),
            transcendentals=0,
        ),
    )(chips, *places, core, h0, h0, h1, h1, *down_mats)
    return out.reshape(count, width)


def expert_ring(rows, back, gate, mats, waiting):
    size = rows.shape[0]
    cut = size // 2
    swap = lambda block: swap_bit(block, "dp", 0)
    chunk = lambda pieces, at, held, *splits: expert_chunk(
        pieces, back, gate, mats, at, held, splits
    )
    rows, pair = together(rows, swap(rows))
    left, right = ahead(rows), behind(rows)
    parts, crossed = cut_rows(waiting, 4), []
    same, cross = {}, {}
    cross_over = lambda token: crossed.append(swap_tensor(after(parts[len(crossed)], token)))
    cross_over(pair)
    (same[0], cross[0]), held = chunk([rows, pair], 6, None, size, size)
    left, right, same[0] = together(left, right, same[0])
    pieces, got = [left, right], [swap(left), swap(right)]
    left, right = ahead(left), behind(right)
    pieces[0], crossed[0] = together(pieces[0], crossed[0])
    cross_over(pieces[0])
    (same[1],), held = chunk(pieces, 7, held, 2 * size)
    left, right, same[1] = together(left, right, same[1])
    pieces, got = [left, right, *got], [swap(left), swap(right)]
    left, right = ahead(left), behind(right)
    pieces[0], crossed[1] = together(pieces[0], crossed[1])
    cross_over(pieces[0])
    (same[2], cross[1]), held = chunk(pieces, 0, held, 2 * size, 2 * size)
    left, right, same[2] = together(left, right, same[2])
    pieces, got = [left, right, *got], [swap(left), swap(right)]
    left, right = ahead(left[:cut]), behind(right[cut:])
    pieces[0], crossed[2] = together(pieces[0], crossed[2])
    cross_over(pieces[0])
    (same[3], cross[2]), held = chunk(pieces, 1, held, 2 * size, 2 * size)
    left, right, crossed[3], same[3] = together(left, right, crossed[3], same[3])
    pieces = [left, right, swap(left), swap(right), *got]
    (same[4], cross[4], cross[3]), held = chunk(pieces, 2, held, size, size, 2 * size)
    waiting = jnp.concatenate(crossed, axis=0)
    return same, cross, held, waiting


def body(
    inputs,
    attn_gain,
    w_query,
    w_key,
    w_value,
    query_gain,
    key_gain,
    w_out,
    moe_gain,
    w_gate,
    w_up,
    w_down,
    experts,
    gates,
    segments,
    gaps,
    cotangent,
):
    dp_count = lax.axis_size("dp")
    dp_index = lax.axis_index("dp")
    side = lax.axis_index("tensor")
    token_count, model_width = inputs.shape
    half_count = token_count // 2
    top_count = experts.shape[1]
    expert_count = w_gate.shape[0] * dp_count
    capacity = token_count * top_count * dp_count * 9 // (8 * expert_count)
    prompt_length = PR_DEV * GROUP
    column_total = HEADS * HEAD
    block = w_query.shape[0]
    local_width = w_query.shape[1]
    local_heads = local_width // HEAD

    def own_half(array):
        return lax.dynamic_slice_in_dim(array, side * half_count, half_count, axis=0)

    def other_half(array):
        return lax.dynamic_slice_in_dim(array, (1 - side) * half_count, half_count, axis=0)

    def both_halves(own, other):
        first = side == 0
        return jnp.concatenate(
            [jnp.where(first, own, other), jnp.where(first, other, own)], axis=0
        )

    gate_mats = (w_gate[0], swap_tensor(w_gate[0]))
    up_mats = (w_up[0], swap_tensor(w_up[0]))

    ring = dp_count == 2 * len(RING)

    gates_high = gates.astype(LOW)
    gates_low = (gates - gates_high.astype(FULL)).astype(LOW)
    routing = jnp.concatenate([experts.astype(LOW).T, gates_high.T, gates_low.T], axis=1)
    routing = jnp.pad(routing, ((0, 0), (0, local_width - 3 * token_count)))
    gains = jnp.concatenate([attn_gain, moe_gain, query_gain, key_gain])
    gains = jnp.pad(gains[None], ((0, 7), (0, local_width - 4 * block)))
    packed = pack_weights(
        w_query, w_key, w_value, w_out, jnp.concatenate([gains, routing], axis=0)
    )
    gathered = lax.all_gather(packed, "dp", axis=0, tiled=False)
    cotangent_half = own_half(cotangent)
    gathered_back = lax.all_gather(cotangent_half.astype(LOW), "dp", axis=0, tiled=False)
    core = dp_index % 2
    tokens_f = inputs.astype(FULL)
    prompt_pos = dp_index % GROUP * PR_DEV + jnp.arange(PR_DEV, dtype=jnp.int32)
    later_pos = cont_positions(segments[0], gaps[0], prompt_length)
    positions = jnp.concatenate([prompt_pos, later_pos], axis=0)
    cosine, sine = rope_tables(positions, HEAD)
    sine = jnp.where(jnp.arange(HEAD) < HEAD // 2, -sine, sine)
    prompt_query = jnp.arange(token_count, dtype=jnp.int32) < PR_DEV
    prompt_at = jnp.arange(prompt_length, dtype=jnp.int32)
    prompt_keypos = ((dp_index % GROUP) ^ (prompt_at // PR_DEV)) * PR_DEV + prompt_at % PR_DEV
    allowed_prompt = (~prompt_query)[:, None] | (prompt_keypos[None, :] <= positions[:, None])
    query_segment = jnp.concatenate([jnp.full((PR_DEV,), -1, jnp.int32), segments[0]], axis=0)
    allowed_cont = (query_segment[:, None] == segments[0][None, :]) & (
        later_pos[None, :] <= positions[:, None]
    )
    allowed = jnp.concatenate([allowed_prompt, allowed_cont], axis=1)
    bias = jnp.where(allowed, 0.0, -1e30).astype(LOW)
    gathered, cosine, sine, bias, *early = together(
        gathered, cosine, sine, bias, gate_mats[1], up_mats[1]
    )
    gate_mats, up_mats = (gate_mats[0], early[0]), (up_mats[0], early[1])
    rest = gathered[:, 4 * block : 4 * block + 16]
    gain_rows = rest[:, 0].astype(FULL)
    gain_one, gain_two, gain_q, gain_k = (
        gain_rows[:, j * block : (j + 1) * block].reshape(-1) for j in range(4)
    )
    gain_query_local = lax.dynamic_slice_in_dim(gain_q, side * local_width, local_width)
    gain_key_local = lax.dynamic_slice_in_dim(gain_k, side * local_width, local_width)

    names, *parts = (
        rest[:, 8:, j * token_count : (j + 1) * token_count] for j in range(3)
    )
    weights = parts[0].astype(FULL) + parts[1].astype(FULL)
    named = names == dp_index.astype(LOW)
    picked = jnp.sum(named.astype(FULL), axis=1)
    weight = jnp.sum(jnp.where(named, weights, 0.0), axis=1)
    order = jnp.arange(token_count, dtype=jnp.int32)
    earlier = (order[:, None] < order[None, :]).astype(LOW)
    within = dot_nn(picked.astype(LOW), earlier)
    per_row = jnp.sum(picked, axis=1)
    rows_order = jnp.arange(dp_count, dtype=jnp.int32)
    ahead = jnp.sum(
        jnp.where(rows_order[None, :] < rows_order[:, None], per_row[None, :], 0.0), axis=1
    )
    kept = (picked > 0.0) & (within + ahead[:, None] < capacity)
    weight = jnp.where(kept, weight, 0.0)
    weight = lax.dynamic_slice_in_dim(weight, side * half_count, half_count, axis=1)
    if ring:
        blocks, chips = ring_blocks(dp_index), ring_chips(dp_index, HOPS)
        weight = weight[blocks]
    weight = weight.reshape(-1, 1)

    normed_b = rms_norm(tokens_f, gain_one).astype(LOW)
    query_flat, key_flat, values_b = project(
        normed_b, gathered, block, (0, 1, 2), (FULL, FULL, LOW)
    )
    key_sq = jnp.sum(key_flat * key_flat, axis=1)
    key_sq, value_prompt = together(key_sq, values_b[:PR_DEV])
    value_pieces = collect_prompt(value_prompt, 1, 2)
    query_sq, key_sq = lax.psum(
        (jnp.sum(query_flat * query_flat, axis=1), key_sq), "tensor"
    )
    query_sq, down_mat = lax.optimization_barrier((query_sq, w_down[0]))
    down_mats = (down_mat, swap_tensor(down_mat))
    query_scale = lax.rsqrt(query_sq / column_total + EPSILON)[:, None]
    key_scale = lax.rsqrt(key_sq / column_total + EPSILON)[:, None]
    keys_b = rope_pass(key_flat, gain_key_local[None], key_scale, cosine, sine)
    pieces = (*collect_prompt(keys_b[:PR_DEV], 2, 1), *value_pieces)
    turned_by = (gain_query_local[None], query_scale, cosine, sine, bias)
    context_b = attend(query_flat, *turned_by, keys_b, values_b, pieces)
    attn_part = project_back([context_b], gathered, block, (3,))
    attn_part, late, weight = together(attn_part, down_mats[1], weight)
    down_mats = (down_mats[0], late)
    mats = (*gate_mats, *up_mats, *down_mats)
    attn_other = swap_tensor(other_half(attn_part).astype(LOW))
    gathered_back = after(gathered_back, attn_part)
    if ring:
        back_rows = unpack_rows(gathered_back, blocks, 0, model_width)
    else:
        back_rows = gathered_back.reshape(-1, model_width)
    attn_other, back_rows, weight = together(attn_other, back_rows, weight)
    hidden_state = own_half(tokens_f) + own_half(attn_part) + attn_other.astype(FULL)
    normed_two_b = rms_norm(hidden_state, gain_two).astype(LOW)

    low_tn = lambda left, right: dot_tn(left, right).astype(LOW)
    upper = lambda array: array[: array.shape[0] // 2]
    lower = lambda array: array[array.shape[0] // 2 :]
    if ring:
        same, cross, held, hidden_other = expert_ring(
            normed_two_b, back_rows, weight, mats, hidden_state
        )
        expert_in, h0, h1, g0, g1, u0, u1 = held
        late = {}

        def down_stage(gated):
            late["down"] = swap_tensor(low_tn(gated(h1), back_rows))

        def gate_stage(gated):
            late["gate"] = low_tn(gated(expert_in), g1)

        def up_stage(gated):
            late["up"] = low_tn(gated(expert_in), u1)

        def mixed_stage(gated):
            late["mixed"] = mixed_pass(gated(h0), h1, down_mats, chips, core[None])

        fillers = Fillers(down_stage, gate_stage, up_stage, mixed_stage)
        normed_two_grad = ring_sum(same, cross, fillers)
        gate_sent, up_sent, mixed_rows = late["gate"], late["up"], late["mixed"]
        down_got = late["down"]
    else:
        hidden_other = swap_tensor(hidden_state)
        expert_in = lax.all_gather(normed_two_b, "dp", axis=0, tiled=True)
        grad_rows, h0, h1, g0, g1, u0, u1 = expert_pass(
            expert_in, back_rows, weight, gate_mats, up_mats, down_mats
        )
        normed_two_grad = lax.psum_scatter(
            grad_rows, "dp", scatter_dimension=0, tiled=True
        ).astype(FULL)
        mixed_rows = (dot_nn(h0, down_mats[0]) + dot_nn(h1, down_mats[1])).astype(LOW)
        down_got = swap_tensor(low_tn(h1, back_rows))
        gate_sent = low_tn(expert_in, g1)
        up_sent = low_tn(expert_in, u1)
    gate_first = swap_tensor(upper(gate_sent))
    normed_two_grad, down_got, gate_first, mixed_rows, up_sent = together(
        normed_two_grad, down_got, gate_first, mixed_rows, up_sent
    )
    mixed = lax.psum_scatter(mixed_rows, "dp", scatter_dimension=0, tiled=True)

    unused_two, norm_two_back = jax.vjp(rms_norm, hidden_state, gain_two)
    state_part, gain_two_grad = norm_two_back(normed_two_grad)
    state_half = cotangent_half + state_part
    attn_grad_half = state_half.astype(LOW)
    attn_grad_b = both_halves(attn_grad_half, swap_tensor(attn_grad_half))
    attn_grad_b, gate_sent, up_sent = together(attn_grad_b, gate_sent, up_sent)
    (context_grad_b,) = project(attn_grad_b, gathered, block, (3,), (LOW,))
    soon = swap_in_turn([lower(gate_sent), upper(up_sent)], context_grad_b)
    if ring:
        pair = lambda own: (own, swap_bit(own, "dp", 0))
        columns = local_width // 2
        context_sent = lax.dynamic_slice_in_dim(context_b, (1 - core) * columns, columns, axis=1)
        normed_pair, attn_grad_pair = pair(normed_b), pair(attn_grad_b)
        context_got = swap_bit(context_sent, "dp", 0)
    query_normed_grad, query_inner, query_gain_part, key_grad, value_grad, even, *odd = attend_back(
        query_flat, *turned_by, keys_b, values_b, pieces, context_grad_b
    )
    returned = return_prompt(odd, even)
    if ring:
        key_grad, context_got, *pairs = together(
            key_grad, context_got, normed_pair[1], attn_grad_pair[1]
        )
        normed_pair, attn_grad_pair = (normed_b, pairs[0]), (attn_grad_b, pairs[1])
    key_normed_grad, key_inner, key_gain_part, value_pre_grad = key_back(
        key_grad, value_grad, key_flat, gain_key_local[None], key_scale, cosine, sine, returned
    )
    query_inner, *soon = together(query_inner, *soon)
    query_inner, key_inner = lax.psum(
        jnp.stack([query_inner[:, 0], key_inner[:, 0]], axis=0), "tensor"
    )
    query_pre_grad, key_pre_grad, pre_sent = pre_grads_pass(
        core[None],
        (
            query_flat,
            query_normed_grad,
            gain_query_local[None],
            query_scale,
            query_inner[:, None],
        ),
        (key_flat, key_normed_grad, gain_key_local[None], key_scale, key_inner[:, None]),
        value_pre_grad,
    )
    gate_got = jnp.concatenate([gate_first, soon[0]], axis=0)
    pre_grads = (query_pre_grad, key_pre_grad, value_pre_grad)
    grad_sum = lambda left, right, got: dot_tn(left, right) + got.astype(FULL)
    back_all = lambda *grads: project_back(grads, gathered, block, (0, 1, 2))

    wide = lambda part: lax.dynamic_update_slice_in_dim(
        jnp.zeros((column_total,), FULL), part, side * local_width, 0
    )

    def share(part):
        return own_half(part), swap_tensor(other_half(part).astype(LOW)), gain_part(part)

    def input_side(own, other):
        unused_one, norm_one_back = jax.vjp(
            lambda values: rms_norm(values, gain_one), own_half(tokens_f)
        )
        input_half = state_half + norm_one_back(own + other.astype(FULL))[0]
        return input_half, swap_tensor(input_half)

    def gain_part(part):
        return jnp.sum(part * rms_norm(tokens_f, 1.0), axis=0)

    def gain_side(gain_one_grad):
        grads = jnp.stack(
            [gain_one_grad, gain_two_grad, wide(query_gain_part[0]), wide(key_gain_part[0])]
        ).reshape(4, dp_count, block)
        grads = jnp.swapaxes(grads, 0, 1).reshape(dp_count, 1, 4 * block)
        sides = lax.axis_size("tensor")
        grads = jnp.broadcast_to(grads, (dp_count, sides, 4 * block))
        grads = grads.reshape(dp_count * sides, 4 * block)
        sums = lax.all_to_all(grads, ("dp", "tensor"), 0, 0, tiled=True)
        return jnp.sum(sums, axis=0).reshape(4, block)

    if ring:
        pre_got = swap_bit(pre_sent, "dp", 0)
        w_blocks, *far = weight_grads(
            chips,
            core[None],
            normed_pair,
            attn_grad_pair,
            pre_grads,
            pre_got,
            context_b,
            context_got,
        )
        w_blocks, mixed, *far = together(w_blocks, mixed, *far)
        up_got = jnp.concatenate(
            [soon[1], *swap_in_turn(cut_rows(lower(up_sent), 2), far[0])], axis=0
        )
        mixed_other = swap_tensor(mixed)
        late = {}

        def normed_stage(gated):
            late["normed"] = share(back_all(*[gated(grad) for grad in pre_grads]))

        def input_stage(gated):
            late["input"] = input_side(late["normed"][0], gated(late["normed"][1]))
            late["down"] = grad_sum(gated(h0), back_rows, down_got)

        def expert_stage(gated):
            late["gains"] = gain_side(gated(late["normed"][2]))
            late["gate"] = grad_sum(gated(expert_in), g0, gate_got)

        fillers = Fillers(normed_stage, input_stage, expert_stage)
        w_half, token = ring_weights(w_blocks, *far, fillers)
        input_half, input_other = late["input"]
        gain_sums = late["gains"]
        down_grad, gate_w_grad = late["down"], late["gate"]
        up_w_grad = grad_sum(after(expert_in, token), u0, up_got)
        own_w = lax.dynamic_slice_in_dim(w_half, core * block, block, axis=0)
        got_w = swap_bit(
            lax.dynamic_slice_in_dim(w_half, (1 - core) * block, block, axis=0), "dp", 0
        )
        left_w, right_w = jnp.where(core == 0, own_w, got_w), jnp.where(core == 0, got_w, own_w)
        w_sums = [
            jnp.concatenate([w[:, j * columns : (j + 1) * columns] for w in (left_w, right_w)], axis=1)
            for j in range(4)
        ]
        mixed_other = after(mixed_other, token)
    else:
        w_grads = jnp.concatenate(
            [low_tn(normed_b, g) for g in pre_grads] + [low_tn(attn_grad_b, context_b)], axis=1
        )
        w_sum = lax.psum_scatter(w_grads, "dp", scatter_dimension=0, tiled=True).astype(FULL)
        w_sums = [w_sum[:, j * local_width : (j + 1) * local_width] for j in range(4)]
        down_grad = grad_sum(h0, back_rows, down_got)
        gate_w_grad = grad_sum(expert_in, g0, gate_got)
        up_got = jnp.concatenate([soon[1], swap_tensor(lower(up_sent))], axis=0)
        up_w_grad = grad_sum(expert_in, u0, up_got)
        mixed_other = swap_tensor(mixed)
        *normed_parts, gain_one_grad = share(back_all(*pre_grads))
        gain_sums = gain_side(gain_one_grad)
        input_half, input_other = input_side(*normed_parts)
    input_grad = both_halves(input_half, input_other)
    output = both_halves(
        hidden_state + mixed.astype(FULL), hidden_other + mixed_other.astype(FULL)
    )
    return (
        output,
        input_grad,
        gain_sums[0],
        w_sums[0],
        w_sums[1],
        w_sums[2],
        gain_sums[2],
        gain_sums[3],
        w_sums[3].T,
        gain_sums[1],
        gate_w_grad[None],
        up_w_grad[None],
        down_grad[None],
    )


def solution(mesh):
    return jax.shard_map(
        body,
        mesh=mesh,
        in_specs=(
            P("dp", None),
            P("dp"),
            P("dp", "tensor"),
            P("dp", "tensor"),
            P("dp", "tensor"),
            P("dp"),
            P("dp"),
            P("tensor", "dp"),
            P("dp"),
            P("dp", None, "tensor"),
            P("dp", None, "tensor"),
            P("dp", "tensor", None),
            P("dp", None),
            P("dp", None),
            P("dp", None),
            P("dp", None),
            P("dp", None),
        ),
        out_specs=(
            P("dp", None),
            P("dp", None),
            P("dp"),
            P("dp", "tensor"),
            P("dp", "tensor"),
            P("dp", "tensor"),
            P("dp"),
            P("dp"),
            P("tensor", "dp"),
            P("dp"),
            P("dp", None, "tensor"),
            P("dp", None, "tensor"),
            P("dp", "tensor", None),
        ),
        check_vma=False,
    )
```

```python
import jax
import jax.numpy as jnp
from jax import lax
from jax.experimental import pallas as pl
from jax.experimental.pallas import tpu as pltpu
from jax.sharding import PartitionSpec as P

HEADS = 16
HEAD = 128
GROUP = 8
PR_DEV = 128


EPSILON = 1e-05
VMEM = 60 * 1024 * 1024
LOW = jnp.bfloat16
FULL = jnp.float32


def swap_bit(block, axis, bit):
    count = lax.axis_size(axis)
    return lax.ppermute(block, axis, [(i, i ^ (1 << bit)) for i in range(count)])


def swap_tensor(block):
    return lax.ppermute(block, "tensor", [(0, 1), (1, 0)])


RING = (0, 2, 4, 6, 7, 5, 3, 1)
AHEAD = [
    (RING[p] * 2 + c, RING[(p + 1) % len(RING)] * 2 + c) for p in range(len(RING)) for c in range(2)
]
BEHIND = [(to, at) for at, to in AHEAD]
HOPS = (-1, 1, -2, 2, -3, 3, 0, 4)
LAYOUT = (
    *((-2, 0), (2, 0), (-1, 1), (1, 1)),
    *((-3, 0), (3, 0), (-2, 1), (2, 1)),
    *((4, 0), (4, 1), (-3, 1), (3, 1)),
    *((0, 0), (0, 1)),
    *((-1, 0), (1, 0)),
)


def ahead(block):
    return lax.ppermute(block, "dp", AHEAD)


def behind(block):
    return lax.ppermute(block, "dp", BEHIND)


def ring_chips(dp_index, hops):
    chip = dp_index // 2
    place = jnp.where(chip % 2 == 0, chip // 2, 7 - chip // 2)
    there = (place + jnp.array(hops, jnp.int32)) % len(RING)
    return jnp.where(there < 4, 2 * there, 2 * (7 - there) + 1)


def ring_blocks(dp_index):
    chips = ring_chips(dp_index, [hop for hop, _ in LAYOUT])
    return 2 * chips + (dp_index % 2 ^ jnp.array([cross for _, cross in LAYOUT], jnp.int32))


def add_low(*parts):
    total = parts[0].astype(FULL)
    for part in parts[1:]:
        total = total + part.astype(FULL)
    return total.astype(LOW)


def together(value, *others):
    return lax.optimization_barrier((value, *others))


def after(value, token):
    return lax.optimization_barrier((value, token))[0]


class Fillers:
    def __init__(self, *stages):
        self.stages = list(stages)

    def next(self, token):
        if self.stages:
            self.stages.pop(0)(lambda value: after(value, token))


def ring_sum(same, cross, fillers):
    both = {hop: add_low(same[hop], swap_bit(cross[hop], "dp", 0)) for hop in (4, 3, 2, 1, 0)}
    rows = both[0].shape[0]
    cut = rows // 2
    fillers.next(both[4])
    right, left = ahead(both[4][:cut]), behind(both[4][cut:])
    fillers.next(left)
    outward, inward = both[3][rows:], both[3][:rows]
    right = jnp.concatenate([add_low(outward[:cut], right), outward[cut:]], axis=0)
    left = jnp.concatenate([inward[:cut], add_low(inward[cut:], left)], axis=0)
    right, left = ahead(right), behind(left)
    fillers.next(left)
    for hop in (2, 1):
        right = ahead(add_low(both[hop][rows:], right))
        left = behind(add_low(both[hop][:rows], left))
        fillers.next(left)
    return both[0].astype(FULL) + right.astype(FULL) + left.astype(FULL)


def swap_in_turn(pieces, token):
    got = []
    for piece in pieces:
        got.append(swap_tensor(after(piece, token)))
        token = got[-1]
    return got


def cut_rows(array, count):
    rows = array.shape[0] // count
    return [array[i * rows : (i + 1) * rows] for i in range(count)]


def rms_norm(values, gain):
    return values * lax.rsqrt(jnp.mean(values * values, axis=-1, keepdims=True) + EPSILON) * gain


def rope_tables(positions, head_size):
    half_size = head_size // 2
    inverse = 10000.0 ** (-(jnp.arange(half_size, dtype=FULL) * 2.0) / head_size)
    angles = positions.astype(FULL)[:, None] * inverse[None, :]
    cosine = jnp.concatenate([jnp.cos(angles), jnp.cos(angles)], axis=-1)
    sine = jnp.concatenate([jnp.sin(angles), jnp.sin(angles)], axis=-1)
    return (cosine, sine)


def cont_positions(segment_row, gap_row, prompt_length):
    order = jnp.arange(segment_row.shape[0], dtype=jnp.int32)
    same = segment_row[:, None] == segment_row[None, :]
    earlier = order[None, :] < order[:, None]
    offset = jnp.sum((same & earlier).astype(jnp.int32), axis=1)
    labels = jnp.arange(gap_row.shape[0], dtype=jnp.int32)
    shifted = jnp.sum(
        jnp.where(segment_row[:, None] == labels[None, :], gap_row[None, :], 0), axis=1
    )
    return prompt_length + shifted + offset


def dot_nn(left, right):
    return jnp.dot(left, right, preferred_element_type=FULL)


def dot_tn(left, right):
    return lax.dot_general(left, right, (((0,), (0,)), ((), ())), preferred_element_type=FULL)


def dot_nt(left, right):
    return lax.dot_general(left, right, (((1,), (1,)), ((), ())), preferred_element_type=FULL)


def collect_prompt(own, first, second):
    near, far = swap_bit(own, "dp", 1), swap_bit(own, "dp", 2)
    last = swap_bit(near if first == 1 else far, "dp", second)
    blocks = []
    for block in (own, near, far, last):
        blocks += [block, swap_bit(block, "dp", 0)]
    return blocks[1:]


SMALL = pl.CostEstimate(flops=1, bytes_accessed=1, transcendentals=0)


def merge_kernel(even_ref, *refs):
    got, (keys_ref, values_ref, far_ref, near_ref) = refs[:3], refs[3:]
    near, far, last = 0, 1, 2
    add = lambda j, which: add_low(even_ref[j, which], got[j][which])
    keys_ref[0], keys_ref[1] = add(near, 0), add(last, 0)
    values_ref[0], values_ref[1] = add(far, 1), add(last, 1)
    far_ref[...], near_ref[...] = add(far, 0), add(near, 1)


def return_prompt(odd, even):
    got = [swap_bit(block, "dp", 0) for block in odd]
    one = jax.ShapeDtypeStruct(even.shape[2:], LOW)
    two = jax.ShapeDtypeStruct(even.shape[1:], LOW)
    keys, values, far, near = pl.pallas_call(
        merge_kernel, out_shape=[two, two, one, one], cost_estimate=SMALL
    )(even, *got[1:])
    keys, values = swap_bit(keys, "dp", 1), swap_bit(values, "dp", 2)
    last_keys = swap_bit(add_low(far, keys[1]), "dp", 2)
    last_values = swap_bit(add_low(near, values[1]), "dp", 1)
    return got[0], keys, values, last_keys, last_values


def turn(values):
    return pltpu.roll(values, HEAD // 2, 1)


def rope_kernel(pre_ref, gain_ref, scale_ref, cos_ref, sin_ref, out_ref, first_ref):
    scale, cosine, sine = scale_ref[...], cos_ref[...], sin_ref[...]
    for at in range(0, pre_ref.shape[1], HEAD):
        span = slice(at, at + HEAD)
        normed = pre_ref[:, span] * scale * gain_ref[:, span]
        out_ref[:, span] = (normed * cosine + turn(normed) * sine).astype(LOW)
    first_ref[...] = out_ref[: first_ref.shape[0]]


def rope_pass(flat, gain, scale, cosine, sine):
    rows, width = flat.shape
    part = width // 2
    wide = lambda rows: pl.BlockSpec((rows, part), lambda h: (0, h))
    return pl.pallas_call(
        rope_kernel,
        grid=(2,),
        in_specs=[wide(rows), wide(1)] + [kept_spec(a) for a in (scale, cosine, sine)],
        out_specs=[wide(rows), wide(PR_DEV)],
        out_shape=[jax.ShapeDtypeStruct((count, width), LOW) for count in (rows, PR_DEV)],
    )(flat, gain, scale, cosine, sine)


PAIR = 2


def head_spec(rows):
    return pl.BlockSpec((rows, PAIR * HEAD), lambda h: (0, h))


def kept_spec(array):
    zeros = (0,) * array.ndim
    return pl.BlockSpec(array.shape, lambda h: zeros, pipeline_mode=pl.Buffered(1))


def all_keys(own_ref, pieces, span):
    return jnp.concatenate(
        [own_ref[:PR_DEV, span]] + [p[:, span] for p in pieces] + [own_ref[PR_DEV:, span]], axis=0
    )


def turned_query(flat_ref, gain_ref, scale, cosine, sine, span):
    normed = flat_ref[:, span] * scale * gain_ref[:, span]
    return (normed * cosine + turn(normed) * sine).astype(LOW)


def softmax_rows(query, keys, bias):
    scores = dot_nt(query, keys) * HEAD ** (-0.5) + bias
    weights = jnp.exp(scores - jnp.max(scores, axis=1, keepdims=True))
    return weights * (1.0 / jnp.sum(weights, axis=1, keepdims=True))


PIECES = GROUP - 1


def attend_kernel(flat_ref, gain_ref, scale_ref, cos_ref, sin_ref, bias_ref, k_ref, v_ref, *refs):
    out_ref = refs[-1]
    bias = bias_ref[...].astype(FULL)
    scale, cosine, sine = scale_ref[...], cos_ref[...], sin_ref[...]
    for at in range(0, PAIR * HEAD, HEAD):
        span = slice(at, at + HEAD)
        query = turned_query(flat_ref, gain_ref, scale, cosine, sine, span)
        probs = softmax_rows(query, all_keys(k_ref, refs[:PIECES], span), bias)
        values = all_keys(v_ref, refs[PIECES : 2 * PIECES], span)
        out_ref[:, span] = dot_nn(probs.astype(LOW), values).astype(LOW)


def attend_specs(rows, scale, cosine, sine, bias):
    return (
        [head_spec(rows), head_spec(1)]
        + [kept_spec(a) for a in (scale, cosine, sine, bias)]
        + [head_spec(rows)] * 2
        + [head_spec(PR_DEV)] * (2 * PIECES)
    )


def attend(flat, gain, scale, cosine, sine, bias, keys, values, pieces):
    rows, width = flat.shape
    return pl.pallas_call(
        attend_kernel,
        grid=(width // HEAD // PAIR,),
        in_specs=attend_specs(rows, scale, cosine, sine, bias),
        out_specs=head_spec(rows),
        out_shape=jax.ShapeDtypeStruct((rows, width), LOW),
        compiler_params=pltpu.CompilerParams(vmem_limit_bytes=VMEM),
    )(flat, gain, scale, cosine, sine, bias, keys, values, *pieces)


def norm_parts(step, at, grad, flat_ref, gain_ref, scale_ref, inner_ref, gain_grad_ref):
    span = slice(at, at + HEAD)
    product = flat_ref[:, span] * grad
    inner = jnp.sum(product * gain_ref[:, span], axis=1, keepdims=True)
    gain_grad_ref[:, span] = jnp.sum(product * scale_ref[...], axis=0, keepdims=True)
    if at:
        inner_ref[...] += inner
    else:
        inner_ref[...] = jnp.where(step == 0, 0.0, inner_ref[...]) + inner


def attend_back_kernel(
    flat_ref, gain_ref, scale_ref, cos_ref, sin_ref, bias_ref, k_ref, v_ref, *refs
):
    back_ref = refs[2 * PIECES]
    qg_ref, inner_ref, gain_grad_ref, kg_ref, vg_ref, even_ref = refs[2 * PIECES + 1 : -4]
    odd_refs = refs[-4:]
    step = pl.program_id(0)
    bias = bias_ref[...].astype(FULL)
    scale, cosine, sine = scale_ref[...], cos_ref[...], sin_ref[...]
    prompt = PR_DEV * GROUP
    for at in range(0, PAIR * HEAD, HEAD):
        span = slice(at, at + HEAD)
        query = turned_query(flat_ref, gain_ref, scale, cosine, sine, span)
        back = back_ref[:, span]
        keys = all_keys(k_ref, refs[:PIECES], span)
        values = all_keys(v_ref, refs[PIECES : 2 * PIECES], span)
        probs = softmax_rows(query, keys, bias)
        prob_grad = dot_nt(back, values)
        value_grad = dot_tn(probs.astype(LOW), back)
        row_dot = jnp.sum(probs * prob_grad, axis=1, keepdims=True)
        score_grad = (probs * (prob_grad - row_dot)).astype(LOW)
        query_grad = dot_nn(score_grad, keys) * HEAD ** (-0.5)
        key_grad = dot_tn(score_grad, query) * HEAD ** (-0.5)
        query_grad = query_grad * cosine - turn(query_grad) * sine
        qg_ref[:, span] = query_grad
        norm_parts(step, at, query_grad, flat_ref, gain_ref, scale_ref, inner_ref, gain_grad_ref)
        for which, grad, own_ref in ((0, key_grad, kg_ref), (1, value_grad, vg_ref)):
            own_ref[:PR_DEV, span] = grad[:PR_DEV]
            own_ref[PR_DEV:, span] = grad[prompt:]
            for j in range(1, GROUP):
                to = odd_refs[j // 2] if j % 2 else even_ref.at[j // 2 - 1]
                to[which, :, span] = grad[j * PR_DEV : (j + 1) * PR_DEV].astype(LOW)


def attend_back(flat, gain, scale, cosine, sine, bias, keys, values, pieces, back):
    rows, width = flat.shape
    wide = jax.ShapeDtypeStruct((rows, width), FULL)
    both = pl.BlockSpec((3, 2, PR_DEV, PAIR * HEAD), lambda h: (0, 0, 0, h))
    return pl.pallas_call(
        attend_back_kernel,
        grid=(width // HEAD // PAIR,),
        in_specs=attend_specs(rows, scale, cosine, sine, bias) + [head_spec(rows)],
        out_specs=[
            head_spec(rows),
            pl.BlockSpec((rows, 1), lambda h: (0, 0)),
            head_spec(1),
            head_spec(rows),
            head_spec(rows),
            both,
        ]
        + [pl.BlockSpec((2, PR_DEV, PAIR * HEAD), lambda h: (0, 0, h))] * 4,
        out_shape=[
            wide,
            jax.ShapeDtypeStruct((rows, 1), FULL),
            jax.ShapeDtypeStruct((1, width), FULL),
            wide,
            wide,
            jax.ShapeDtypeStruct((3, 2, PR_DEV, width), LOW),
        ]
        + [jax.ShapeDtypeStruct((2, PR_DEV, width), LOW)] * 4,
        compiler_params=pltpu.CompilerParams(vmem_limit_bytes=VMEM),
        cost_estimate=pl.CostEstimate(
            flops=20 * 10**9, bytes_accessed=40 * 10**6, transcendentals=4 * 10**6
        ),
    )(flat, gain, scale, cosine, sine, bias, keys, values, *pieces, back)


def key_back_kernel(*refs):
    kg_ref, vg_ref, flat_ref, gain_ref, scale_ref, cos_ref, sin_ref = refs[:7]
    got, keys, values, last_keys, last_values = refs[7:12]
    out_ref, inner_ref, gain_grad_ref, value_ref = refs[12:]
    step = pl.program_id(0)
    for at in range(0, PAIR * HEAD, HEAD):
        span = slice(at, at + HEAD)
        grads = []
        for which, own_ref, near, last in ((0, kg_ref, keys, last_keys), (1, vg_ref, values, last_values)):
            first = own_ref[:PR_DEV, span] + got[which, :, span].astype(FULL)
            first = first + near[0, :, span].astype(FULL) + last[:, span].astype(FULL)
            grads.append(jnp.concatenate([first, own_ref[PR_DEV:, span]], axis=0))
        key_grad = grads[0] * cos_ref[...] - turn(grads[0]) * sin_ref[...]
        out_ref[:, span] = key_grad
        norm_parts(step, at, key_grad, flat_ref, gain_ref, scale_ref, inner_ref, gain_grad_ref)
        value_ref[:, span] = grads[1].astype(LOW)


def key_back(key_grad, value_grad, flat, gain, scale, cosine, sine, returned):
    rows, width = flat.shape
    columns = PAIR * HEAD
    return pl.pallas_call(
        key_back_kernel,
        grid=(width // columns,),
        in_specs=[head_spec(rows)] * 3
        + [head_spec(1)]
        + [kept_spec(a) for a in (scale, cosine, sine)]
        + [pl.BlockSpec((2, PR_DEV, columns), lambda h: (0, 0, h))]
        + [pl.BlockSpec((1, PR_DEV, columns), lambda h: (0, 0, h))] * 2
        + [head_spec(PR_DEV)] * 2,
        out_specs=[
            head_spec(rows),
            pl.BlockSpec((rows, 1), lambda h: (0, 0)),
            head_spec(1),
            head_spec(rows),
        ],
        out_shape=[
            jax.ShapeDtypeStruct((rows, width), FULL),
            jax.ShapeDtypeStruct((rows, 1), FULL),
            jax.ShapeDtypeStruct((1, width), FULL),
            jax.ShapeDtypeStruct((rows, width), LOW),
        ],
        cost_estimate=SMALL,
    )(key_grad, value_grad, flat, gain, scale, cosine, sine, *returned)


def pack_kernel(query, key, value, out, rest, packed):
    at = 0
    for ref in (query, key, value):
        packed[at : at + ref.shape[0]] = ref[...]
        at += ref.shape[0]
    packed[at : at + out.shape[1]] = out[...].T
    packed[at + out.shape[1] :] = rest[...]


def pack_weights(w_query, w_key, w_value, w_out, rest):
    rows = 4 * w_query.shape[0] + rest.shape[0]
    return pl.pallas_call(
        pack_kernel, out_shape=jax.ShapeDtypeStruct((rows, w_query.shape[1]), LOW)
    )(w_query, w_key, w_value, w_out, rest)


def unpack_kernel(first, blocks_ref, packed, out, held, sems):
    width = packed.shape[2]
    parts = out.shape[1] // width
    rows = (packed.shape[1] - first) // parts
    count = packed.shape[0]
    place = lambda i: pl.ds(i * rows, rows)
    loads = [
        pltpu.make_async_copy(
            packed.at[blocks_ref[i], pl.ds(first + j * rows, rows)],
            held.at[place(i), pl.ds(j * width, width)],
            sems.at[i * parts + j],
        )
        for i in range(count)
        for j in range(parts)
    ]
    stores = [
        pltpu.make_async_copy(held.at[place(i)], out.at[place(i)], sems.at[count * parts + i])
        for i in range(count)
    ]
    for one in loads:
        one.start()
    for i, store in enumerate(stores):
        for j in range(parts):
            loads[i * parts + j].wait()
        store.start()
    for store in stores:
        store.wait()


def unpack_rows(packed, blocks, first, width):
    count = packed.shape[0]
    parts = width // packed.shape[2]
    rows = (packed.shape[1] - first) // parts
    return pl.pallas_call(
        lambda *refs: unpack_kernel(first, *refs),
        in_specs=[pl.BlockSpec(memory_space=pltpu.SMEM), pl.BlockSpec(memory_space=pl.ANY)],
        out_specs=pl.BlockSpec(memory_space=pl.ANY),
        out_shape=jax.ShapeDtypeStruct((count * rows, width), LOW),
        scratch_shapes=[
            pltpu.VMEM((count * rows, width), LOW),
            pltpu.SemaphoreType.DMA((count * parts + count,)),
        ],
        compiler_params=pltpu.CompilerParams(vmem_limit_bytes=VMEM),
    )(blocks, packed)


def load_packed(gathered, places, block, held, sems):
    copies = [
        pltpu.make_async_copy(
            gathered.at[:, pl.ds(place * block, block)], held.at[k], sems.at[k]
        )
        for k, place in enumerate(places)
    ]
    for one in copies:
        one.start()
    return copies


def held_pack(gathered, places, block):
    count, columns = gathered.shape[0], gathered.shape[2]
    return [
        pltpu.VMEM((len(places), count, block, columns), LOW),
        pltpu.SemaphoreType.DMA((len(places),)),
    ]


def project_kernel(places, block, heads, rows_ref, gathered, *refs):
    outs, firsts, (held, sems) = refs[: len(places)], refs[len(places) : -2], refs[-2:]
    copies = load_packed(gathered, places, block, held, sems)
    rows = rows_ref[...]
    for k, (one, out) in enumerate(zip(copies, outs)):
        one.wait()
        out[...] = dot_nn(rows, held[k].reshape(-1, out.shape[1])).astype(out.dtype)
    for first, k in zip(firsts, heads):
        first[...] = outs[k][: first.shape[0]]


def project(rows, gathered, block, places, roundings, heads=()):
    count, width = rows.shape
    columns = gathered.shape[2]
    outs = [jax.ShapeDtypeStruct((count, columns), rounding) for rounding in roundings]
    outs += [jax.ShapeDtypeStruct((PR_DEV, columns), roundings[k]) for k in heads]
    fixed = lambda a: pl.BlockSpec(a.shape, lambda i: (0, 0))
    return pl.pallas_call(
        lambda *refs: project_kernel(places, block, heads, *refs),
        grid=(1,),
        in_specs=[fixed(rows), pl.BlockSpec(memory_space=pl.ANY)],
        out_specs=[fixed(out) for out in outs],
        out_shape=outs,
        scratch_shapes=held_pack(gathered, places, block),
        compiler_params=pltpu.CompilerParams(vmem_limit_bytes=VMEM),
        cost_estimate=pl.CostEstimate(
            flops=2 * count * width * columns * len(places),
            bytes_accessed=2 * width * columns * len(places) + 8 * count * columns,
            transcendentals=0,
        ),
    )(rows, gathered)


def pack_specs(gathered, places, steps, at):
    count, width = gathered.shape[0] // steps, gathered.shape[2]
    block = at
    return [
        pl.BlockSpec((count, block, width), lambda i, place=place: (i, place, 0))
        for place in places
    ]


def project_back_kernel(mats, *refs):
    out = refs[-1]
    total = None
    for rows_ref, mat in zip(refs[:mats], refs[mats:-1]):
        part = dot_nt(rows_ref[...], mat[...].reshape(-1, mat.shape[2]))
        total = part if total is None else total + part
    out[...] = total


def project_back(rows, gathered, block, places):
    count, columns = rows[0].shape
    width = gathered.shape[0] * block
    steps = 4 if len(places) > 1 else 2
    fixed = pl.BlockSpec((count, columns), lambda i: (0, 0), pipeline_mode=pl.Buffered(1))
    return pl.pallas_call(
        lambda *refs: project_back_kernel(len(places), *refs),
        grid=(steps,),
        in_specs=[fixed] * len(rows) + pack_specs(gathered, places, steps, block),
        out_specs=pl.BlockSpec((count, width // steps), lambda i: (0, i)),
        out_shape=jax.ShapeDtypeStruct((count, width), FULL),
        compiler_params=pltpu.CompilerParams(vmem_limit_bytes=VMEM),
        cost_estimate=pl.CostEstimate(
            flops=2 * count * width * columns * len(places),
            bytes_accessed=2 * width * columns * len(places) + 4 * count * width,
            transcendentals=0,
        ),
    )(*rows, *[gathered] * len(places))


def pre_kernel(core_ref, *refs):
    inputs, outs = refs[:11], refs[11:]
    step = pl.program_id(0)
    columns = inputs[0].shape[1]
    parts = []
    for flat, grad, gain, scale, inner in (inputs[:5], inputs[5:10]):
        scaled = scale[...]
        mean = inner[...] * (1.0 / (HEADS * HEAD))
        parts.append(
            (
                scaled * gain[...] * grad[...] - flat[...] * (scaled * scaled * scaled) * mean
            ).astype(LOW)
        )
    outs[0][...], outs[1][...] = parts

    @pl.when(step != core_ref[0])
    def _():
        for j, part in enumerate((*parts, inputs[10][...])):
            outs[2][:, j * columns : (j + 1) * columns] = part


def pre_grads_pass(core, query, key, value):
    rows, width = value.shape
    columns = width // 2
    half = lambda rows: pl.BlockSpec((rows, columns), lambda h: (0, h))
    side = [half(rows), half(rows), half(1)] + [pl.BlockSpec((rows, 1), lambda h: (0, 0))] * 2
    return pl.pallas_call(
        pre_kernel,
        grid=(2,),
        in_specs=[pl.BlockSpec(memory_space=pltpu.SMEM)] + side + side + [half(rows)],
        out_specs=[half(rows), half(rows), pl.BlockSpec((rows, 3 * columns), lambda h: (0, 0))],
        out_shape=[jax.ShapeDtypeStruct((rows, width), LOW)] * 2
        + [jax.ShapeDtypeStruct((rows, 3 * columns), LOW)],
    )(core, *query, *key, value)


def weight_kernel(chip_ref, core_ref, *refs):
    normed, normed_got, back, back_got, query, key, value, got, context, context_got = refs[:10]
    out_ref, right_ref, left_ref, pre_both, context_both = refs[10:]
    rows, columns = query.shape

    @pl.when(pl.program_id(0) == 0)
    def _():
        for j, part in enumerate((query, key, value)):
            pre_both[:rows, j * columns : (j + 1) * columns] = part[...]
        pre_both[rows:] = got[...]
        context_both[:rows] = context[...]
        context_both[rows:] = context_got[...]

    left = jnp.concatenate([normed[...], normed_got[...]], axis=0)
    out_ref[0, :, : 3 * columns] = dot_tn(left, pre_both[...]).astype(LOW)
    left = jnp.concatenate([back[...], back_got[...]], axis=0)
    out_ref[0, :, 3 * columns :] = dot_tn(left, context_both[...]).astype(LOW)

    @pl.when(pl.program_id(0) == HOPS.index(4))
    def _():
        right_ref[...] = out_ref[0, :, : 2 * columns]
        left_ref[...] = out_ref[0, :, 2 * columns :]


def weight_grads(chips, core, normed, back, pre_grads, got, context, context_got):
    rows, width = normed[0].shape
    columns = context_got.shape[1]
    count = chips.shape[0]
    block = width // count
    tall = pl.BlockSpec((rows, block), lambda i, chip, core: (0, chip[i]))
    mine = pl.BlockSpec((rows, columns), lambda i, chip, core: (0, core[0]))
    fixed = lambda a: pl.BlockSpec(a.shape, lambda i, chip, core: (0, 0))
    return pl.pallas_call(
        weight_kernel,
        grid_spec=pltpu.PrefetchScalarGridSpec(
            num_scalar_prefetch=2,
            grid=(count,),
            in_specs=[tall] * 4 + [mine] * 3 + [fixed(got), mine, fixed(context_got)],
            out_specs=[pl.BlockSpec((1, block, 4 * columns), lambda i, chip, core: (i, 0, 0))]
            + [pl.BlockSpec((block, 2 * columns), lambda i, chip, core: (0, 0))] * 2,
            scratch_shapes=[
                pltpu.VMEM((2 * rows, 3 * columns), LOW),
                pltpu.VMEM((2 * rows, columns), LOW),
            ],
        ),
        out_shape=[jax.ShapeDtypeStruct((count, block, 4 * columns), LOW)]
        + [jax.ShapeDtypeStruct((block, 2 * columns), LOW)] * 2,
        compiler_params=pltpu.CompilerParams(vmem_limit_bytes=VMEM),
        cost_estimate=pl.CostEstimate(
            flops=16 * rows * width * columns,
            bytes_accessed=2 * (4 * rows * width + 8 * rows * columns + 4 * width * columns),
            transcendentals=0,
        ),
    )(chips, core, *normed, *back, *pre_grads, got, context, context_got)


def ring_weights(blocks, right, left, fillers):
    part = lambda hop: blocks[HOPS.index(hop)]
    cut = blocks.shape[2] // 2
    right, left = ahead(right), behind(left)
    fillers.next(left)
    outward, inward = part(3), part(-3)
    right = jnp.concatenate([add_low(outward[:, :cut], right), outward[:, cut:]], axis=1)
    left = jnp.concatenate([inward[:, :cut], add_low(inward[:, cut:], left)], axis=1)
    right, left = together(right, left)
    right, left = ahead(right), behind(left)
    fillers.next(left)
    token = left
    for hop in (2, 1):
        right, left = together(add_low(part(hop), right), add_low(part(-hop), left))
        right, left = ahead(right), behind(left)
        fillers.next(left)
        token = left if hop == 2 else token
    return (blocks, right, left), token


def sum_kernel(core_ref, blocks_ref, right_ref, left_ref, own_ref, sent_ref):
    rows = own_ref.shape[0]
    for k, out in enumerate((own_ref, sent_ref)):
        side = core_ref[0] if k == 0 else 1 - core_ref[0]
        span = pl.ds(pl.multiple_of(side * rows, rows), rows)
        out[...] = (
            blocks_ref[0, span].astype(FULL)
            + right_ref[span].astype(FULL)
            + left_ref[span].astype(FULL)
        )


def sum_weights(core, blocks, right, left):
    rows, width = right.shape
    whole = pl.BlockSpec((rows, width), lambda i: (0, 0))
    half = pl.BlockSpec((rows // 2, width), lambda i: (0, 0))
    return pl.pallas_call(
        sum_kernel,
        grid=(1,),
        in_specs=[
            pl.BlockSpec(memory_space=pltpu.SMEM),
            pl.BlockSpec((1, rows, width), lambda i: (HOPS.index(0), 0, 0)),
            whole,
            whole,
        ],
        out_specs=[half, half],
        out_shape=[jax.ShapeDtypeStruct((rows // 2, width), FULL)] * 2,
    )(core, blocks, right, left)


def place_kernel(core_ref, own_ref, got_ref, *outs):
    columns = own_ref.shape[1] // 4
    first = core_ref[0] == 0
    for k, out in enumerate(outs):
        span = slice(k * columns, (k + 1) * columns)
        own, got = own_ref[:, span], got_ref[:, span]
        left, right = jnp.where(first, own, got), jnp.where(first, got, own)
        if k < 3:
            out[:, :columns], out[:, columns:] = left, right
        else:
            out[:columns], out[columns:] = left.T, right.T


def place_weights(core, own, got):
    rows, width = own.shape
    columns = width // 2
    shapes = [(rows, columns)] * 3 + [(columns, rows)]
    return pl.pallas_call(
        place_kernel,
        grid=(1,),
        in_specs=[pl.BlockSpec(memory_space=pltpu.SMEM)]
        + [pl.BlockSpec((rows, width), lambda i: (0, 0))] * 2,
        out_specs=[pl.BlockSpec(shape, lambda i: (0, 0)) for shape in shapes],
        out_shape=[jax.ShapeDtypeStruct(shape, FULL) for shape in shapes],
    )(core, own, got)


def expert_kernel(
    rows_ref, back_ref, gate_ref, wg0, wg1, wu0, wu1, wd0, wd1, grad_ref, h0, h1, g0, g1, u0, u1
):
    rows = rows_ref[...]
    back = back_ref[...]
    gate = gate_ref[...]
    total = None
    for wg, wu, wd, h, g, u in ((wg0, wu0, wd0, h0, g0, u0), (wg1, wu1, wd1, h1, g1, u1)):
        gate_pre = dot_nn(rows, wg[...])
        up_pre = dot_nn(rows, wu[...])
        hidden_grad = gate * dot_nt(back, wd[...])
        sig = 1.0 / (1.0 + jnp.exp(-gate_pre))
        act = gate_pre * sig
        h[...] = (gate * (act * up_pre)).astype(LOW)
        gate_grad = (hidden_grad * up_pre * (sig * (1.0 + gate_pre * (1.0 - sig)))).astype(LOW)
        up_grad = (hidden_grad * act).astype(LOW)
        g[...] = gate_grad
        u[...] = up_grad
        part = dot_nt(gate_grad, wg[...]) + dot_nt(up_grad, wu[...])
        total = part if total is None else total + part
    grad_ref[...] = total.astype(LOW)


def expert_pass(rows, back, gate, gate_mats, up_mats, down_mats):
    count, width = rows.shape
    hidden = gate_mats[0].shape[1]
    tile = 256
    whole = lambda array: pl.BlockSpec(
        array.shape, lambda i: (0, 0), pipeline_mode=pl.Buffered(1)
    )
    tall = lambda columns: pl.BlockSpec((tile, columns), lambda i: (i, 0))
    mats = [*gate_mats, *up_mats, *down_mats]
    flops = 2 * 5 * count * width * hidden * 2
    return pl.pallas_call(
        expert_kernel,
        grid=(count // tile,),
        in_specs=[tall(width), tall(width), tall(1)] + [whole(m) for m in mats],
        out_specs=[tall(width)] + [tall(hidden)] * 6,
        out_shape=[jax.ShapeDtypeStruct((count, width), LOW)]
        + [jax.ShapeDtypeStruct((count, hidden), LOW)] * 6,
        compiler_params=pltpu.CompilerParams(vmem_limit_bytes=VMEM),
        cost_estimate=pl.CostEstimate(
            flops=flops,
            bytes_accessed=2 * (3 * count * width + 6 * count * hidden + 6 * width * hidden),
            transcendentals=2 * count * hidden,
        ),
    )(rows, back, gate, *mats)


def chunk_kernel(pieces, held, at, splits, gate_ref, *refs):
    piece_refs, refs = refs[:pieces], refs[pieces:]
    back_ref, mats, refs = refs[0], refs[1:7], refs[7 + held :]
    grad_outs, refs = refs[: len(splits)], refs[len(splits) :]
    rows_out, outs = refs[0], refs[1:7]
    rows, back, wide, wd, hidden, both_grads, grads, sems = refs[7:]
    count = rows.shape[0]
    part = wd.shape[1]
    slab = wide.shape[0] // 4
    across = lambda k, half: pl.ds((2 * k + half) * part, part)
    place = pl.ds(at * count, count)
    copy = pltpu.make_async_copy
    load_rows, start = [], 0
    for piece in piece_refs:
        span = pl.ds(start, piece.shape[0])
        load_rows.append(copy(piece, rows.at[span], sems.at[len(load_rows)]))
        start += piece.shape[0]
    load_back = copy(back_ref.at[place], back, sems.at[6])
    loads = []
    for half in range(2):
        places = [wide.at[:, across(0, half)], wide.at[:, across(1, half)], wd.at[half]]
        loads.append(
            [copy(mats[2 * k + half], to, sems.at[7 + 3 * half + k]) for k, to in enumerate(places)]
        )
    for one in load_rows + loads[0][:2] + [load_back] + loads[0][2:] + loads[1]:
        one.start()
    gate = gate_ref[...]
    for one in load_rows:
        one.wait()
    stores = [copy(rows, rows_out.at[place], sems.at[13])]
    stores[0].start()
    for half in range(2):
        columns = pl.ds(half * part, part)
        loads[half][0].wait()
        gate_pre = dot_nn(rows[...], wide[:, across(0, half)])
        loads[half][1].wait()
        up_pre = dot_nn(rows[...], wide[:, across(1, half)])
        if half == 0:
            load_back.wait()
        loads[half][2].wait()
        hidden_grad = gate * dot_nt(back[...], wd[half])
        sig = 1.0 / (1.0 + jnp.exp(-gate_pre))
        act = gate_pre * sig
        hidden[:, columns] = (gate * (act * up_pre)).astype(LOW)
        both_grads[:, across(0, half)] = (
            hidden_grad * up_pre * (sig * (1.0 + gate_pre * (1.0 - sig)))
        ).astype(LOW)
        both_grads[:, across(1, half)] = (hidden_grad * act).astype(LOW)
    for half in range(2):
        held_in = (
            hidden.at[:, pl.ds(half * part, part)],
            both_grads.at[:, across(0, half)],
            both_grads.at[:, across(1, half)],
        )
        for k, source in enumerate(held_in):
            stores.append(copy(source, outs[2 * k + half].at[place], sems.at[14 + 3 * half + k]))
            stores[-1].start()

    @pl.loop(0, 4)
    def _(j):
        span = pl.ds(pl.multiple_of(j * slab, slab), slab)
        grads[:, span] = dot_nt(both_grads[...], wide[span]).astype(LOW)

    start = 0
    for k, (split, to) in enumerate(zip(splits, grad_outs)):
        stores.append(copy(grads.at[pl.ds(start, split)], to, sems.at[20 + k]))
        stores[-1].start()
        start += split
    for one in stores:
        one.wait()


def expert_chunk(pieces, back, gate, mats, at, held, splits):
    all_rows, width = back.shape
    part = mats[0].shape[1]
    hidden = 2 * part
    count = sum(piece.shape[0] for piece in pieces)
    anywhere = pl.BlockSpec(memory_space=pl.ANY)
    held = [] if held is None else list(held)
    args = [gate, *pieces, back, *mats, *held]
    out = pl.pallas_call(
        lambda *refs: chunk_kernel(len(pieces), len(held), at, splits, *refs),
        grid=(1,),
        in_specs=[pl.BlockSpec((count, 1), lambda j: (at, 0))] + [anywhere] * (len(args) - 1),
        out_specs=[anywhere] * (len(splits) + 7),
        out_shape=[jax.ShapeDtypeStruct((split, width), LOW) for split in splits]
        + [jax.ShapeDtypeStruct((all_rows, width), LOW)]
        + [jax.ShapeDtypeStruct((all_rows, part), LOW)] * 6,
        scratch_shapes=[
            pltpu.VMEM((count, width), LOW),
            pltpu.VMEM((count, width), LOW),
            pltpu.VMEM((width, 2 * hidden), LOW),
            pltpu.VMEM((2, part, width), LOW),
            pltpu.VMEM((count, hidden), LOW),
            pltpu.VMEM((count, 2 * hidden), LOW),
            pltpu.VMEM((count, width), LOW),
            pltpu.SemaphoreType.DMA((23,)),
        ],
        input_output_aliases={
            len(args) - len(held) + k: len(splits) + k for k in range(len(held))
        },
        compiler_params=pltpu.CompilerParams(vmem_limit_bytes=VMEM),
        cost_estimate=pl.CostEstimate(
            flops=2 * 5 * count * width * hidden,
            bytes_accessed=2 * (4 * count * width + 3 * count * hidden + 3 * width * hidden),
            transcendentals=count * hidden,
        ),
    )(*args)
    return out[: len(splits)], out[len(splits) :]


def mixed_kernel(chip_ref, same_ref, cross_ref, core_ref, *refs):
    first_ref, second_ref, out_ref = refs[4:]
    rows = out_ref.shape[2]
    first, second = (
        jnp.concatenate([refs[k][...], refs[k + 1][...]], axis=0) for k in (0, 2)
    )
    result = (dot_nn(first, first_ref[...]) + dot_nn(second, second_ref[...])).astype(LOW)
    out_ref[0, core_ref[0]] = result[:rows]
    out_ref[0, 1 - core_ref[0]] = result[rows:]


def mixed_pass(h0, h1, down_mats, chips, core):
    count, columns = h0.shape
    width = down_mats[0].shape[1]
    rows = count // len(LAYOUT)
    places = [
        jnp.array([LAYOUT.index((hop, cross)) for hop in HOPS], jnp.int32) for cross in (0, 1)
    ]
    once = pl.Buffered(1)
    fixed = lambda m: pl.BlockSpec(m.shape, lambda i, *tables: (0, 0), pipeline_mode=once)
    block = lambda k: pl.BlockSpec((rows, columns), lambda i, *tables: (tables[k][i], 0))
    out = pl.pallas_call(
        mixed_kernel,
        grid_spec=pltpu.PrefetchScalarGridSpec(
            num_scalar_prefetch=4,
            grid=(len(HOPS),),
            in_specs=[block(1), block(2), block(1), block(2)] + [fixed(m) for m in down_mats],
            out_specs=pl.BlockSpec(
                (1, 2, rows, width), lambda i, chip, *tables: (chip[i], 0, 0, 0)
            ),
        ),
        out_shape=jax.ShapeDtypeStruct((len(HOPS), 2, rows, width), LOW),
        compiler_params=pltpu.CompilerParams(vmem_limit_bytes=VMEM),
        cost_estimate=pl.CostEstimate(
            flops=4 * count * columns * width,
            bytes_accessed=2 * (count * (2 * columns + width) + 2 * columns * width),
            transcendentals=0,
        ),
    )(chips, *places, core, h0, h0, h1, h1, *down_mats)
    return out.reshape(count, width)


def expert_ring(rows, back, gate, mats, waiting):
    size = rows.shape[0]
    cut = size // 2
    swap = lambda block: swap_bit(block, "dp", 0)
    chunk = lambda pieces, at, held, *splits: expert_chunk(
        pieces, back, gate, mats, at, held, splits
    )
    rows, pair = together(rows, swap(rows))
    left, right = ahead(rows), behind(rows)
    parts, crossed = cut_rows(waiting, 4), []
    same, cross = {}, {}
    cross_over = lambda token: crossed.append(swap_tensor(after(parts[len(crossed)], token)))
    cross_over(pair)
    (same[0], cross[0]), held = chunk([rows, pair], 6, None, size, size)
    left, right, same[0] = together(left, right, same[0])
    pieces, got = [left, right], [swap(left), swap(right)]
    left, right = ahead(left), behind(right)
    pieces[0], crossed[0] = together(pieces[0], crossed[0])
    cross_over(pieces[0])
    (same[1],), held = chunk(pieces, 7, held, 2 * size)
    left, right, same[1] = together(left, right, same[1])
    pieces, got = [left, right, *got], [swap(left), swap(right)]
    left, right = ahead(left), behind(right)
    pieces[0], crossed[1] = together(pieces[0], crossed[1])
    cross_over(pieces[0])
    (same[2], cross[1]), held = chunk(pieces, 0, held, 2 * size, 2 * size)
    left, right, same[2] = together(left, right, same[2])
    pieces, got = [left, right, *got], [swap(left), swap(right)]
    left, right = ahead(left[:cut]), behind(right[cut:])
    pieces[0], crossed[2] = together(pieces[0], crossed[2])
    cross_over(pieces[0])
    (same[3], cross[2]), held = chunk(pieces, 1, held, 2 * size, 2 * size)
    left, right, crossed[3], same[3] = together(left, right, crossed[3], same[3])
    pieces = [left, right, swap(left), swap(right), *got]
    (same[4], cross[4], cross[3]), held = chunk(pieces, 2, held, size, size, 2 * size)
    waiting = jnp.concatenate(crossed, axis=0)
    return same, cross, held, waiting


def body(
    inputs,
    attn_gain,
    w_query,
    w_key,
    w_value,
    query_gain,
    key_gain,
    w_out,
    moe_gain,
    w_gate,
    w_up,
    w_down,
    experts,
    gates,
    segments,
    gaps,
    cotangent,
):
    dp_count = lax.axis_size("dp")
    dp_index = lax.axis_index("dp")
    side = lax.axis_index("tensor")
    token_count, model_width = inputs.shape
    half_count = token_count // 2
    top_count = experts.shape[1]
    expert_count = w_gate.shape[0] * dp_count
    capacity = token_count * top_count * dp_count * 9 // (8 * expert_count)
    prompt_length = PR_DEV * GROUP
    column_total = HEADS * HEAD
    block = w_query.shape[0]
    local_width = w_query.shape[1]
    local_heads = local_width // HEAD

    def own_half(array):
        return lax.dynamic_slice_in_dim(array, side * half_count, half_count, axis=0)

    def other_half(array):
        return lax.dynamic_slice_in_dim(array, (1 - side) * half_count, half_count, axis=0)

    def both_halves(own, other):
        first = side == 0
        return jnp.concatenate(
            [jnp.where(first, own, other), jnp.where(first, other, own)], axis=0
        )

    gate_mats = (w_gate[0], swap_tensor(w_gate[0]))
    up_mats = (w_up[0], swap_tensor(w_up[0]))

    ring = dp_count == 2 * len(RING)

    gates_high = gates.astype(LOW)
    gates_low = (gates - gates_high.astype(FULL)).astype(LOW)
    routing = jnp.concatenate([experts.astype(LOW).T, gates_high.T, gates_low.T], axis=1)
    routing = jnp.pad(routing, ((0, 0), (0, local_width - 3 * token_count)))
    gains = jnp.concatenate([attn_gain, moe_gain, query_gain, key_gain])
    gains = jnp.pad(gains[None], ((0, 7), (0, local_width - 4 * block)))
    packed = pack_weights(
        w_query, w_key, w_value, w_out, jnp.concatenate([gains, routing], axis=0)
    )
    gathered = lax.all_gather(packed, "dp", axis=0, tiled=False)
    cotangent_half = own_half(cotangent)
    gathered_back = lax.all_gather(cotangent_half.astype(LOW), "dp", axis=0, tiled=False)
    core = dp_index % 2
    tokens_f = inputs.astype(FULL)
    prompt_pos = dp_index % GROUP * PR_DEV + jnp.arange(PR_DEV, dtype=jnp.int32)
    later_pos = cont_positions(segments[0], gaps[0], prompt_length)
    positions = jnp.concatenate([prompt_pos, later_pos], axis=0)
    cosine, sine = rope_tables(positions, HEAD)
    sine = jnp.where(jnp.arange(HEAD) < HEAD // 2, -sine, sine)
    prompt_query = jnp.arange(token_count, dtype=jnp.int32) < PR_DEV
    prompt_at = jnp.arange(prompt_length, dtype=jnp.int32)
    prompt_keypos = ((dp_index % GROUP) ^ (prompt_at // PR_DEV)) * PR_DEV + prompt_at % PR_DEV
    allowed_prompt = (~prompt_query)[:, None] | (prompt_keypos[None, :] <= positions[:, None])
    query_segment = jnp.concatenate([jnp.full((PR_DEV,), -1, jnp.int32), segments[0]], axis=0)
    allowed_cont = (query_segment[:, None] == segments[0][None, :]) & (
        later_pos[None, :] <= positions[:, None]
    )
    allowed = jnp.concatenate([allowed_prompt, allowed_cont], axis=1)
    bias = jnp.where(allowed, 0.0, -1e30).astype(LOW)
    gathered, cosine, sine, bias, *early = together(
        gathered, cosine, sine, bias, gate_mats[1], up_mats[1]
    )
    gate_mats, up_mats = (gate_mats[0], early[0]), (up_mats[0], early[1])
    rest = gathered[:, 4 * block : 4 * block + 16]
    gain_rows = rest[:, 0].astype(FULL)
    gain_one, gain_two, gain_q, gain_k = (
        gain_rows[:, j * block : (j + 1) * block].reshape(-1) for j in range(4)
    )
    gain_query_local = lax.dynamic_slice_in_dim(gain_q, side * local_width, local_width)
    gain_key_local = lax.dynamic_slice_in_dim(gain_k, side * local_width, local_width)

    names, *parts = (
        rest[:, 8:, j * token_count : (j + 1) * token_count] for j in range(3)
    )
    weights = parts[0].astype(FULL) + parts[1].astype(FULL)
    named = names == dp_index.astype(LOW)
    picked = jnp.sum(named.astype(FULL), axis=1)
    weight = jnp.sum(jnp.where(named, weights, 0.0), axis=1)
    order = jnp.arange(token_count, dtype=jnp.int32)
    earlier = (order[:, None] < order[None, :]).astype(LOW)
    within = dot_nn(picked.astype(LOW), earlier)
    per_row = jnp.sum(picked, axis=1)
    rows_order = jnp.arange(dp_count, dtype=jnp.int32)
    ahead = jnp.sum(
        jnp.where(rows_order[None, :] < rows_order[:, None], per_row[None, :], 0.0), axis=1
    )
    kept = (picked > 0.0) & (within + ahead[:, None] < capacity)
    weight = jnp.where(kept, weight, 0.0)
    weight = lax.dynamic_slice_in_dim(weight, side * half_count, half_count, axis=1)
    if ring:
        blocks, chips = ring_blocks(dp_index), ring_chips(dp_index, HOPS)
        weight = weight[blocks]
    weight = weight.reshape(-1, 1)

    normed_b = rms_norm(tokens_f, gain_one).astype(LOW)
    query_flat, key_flat, values_b, value_prompt = project(
        normed_b, gathered, block, (0, 1, 2), (FULL, FULL, LOW), (2,)
    )
    key_sq = jnp.sum(key_flat * key_flat, axis=1)
    key_sq, value_prompt = together(key_sq, value_prompt)
    value_pieces = collect_prompt(value_prompt, 1, 2)
    query_sq, key_sq = lax.psum(
        (jnp.sum(query_flat * query_flat, axis=1), key_sq), "tensor"
    )
    query_sq, down_mat = lax.optimization_barrier((query_sq, w_down[0]))
    down_mats = (down_mat, swap_tensor(down_mat))
    query_scale = lax.rsqrt(query_sq / column_total + EPSILON)[:, None]
    key_scale = lax.rsqrt(key_sq / column_total + EPSILON)[:, None]
    keys_b, key_prompt = rope_pass(key_flat, gain_key_local[None], key_scale, cosine, sine)
    pieces = (*collect_prompt(key_prompt, 2, 1), *value_pieces)
    turned_by = (gain_query_local[None], query_scale, cosine, sine, bias)
    context_b = attend(query_flat, *turned_by, keys_b, values_b, pieces)
    attn_part = project_back([context_b], gathered, block, (3,))
    attn_part, late, weight = together(attn_part, down_mats[1], weight)
    down_mats = (down_mats[0], late)
    mats = (*gate_mats, *up_mats, *down_mats)
    attn_other = swap_tensor(other_half(attn_part).astype(LOW))
    gathered_back = after(gathered_back, attn_part)
    if ring:
        back_rows = unpack_rows(gathered_back, blocks, 0, model_width)
    else:
        back_rows = gathered_back.reshape(-1, model_width)
    attn_other, back_rows, weight = together(attn_other, back_rows, weight)
    hidden_state = own_half(tokens_f) + own_half(attn_part) + attn_other.astype(FULL)
    normed_two_b = rms_norm(hidden_state, gain_two).astype(LOW)

    low_tn = lambda left, right: dot_tn(left, right).astype(LOW)
    upper = lambda array: array[: array.shape[0] // 2]
    lower = lambda array: array[array.shape[0] // 2 :]
    if ring:
        same, cross, held, hidden_other = expert_ring(
            normed_two_b, back_rows, weight, mats, hidden_state
        )
        expert_in, h0, h1, g0, g1, u0, u1 = held
        late = {}

        def down_stage(gated):
            late["down"] = swap_tensor(low_tn(gated(h1), back_rows))

        def gate_stage(gated):
            late["gate"] = low_tn(gated(expert_in), g1)

        def up_stage(gated):
            late["up"] = low_tn(gated(expert_in), u1)

        def mixed_stage(gated):
            late["mixed"] = mixed_pass(gated(h0), h1, down_mats, chips, core[None])

        fillers = Fillers(down_stage, gate_stage, up_stage, mixed_stage)
        normed_two_grad = ring_sum(same, cross, fillers)
        gate_sent, up_sent, mixed_rows = late["gate"], late["up"], late["mixed"]
        down_got = late["down"]
    else:
        hidden_other = swap_tensor(hidden_state)
        expert_in = lax.all_gather(normed_two_b, "dp", axis=0, tiled=True)
        grad_rows, h0, h1, g0, g1, u0, u1 = expert_pass(
            expert_in, back_rows, weight, gate_mats, up_mats, down_mats
        )
        normed_two_grad = lax.psum_scatter(
            grad_rows, "dp", scatter_dimension=0, tiled=True
        ).astype(FULL)
        mixed_rows = (dot_nn(h0, down_mats[0]) + dot_nn(h1, down_mats[1])).astype(LOW)
        down_got = swap_tensor(low_tn(h1, back_rows))
        gate_sent = low_tn(expert_in, g1)
        up_sent = low_tn(expert_in, u1)
    quarter = gate_sent.shape[0] // 4
    gate_first = swap_tensor(gate_sent[:quarter])
    normed_two_grad, down_got, gate_first, mixed_rows, up_sent = together(
        normed_two_grad, down_got, gate_first, mixed_rows, up_sent
    )
    mixed = lax.psum_scatter(mixed_rows, "dp", scatter_dimension=0, tiled=True)

    unused_two, norm_two_back = jax.vjp(rms_norm, hidden_state, gain_two)
    state_part, gain_two_grad = norm_two_back(normed_two_grad)
    state_half = cotangent_half + state_part
    attn_grad_half = state_half.astype(LOW)
    attn_grad_b = both_halves(attn_grad_half, swap_tensor(attn_grad_half))
    attn_grad_b, gate_sent, up_sent = together(attn_grad_b, gate_sent, up_sent)
    (context_grad_b,) = project(attn_grad_b, gathered, block, (3,), (LOW,))
    (gate_middle,) = swap_in_turn([gate_sent[quarter : 3 * quarter]], context_grad_b)
    soon = [
        swap_tensor(after(piece, gate_middle))
        for piece in (gate_sent[3 * quarter :], upper(up_sent))
    ]
    if ring:
        pair = lambda own: (own, swap_bit(own, "dp", 0))
        columns = local_width // 2
        context_sent = lax.dynamic_slice_in_dim(context_b, (1 - core) * columns, columns, axis=1)
        normed_pair, attn_grad_pair = pair(normed_b), pair(attn_grad_b)
        context_got = swap_bit(context_sent, "dp", 0)
    query_normed_grad, query_inner, query_gain_part, key_grad, value_grad, even, *odd = attend_back(
        query_flat, *turned_by, keys_b, values_b, pieces, context_grad_b
    )
    returned = return_prompt(odd, even)
    if ring:
        key_grad, context_got, *pairs = together(
            key_grad, context_got, normed_pair[1], attn_grad_pair[1]
        )
        normed_pair, attn_grad_pair = (normed_b, pairs[0]), (attn_grad_b, pairs[1])
    key_normed_grad, key_inner, key_gain_part, value_pre_grad = key_back(
        key_grad, value_grad, key_flat, gain_key_local[None], key_scale, cosine, sine, returned
    )
    query_inner, *soon = together(query_inner, *soon)
    query_inner, key_inner = lax.psum(
        jnp.stack([query_inner[:, 0], key_inner[:, 0]], axis=0), "tensor"
    )
    query_pre_grad, key_pre_grad, pre_sent = pre_grads_pass(
        core[None],
        (
            query_flat,
            query_normed_grad,
            gain_query_local[None],
            query_scale,
            query_inner[:, None],
        ),
        (key_flat, key_normed_grad, gain_key_local[None], key_scale, key_inner[:, None]),
        value_pre_grad,
    )
    gate_got = jnp.concatenate([gate_first, gate_middle, soon[0]], axis=0)
    pre_grads = (query_pre_grad, key_pre_grad, value_pre_grad)
    grad_sum = lambda left, right, got: dot_tn(left, right) + got.astype(FULL)
    back_all = lambda *grads: project_back(grads, gathered, block, (0, 1, 2))

    wide = lambda part: lax.dynamic_update_slice_in_dim(
        jnp.zeros((column_total,), FULL), part, side * local_width, 0
    )

    def share(part):
        return own_half(part), swap_tensor(other_half(part).astype(LOW)), gain_part(part)

    def input_side(own, other):
        unused_one, norm_one_back = jax.vjp(
            lambda values: rms_norm(values, gain_one), own_half(tokens_f)
        )
        input_half = state_half + norm_one_back(own + other.astype(FULL))[0]
        return input_half, swap_tensor(input_half)

    def gain_part(part):
        return jnp.sum(part * rms_norm(tokens_f, 1.0), axis=0)

    def gain_side(gain_one_grad):
        grads = jnp.stack(
            [gain_one_grad, gain_two_grad, wide(query_gain_part[0]), wide(key_gain_part[0])]
        ).reshape(4, dp_count, block)
        grads = jnp.swapaxes(grads, 0, 1).reshape(dp_count, 1, 4 * block)
        sides = lax.axis_size("tensor")
        grads = jnp.broadcast_to(grads, (dp_count, sides, 4 * block))
        grads = grads.reshape(dp_count * sides, 4 * block)
        sums = lax.all_to_all(grads, ("dp", "tensor"), 0, 0, tiled=True)
        return jnp.sum(sums, axis=0).reshape(4, block)

    if ring:
        pre_got = swap_bit(pre_sent, "dp", 0)
        w_blocks, *far = weight_grads(
            chips,
            core[None],
            normed_pair,
            attn_grad_pair,
            pre_grads,
            pre_got,
            context_b,
            context_got,
        )
        w_blocks, mixed, *far = together(w_blocks, mixed, *far)
        up_third, up_last = cut_rows(lower(up_sent), 2)
        up_third = swap_tensor(after(up_third, far[0]))
        late = {}

        def normed_stage(gated):
            late["normed"] = share(back_all(*[gated(grad) for grad in pre_grads]))

        def input_stage(gated):
            late["input"] = input_side(late["normed"][0], gated(late["normed"][1]))
            late["up"] = swap_tensor(after(up_last, late["input"][0]))
            late["down"] = grad_sum(gated(h0), back_rows, down_got)

        def expert_stage(gated):
            late["gains"] = gain_side(gated(late["normed"][2]))
            late["mixed"] = swap_tensor(gated(mixed))
            late["gate"] = grad_sum(gated(expert_in), g0, gate_got)

        fillers = Fillers(normed_stage, input_stage, expert_stage)
        w_parts, token = ring_weights(w_blocks, *far, fillers)
        input_half, input_other = late["input"]
        gain_sums = late["gains"]
        down_grad, gate_w_grad = late["down"], late["gate"]
        up_got = jnp.concatenate([soon[1], up_third, late["up"]], axis=0)
        up_w_grad = grad_sum(after(expert_in, token), u0, up_got)
        own_w, sent_w = sum_weights(core[None], *w_parts)
        w_sums = place_weights(core[None], own_w, swap_bit(sent_w, "dp", 0))
        mixed_other = late["mixed"]
    else:
        w_grads = jnp.concatenate(
            [low_tn(normed_b, g) for g in pre_grads] + [low_tn(attn_grad_b, context_b)], axis=1
        )
        w_sum = lax.psum_scatter(w_grads, "dp", scatter_dimension=0, tiled=True).astype(FULL)
        w_sums = [w_sum[:, j * local_width : (j + 1) * local_width] for j in range(4)]
        w_sums[3] = w_sums[3].T
        down_grad = grad_sum(h0, back_rows, down_got)
        gate_w_grad = grad_sum(expert_in, g0, gate_got)
        up_got = jnp.concatenate([soon[1], swap_tensor(lower(up_sent))], axis=0)
        up_w_grad = grad_sum(expert_in, u0, up_got)
        mixed_other = swap_tensor(mixed)
        *normed_parts, gain_one_grad = share(back_all(*pre_grads))
        gain_sums = gain_side(gain_one_grad)
        input_half, input_other = input_side(*normed_parts)
    input_grad = both_halves(input_half, input_other)
    output = both_halves(
        hidden_state + mixed.astype(FULL), hidden_other + mixed_other.astype(FULL)
    )
    return (
        output,
        input_grad,
        gain_sums[0],
        w_sums[0],
        w_sums[1],
        w_sums[2],
        gain_sums[2],
        gain_sums[3],
        w_sums[3],
        gain_sums[1],
        gate_w_grad[None],
        up_w_grad[None],
        down_grad[None],
    )


def solution(mesh):
    return jax.shard_map(
        body,
        mesh=mesh,
        in_specs=(
            P("dp", None),
            P("dp"),
            P("dp", "tensor"),
            P("dp", "tensor"),
            P("dp", "tensor"),
            P("dp"),
            P("dp"),
            P("tensor", "dp"),
            P("dp"),
            P("dp", None, "tensor"),
            P("dp", None, "tensor"),
            P("dp", "tensor", None),
            P("dp", None),
            P("dp", None),
            P("dp", None),
            P("dp", None),
            P("dp", None),
        ),
        out_specs=(
            P("dp", None),
            P("dp", None),
            P("dp"),
            P("dp", "tensor"),
            P("dp", "tensor"),
            P("dp", "tensor"),
            P("dp"),
            P("dp"),
            P("tensor", "dp"),
            P("dp"),
            P("dp", None, "tensor"),
            P("dp", None, "tensor"),
            P("dp", "tensor", None),
        ),
        check_vma=False,
    )
```

```python
import jax
import jax.numpy as jnp
from jax import lax
from jax.experimental import pallas as pl
from jax.experimental.pallas import tpu as pltpu
from jax.sharding import PartitionSpec as P

HEADS = 16
HEAD = 128
GROUP = 8
PR_DEV = 128


EPSILON = 1e-05
VMEM = 60 * 1024 * 1024
LOW = jnp.bfloat16
FULL = jnp.float32


def swap_bit(block, axis, bit):
    count = lax.axis_size(axis)
    return lax.ppermute(block, axis, [(i, i ^ (1 << bit)) for i in range(count)])


def swap_tensor(block):
    return lax.ppermute(block, "tensor", [(0, 1), (1, 0)])


RING = (0, 2, 4, 6, 7, 5, 3, 1)
AHEAD = [
    (RING[p] * 2 + c, RING[(p + 1) % len(RING)] * 2 + c) for p in range(len(RING)) for c in range(2)
]
BEHIND = [(to, at) for at, to in AHEAD]
HOPS = (-1, 1, -2, 2, -3, 3, 0, 4)
LAYOUT = (
    *((-2, 0), (2, 0), (-1, 1), (1, 1)),
    *((-3, 0), (3, 0), (-2, 1), (2, 1)),
    *((4, 0), (4, 1), (-3, 1), (3, 1)),
    *((0, 0), (0, 1)),
    *((-1, 0), (1, 0)),
)


def ahead(block):
    return lax.ppermute(block, "dp", AHEAD)


def behind(block):
    return lax.ppermute(block, "dp", BEHIND)


def ring_chips(dp_index, hops):
    chip = dp_index // 2
    place = jnp.where(chip % 2 == 0, chip // 2, 7 - chip // 2)
    there = (place + jnp.array(hops, jnp.int32)) % len(RING)
    return jnp.where(there < 4, 2 * there, 2 * (7 - there) + 1)


def ring_blocks(dp_index):
    chips = ring_chips(dp_index, [hop for hop, _ in LAYOUT])
    return 2 * chips + (dp_index % 2 ^ jnp.array([cross for _, cross in LAYOUT], jnp.int32))


def add_low(*parts):
    total = parts[0].astype(FULL)
    for part in parts[1:]:
        total = total + part.astype(FULL)
    return total.astype(LOW)


def together(value, *others):
    return lax.optimization_barrier((value, *others))


def after(value, token):
    return lax.optimization_barrier((value, token))[0]


class Fillers:
    def __init__(self, *stages):
        self.stages = list(stages)

    def next(self, token):
        if self.stages:
            self.stages.pop(0)(lambda value: after(value, token))


def ring_sum(same, cross, fillers):
    both = {hop: add_low(same[hop], swap_bit(cross[hop], "dp", 0)) for hop in (4, 3, 2, 1, 0)}
    rows = both[0].shape[0]
    cut = rows // 2
    fillers.next(both[4])
    right, left = ahead(both[4][:cut]), behind(both[4][cut:])
    fillers.next(left)
    outward, inward = both[3][rows:], both[3][:rows]
    right = jnp.concatenate([add_low(outward[:cut], right), outward[cut:]], axis=0)
    left = jnp.concatenate([inward[:cut], add_low(inward[cut:], left)], axis=0)
    right, left = ahead(right), behind(left)
    fillers.next(left)
    for hop in (2, 1):
        right = ahead(add_low(both[hop][rows:], right))
        left = behind(add_low(both[hop][:rows], left))
        fillers.next(left)
    return both[0].astype(FULL) + right.astype(FULL) + left.astype(FULL)


def swap_in_turn(pieces, token):
    got = []
    for piece in pieces:
        got.append(swap_tensor(after(piece, token)))
        token = got[-1]
    return got


def cut_rows(array, count):
    rows = array.shape[0] // count
    return [array[i * rows : (i + 1) * rows] for i in range(count)]


def rms_norm(values, gain):
    return values * lax.rsqrt(jnp.mean(values * values, axis=-1, keepdims=True) + EPSILON) * gain


def rope_tables(positions, head_size):
    half_size = head_size // 2
    inverse = 10000.0 ** (-(jnp.arange(half_size, dtype=FULL) * 2.0) / head_size)
    angles = positions.astype(FULL)[:, None] * inverse[None, :]
    cosine = jnp.concatenate([jnp.cos(angles), jnp.cos(angles)], axis=-1)
    sine = jnp.concatenate([jnp.sin(angles), jnp.sin(angles)], axis=-1)
    return (cosine, sine)


def cont_positions(segment_row, gap_row, prompt_length):
    order = jnp.arange(segment_row.shape[0], dtype=jnp.int32)
    same = segment_row[:, None] == segment_row[None, :]
    earlier = order[None, :] < order[:, None]
    offset = jnp.sum((same & earlier).astype(jnp.int32), axis=1)
    labels = jnp.arange(gap_row.shape[0], dtype=jnp.int32)
    shifted = jnp.sum(
        jnp.where(segment_row[:, None] == labels[None, :], gap_row[None, :], 0), axis=1
    )
    return prompt_length + shifted + offset


def dot_nn(left, right):
    return jnp.dot(left, right, preferred_element_type=FULL)


def dot_tn(left, right):
    return lax.dot_general(left, right, (((0,), (0,)), ((), ())), preferred_element_type=FULL)


def dot_nt(left, right):
    return lax.dot_general(left, right, (((1,), (1,)), ((), ())), preferred_element_type=FULL)


def collect_prompt(own, first, second):
    near, far = swap_bit(own, "dp", 1), swap_bit(own, "dp", 2)
    last = swap_bit(near if first == 1 else far, "dp", second)
    blocks = []
    for block in (own, near, far, last):
        blocks += [block, swap_bit(block, "dp", 0)]
    return blocks[1:]


SMALL = pl.CostEstimate(flops=1, bytes_accessed=1, transcendentals=0)


def merge_kernel(even_ref, *refs):
    got, (keys_ref, values_ref, far_ref, near_ref) = refs[:3], refs[3:]
    near, far, last = 0, 1, 2
    add = lambda j, which: add_low(even_ref[j, which], got[j][which])
    keys_ref[0], keys_ref[1] = add(near, 0), add(last, 0)
    values_ref[0], values_ref[1] = add(far, 1), add(last, 1)
    far_ref[...], near_ref[...] = add(far, 0), add(near, 1)


def return_prompt(odd, even):
    got = [swap_bit(block, "dp", 0) for block in odd]
    one = jax.ShapeDtypeStruct(even.shape[2:], LOW)
    two = jax.ShapeDtypeStruct(even.shape[1:], LOW)
    keys, values, far, near = pl.pallas_call(
        merge_kernel, out_shape=[two, two, one, one], cost_estimate=SMALL
    )(even, *got[1:])
    keys, values = swap_bit(keys, "dp", 1), swap_bit(values, "dp", 2)
    last_keys = swap_bit(add_low(far, keys[1]), "dp", 2)
    last_values = swap_bit(add_low(near, values[1]), "dp", 1)
    return got[0], keys, values, last_keys, last_values


def turn(values):
    return pltpu.roll(values, HEAD // 2, 1)


def rope_kernel(pre_ref, gain_ref, scale_ref, cos_ref, sin_ref, out_ref, first_ref):
    scale, cosine, sine = scale_ref[...], cos_ref[...], sin_ref[...]
    for at in range(0, pre_ref.shape[1], HEAD):
        span = slice(at, at + HEAD)
        normed = pre_ref[:, span] * scale * gain_ref[:, span]
        out_ref[:, span] = (normed * cosine + turn(normed) * sine).astype(LOW)
    first_ref[...] = out_ref[: first_ref.shape[0]]


def rope_pass(flat, gain, scale, cosine, sine):
    rows, width = flat.shape
    part = width // 2
    wide = lambda rows: pl.BlockSpec((rows, part), lambda h: (0, h))
    return pl.pallas_call(
        rope_kernel,
        grid=(2,),
        in_specs=[wide(rows), wide(1)] + [kept_spec(a) for a in (scale, cosine, sine)],
        out_specs=[wide(rows), wide(PR_DEV)],
        out_shape=[jax.ShapeDtypeStruct((count, width), LOW) for count in (rows, PR_DEV)],
    )(flat, gain, scale, cosine, sine)


PAIR = 2


def head_spec(rows):
    return pl.BlockSpec((rows, PAIR * HEAD), lambda h: (0, h))


def kept_spec(array):
    zeros = (0,) * array.ndim
    return pl.BlockSpec(array.shape, lambda h: zeros, pipeline_mode=pl.Buffered(1))


def all_keys(own_ref, pieces, span):
    return jnp.concatenate(
        [own_ref[:PR_DEV, span]] + [p[:, span] for p in pieces] + [own_ref[PR_DEV:, span]], axis=0
    )


def turned_query(flat_ref, gain_ref, scale, cosine, sine, span):
    normed = flat_ref[:, span] * scale * gain_ref[:, span]
    return (normed * cosine + turn(normed) * sine).astype(LOW)


def softmax_rows(query, keys, bias):
    scores = dot_nt(query, keys) * HEAD ** (-0.5) + bias
    weights = jnp.exp(scores - jnp.max(scores, axis=1, keepdims=True))
    return weights * (1.0 / jnp.sum(weights, axis=1, keepdims=True))


PIECES = GROUP - 1


def attend_kernel(flat_ref, gain_ref, scale_ref, cos_ref, sin_ref, bias_ref, k_ref, v_ref, *refs):
    out_ref = refs[-1]
    bias = bias_ref[...].astype(FULL)
    scale, cosine, sine = scale_ref[...], cos_ref[...], sin_ref[...]
    for at in range(0, PAIR * HEAD, HEAD):
        span = slice(at, at + HEAD)
        query = turned_query(flat_ref, gain_ref, scale, cosine, sine, span)
        probs = softmax_rows(query, all_keys(k_ref, refs[:PIECES], span), bias)
        values = all_keys(v_ref, refs[PIECES : 2 * PIECES], span)
        out_ref[:, span] = dot_nn(probs.astype(LOW), values).astype(LOW)


def attend_specs(rows, scale, cosine, sine, bias):
    return (
        [head_spec(rows), head_spec(1)]
        + [kept_spec(a) for a in (scale, cosine, sine, bias)]
        + [head_spec(rows)] * 2
        + [head_spec(PR_DEV)] * (2 * PIECES)
    )


def attend(flat, gain, scale, cosine, sine, bias, keys, values, pieces):
    rows, width = flat.shape
    return pl.pallas_call(
        attend_kernel,
        grid=(width // HEAD // PAIR,),
        in_specs=attend_specs(rows, scale, cosine, sine, bias),
        out_specs=head_spec(rows),
        out_shape=jax.ShapeDtypeStruct((rows, width), LOW),
        compiler_params=pltpu.CompilerParams(vmem_limit_bytes=VMEM),
    )(flat, gain, scale, cosine, sine, bias, keys, values, *pieces)


def norm_parts(step, at, grad, flat_ref, gain_ref, scale_ref, inner_ref, gain_grad_ref):
    span = slice(at, at + HEAD)
    product = flat_ref[:, span] * grad
    inner = jnp.sum(product * gain_ref[:, span], axis=1, keepdims=True)
    gain_grad_ref[:, span] = jnp.sum(product * scale_ref[...], axis=0, keepdims=True)
    if at:
        inner_ref[...] += inner
    else:
        inner_ref[...] = jnp.where(step == 0, 0.0, inner_ref[...]) + inner


def attend_back_kernel(
    flat_ref, gain_ref, scale_ref, cos_ref, sin_ref, bias_ref, k_ref, v_ref, *refs
):
    back_ref = refs[2 * PIECES]
    qg_ref, inner_ref, gain_grad_ref, kg_ref, vg_ref, even_ref = refs[2 * PIECES + 1 : -4]
    odd_refs = refs[-4:]
    step = pl.program_id(0)
    bias = bias_ref[...].astype(FULL)
    scale, cosine, sine = scale_ref[...], cos_ref[...], sin_ref[...]
    prompt = PR_DEV * GROUP
    for at in range(0, PAIR * HEAD, HEAD):
        span = slice(at, at + HEAD)
        query = turned_query(flat_ref, gain_ref, scale, cosine, sine, span)
        back = back_ref[:, span]
        keys = all_keys(k_ref, refs[:PIECES], span)
        values = all_keys(v_ref, refs[PIECES : 2 * PIECES], span)
        probs = softmax_rows(query, keys, bias)
        prob_grad = dot_nt(back, values)
        value_grad = dot_tn(probs.astype(LOW), back)
        row_dot = jnp.sum(probs * prob_grad, axis=1, keepdims=True)
        score_grad = (probs * (prob_grad - row_dot)).astype(LOW)
        query_grad = dot_nn(score_grad, keys) * HEAD ** (-0.5)
        key_grad = dot_tn(score_grad, query) * HEAD ** (-0.5)
        query_grad = query_grad * cosine - turn(query_grad) * sine
        qg_ref[:, span] = query_grad
        norm_parts(step, at, query_grad, flat_ref, gain_ref, scale_ref, inner_ref, gain_grad_ref)
        for which, grad, own_ref in ((0, key_grad, kg_ref), (1, value_grad, vg_ref)):
            own_ref[:PR_DEV, span] = grad[:PR_DEV]
            own_ref[PR_DEV:, span] = grad[prompt:]
            for j in range(1, GROUP):
                to = odd_refs[j // 2] if j % 2 else even_ref.at[j // 2 - 1]
                to[which, :, span] = grad[j * PR_DEV : (j + 1) * PR_DEV].astype(LOW)


def attend_back(flat, gain, scale, cosine, sine, bias, keys, values, pieces, back):
    rows, width = flat.shape
    wide = jax.ShapeDtypeStruct((rows, width), FULL)
    both = pl.BlockSpec((3, 2, PR_DEV, PAIR * HEAD), lambda h: (0, 0, 0, h))
    return pl.pallas_call(
        attend_back_kernel,
        grid=(width // HEAD // PAIR,),
        in_specs=attend_specs(rows, scale, cosine, sine, bias) + [head_spec(rows)],
        out_specs=[
            head_spec(rows),
            pl.BlockSpec((rows, 1), lambda h: (0, 0)),
            head_spec(1),
            head_spec(rows),
            head_spec(rows),
            both,
        ]
        + [pl.BlockSpec((2, PR_DEV, PAIR * HEAD), lambda h: (0, 0, h))] * 4,
        out_shape=[
            wide,
            jax.ShapeDtypeStruct((rows, 1), FULL),
            jax.ShapeDtypeStruct((1, width), FULL),
            wide,
            wide,
            jax.ShapeDtypeStruct((3, 2, PR_DEV, width), LOW),
        ]
        + [jax.ShapeDtypeStruct((2, PR_DEV, width), LOW)] * 4,
        compiler_params=pltpu.CompilerParams(vmem_limit_bytes=VMEM),
        cost_estimate=pl.CostEstimate(
            flops=20 * 10**9, bytes_accessed=40 * 10**6, transcendentals=4 * 10**6
        ),
    )(flat, gain, scale, cosine, sine, bias, keys, values, *pieces, back)


def key_back_kernel(*refs):
    kg_ref, vg_ref, flat_ref, gain_ref, scale_ref, cos_ref, sin_ref = refs[:7]
    got, keys, values, last_keys, last_values = refs[7:12]
    out_ref, inner_ref, gain_grad_ref, value_ref = refs[12:]
    step = pl.program_id(0)
    for at in range(0, PAIR * HEAD, HEAD):
        span = slice(at, at + HEAD)
        grads = []
        for which, own_ref, near, last in ((0, kg_ref, keys, last_keys), (1, vg_ref, values, last_values)):
            first = own_ref[:PR_DEV, span] + got[which, :, span].astype(FULL)
            first = first + near[0, :, span].astype(FULL) + last[:, span].astype(FULL)
            grads.append(jnp.concatenate([first, own_ref[PR_DEV:, span]], axis=0))
        key_grad = grads[0] * cos_ref[...] - turn(grads[0]) * sin_ref[...]
        out_ref[:, span] = key_grad
        norm_parts(step, at, key_grad, flat_ref, gain_ref, scale_ref, inner_ref, gain_grad_ref)
        value_ref[:, span] = grads[1].astype(LOW)


def key_back(key_grad, value_grad, flat, gain, scale, cosine, sine, returned):
    rows, width = flat.shape
    columns = PAIR * HEAD
    return pl.pallas_call(
        key_back_kernel,
        grid=(width // columns,),
        in_specs=[head_spec(rows)] * 3
        + [head_spec(1)]
        + [kept_spec(a) for a in (scale, cosine, sine)]
        + [pl.BlockSpec((2, PR_DEV, columns), lambda h: (0, 0, h))]
        + [pl.BlockSpec((1, PR_DEV, columns), lambda h: (0, 0, h))] * 2
        + [head_spec(PR_DEV)] * 2,
        out_specs=[
            head_spec(rows),
            pl.BlockSpec((rows, 1), lambda h: (0, 0)),
            head_spec(1),
            head_spec(rows),
        ],
        out_shape=[
            jax.ShapeDtypeStruct((rows, width), FULL),
            jax.ShapeDtypeStruct((rows, 1), FULL),
            jax.ShapeDtypeStruct((1, width), FULL),
            jax.ShapeDtypeStruct((rows, width), LOW),
        ],
        cost_estimate=SMALL,
    )(key_grad, value_grad, flat, gain, scale, cosine, sine, *returned)


def pack_kernel(query, key, value, out, rest, packed):
    at = 0
    for ref in (query, key, value):
        packed[at : at + ref.shape[0]] = ref[...]
        at += ref.shape[0]
    packed[at : at + out.shape[1]] = out[...].T
    packed[at + out.shape[1] :] = rest[...]


def pack_weights(w_query, w_key, w_value, w_out, rest):
    rows = 4 * w_query.shape[0] + rest.shape[0]
    return pl.pallas_call(
        pack_kernel, out_shape=jax.ShapeDtypeStruct((rows, w_query.shape[1]), LOW)
    )(w_query, w_key, w_value, w_out, rest)


def unpack_kernel(first, blocks_ref, packed, out, held, sems):
    width = packed.shape[2]
    parts = out.shape[1] // width
    rows = (packed.shape[1] - first) // parts
    count = packed.shape[0]
    place = lambda i: pl.ds(i * rows, rows)
    loads = [
        pltpu.make_async_copy(
            packed.at[blocks_ref[i], pl.ds(first + j * rows, rows)],
            held.at[place(i), pl.ds(j * width, width)],
            sems.at[i * parts + j],
        )
        for i in range(count)
        for j in range(parts)
    ]
    stores = [
        pltpu.make_async_copy(held.at[place(i)], out.at[place(i)], sems.at[count * parts + i])
        for i in range(count)
    ]
    for one in loads:
        one.start()
    for i, store in enumerate(stores):
        for j in range(parts):
            loads[i * parts + j].wait()
        store.start()
    for store in stores:
        store.wait()


def unpack_rows(packed, blocks, first, width):
    count = packed.shape[0]
    parts = width // packed.shape[2]
    rows = (packed.shape[1] - first) // parts
    return pl.pallas_call(
        lambda *refs: unpack_kernel(first, *refs),
        in_specs=[pl.BlockSpec(memory_space=pltpu.SMEM), pl.BlockSpec(memory_space=pl.ANY)],
        out_specs=pl.BlockSpec(memory_space=pl.ANY),
        out_shape=jax.ShapeDtypeStruct((count * rows, width), LOW),
        scratch_shapes=[
            pltpu.VMEM((count * rows, width), LOW),
            pltpu.SemaphoreType.DMA((count * parts + count,)),
        ],
        compiler_params=pltpu.CompilerParams(vmem_limit_bytes=VMEM),
    )(blocks, packed)


def load_packed(gathered, places, block, held, sems):
    copies = [
        pltpu.make_async_copy(
            gathered.at[:, pl.ds(place * block, block)], held.at[k], sems.at[k]
        )
        for k, place in enumerate(places)
    ]
    for one in copies:
        one.start()
    return copies


def held_pack(gathered, places, block):
    count, columns = gathered.shape[0], gathered.shape[2]
    return [
        pltpu.VMEM((len(places), count, block, columns), LOW),
        pltpu.SemaphoreType.DMA((len(places),)),
    ]


def project_kernel(places, block, heads, rows_ref, gathered, *refs):
    outs, firsts, (held, sems) = refs[: len(places)], refs[len(places) : -2], refs[-2:]
    copies = load_packed(gathered, places, block, held, sems)
    rows = rows_ref[...]
    for k, (one, out) in enumerate(zip(copies, outs)):
        one.wait()
        out[...] = dot_nn(rows, held[k].reshape(-1, out.shape[1])).astype(out.dtype)
    for first, k in zip(firsts, heads):
        first[...] = outs[k][: first.shape[0]]


def project(rows, gathered, block, places, roundings, heads=()):
    count, width = rows.shape
    columns = gathered.shape[2]
    outs = [jax.ShapeDtypeStruct((count, columns), rounding) for rounding in roundings]
    outs += [jax.ShapeDtypeStruct((PR_DEV, columns), roundings[k]) for k in heads]
    fixed = lambda a: pl.BlockSpec(a.shape, lambda i: (0, 0))
    return pl.pallas_call(
        lambda *refs: project_kernel(places, block, heads, *refs),
        grid=(1,),
        in_specs=[fixed(rows), pl.BlockSpec(memory_space=pl.ANY)],
        out_specs=[fixed(out) for out in outs],
        out_shape=outs,
        scratch_shapes=held_pack(gathered, places, block),
        compiler_params=pltpu.CompilerParams(vmem_limit_bytes=VMEM),
        cost_estimate=pl.CostEstimate(
            flops=2 * count * width * columns * len(places),
            bytes_accessed=2 * width * columns * len(places) + 8 * count * columns,
            transcendentals=0,
        ),
    )(rows, gathered)


def pack_specs(gathered, places, steps, at):
    count, width = gathered.shape[0] // steps, gathered.shape[2]
    block = at
    return [
        pl.BlockSpec((count, block, width), lambda i, place=place: (i, place, 0))
        for place in places
    ]


def project_back_kernel(mats, *refs):
    out = refs[-1]
    total = None
    for rows_ref, mat in zip(refs[:mats], refs[mats:-1]):
        part = dot_nt(rows_ref[...], mat[...].reshape(-1, mat.shape[2]))
        total = part if total is None else total + part
    out[...] = total


def project_back(rows, gathered, block, places):
    count, columns = rows[0].shape
    width = gathered.shape[0] * block
    steps = 4 if len(places) > 1 else 2
    fixed = pl.BlockSpec((count, columns), lambda i: (0, 0), pipeline_mode=pl.Buffered(1))
    return pl.pallas_call(
        lambda *refs: project_back_kernel(len(places), *refs),
        grid=(steps,),
        in_specs=[fixed] * len(rows) + pack_specs(gathered, places, steps, block),
        out_specs=pl.BlockSpec((count, width // steps), lambda i: (0, i)),
        out_shape=jax.ShapeDtypeStruct((count, width), FULL),
        compiler_params=pltpu.CompilerParams(vmem_limit_bytes=VMEM),
        cost_estimate=pl.CostEstimate(
            flops=2 * count * width * columns * len(places),
            bytes_accessed=2 * width * columns * len(places) + 4 * count * width,
            transcendentals=0,
        ),
    )(*rows, *[gathered] * len(places))


def pre_kernel(core_ref, *refs):
    inputs, outs = refs[:11], refs[11:]
    step = pl.program_id(0)
    columns = inputs[0].shape[1]
    parts = []
    for flat, grad, gain, scale, inner in (inputs[:5], inputs[5:10]):
        scaled = scale[...]
        mean = inner[...] * (1.0 / (HEADS * HEAD))
        parts.append(
            (
                scaled * gain[...] * grad[...] - flat[...] * (scaled * scaled * scaled) * mean
            ).astype(LOW)
        )
    outs[0][...], outs[1][...] = parts

    @pl.when(step != core_ref[0])
    def _():
        for j, part in enumerate((*parts, inputs[10][...])):
            outs[2][:, j * columns : (j + 1) * columns] = part


def pre_grads_pass(core, query, key, value):
    rows, width = value.shape
    columns = width // 2
    half = lambda rows: pl.BlockSpec((rows, columns), lambda h: (0, h))
    side = [half(rows), half(rows), half(1)] + [pl.BlockSpec((rows, 1), lambda h: (0, 0))] * 2
    return pl.pallas_call(
        pre_kernel,
        grid=(2,),
        in_specs=[pl.BlockSpec(memory_space=pltpu.SMEM)] + side + side + [half(rows)],
        out_specs=[half(rows), half(rows), pl.BlockSpec((rows, 3 * columns), lambda h: (0, 0))],
        out_shape=[jax.ShapeDtypeStruct((rows, width), LOW)] * 2
        + [jax.ShapeDtypeStruct((rows, 3 * columns), LOW)],
    )(core, *query, *key, value)


def weight_kernel(chip_ref, core_ref, *refs):
    normed, normed_got, back, back_got, query, key, value, got, context, context_got = refs[:10]
    out_ref, right_ref, left_ref, pre_both, context_both = refs[10:]
    rows, columns = query.shape

    @pl.when(pl.program_id(0) == 0)
    def _():
        for j, part in enumerate((query, key, value)):
            pre_both[:rows, j * columns : (j + 1) * columns] = part[...]
        pre_both[rows:] = got[...]
        context_both[:rows] = context[...]
        context_both[rows:] = context_got[...]

    left = jnp.concatenate([normed[...], normed_got[...]], axis=0)
    out_ref[0, :, : 3 * columns] = dot_tn(left, pre_both[...]).astype(LOW)
    left = jnp.concatenate([back[...], back_got[...]], axis=0)
    out_ref[0, :, 3 * columns :] = dot_tn(left, context_both[...]).astype(LOW)

    @pl.when(pl.program_id(0) == HOPS.index(4))
    def _():
        right_ref[...] = out_ref[0, :, : 2 * columns]
        left_ref[...] = out_ref[0, :, 2 * columns :]


def weight_grads(chips, core, normed, back, pre_grads, got, context, context_got):
    rows, width = normed[0].shape
    columns = context_got.shape[1]
    count = chips.shape[0]
    block = width // count
    tall = pl.BlockSpec((rows, block), lambda i, chip, core: (0, chip[i]))
    mine = pl.BlockSpec((rows, columns), lambda i, chip, core: (0, core[0]))
    fixed = lambda a: pl.BlockSpec(a.shape, lambda i, chip, core: (0, 0))
    return pl.pallas_call(
        weight_kernel,
        grid_spec=pltpu.PrefetchScalarGridSpec(
            num_scalar_prefetch=2,
            grid=(count,),
            in_specs=[tall] * 4 + [mine] * 3 + [fixed(got), mine, fixed(context_got)],
            out_specs=[pl.BlockSpec((1, block, 4 * columns), lambda i, chip, core: (i, 0, 0))]
            + [pl.BlockSpec((block, 2 * columns), lambda i, chip, core: (0, 0))] * 2,
            scratch_shapes=[
                pltpu.VMEM((2 * rows, 3 * columns), LOW),
                pltpu.VMEM((2 * rows, columns), LOW),
            ],
        ),
        out_shape=[jax.ShapeDtypeStruct((count, block, 4 * columns), LOW)]
        + [jax.ShapeDtypeStruct((block, 2 * columns), LOW)] * 2,
        compiler_params=pltpu.CompilerParams(vmem_limit_bytes=VMEM),
        cost_estimate=pl.CostEstimate(
            flops=16 * rows * width * columns,
            bytes_accessed=2 * (4 * rows * width + 8 * rows * columns + 4 * width * columns),
            transcendentals=0,
        ),
    )(chips, core, *normed, *back, *pre_grads, got, context, context_got)


def ring_weights(blocks, right, left, fillers):
    part = lambda hop: blocks[HOPS.index(hop)]
    cut = blocks.shape[2] // 2
    right, left = ahead(right), behind(left)
    fillers.next(left)
    outward, inward = part(3), part(-3)
    right = jnp.concatenate([add_low(outward[:, :cut], right), outward[:, cut:]], axis=1)
    left = jnp.concatenate([inward[:, :cut], add_low(inward[:, cut:], left)], axis=1)
    right, left = together(right, left)
    right, left = ahead(right), behind(left)
    fillers.next(left)
    token = left
    for hop in (2, 1):
        right, left = together(add_low(part(hop), right), add_low(part(-hop), left))
        right, left = ahead(right), behind(left)
        fillers.next(left)
        token = left if hop == 2 else token
    return (blocks, right, left), token


def sum_kernel(core_ref, blocks_ref, right_ref, left_ref, own_ref, sent_ref):
    rows = own_ref.shape[0]
    for k, out in enumerate((own_ref, sent_ref)):
        side = core_ref[0] if k == 0 else 1 - core_ref[0]
        span = pl.ds(pl.multiple_of(side * rows, rows), rows)
        out[...] = (
            blocks_ref[0, span].astype(FULL)
            + right_ref[span].astype(FULL)
            + left_ref[span].astype(FULL)
        )


def sum_weights(core, blocks, right, left):
    rows, width = right.shape
    whole = pl.BlockSpec((rows, width), lambda i: (0, 0))
    half = pl.BlockSpec((rows // 2, width), lambda i: (0, 0))
    return pl.pallas_call(
        sum_kernel,
        grid=(1,),
        in_specs=[
            pl.BlockSpec(memory_space=pltpu.SMEM),
            pl.BlockSpec((1, rows, width), lambda i: (HOPS.index(0), 0, 0)),
            whole,
            whole,
        ],
        out_specs=[half, half],
        out_shape=[jax.ShapeDtypeStruct((rows // 2, width), FULL)] * 2,
    )(core, blocks, right, left)


def place_kernel(core_ref, own_ref, got_ref, *outs):
    columns = own_ref.shape[1] // 4
    first = core_ref[0] == 0
    for k, out in enumerate(outs):
        span = slice(k * columns, (k + 1) * columns)
        own, got = own_ref[:, span], got_ref[:, span]
        left, right = jnp.where(first, own, got), jnp.where(first, got, own)
        if k < 3:
            out[:, :columns], out[:, columns:] = left, right
        else:
            out[:columns], out[columns:] = left.T, right.T


def place_weights(core, own, got):
    rows, width = own.shape
    columns = width // 2
    shapes = [(rows, columns)] * 3 + [(columns, rows)]
    return pl.pallas_call(
        place_kernel,
        grid=(1,),
        in_specs=[pl.BlockSpec(memory_space=pltpu.SMEM)]
        + [pl.BlockSpec((rows, width), lambda i: (0, 0))] * 2,
        out_specs=[pl.BlockSpec(shape, lambda i: (0, 0)) for shape in shapes],
        out_shape=[jax.ShapeDtypeStruct(shape, FULL) for shape in shapes],
    )(core, own, got)


def join_kernel(parts, side_ref, *refs):
    out_ref = refs[-1]
    rows = out_ref.shape[0] // 2
    for k, side in ((0, side_ref[0]), (1, 1 - side_ref[0])):
        total = refs[k * parts][...].astype(FULL)
        for j in range(1, parts):
            total = total + refs[k * parts + j][...].astype(FULL)
        out_ref[pl.ds(pl.multiple_of(side * rows, rows), rows)] = total


def join_halves(side, own, other):
    rows, width = own[0].shape
    columns = width // 2
    half = pl.BlockSpec((rows, columns), lambda i: (0, i))
    return pl.pallas_call(
        lambda *refs: join_kernel(len(own), *refs),
        grid=(2,),
        in_specs=[pl.BlockSpec(memory_space=pltpu.SMEM)] + [half] * (2 * len(own)),
        out_specs=pl.BlockSpec((2 * rows, columns), lambda i: (0, i)),
        out_shape=jax.ShapeDtypeStruct((2 * rows, width), FULL),
    )(side, *own, *other)


def expert_kernel(
    rows_ref, back_ref, gate_ref, wg0, wg1, wu0, wu1, wd0, wd1, grad_ref, h0, h1, g0, g1, u0, u1
):
    rows = rows_ref[...]
    back = back_ref[...]
    gate = gate_ref[...]
    total = None
    for wg, wu, wd, h, g, u in ((wg0, wu0, wd0, h0, g0, u0), (wg1, wu1, wd1, h1, g1, u1)):
        gate_pre = dot_nn(rows, wg[...])
        up_pre = dot_nn(rows, wu[...])
        hidden_grad = gate * dot_nt(back, wd[...])
        sig = 1.0 / (1.0 + jnp.exp(-gate_pre))
        act = gate_pre * sig
        h[...] = (gate * (act * up_pre)).astype(LOW)
        gate_grad = (hidden_grad * up_pre * (sig * (1.0 + gate_pre * (1.0 - sig)))).astype(LOW)
        up_grad = (hidden_grad * act).astype(LOW)
        g[...] = gate_grad
        u[...] = up_grad
        part = dot_nt(gate_grad, wg[...]) + dot_nt(up_grad, wu[...])
        total = part if total is None else total + part
    grad_ref[...] = total.astype(LOW)


def expert_pass(rows, back, gate, gate_mats, up_mats, down_mats):
    count, width = rows.shape
    hidden = gate_mats[0].shape[1]
    tile = 256
    whole = lambda array: pl.BlockSpec(
        array.shape, lambda i: (0, 0), pipeline_mode=pl.Buffered(1)
    )
    tall = lambda columns: pl.BlockSpec((tile, columns), lambda i: (i, 0))
    mats = [*gate_mats, *up_mats, *down_mats]
    flops = 2 * 5 * count * width * hidden * 2
    return pl.pallas_call(
        expert_kernel,
        grid=(count // tile,),
        in_specs=[tall(width), tall(width), tall(1)] + [whole(m) for m in mats],
        out_specs=[tall(width)] + [tall(hidden)] * 6,
        out_shape=[jax.ShapeDtypeStruct((count, width), LOW)]
        + [jax.ShapeDtypeStruct((count, hidden), LOW)] * 6,
        compiler_params=pltpu.CompilerParams(vmem_limit_bytes=VMEM),
        cost_estimate=pl.CostEstimate(
            flops=flops,
            bytes_accessed=2 * (3 * count * width + 6 * count * hidden + 6 * width * hidden),
            transcendentals=2 * count * hidden,
        ),
    )(rows, back, gate, *mats)


def chunk_kernel(pieces, held, at, splits, gate_ref, *refs):
    piece_refs, refs = refs[:pieces], refs[pieces:]
    back_ref, mats, refs = refs[0], refs[1:7], refs[7 + held :]
    grad_outs, refs = refs[: len(splits)], refs[len(splits) :]
    rows_out, outs = refs[0], refs[1:7]
    rows, back, wide, wd, hidden, both_grads, grads, sems = refs[7:]
    count = rows.shape[0]
    part = wd.shape[1]
    slab = wide.shape[0] // 4
    across = lambda k, half: pl.ds((2 * k + half) * part, part)
    place = pl.ds(at * count, count)
    copy = pltpu.make_async_copy
    load_rows, start = [], 0
    for piece in piece_refs:
        span = pl.ds(start, piece.shape[0])
        load_rows.append(copy(piece, rows.at[span], sems.at[len(load_rows)]))
        start += piece.shape[0]
    load_back = copy(back_ref.at[place], back, sems.at[6])
    loads = []
    for half in range(2):
        places = [wide.at[:, across(0, half)], wide.at[:, across(1, half)], wd.at[half]]
        loads.append(
            [copy(mats[2 * k + half], to, sems.at[7 + 3 * half + k]) for k, to in enumerate(places)]
        )
    for one in load_rows + loads[0][:2] + [load_back] + loads[0][2:] + loads[1]:
        one.start()
    gate = gate_ref[...]
    for one in load_rows:
        one.wait()
    stores = [copy(rows, rows_out.at[place], sems.at[13])]
    stores[0].start()
    for half in range(2):
        columns = pl.ds(half * part, part)
        loads[half][0].wait()
        gate_pre = dot_nn(rows[...], wide[:, across(0, half)])
        loads[half][1].wait()
        up_pre = dot_nn(rows[...], wide[:, across(1, half)])
        if half == 0:
            load_back.wait()
        loads[half][2].wait()
        hidden_grad = gate * dot_nt(back[...], wd[half])
        sig = 1.0 / (1.0 + jnp.exp(-gate_pre))
        act = gate_pre * sig
        hidden[:, columns] = (gate * (act * up_pre)).astype(LOW)
        both_grads[:, across(0, half)] = (
            hidden_grad * up_pre * (sig * (1.0 + gate_pre * (1.0 - sig)))
        ).astype(LOW)
        both_grads[:, across(1, half)] = (hidden_grad * act).astype(LOW)
    for half in range(2):
        held_in = (
            hidden.at[:, pl.ds(half * part, part)],
            both_grads.at[:, across(0, half)],
            both_grads.at[:, across(1, half)],
        )
        for k, source in enumerate(held_in):
            stores.append(copy(source, outs[2 * k + half].at[place], sems.at[14 + 3 * half + k]))
            stores[-1].start()

    @pl.loop(0, 4)
    def _(j):
        span = pl.ds(pl.multiple_of(j * slab, slab), slab)
        grads[:, span] = dot_nt(both_grads[...], wide[span]).astype(LOW)

    start = 0
    for k, (split, to) in enumerate(zip(splits, grad_outs)):
        stores.append(copy(grads.at[pl.ds(start, split)], to, sems.at[20 + k]))
        stores[-1].start()
        start += split
    for one in stores:
        one.wait()


def expert_chunk(pieces, back, gate, mats, at, held, splits):
    all_rows, width = back.shape
    part = mats[0].shape[1]
    hidden = 2 * part
    count = sum(piece.shape[0] for piece in pieces)
    anywhere = pl.BlockSpec(memory_space=pl.ANY)
    held = [] if held is None else list(held)
    args = [gate, *pieces, back, *mats, *held]
    out = pl.pallas_call(
        lambda *refs: chunk_kernel(len(pieces), len(held), at, splits, *refs),
        grid=(1,),
        in_specs=[pl.BlockSpec((count, 1), lambda j: (at, 0))] + [anywhere] * (len(args) - 1),
        out_specs=[anywhere] * (len(splits) + 7),
        out_shape=[jax.ShapeDtypeStruct((split, width), LOW) for split in splits]
        + [jax.ShapeDtypeStruct((all_rows, width), LOW)]
        + [jax.ShapeDtypeStruct((all_rows, part), LOW)] * 6,
        scratch_shapes=[
            pltpu.VMEM((count, width), LOW),
            pltpu.VMEM((count, width), LOW),
            pltpu.VMEM((width, 2 * hidden), LOW),
            pltpu.VMEM((2, part, width), LOW),
            pltpu.VMEM((count, hidden), LOW),
            pltpu.VMEM((count, 2 * hidden), LOW),
            pltpu.VMEM((count, width), LOW),
            pltpu.SemaphoreType.DMA((23,)),
        ],
        input_output_aliases={
            len(args) - len(held) + k: len(splits) + k for k in range(len(held))
        },
        compiler_params=pltpu.CompilerParams(vmem_limit_bytes=VMEM),
        cost_estimate=pl.CostEstimate(
            flops=2 * 5 * count * width * hidden,
            bytes_accessed=2 * (4 * count * width + 3 * count * hidden + 3 * width * hidden),
            transcendentals=count * hidden,
        ),
    )(*args)
    return out[: len(splits)], out[len(splits) :]


def mixed_kernel(chip_ref, same_ref, cross_ref, core_ref, *refs):
    first_ref, second_ref, out_ref = refs[4:]
    rows = out_ref.shape[2]
    first, second = (
        jnp.concatenate([refs[k][...], refs[k + 1][...]], axis=0) for k in (0, 2)
    )
    result = (dot_nn(first, first_ref[...]) + dot_nn(second, second_ref[...])).astype(LOW)
    out_ref[0, core_ref[0]] = result[:rows]
    out_ref[0, 1 - core_ref[0]] = result[rows:]


def mixed_pass(h0, h1, down_mats, chips, core):
    count, columns = h0.shape
    width = down_mats[0].shape[1]
    rows = count // len(LAYOUT)
    places = [
        jnp.array([LAYOUT.index((hop, cross)) for hop in HOPS], jnp.int32) for cross in (0, 1)
    ]
    once = pl.Buffered(1)
    fixed = lambda m: pl.BlockSpec(m.shape, lambda i, *tables: (0, 0), pipeline_mode=once)
    block = lambda k: pl.BlockSpec((rows, columns), lambda i, *tables: (tables[k][i], 0))
    out = pl.pallas_call(
        mixed_kernel,
        grid_spec=pltpu.PrefetchScalarGridSpec(
            num_scalar_prefetch=4,
            grid=(len(HOPS),),
            in_specs=[block(1), block(2), block(1), block(2)] + [fixed(m) for m in down_mats],
            out_specs=pl.BlockSpec(
                (1, 2, rows, width), lambda i, chip, *tables: (chip[i], 0, 0, 0)
            ),
        ),
        out_shape=jax.ShapeDtypeStruct((len(HOPS), 2, rows, width), LOW),
        compiler_params=pltpu.CompilerParams(vmem_limit_bytes=VMEM),
        cost_estimate=pl.CostEstimate(
            flops=4 * count * columns * width,
            bytes_accessed=2 * (count * (2 * columns + width) + 2 * columns * width),
            transcendentals=0,
        ),
    )(chips, *places, core, h0, h0, h1, h1, *down_mats)
    return out.reshape(count, width)


def expert_ring(rows, back, gate, mats, waiting):
    size = rows.shape[0]
    cut = size // 2
    swap = lambda block: swap_bit(block, "dp", 0)
    chunk = lambda pieces, at, held, *splits: expert_chunk(
        pieces, back, gate, mats, at, held, splits
    )
    rows, pair = together(rows, swap(rows))
    left, right = ahead(rows), behind(rows)
    parts, crossed = cut_rows(waiting, 4), []
    same, cross = {}, {}
    cross_over = lambda token: crossed.append(swap_tensor(after(parts[len(crossed)], token)))
    cross_over(pair)
    (same[0], cross[0]), held = chunk([rows, pair], 6, None, size, size)
    left, right, same[0] = together(left, right, same[0])
    pieces, got = [left, right], [swap(left), swap(right)]
    left, right = ahead(left), behind(right)
    pieces[0], crossed[0] = together(pieces[0], crossed[0])
    cross_over(pieces[0])
    (same[1],), held = chunk(pieces, 7, held, 2 * size)
    left, right, same[1] = together(left, right, same[1])
    pieces, got = [left, right, *got], [swap(left), swap(right)]
    left, right = ahead(left), behind(right)
    pieces[0], crossed[1] = together(pieces[0], crossed[1])
    cross_over(pieces[0])
    (same[2], cross[1]), held = chunk(pieces, 0, held, 2 * size, 2 * size)
    left, right, same[2] = together(left, right, same[2])
    pieces, got = [left, right, *got], [swap(left), swap(right)]
    left, right = ahead(left[:cut]), behind(right[cut:])
    pieces[0], crossed[2] = together(pieces[0], crossed[2])
    cross_over(pieces[0])
    (same[3], cross[2]), held = chunk(pieces, 1, held, 2 * size, 2 * size)
    left, right, crossed[3], same[3] = together(left, right, crossed[3], same[3])
    pieces = [left, right, swap(left), swap(right), *got]
    (same[4], cross[4], cross[3]), held = chunk(pieces, 2, held, size, size, 2 * size)
    waiting = jnp.concatenate(crossed, axis=0)
    return same, cross, held, waiting


def body(
    inputs,
    attn_gain,
    w_query,
    w_key,
    w_value,
    query_gain,
    key_gain,
    w_out,
    moe_gain,
    w_gate,
    w_up,
    w_down,
    experts,
    gates,
    segments,
    gaps,
    cotangent,
):
    dp_count = lax.axis_size("dp")
    dp_index = lax.axis_index("dp")
    side = lax.axis_index("tensor")
    token_count, model_width = inputs.shape
    half_count = token_count // 2
    top_count = experts.shape[1]
    expert_count = w_gate.shape[0] * dp_count
    capacity = token_count * top_count * dp_count * 9 // (8 * expert_count)
    prompt_length = PR_DEV * GROUP
    column_total = HEADS * HEAD
    block = w_query.shape[0]
    local_width = w_query.shape[1]
    local_heads = local_width // HEAD

    def own_half(array):
        return lax.dynamic_slice_in_dim(array, side * half_count, half_count, axis=0)

    def other_half(array):
        return lax.dynamic_slice_in_dim(array, (1 - side) * half_count, half_count, axis=0)

    def both_halves(own, other):
        first = side == 0
        return jnp.concatenate(
            [jnp.where(first, own, other), jnp.where(first, other, own)], axis=0
        )

    gate_mats = (w_gate[0], swap_tensor(w_gate[0]))
    up_mats = (w_up[0], swap_tensor(w_up[0]))

    ring = dp_count == 2 * len(RING)

    gates_high = gates.astype(LOW)
    gates_low = (gates - gates_high.astype(FULL)).astype(LOW)
    routing = jnp.concatenate([experts.astype(LOW).T, gates_high.T, gates_low.T], axis=1)
    routing = jnp.pad(routing, ((0, 0), (0, local_width - 3 * token_count)))
    gains = jnp.concatenate([attn_gain, moe_gain, query_gain, key_gain])
    gains = jnp.pad(gains[None], ((0, 7), (0, local_width - 4 * block)))
    packed = pack_weights(
        w_query, w_key, w_value, w_out, jnp.concatenate([gains, routing], axis=0)
    )
    gathered = lax.all_gather(packed, "dp", axis=0, tiled=False)
    cotangent_half = own_half(cotangent)
    gathered_back = lax.all_gather(cotangent_half.astype(LOW), "dp", axis=0, tiled=False)
    core = dp_index % 2
    tokens_f = inputs.astype(FULL)
    prompt_pos = dp_index % GROUP * PR_DEV + jnp.arange(PR_DEV, dtype=jnp.int32)
    later_pos = cont_positions(segments[0], gaps[0], prompt_length)
    positions = jnp.concatenate([prompt_pos, later_pos], axis=0)
    cosine, sine = rope_tables(positions, HEAD)
    sine = jnp.where(jnp.arange(HEAD) < HEAD // 2, -sine, sine)
    prompt_query = jnp.arange(token_count, dtype=jnp.int32) < PR_DEV
    prompt_at = jnp.arange(prompt_length, dtype=jnp.int32)
    prompt_keypos = ((dp_index % GROUP) ^ (prompt_at // PR_DEV)) * PR_DEV + prompt_at % PR_DEV
    allowed_prompt = (~prompt_query)[:, None] | (prompt_keypos[None, :] <= positions[:, None])
    query_segment = jnp.concatenate([jnp.full((PR_DEV,), -1, jnp.int32), segments[0]], axis=0)
    allowed_cont = (query_segment[:, None] == segments[0][None, :]) & (
        later_pos[None, :] <= positions[:, None]
    )
    allowed = jnp.concatenate([allowed_prompt, allowed_cont], axis=1)
    bias = jnp.where(allowed, 0.0, -1e30).astype(LOW)
    gathered, cosine, sine, bias, *early = together(
        gathered, cosine, sine, bias, gate_mats[1], up_mats[1]
    )
    gate_mats, up_mats = (gate_mats[0], early[0]), (up_mats[0], early[1])
    rest = gathered[:, 4 * block : 4 * block + 16]
    gain_rows = rest[:, 0].astype(FULL)
    gain_one, gain_two, gain_q, gain_k = (
        gain_rows[:, j * block : (j + 1) * block].reshape(-1) for j in range(4)
    )
    gain_query_local = lax.dynamic_slice_in_dim(gain_q, side * local_width, local_width)
    gain_key_local = lax.dynamic_slice_in_dim(gain_k, side * local_width, local_width)

    names, *parts = (
        rest[:, 8:, j * token_count : (j + 1) * token_count] for j in range(3)
    )
    weights = parts[0].astype(FULL) + parts[1].astype(FULL)
    named = names == dp_index.astype(LOW)
    picked = jnp.sum(named.astype(FULL), axis=1)
    weight = jnp.sum(jnp.where(named, weights, 0.0), axis=1)
    order = jnp.arange(token_count, dtype=jnp.int32)
    earlier = (order[:, None] < order[None, :]).astype(LOW)
    within = dot_nn(picked.astype(LOW), earlier)
    per_row = jnp.sum(picked, axis=1)
    rows_order = jnp.arange(dp_count, dtype=jnp.int32)
    ahead = jnp.sum(
        jnp.where(rows_order[None, :] < rows_order[:, None], per_row[None, :], 0.0), axis=1
    )
    kept = (picked > 0.0) & (within + ahead[:, None] < capacity)
    weight = jnp.where(kept, weight, 0.0)
    weight = lax.dynamic_slice_in_dim(weight, side * half_count, half_count, axis=1)
    if ring:
        blocks, chips = ring_blocks(dp_index), ring_chips(dp_index, HOPS)
        weight = weight[blocks]
    weight = weight.reshape(-1, 1)

    normed_b = rms_norm(tokens_f, gain_one).astype(LOW)
    query_flat, key_flat, values_b, value_prompt = project(
        normed_b, gathered, block, (0, 1, 2), (FULL, FULL, LOW), (2,)
    )
    key_sq = jnp.sum(key_flat * key_flat, axis=1)
    key_sq, value_prompt = together(key_sq, value_prompt)
    value_pieces = collect_prompt(value_prompt, 1, 2)
    query_sq, key_sq = lax.psum(
        (jnp.sum(query_flat * query_flat, axis=1), key_sq), "tensor"
    )
    query_sq, down_mat = lax.optimization_barrier((query_sq, w_down[0]))
    down_mats = (down_mat, swap_tensor(down_mat))
    query_scale = lax.rsqrt(query_sq / column_total + EPSILON)[:, None]
    key_scale = lax.rsqrt(key_sq / column_total + EPSILON)[:, None]
    keys_b, key_prompt = rope_pass(key_flat, gain_key_local[None], key_scale, cosine, sine)
    pieces = (*collect_prompt(key_prompt, 2, 1), *value_pieces)
    turned_by = (gain_query_local[None], query_scale, cosine, sine, bias)
    context_b = attend(query_flat, *turned_by, keys_b, values_b, pieces)
    attn_part = project_back([context_b], gathered, block, (3,))
    attn_part, late, weight = together(attn_part, down_mats[1], weight)
    down_mats = (down_mats[0], late)
    mats = (*gate_mats, *up_mats, *down_mats)
    attn_other = swap_tensor(other_half(attn_part).astype(LOW))
    gathered_back = after(gathered_back, attn_part)
    if ring:
        back_rows = unpack_rows(gathered_back, blocks, 0, model_width)
    else:
        back_rows = gathered_back.reshape(-1, model_width)
    attn_other, back_rows, weight = together(attn_other, back_rows, weight)
    hidden_state = own_half(tokens_f) + own_half(attn_part) + attn_other.astype(FULL)
    normed_two_b = rms_norm(hidden_state, gain_two).astype(LOW)

    low_tn = lambda left, right: dot_tn(left, right).astype(LOW)
    upper = lambda array: array[: array.shape[0] // 2]
    lower = lambda array: array[array.shape[0] // 2 :]
    if ring:
        same, cross, held, hidden_other = expert_ring(
            normed_two_b, back_rows, weight, mats, hidden_state
        )
        expert_in, h0, h1, g0, g1, u0, u1 = held
        late = {}

        def down_stage(gated):
            late["down"] = swap_tensor(low_tn(gated(h1), back_rows))

        def gate_stage(gated):
            late["gate"] = low_tn(gated(expert_in), g1)

        def up_stage(gated):
            late["up"] = low_tn(gated(expert_in), u1)

        def mixed_stage(gated):
            late["mixed"] = mixed_pass(gated(h0), h1, down_mats, chips, core[None])

        fillers = Fillers(down_stage, gate_stage, up_stage, mixed_stage)
        normed_two_grad = ring_sum(same, cross, fillers)
        gate_sent, up_sent, mixed_rows = late["gate"], late["up"], late["mixed"]
        down_got = late["down"]
    else:
        hidden_other = swap_tensor(hidden_state)
        expert_in = lax.all_gather(normed_two_b, "dp", axis=0, tiled=True)
        grad_rows, h0, h1, g0, g1, u0, u1 = expert_pass(
            expert_in, back_rows, weight, gate_mats, up_mats, down_mats
        )
        normed_two_grad = lax.psum_scatter(
            grad_rows, "dp", scatter_dimension=0, tiled=True
        ).astype(FULL)
        mixed_rows = (dot_nn(h0, down_mats[0]) + dot_nn(h1, down_mats[1])).astype(LOW)
        down_got = swap_tensor(low_tn(h1, back_rows))
        gate_sent = low_tn(expert_in, g1)
        up_sent = low_tn(expert_in, u1)
    quarter = gate_sent.shape[0] // 4
    gate_first = swap_tensor(gate_sent[:quarter])
    normed_two_grad, down_got, gate_first, mixed_rows, up_sent = together(
        normed_two_grad, down_got, gate_first, mixed_rows, up_sent
    )
    mixed = lax.psum_scatter(mixed_rows, "dp", scatter_dimension=0, tiled=True)

    unused_two, norm_two_back = jax.vjp(rms_norm, hidden_state, gain_two)
    state_part, gain_two_grad = norm_two_back(normed_two_grad)
    state_half = cotangent_half + state_part
    attn_grad_half = state_half.astype(LOW)
    attn_grad_b = both_halves(attn_grad_half, swap_tensor(attn_grad_half))
    attn_grad_b, gate_sent, up_sent = together(attn_grad_b, gate_sent, up_sent)
    (context_grad_b,) = project(attn_grad_b, gathered, block, (3,), (LOW,))
    (gate_middle,) = swap_in_turn([gate_sent[quarter : 3 * quarter]], context_grad_b)
    soon = [
        swap_tensor(after(piece, gate_middle))
        for piece in (gate_sent[3 * quarter :], upper(up_sent))
    ]
    if ring:
        pair = lambda own: (own, swap_bit(own, "dp", 0))
        columns = local_width // 2
        context_sent = lax.dynamic_slice_in_dim(context_b, (1 - core) * columns, columns, axis=1)
        normed_pair, attn_grad_pair = pair(normed_b), pair(attn_grad_b)
        context_got = swap_bit(context_sent, "dp", 0)
    query_normed_grad, query_inner, query_gain_part, key_grad, value_grad, even, *odd = attend_back(
        query_flat, *turned_by, keys_b, values_b, pieces, context_grad_b
    )
    returned = return_prompt(odd, even)
    if ring:
        key_grad, context_got, *pairs = together(
            key_grad, context_got, normed_pair[1], attn_grad_pair[1]
        )
        normed_pair, attn_grad_pair = (normed_b, pairs[0]), (attn_grad_b, pairs[1])
    key_normed_grad, key_inner, key_gain_part, value_pre_grad = key_back(
        key_grad, value_grad, key_flat, gain_key_local[None], key_scale, cosine, sine, returned
    )
    query_inner, *soon = together(query_inner, *soon)
    query_inner, key_inner = lax.psum(
        jnp.stack([query_inner[:, 0], key_inner[:, 0]], axis=0), "tensor"
    )
    query_pre_grad, key_pre_grad, pre_sent = pre_grads_pass(
        core[None],
        (
            query_flat,
            query_normed_grad,
            gain_query_local[None],
            query_scale,
            query_inner[:, None],
        ),
        (key_flat, key_normed_grad, gain_key_local[None], key_scale, key_inner[:, None]),
        value_pre_grad,
    )
    gate_got = jnp.concatenate([gate_first, gate_middle, soon[0]], axis=0)
    pre_grads = (query_pre_grad, key_pre_grad, value_pre_grad)
    grad_sum = lambda left, right, got: dot_tn(left, right) + got.astype(FULL)
    back_all = lambda *grads: project_back(grads, gathered, block, (0, 1, 2))

    wide = lambda part: lax.dynamic_update_slice_in_dim(
        jnp.zeros((column_total,), FULL), part, side * local_width, 0
    )

    def share(part):
        return own_half(part), swap_tensor(other_half(part).astype(LOW)), gain_part(part)

    def input_side(own, other):
        unused_one, norm_one_back = jax.vjp(
            lambda values: rms_norm(values, gain_one), own_half(tokens_f)
        )
        input_half = state_half + norm_one_back(own + other.astype(FULL))[0]
        return input_half, swap_tensor(input_half)

    def gain_part(part):
        return jnp.sum(part * rms_norm(tokens_f, 1.0), axis=0)

    def gain_side(gain_one_grad):
        grads = jnp.stack(
            [gain_one_grad, gain_two_grad, wide(query_gain_part[0]), wide(key_gain_part[0])]
        ).reshape(4, dp_count, block)
        grads = jnp.swapaxes(grads, 0, 1).reshape(dp_count, 1, 4 * block)
        sides = lax.axis_size("tensor")
        grads = jnp.broadcast_to(grads, (dp_count, sides, 4 * block))
        grads = grads.reshape(dp_count * sides, 4 * block)
        sums = lax.all_to_all(grads, ("dp", "tensor"), 0, 0, tiled=True)
        return jnp.sum(sums, axis=0).reshape(4, block)

    if ring:
        pre_got = swap_bit(pre_sent, "dp", 0)
        normed_own, normed_other, gain_one_grad = share(back_all(*pre_grads))
        pre_got, normed_own = together(pre_got, normed_own)
        w_blocks, *far = weight_grads(
            chips,
            core[None],
            normed_pair,
            attn_grad_pair,
            pre_grads,
            pre_got,
            context_b,
            context_got,
        )
        w_blocks, mixed, *far = together(w_blocks, mixed, *far)
        up_third, up_last = cut_rows(lower(up_sent), 2)
        up_third = swap_tensor(after(up_third, far[0]))
        late = {}

        def input_stage(gated):
            late["input"] = input_side(normed_own, gated(normed_other))
            late["up"] = swap_tensor(after(up_last, late["input"][0]))
            late["down"] = grad_sum(gated(h0), back_rows, down_got)

        def expert_stage(gated):
            late["gate"] = grad_sum(gated(expert_in), g0, gate_got)
            late["mixed"] = swap_tensor(gated(mixed))

        def gain_stage(gated):
            late["gains"] = gain_side(gated(gain_one_grad))

        fillers = Fillers(input_stage, expert_stage, gain_stage)
        w_parts, token = ring_weights(w_blocks, *far, fillers)
        input_half, input_other = late["input"]
        gain_sums = late["gains"]
        down_grad, gate_w_grad = late["down"], late["gate"]
        up_got = jnp.concatenate([soon[1], up_third, late["up"]], axis=0)
        up_w_grad = grad_sum(after(expert_in, token), u0, up_got)
        own_w, sent_w = sum_weights(core[None], *w_parts)
        w_sums = place_weights(core[None], own_w, swap_bit(sent_w, "dp", 0))
        mixed_other = late["mixed"]
    else:
        w_grads = jnp.concatenate(
            [low_tn(normed_b, g) for g in pre_grads] + [low_tn(attn_grad_b, context_b)], axis=1
        )
        w_sum = lax.psum_scatter(w_grads, "dp", scatter_dimension=0, tiled=True).astype(FULL)
        w_sums = [w_sum[:, j * local_width : (j + 1) * local_width] for j in range(4)]
        w_sums[3] = w_sums[3].T
        down_grad = grad_sum(h0, back_rows, down_got)
        gate_w_grad = grad_sum(expert_in, g0, gate_got)
        up_got = jnp.concatenate([soon[1], swap_tensor(lower(up_sent))], axis=0)
        up_w_grad = grad_sum(expert_in, u0, up_got)
        mixed_other = swap_tensor(mixed)
        *normed_parts, gain_one_grad = share(back_all(*pre_grads))
        gain_sums = gain_side(gain_one_grad)
        input_half, input_other = input_side(*normed_parts)
    input_grad = join_halves(side[None], [input_half], [input_other])
    output = join_halves(side[None], [hidden_state, mixed], [hidden_other, mixed_other])
    return (
        output,
        input_grad,
        gain_sums[0],
        w_sums[0],
        w_sums[1],
        w_sums[2],
        gain_sums[2],
        gain_sums[3],
        w_sums[3],
        gain_sums[1],
        gate_w_grad[None],
        up_w_grad[None],
        down_grad[None],
    )


def solution(mesh):
    return jax.shard_map(
        body,
        mesh=mesh,
        in_specs=(
            P("dp", None),
            P("dp"),
            P("dp", "tensor"),
            P("dp", "tensor"),
            P("dp", "tensor"),
            P("dp"),
            P("dp"),
            P("tensor", "dp"),
            P("dp"),
            P("dp", None, "tensor"),
            P("dp", None, "tensor"),
            P("dp", "tensor", None),
            P("dp", None),
            P("dp", None),
            P("dp", None),
            P("dp", None),
            P("dp", None),
        ),
        out_specs=(
            P("dp", None),
            P("dp", None),
            P("dp"),
            P("dp", "tensor"),
            P("dp", "tensor"),
            P("dp", "tensor"),
            P("dp"),
            P("dp"),
            P("tensor", "dp"),
            P("dp"),
            P("dp", None, "tensor"),
            P("dp", None, "tensor"),
            P("dp", "tensor", None),
        ),
        check_vma=False,
    )
```

```python
import jax
import jax.numpy as jnp
from jax import lax
from jax.experimental import pallas as pl
from jax.experimental.pallas import tpu as pltpu
from jax.sharding import PartitionSpec as P

HEADS = 16
HEAD = 128
GROUP = 8
PR_DEV = 128


EPSILON = 1e-05
VMEM = 60 * 1024 * 1024
LOW = jnp.bfloat16
FULL = jnp.float32


def swap_bit(block, axis, bit):
    count = lax.axis_size(axis)
    return lax.ppermute(block, axis, [(i, i ^ (1 << bit)) for i in range(count)])


def swap_tensor(block):
    return lax.ppermute(block, "tensor", [(0, 1), (1, 0)])


RING = (0, 2, 4, 6, 7, 5, 3, 1)
AHEAD = [
    (RING[p] * 2 + c, RING[(p + 1) % len(RING)] * 2 + c) for p in range(len(RING)) for c in range(2)
]
BEHIND = [(to, at) for at, to in AHEAD]
HOPS = (-1, 1, -2, 2, -3, 3, 0, 4)
LAYOUT = (
    *((-2, 0), (2, 0), (-1, 1), (1, 1)),
    *((-3, 0), (3, 0), (-2, 1), (2, 1)),
    *((4, 0), (4, 1), (-3, 1), (3, 1)),
    *((0, 0), (0, 1)),
    *((-1, 0), (1, 0)),
)


def ahead(block):
    return lax.ppermute(block, "dp", AHEAD)


def behind(block):
    return lax.ppermute(block, "dp", BEHIND)


def ring_chips(dp_index, hops):
    chip = dp_index // 2
    place = jnp.where(chip % 2 == 0, chip // 2, 7 - chip // 2)
    there = (place + jnp.array(hops, jnp.int32)) % len(RING)
    return jnp.where(there < 4, 2 * there, 2 * (7 - there) + 1)


def ring_blocks(dp_index):
    chips = ring_chips(dp_index, [hop for hop, _ in LAYOUT])
    return 2 * chips + (dp_index % 2 ^ jnp.array([cross for _, cross in LAYOUT], jnp.int32))


def add_low(*parts):
    total = parts[0].astype(FULL)
    for part in parts[1:]:
        total = total + part.astype(FULL)
    return total.astype(LOW)


def together(value, *others):
    return lax.optimization_barrier((value, *others))


def after(value, token):
    return lax.optimization_barrier((value, token))[0]


class Fillers:
    def __init__(self, late, *stages):
        self.late, self.stages, self.seen = late, list(stages), set(late)

    def next(self, token):
        if self.stages:
            self.stages.pop(0)(lambda value: after(value, token))

    def settle(self, *blocks):
        due = {key: value for key, value in self.late.items() if key not in self.seen}
        self.seen.update(due)
        *blocks, due = lax.optimization_barrier((*blocks, due))
        self.late.update(due)
        return blocks


def ring_sum(same, cross, fillers):
    both = {hop: add_low(same[hop], swap_bit(cross[hop], "dp", 0)) for hop in (4, 3, 2, 1, 0)}
    rows = both[0].shape[0]
    cut = rows // 2
    fillers.next(both[4])
    right, left = ahead(both[4][:cut]), behind(both[4][cut:])
    fillers.next(left)
    outward, inward = both[3][rows:], both[3][:rows]
    right = jnp.concatenate([add_low(outward[:cut], right), outward[cut:]], axis=0)
    left = jnp.concatenate([inward[:cut], add_low(inward[cut:], left)], axis=0)
    right, left = ahead(right), behind(left)
    fillers.next(left)
    for hop in (2, 1):
        right = ahead(add_low(both[hop][rows:], right))
        left = behind(add_low(both[hop][:rows], left))
        fillers.next(left)
    return both[0].astype(FULL) + right.astype(FULL) + left.astype(FULL)


def swap_in_turn(pieces, token):
    got = []
    for piece in pieces:
        got.append(swap_tensor(after(piece, token)))
        token = got[-1]
    return got


def cut_rows(array, count):
    rows = array.shape[0] // count
    return [array[i * rows : (i + 1) * rows] for i in range(count)]


def rms_norm(values, gain):
    return values * lax.rsqrt(jnp.mean(values * values, axis=-1, keepdims=True) + EPSILON) * gain


def rope_tables(positions, head_size):
    half_size = head_size // 2
    inverse = 10000.0 ** (-(jnp.arange(half_size, dtype=FULL) * 2.0) / head_size)
    angles = positions.astype(FULL)[:, None] * inverse[None, :]
    cosine = jnp.concatenate([jnp.cos(angles), jnp.cos(angles)], axis=-1)
    sine = jnp.concatenate([jnp.sin(angles), jnp.sin(angles)], axis=-1)
    return (cosine, sine)


def cont_positions(segment_row, gap_row, prompt_length):
    order = jnp.arange(segment_row.shape[0], dtype=jnp.int32)
    same = segment_row[:, None] == segment_row[None, :]
    earlier = order[None, :] < order[:, None]
    offset = jnp.sum((same & earlier).astype(jnp.int32), axis=1)
    labels = jnp.arange(gap_row.shape[0], dtype=jnp.int32)
    shifted = jnp.sum(
        jnp.where(segment_row[:, None] == labels[None, :], gap_row[None, :], 0), axis=1
    )
    return prompt_length + shifted + offset


def dot_nn(left, right):
    return jnp.dot(left, right, preferred_element_type=FULL)


def dot_tn(left, right):
    return lax.dot_general(left, right, (((0,), (0,)), ((), ())), preferred_element_type=FULL)


def dot_nt(left, right):
    return lax.dot_general(left, right, (((1,), (1,)), ((), ())), preferred_element_type=FULL)


def collect_prompt(own, first, second):
    near, far = swap_bit(own, "dp", 1), swap_bit(own, "dp", 2)
    last = swap_bit(near if first == 1 else far, "dp", second)
    blocks = []
    for block in (own, near, far, last):
        blocks += [block, swap_bit(block, "dp", 0)]
    return blocks[1:]


SMALL = pl.CostEstimate(flops=1, bytes_accessed=1, transcendentals=0)


def merge_kernel(even_ref, *refs):
    got, (keys_ref, values_ref, far_ref, near_ref) = refs[:3], refs[3:]
    near, far, last = 0, 1, 2
    add = lambda j, which: add_low(even_ref[j, which], got[j][which])
    keys_ref[0], keys_ref[1] = add(near, 0), add(last, 0)
    values_ref[0], values_ref[1] = add(far, 1), add(last, 1)
    far_ref[...], near_ref[...] = add(far, 0), add(near, 1)


def return_prompt(odd, even):
    got = [swap_bit(block, "dp", 0) for block in odd]
    one = jax.ShapeDtypeStruct(even.shape[2:], LOW)
    two = jax.ShapeDtypeStruct(even.shape[1:], LOW)
    keys, values, far, near = pl.pallas_call(
        merge_kernel, out_shape=[two, two, one, one], cost_estimate=SMALL
    )(even, *got[1:])
    keys, values = swap_bit(keys, "dp", 1), swap_bit(values, "dp", 2)
    last_keys = swap_bit(add_low(far, keys[1]), "dp", 2)
    last_values = swap_bit(add_low(near, values[1]), "dp", 1)
    return got[0], keys, values, last_keys, last_values


def turn(values):
    return pltpu.roll(values, HEAD // 2, 1)


def rope_kernel(pre_ref, gain_ref, scale_ref, cos_ref, sin_ref, out_ref, first_ref):
    scale, cosine, sine = scale_ref[...], cos_ref[...], sin_ref[...]
    for at in range(0, pre_ref.shape[1], HEAD):
        span = slice(at, at + HEAD)
        normed = pre_ref[:, span] * scale * gain_ref[:, span]
        out_ref[:, span] = (normed * cosine + turn(normed) * sine).astype(LOW)
    first_ref[...] = out_ref[: first_ref.shape[0]]


def rope_pass(flat, gain, scale, cosine, sine):
    rows, width = flat.shape
    part = width // 2
    wide = lambda rows: pl.BlockSpec((rows, part), lambda h: (0, h))
    return pl.pallas_call(
        rope_kernel,
        grid=(2,),
        in_specs=[wide(rows), wide(1)] + [kept_spec(a) for a in (scale, cosine, sine)],
        out_specs=[wide(rows), wide(PR_DEV)],
        out_shape=[jax.ShapeDtypeStruct((count, width), LOW) for count in (rows, PR_DEV)],
    )(flat, gain, scale, cosine, sine)


PAIR = 2


def head_spec(rows):
    return pl.BlockSpec((rows, PAIR * HEAD), lambda h: (0, h))


def kept_spec(array):
    zeros = (0,) * array.ndim
    return pl.BlockSpec(array.shape, lambda h: zeros, pipeline_mode=pl.Buffered(1))


def all_keys(own_ref, pieces, span):
    return jnp.concatenate(
        [own_ref[:PR_DEV, span]] + [p[:, span] for p in pieces] + [own_ref[PR_DEV:, span]], axis=0
    )


def turned_query(flat_ref, gain_ref, scale, cosine, sine, span):
    normed = flat_ref[:, span] * scale * gain_ref[:, span]
    return (normed * cosine + turn(normed) * sine).astype(LOW)


def softmax_rows(query, keys, bias):
    scores = dot_nt(query, keys) * HEAD ** (-0.5) + bias
    weights = jnp.exp(scores - jnp.max(scores, axis=1, keepdims=True))
    return weights * (1.0 / jnp.sum(weights, axis=1, keepdims=True))


PIECES = GROUP - 1


def attend_kernel(flat_ref, gain_ref, scale_ref, cos_ref, sin_ref, bias_ref, k_ref, v_ref, *refs):
    out_ref = refs[-1]
    bias = bias_ref[...].astype(FULL)
    scale, cosine, sine = scale_ref[...], cos_ref[...], sin_ref[...]
    for at in range(0, PAIR * HEAD, HEAD):
        span = slice(at, at + HEAD)
        query = turned_query(flat_ref, gain_ref, scale, cosine, sine, span)
        probs = softmax_rows(query, all_keys(k_ref, refs[:PIECES], span), bias)
        values = all_keys(v_ref, refs[PIECES : 2 * PIECES], span)
        out_ref[:, span] = dot_nn(probs.astype(LOW), values).astype(LOW)


def attend_specs(rows, scale, cosine, sine, bias):
    return (
        [head_spec(rows), head_spec(1)]
        + [kept_spec(a) for a in (scale, cosine, sine, bias)]
        + [head_spec(rows)] * 2
        + [head_spec(PR_DEV)] * (2 * PIECES)
    )


def attend(flat, gain, scale, cosine, sine, bias, keys, values, pieces):
    rows, width = flat.shape
    return pl.pallas_call(
        attend_kernel,
        grid=(width // HEAD // PAIR,),
        in_specs=attend_specs(rows, scale, cosine, sine, bias),
        out_specs=head_spec(rows),
        out_shape=jax.ShapeDtypeStruct((rows, width), LOW),
        compiler_params=pltpu.CompilerParams(vmem_limit_bytes=VMEM),
    )(flat, gain, scale, cosine, sine, bias, keys, values, *pieces)


def norm_parts(step, at, grad, flat_ref, gain_ref, scale_ref, inner_ref, gain_grad_ref):
    span = slice(at, at + HEAD)
    product = flat_ref[:, span] * grad
    inner = jnp.sum(product * gain_ref[:, span], axis=1, keepdims=True)
    gain_grad_ref[:, span] = jnp.sum(product * scale_ref[...], axis=0, keepdims=True)
    if at:
        inner_ref[...] += inner
    else:
        inner_ref[...] = jnp.where(step == 0, 0.0, inner_ref[...]) + inner


def attend_back_kernel(
    flat_ref, gain_ref, scale_ref, cos_ref, sin_ref, bias_ref, k_ref, v_ref, *refs
):
    back_ref = refs[2 * PIECES]
    qg_ref, inner_ref, gain_grad_ref, kg_ref, vg_ref, even_ref = refs[2 * PIECES + 1 : -4]
    odd_refs = refs[-4:]
    step = pl.program_id(0)
    bias = bias_ref[...].astype(FULL)
    scale, cosine, sine = scale_ref[...], cos_ref[...], sin_ref[...]
    prompt = PR_DEV * GROUP
    for at in range(0, PAIR * HEAD, HEAD):
        span = slice(at, at + HEAD)
        query = turned_query(flat_ref, gain_ref, scale, cosine, sine, span)
        back = back_ref[:, span]
        keys = all_keys(k_ref, refs[:PIECES], span)
        values = all_keys(v_ref, refs[PIECES : 2 * PIECES], span)
        probs = softmax_rows(query, keys, bias)
        prob_grad = dot_nt(back, values)
        value_grad = dot_tn(probs.astype(LOW), back)
        row_dot = jnp.sum(probs * prob_grad, axis=1, keepdims=True)
        score_grad = (probs * (prob_grad - row_dot)).astype(LOW)
        query_grad = dot_nn(score_grad, keys) * HEAD ** (-0.5)
        key_grad = dot_tn(score_grad, query) * HEAD ** (-0.5)
        query_grad = query_grad * cosine - turn(query_grad) * sine
        qg_ref[:, span] = query_grad
        norm_parts(step, at, query_grad, flat_ref, gain_ref, scale_ref, inner_ref, gain_grad_ref)
        for which, grad, own_ref in ((0, key_grad, kg_ref), (1, value_grad, vg_ref)):
            own_ref[:PR_DEV, span] = grad[:PR_DEV]
            own_ref[PR_DEV:, span] = grad[prompt:]
            for j in range(1, GROUP):
                to = odd_refs[j // 2] if j % 2 else even_ref.at[j // 2 - 1]
                to[which, :, span] = grad[j * PR_DEV : (j + 1) * PR_DEV].astype(LOW)


def attend_back(flat, gain, scale, cosine, sine, bias, keys, values, pieces, back):
    rows, width = flat.shape
    wide = jax.ShapeDtypeStruct((rows, width), FULL)
    both = pl.BlockSpec((3, 2, PR_DEV, PAIR * HEAD), lambda h: (0, 0, 0, h))
    return pl.pallas_call(
        attend_back_kernel,
        grid=(width // HEAD // PAIR,),
        in_specs=attend_specs(rows, scale, cosine, sine, bias) + [head_spec(rows)],
        out_specs=[
            head_spec(rows),
            pl.BlockSpec((rows, 1), lambda h: (0, 0)),
            head_spec(1),
            head_spec(rows),
            head_spec(rows),
            both,
        ]
        + [pl.BlockSpec((2, PR_DEV, PAIR * HEAD), lambda h: (0, 0, h))] * 4,
        out_shape=[
            wide,
            jax.ShapeDtypeStruct((rows, 1), FULL),
            jax.ShapeDtypeStruct((1, width), FULL),
            wide,
            wide,
            jax.ShapeDtypeStruct((3, 2, PR_DEV, width), LOW),
        ]
        + [jax.ShapeDtypeStruct((2, PR_DEV, width), LOW)] * 4,
        compiler_params=pltpu.CompilerParams(vmem_limit_bytes=VMEM),
        cost_estimate=pl.CostEstimate(
            flops=20 * 10**9, bytes_accessed=40 * 10**6, transcendentals=4 * 10**6
        ),
    )(flat, gain, scale, cosine, sine, bias, keys, values, *pieces, back)


def key_back_kernel(*refs):
    kg_ref, vg_ref, flat_ref, gain_ref, scale_ref, cos_ref, sin_ref = refs[:7]
    got, keys, values, last_keys, last_values = refs[7:12]
    out_ref, inner_ref, gain_grad_ref, value_ref = refs[12:]
    step = pl.program_id(0)
    for at in range(0, PAIR * HEAD, HEAD):
        span = slice(at, at + HEAD)
        grads = []
        for which, own_ref, near, last in ((0, kg_ref, keys, last_keys), (1, vg_ref, values, last_values)):
            first = own_ref[:PR_DEV, span] + got[which, :, span].astype(FULL)
            first = first + near[0, :, span].astype(FULL) + last[:, span].astype(FULL)
            grads.append(jnp.concatenate([first, own_ref[PR_DEV:, span]], axis=0))
        key_grad = grads[0] * cos_ref[...] - turn(grads[0]) * sin_ref[...]
        out_ref[:, span] = key_grad
        norm_parts(step, at, key_grad, flat_ref, gain_ref, scale_ref, inner_ref, gain_grad_ref)
        value_ref[:, span] = grads[1].astype(LOW)


def key_back(key_grad, value_grad, flat, gain, scale, cosine, sine, returned):
    rows, width = flat.shape
    columns = PAIR * HEAD
    return pl.pallas_call(
        key_back_kernel,
        grid=(width // columns,),
        in_specs=[head_spec(rows)] * 3
        + [head_spec(1)]
        + [kept_spec(a) for a in (scale, cosine, sine)]
        + [pl.BlockSpec((2, PR_DEV, columns), lambda h: (0, 0, h))]
        + [pl.BlockSpec((1, PR_DEV, columns), lambda h: (0, 0, h))] * 2
        + [head_spec(PR_DEV)] * 2,
        out_specs=[
            head_spec(rows),
            pl.BlockSpec((rows, 1), lambda h: (0, 0)),
            head_spec(1),
            head_spec(rows),
        ],
        out_shape=[
            jax.ShapeDtypeStruct((rows, width), FULL),
            jax.ShapeDtypeStruct((rows, 1), FULL),
            jax.ShapeDtypeStruct((1, width), FULL),
            jax.ShapeDtypeStruct((rows, width), LOW),
        ],
        cost_estimate=SMALL,
    )(key_grad, value_grad, flat, gain, scale, cosine, sine, *returned)


def pack_kernel(query, key, value, out, rest, packed):
    at = 0
    for ref in (query, key, value):
        packed[at : at + ref.shape[0]] = ref[...]
        at += ref.shape[0]
    packed[at : at + out.shape[1]] = out[...].T
    packed[at + out.shape[1] :] = rest[...]


def pack_weights(w_query, w_key, w_value, w_out, rest):
    rows = 4 * w_query.shape[0] + rest.shape[0]
    return pl.pallas_call(
        pack_kernel, out_shape=jax.ShapeDtypeStruct((rows, w_query.shape[1]), LOW)
    )(w_query, w_key, w_value, w_out, rest)


def unpack_kernel(first, blocks_ref, packed, out, held, sems):
    width = packed.shape[2]
    parts = out.shape[1] // width
    rows = (packed.shape[1] - first) // parts
    count = packed.shape[0]
    place = lambda i: pl.ds(i * rows, rows)
    loads = [
        pltpu.make_async_copy(
            packed.at[blocks_ref[i], pl.ds(first + j * rows, rows)],
            held.at[place(i), pl.ds(j * width, width)],
            sems.at[i * parts + j],
        )
        for i in range(count)
        for j in range(parts)
    ]
    stores = [
        pltpu.make_async_copy(held.at[place(i)], out.at[place(i)], sems.at[count * parts + i])
        for i in range(count)
    ]
    for one in loads:
        one.start()
    for i, store in enumerate(stores):
        for j in range(parts):
            loads[i * parts + j].wait()
        store.start()
    for store in stores:
        store.wait()


def unpack_rows(packed, blocks, first, width):
    count = packed.shape[0]
    parts = width // packed.shape[2]
    rows = (packed.shape[1] - first) // parts
    return pl.pallas_call(
        lambda *refs: unpack_kernel(first, *refs),
        in_specs=[pl.BlockSpec(memory_space=pltpu.SMEM), pl.BlockSpec(memory_space=pl.ANY)],
        out_specs=pl.BlockSpec(memory_space=pl.ANY),
        out_shape=jax.ShapeDtypeStruct((count * rows, width), LOW),
        scratch_shapes=[
            pltpu.VMEM((count * rows, width), LOW),
            pltpu.SemaphoreType.DMA((count * parts + count,)),
        ],
        compiler_params=pltpu.CompilerParams(vmem_limit_bytes=VMEM),
    )(blocks, packed)


def load_packed(gathered, places, block, held, sems):
    copies = [
        pltpu.make_async_copy(
            gathered.at[:, pl.ds(place * block, block)], held.at[k], sems.at[k]
        )
        for k, place in enumerate(places)
    ]
    for one in copies:
        one.start()
    return copies


def held_pack(gathered, places, block):
    count, columns = gathered.shape[0], gathered.shape[2]
    return [
        pltpu.VMEM((len(places), count, block, columns), LOW),
        pltpu.SemaphoreType.DMA((len(places),)),
    ]


def project_kernel(places, block, heads, rows_ref, gathered, *refs):
    outs, firsts, (held, sems) = refs[: len(places)], refs[len(places) : -2], refs[-2:]
    copies = load_packed(gathered, places, block, held, sems)
    rows = rows_ref[...]
    for k, (one, out) in enumerate(zip(copies, outs)):
        one.wait()
        out[...] = dot_nn(rows, held[k].reshape(-1, out.shape[1])).astype(out.dtype)
    for first, k in zip(firsts, heads):
        first[...] = outs[k][: first.shape[0]]


def project(rows, gathered, block, places, roundings, heads=()):
    count, width = rows.shape
    columns = gathered.shape[2]
    outs = [jax.ShapeDtypeStruct((count, columns), rounding) for rounding in roundings]
    outs += [jax.ShapeDtypeStruct((PR_DEV, columns), roundings[k]) for k in heads]
    fixed = lambda a: pl.BlockSpec(a.shape, lambda i: (0, 0))
    return pl.pallas_call(
        lambda *refs: project_kernel(places, block, heads, *refs),
        grid=(1,),
        in_specs=[fixed(rows), pl.BlockSpec(memory_space=pl.ANY)],
        out_specs=[fixed(out) for out in outs],
        out_shape=outs,
        scratch_shapes=held_pack(gathered, places, block),
        compiler_params=pltpu.CompilerParams(vmem_limit_bytes=VMEM),
        cost_estimate=pl.CostEstimate(
            flops=2 * count * width * columns * len(places),
            bytes_accessed=2 * width * columns * len(places) + 8 * count * columns,
            transcendentals=0,
        ),
    )(rows, gathered)


def pack_specs(gathered, places, steps, at):
    count, width = gathered.shape[0] // steps, gathered.shape[2]
    block = at
    return [
        pl.BlockSpec((count, block, width), lambda i, place=place: (i, place, 0))
        for place in places
    ]


def project_back_kernel(mats, *refs):
    out = refs[-1]
    total = None
    for rows_ref, mat in zip(refs[:mats], refs[mats:-1]):
        part = dot_nt(rows_ref[...], mat[...].reshape(-1, mat.shape[2]))
        total = part if total is None else total + part
    out[...] = total


def project_back(rows, gathered, block, places):
    count, columns = rows[0].shape
    width = gathered.shape[0] * block
    steps = 4 if len(places) > 1 else 2
    fixed = pl.BlockSpec((count, columns), lambda i: (0, 0), pipeline_mode=pl.Buffered(1))
    return pl.pallas_call(
        lambda *refs: project_back_kernel(len(places), *refs),
        grid=(steps,),
        in_specs=[fixed] * len(rows) + pack_specs(gathered, places, steps, block),
        out_specs=pl.BlockSpec((count, width // steps), lambda i: (0, i)),
        out_shape=jax.ShapeDtypeStruct((count, width), FULL),
        compiler_params=pltpu.CompilerParams(vmem_limit_bytes=VMEM),
        cost_estimate=pl.CostEstimate(
            flops=2 * count * width * columns * len(places),
            bytes_accessed=2 * width * columns * len(places) + 4 * count * width,
            transcendentals=0,
        ),
    )(*rows, *[gathered] * len(places))


def pre_kernel(core_ref, *refs):
    inputs, outs = refs[:11], refs[11:]
    step = pl.program_id(0)
    columns = inputs[0].shape[1]
    parts = []
    for flat, grad, gain, scale, inner in (inputs[:5], inputs[5:10]):
        scaled = scale[...]
        mean = inner[...] * (1.0 / (HEADS * HEAD))
        parts.append(
            (
                scaled * gain[...] * grad[...] - flat[...] * (scaled * scaled * scaled) * mean
            ).astype(LOW)
        )
    outs[0][...], outs[1][...] = parts

    @pl.when(step != core_ref[0])
    def _():
        for j, part in enumerate((*parts, inputs[10][...])):
            outs[2][:, j * columns : (j + 1) * columns] = part


def pre_grads_pass(core, query, key, value):
    rows, width = value.shape
    columns = width // 2
    half = lambda rows: pl.BlockSpec((rows, columns), lambda h: (0, h))
    side = [half(rows), half(rows), half(1)] + [pl.BlockSpec((rows, 1), lambda h: (0, 0))] * 2
    return pl.pallas_call(
        pre_kernel,
        grid=(2,),
        in_specs=[pl.BlockSpec(memory_space=pltpu.SMEM)] + side + side + [half(rows)],
        out_specs=[half(rows), half(rows), pl.BlockSpec((rows, 3 * columns), lambda h: (0, 0))],
        out_shape=[jax.ShapeDtypeStruct((rows, width), LOW)] * 2
        + [jax.ShapeDtypeStruct((rows, 3 * columns), LOW)],
    )(core, *query, *key, value)


def weight_kernel(chip_ref, core_ref, *refs):
    normed, normed_got, back, back_got, query, key, value, got, context, context_got = refs[:10]
    out_ref, right_ref, left_ref, pre_both, context_both = refs[10:]
    rows, columns = query.shape

    @pl.when(pl.program_id(0) == 0)
    def _():
        for j, part in enumerate((query, key, value)):
            pre_both[:rows, j * columns : (j + 1) * columns] = part[...]
        pre_both[rows:] = got[...]
        context_both[:rows] = context[...]
        context_both[rows:] = context_got[...]

    left = jnp.concatenate([normed[...], normed_got[...]], axis=0)
    out_ref[0, :, : 3 * columns] = dot_tn(left, pre_both[...]).astype(LOW)
    left = jnp.concatenate([back[...], back_got[...]], axis=0)
    out_ref[0, :, 3 * columns :] = dot_tn(left, context_both[...]).astype(LOW)

    @pl.when(pl.program_id(0) == HOPS.index(4))
    def _():
        right_ref[...] = out_ref[0, :, : 2 * columns]
        left_ref[...] = out_ref[0, :, 2 * columns :]


def weight_grads(chips, core, normed, back, pre_grads, got, context, context_got):
    rows, width = normed[0].shape
    columns = context_got.shape[1]
    count = chips.shape[0]
    block = width // count
    tall = pl.BlockSpec((rows, block), lambda i, chip, core: (0, chip[i]))
    mine = pl.BlockSpec((rows, columns), lambda i, chip, core: (0, core[0]))
    fixed = lambda a: pl.BlockSpec(a.shape, lambda i, chip, core: (0, 0))
    return pl.pallas_call(
        weight_kernel,
        grid_spec=pltpu.PrefetchScalarGridSpec(
            num_scalar_prefetch=2,
            grid=(count,),
            in_specs=[tall] * 4 + [mine] * 3 + [fixed(got), mine, fixed(context_got)],
            out_specs=[pl.BlockSpec((1, block, 4 * columns), lambda i, chip, core: (i, 0, 0))]
            + [pl.BlockSpec((block, 2 * columns), lambda i, chip, core: (0, 0))] * 2,
            scratch_shapes=[
                pltpu.VMEM((2 * rows, 3 * columns), LOW),
                pltpu.VMEM((2 * rows, columns), LOW),
            ],
        ),
        out_shape=[jax.ShapeDtypeStruct((count, block, 4 * columns), LOW)]
        + [jax.ShapeDtypeStruct((block, 2 * columns), LOW)] * 2,
        compiler_params=pltpu.CompilerParams(vmem_limit_bytes=VMEM),
        cost_estimate=pl.CostEstimate(
            flops=16 * rows * width * columns,
            bytes_accessed=2 * (4 * rows * width + 8 * rows * columns + 4 * width * columns),
            transcendentals=0,
        ),
    )(chips, core, *normed, *back, *pre_grads, got, context, context_got)


def ring_weights(blocks, right, left, fillers):
    part = lambda hop: blocks[HOPS.index(hop)]
    cut = blocks.shape[2] // 2
    fillers.next(right)
    right, left = ahead(right), behind(left)
    right, left = fillers.settle(right, left)
    fillers.next(left)
    outward, inward = part(3), part(-3)
    right = jnp.concatenate([add_low(outward[:, :cut], right), outward[:, cut:]], axis=1)
    left = jnp.concatenate([inward[:, :cut], add_low(inward[:, cut:], left)], axis=1)
    right, left = together(right, left)
    right, left = ahead(right), behind(left)
    for hop in (2, 1):
        right, left = fillers.settle(right, left)
        fillers.next(left)
        right, left = together(add_low(part(hop), right), add_low(part(-hop), left))
        right, left = ahead(right), behind(left)
    right, left = fillers.settle(right, left)
    return blocks, right, left


def sum_kernel(core_ref, blocks_ref, right_ref, left_ref, own_ref, sent_ref):
    rows = own_ref.shape[0]
    for k, out in enumerate((own_ref, sent_ref)):
        side = core_ref[0] if k == 0 else 1 - core_ref[0]
        span = pl.ds(pl.multiple_of(side * rows, rows), rows)
        out[...] = (
            blocks_ref[0, span].astype(FULL)
            + right_ref[span].astype(FULL)
            + left_ref[span].astype(FULL)
        )


def sum_weights(core, blocks, right, left):
    rows, width = right.shape
    whole = pl.BlockSpec((rows, width), lambda i: (0, 0))
    half = pl.BlockSpec((rows // 2, width), lambda i: (0, 0))
    return pl.pallas_call(
        sum_kernel,
        grid=(1,),
        in_specs=[
            pl.BlockSpec(memory_space=pltpu.SMEM),
            pl.BlockSpec((1, rows, width), lambda i: (HOPS.index(0), 0, 0)),
            whole,
            whole,
        ],
        out_specs=[half, half],
        out_shape=[jax.ShapeDtypeStruct((rows // 2, width), FULL)] * 2,
    )(core, blocks, right, left)


def place_kernel(core_ref, own_ref, got_ref, *outs):
    columns = own_ref.shape[1] // 4
    first = core_ref[0] == 0
    for k, out in enumerate(outs):
        span = slice(k * columns, (k + 1) * columns)
        own, got = own_ref[:, span], got_ref[:, span]
        left, right = jnp.where(first, own, got), jnp.where(first, got, own)
        if k < 3:
            out[:, :columns], out[:, columns:] = left, right
        else:
            out[:columns], out[columns:] = left.T, right.T


def place_weights(core, own, got):
    rows, width = own.shape
    columns = width // 2
    shapes = [(rows, columns)] * 3 + [(columns, rows)]
    return pl.pallas_call(
        place_kernel,
        grid=(1,),
        in_specs=[pl.BlockSpec(memory_space=pltpu.SMEM)]
        + [pl.BlockSpec((rows, width), lambda i: (0, 0))] * 2,
        out_specs=[pl.BlockSpec(shape, lambda i: (0, 0)) for shape in shapes],
        out_shape=[jax.ShapeDtypeStruct(shape, FULL) for shape in shapes],
    )(core, own, got)


def join_kernel(parts, side_ref, *refs):
    out_ref = refs[-1]
    rows = out_ref.shape[0] // 2
    for k, side in ((0, side_ref[0]), (1, 1 - side_ref[0])):
        total = refs[k * parts][...].astype(FULL)
        for j in range(1, parts):
            total = total + refs[k * parts + j][...].astype(FULL)
        out_ref[pl.ds(pl.multiple_of(side * rows, rows), rows)] = total


def join_halves(side, own, other):
    rows, width = own[0].shape
    columns = width // 2
    half = pl.BlockSpec((rows, columns), lambda i: (0, i))
    return pl.pallas_call(
        lambda *refs: join_kernel(len(own), *refs),
        grid=(2,),
        in_specs=[pl.BlockSpec(memory_space=pltpu.SMEM)] + [half] * (2 * len(own)),
        out_specs=pl.BlockSpec((2 * rows, columns), lambda i: (0, i)),
        out_shape=jax.ShapeDtypeStruct((2 * rows, width), FULL),
    )(side, *own, *other)


def expert_kernel(
    rows_ref, back_ref, gate_ref, wg0, wg1, wu0, wu1, wd0, wd1, grad_ref, h0, h1, g0, g1, u0, u1
):
    rows = rows_ref[...]
    back = back_ref[...]
    gate = gate_ref[...]
    total = None
    for wg, wu, wd, h, g, u in ((wg0, wu0, wd0, h0, g0, u0), (wg1, wu1, wd1, h1, g1, u1)):
        gate_pre = dot_nn(rows, wg[...])
        up_pre = dot_nn(rows, wu[...])
        hidden_grad = gate * dot_nt(back, wd[...])
        sig = 1.0 / (1.0 + jnp.exp(-gate_pre))
        act = gate_pre * sig
        h[...] = (gate * (act * up_pre)).astype(LOW)
        gate_grad = (hidden_grad * up_pre * (sig * (1.0 + gate_pre * (1.0 - sig)))).astype(LOW)
        up_grad = (hidden_grad * act).astype(LOW)
        g[...] = gate_grad
        u[...] = up_grad
        part = dot_nt(gate_grad, wg[...]) + dot_nt(up_grad, wu[...])
        total = part if total is None else total + part
    grad_ref[...] = total.astype(LOW)


def expert_pass(rows, back, gate, gate_mats, up_mats, down_mats):
    count, width = rows.shape
    hidden = gate_mats[0].shape[1]
    tile = 256
    whole = lambda array: pl.BlockSpec(
        array.shape, lambda i: (0, 0), pipeline_mode=pl.Buffered(1)
    )
    tall = lambda columns: pl.BlockSpec((tile, columns), lambda i: (i, 0))
    mats = [*gate_mats, *up_mats, *down_mats]
    flops = 2 * 5 * count * width * hidden * 2
    return pl.pallas_call(
        expert_kernel,
        grid=(count // tile,),
        in_specs=[tall(width), tall(width), tall(1)] + [whole(m) for m in mats],
        out_specs=[tall(width)] + [tall(hidden)] * 6,
        out_shape=[jax.ShapeDtypeStruct((count, width), LOW)]
        + [jax.ShapeDtypeStruct((count, hidden), LOW)] * 6,
        compiler_params=pltpu.CompilerParams(vmem_limit_bytes=VMEM),
        cost_estimate=pl.CostEstimate(
            flops=flops,
            bytes_accessed=2 * (3 * count * width + 6 * count * hidden + 6 * width * hidden),
            transcendentals=2 * count * hidden,
        ),
    )(rows, back, gate, *mats)


def chunk_kernel(pieces, held, at, splits, gate_ref, *refs):
    piece_refs, refs = refs[:pieces], refs[pieces:]
    back_ref, mats, refs = refs[0], refs[1:7], refs[7 + held :]
    grad_outs, refs = refs[: len(splits)], refs[len(splits) :]
    rows_out, outs = refs[0], refs[1:7]
    rows, back, wide, wd, hidden, both_grads, grads, sems = refs[7:]
    count = rows.shape[0]
    part = wd.shape[1]
    slab = wide.shape[0] // 4
    across = lambda k, half: pl.ds((2 * k + half) * part, part)
    place = pl.ds(at * count, count)
    copy = pltpu.make_async_copy
    load_rows, start = [], 0
    for piece in piece_refs:
        span = pl.ds(start, piece.shape[0])
        load_rows.append(copy(piece, rows.at[span], sems.at[len(load_rows)]))
        start += piece.shape[0]
    load_back = copy(back_ref.at[place], back, sems.at[6])
    loads = []
    for half in range(2):
        places = [wide.at[:, across(0, half)], wide.at[:, across(1, half)], wd.at[half]]
        loads.append(
            [copy(mats[2 * k + half], to, sems.at[7 + 3 * half + k]) for k, to in enumerate(places)]
        )
    for one in load_rows + loads[0][:2] + [load_back] + loads[0][2:] + loads[1]:
        one.start()
    gate = gate_ref[...]
    for one in load_rows:
        one.wait()
    stores = [copy(rows, rows_out.at[place], sems.at[13])]
    stores[0].start()
    for half in range(2):
        columns = pl.ds(half * part, part)
        loads[half][0].wait()
        gate_pre = dot_nn(rows[...], wide[:, across(0, half)])
        loads[half][1].wait()
        up_pre = dot_nn(rows[...], wide[:, across(1, half)])
        if half == 0:
            load_back.wait()
        loads[half][2].wait()
        hidden_grad = gate * dot_nt(back[...], wd[half])
        sig = 1.0 / (1.0 + jnp.exp(-gate_pre))
        act = gate_pre * sig
        hidden[:, columns] = (gate * (act * up_pre)).astype(LOW)
        both_grads[:, across(0, half)] = (
            hidden_grad * up_pre * (sig * (1.0 + gate_pre * (1.0 - sig)))
        ).astype(LOW)
        both_grads[:, across(1, half)] = (hidden_grad * act).astype(LOW)
    for half in range(2):
        held_in = (
            hidden.at[:, pl.ds(half * part, part)],
            both_grads.at[:, across(0, half)],
            both_grads.at[:, across(1, half)],
        )
        for k, source in enumerate(held_in):
            stores.append(copy(source, outs[2 * k + half].at[place], sems.at[14 + 3 * half + k]))
            stores[-1].start()

    @pl.loop(0, 4)
    def _(j):
        span = pl.ds(pl.multiple_of(j * slab, slab), slab)
        grads[:, span] = dot_nt(both_grads[...], wide[span]).astype(LOW)

    start = 0
    for k, (split, to) in enumerate(zip(splits, grad_outs)):
        stores.append(copy(grads.at[pl.ds(start, split)], to, sems.at[20 + k]))
        stores[-1].start()
        start += split
    for one in stores:
        one.wait()


def expert_chunk(pieces, back, gate, mats, at, held, splits):
    all_rows, width = back.shape
    part = mats[0].shape[1]
    hidden = 2 * part
    count = sum(piece.shape[0] for piece in pieces)
    anywhere = pl.BlockSpec(memory_space=pl.ANY)
    held = [] if held is None else list(held)
    args = [gate, *pieces, back, *mats, *held]
    out = pl.pallas_call(
        lambda *refs: chunk_kernel(len(pieces), len(held), at, splits, *refs),
        grid=(1,),
        in_specs=[pl.BlockSpec((count, 1), lambda j: (at, 0))] + [anywhere] * (len(args) - 1),
        out_specs=[anywhere] * (len(splits) + 7),
        out_shape=[jax.ShapeDtypeStruct((split, width), LOW) for split in splits]
        + [jax.ShapeDtypeStruct((all_rows, width), LOW)]
        + [jax.ShapeDtypeStruct((all_rows, part), LOW)] * 6,
        scratch_shapes=[
            pltpu.VMEM((count, width), LOW),
            pltpu.VMEM((count, width), LOW),
            pltpu.VMEM((width, 2 * hidden), LOW),
            pltpu.VMEM((2, part, width), LOW),
            pltpu.VMEM((count, hidden), LOW),
            pltpu.VMEM((count, 2 * hidden), LOW),
            pltpu.VMEM((count, width), LOW),
            pltpu.SemaphoreType.DMA((23,)),
        ],
        input_output_aliases={
            len(args) - len(held) + k: len(splits) + k for k in range(len(held))
        },
        compiler_params=pltpu.CompilerParams(vmem_limit_bytes=VMEM),
        cost_estimate=pl.CostEstimate(
            flops=2 * 5 * count * width * hidden,
            bytes_accessed=2 * (4 * count * width + 3 * count * hidden + 3 * width * hidden),
            transcendentals=count * hidden,
        ),
    )(*args)
    return out[: len(splits)], out[len(splits) :]


def mixed_kernel(chip_ref, same_ref, cross_ref, core_ref, *refs):
    first_ref, second_ref, out_ref = refs[4:]
    rows = out_ref.shape[2]
    first, second = (
        jnp.concatenate([refs[k][...], refs[k + 1][...]], axis=0) for k in (0, 2)
    )
    result = (dot_nn(first, first_ref[...]) + dot_nn(second, second_ref[...])).astype(LOW)
    out_ref[0, core_ref[0]] = result[:rows]
    out_ref[0, 1 - core_ref[0]] = result[rows:]


def mixed_pass(h0, h1, down_mats, chips, core):
    count, columns = h0.shape
    width = down_mats[0].shape[1]
    rows = count // len(LAYOUT)
    places = [
        jnp.array([LAYOUT.index((hop, cross)) for hop in HOPS], jnp.int32) for cross in (0, 1)
    ]
    once = pl.Buffered(1)
    fixed = lambda m: pl.BlockSpec(m.shape, lambda i, *tables: (0, 0), pipeline_mode=once)
    block = lambda k: pl.BlockSpec((rows, columns), lambda i, *tables: (tables[k][i], 0))
    out = pl.pallas_call(
        mixed_kernel,
        grid_spec=pltpu.PrefetchScalarGridSpec(
            num_scalar_prefetch=4,
            grid=(len(HOPS),),
            in_specs=[block(1), block(2), block(1), block(2)] + [fixed(m) for m in down_mats],
            out_specs=pl.BlockSpec(
                (1, 2, rows, width), lambda i, chip, *tables: (chip[i], 0, 0, 0)
            ),
        ),
        out_shape=jax.ShapeDtypeStruct((len(HOPS), 2, rows, width), LOW),
        compiler_params=pltpu.CompilerParams(vmem_limit_bytes=VMEM),
        cost_estimate=pl.CostEstimate(
            flops=4 * count * columns * width,
            bytes_accessed=2 * (count * (2 * columns + width) + 2 * columns * width),
            transcendentals=0,
        ),
    )(chips, *places, core, h0, h0, h1, h1, *down_mats)
    return out.reshape(count, width)


def expert_ring(rows, back, gate, mats, waiting):
    size = rows.shape[0]
    cut = size // 2
    swap = lambda block: swap_bit(block, "dp", 0)
    chunk = lambda pieces, at, held, *splits: expert_chunk(
        pieces, back, gate, mats, at, held, splits
    )
    rows, pair = together(rows, swap(rows))
    left, right = ahead(rows), behind(rows)
    parts, crossed = cut_rows(waiting, 4), []
    same, cross = {}, {}
    cross_over = lambda token: crossed.append(swap_tensor(after(parts[len(crossed)], token)))
    cross_over(pair)
    (same[0], cross[0]), held = chunk([rows, pair], 6, None, size, size)
    left, right, same[0] = together(left, right, same[0])
    pieces, got = [left, right], [swap(left), swap(right)]
    left, right = ahead(left), behind(right)
    pieces[0], crossed[0] = together(pieces[0], crossed[0])
    cross_over(pieces[0])
    (same[1],), held = chunk(pieces, 7, held, 2 * size)
    left, right, same[1] = together(left, right, same[1])
    pieces, got = [left, right, *got], [swap(left), swap(right)]
    left, right = ahead(left), behind(right)
    pieces[0], crossed[1] = together(pieces[0], crossed[1])
    cross_over(pieces[0])
    (same[2], cross[1]), held = chunk(pieces, 0, held, 2 * size, 2 * size)
    left, right, same[2] = together(left, right, same[2])
    pieces, got = [left, right, *got], [swap(left), swap(right)]
    left, right = ahead(left[:cut]), behind(right[cut:])
    pieces[0], crossed[2] = together(pieces[0], crossed[2])
    cross_over(pieces[0])
    (same[3], cross[2]), held = chunk(pieces, 1, held, 2 * size, 2 * size)
    left, right, crossed[3], same[3] = together(left, right, crossed[3], same[3])
    pieces = [left, right, swap(left), swap(right), *got]
    (same[4], cross[4], cross[3]), held = chunk(pieces, 2, held, size, size, 2 * size)
    waiting = jnp.concatenate(crossed, axis=0)
    return same, cross, held, waiting


def body(
    inputs,
    attn_gain,
    w_query,
    w_key,
    w_value,
    query_gain,
    key_gain,
    w_out,
    moe_gain,
    w_gate,
    w_up,
    w_down,
    experts,
    gates,
    segments,
    gaps,
    cotangent,
):
    dp_count = lax.axis_size("dp")
    dp_index = lax.axis_index("dp")
    side = lax.axis_index("tensor")
    token_count, model_width = inputs.shape
    half_count = token_count // 2
    top_count = experts.shape[1]
    expert_count = w_gate.shape[0] * dp_count
    capacity = token_count * top_count * dp_count * 9 // (8 * expert_count)
    prompt_length = PR_DEV * GROUP
    column_total = HEADS * HEAD
    block = w_query.shape[0]
    local_width = w_query.shape[1]
    local_heads = local_width // HEAD

    def own_half(array):
        return lax.dynamic_slice_in_dim(array, side * half_count, half_count, axis=0)

    def other_half(array):
        return lax.dynamic_slice_in_dim(array, (1 - side) * half_count, half_count, axis=0)

    def both_halves(own, other):
        first = side == 0
        return jnp.concatenate(
            [jnp.where(first, own, other), jnp.where(first, other, own)], axis=0
        )

    gate_mats = (w_gate[0], swap_tensor(w_gate[0]))
    up_mats = (w_up[0], swap_tensor(w_up[0]))

    ring = dp_count == 2 * len(RING)

    gates_high = gates.astype(LOW)
    gates_low = (gates - gates_high.astype(FULL)).astype(LOW)
    routing = jnp.concatenate([experts.astype(LOW).T, gates_high.T, gates_low.T], axis=1)
    routing = jnp.pad(routing, ((0, 0), (0, local_width - 3 * token_count)))
    gains = jnp.concatenate([attn_gain, moe_gain, query_gain, key_gain])
    gains = jnp.pad(gains[None], ((0, 7), (0, local_width - 4 * block)))
    packed = pack_weights(
        w_query, w_key, w_value, w_out, jnp.concatenate([gains, routing], axis=0)
    )
    gathered = lax.all_gather(packed, "dp", axis=0, tiled=False)
    cotangent_half = own_half(cotangent)
    gathered_back = lax.all_gather(cotangent_half.astype(LOW), "dp", axis=0, tiled=False)
    core = dp_index % 2
    tokens_f = inputs.astype(FULL)
    prompt_pos = dp_index % GROUP * PR_DEV + jnp.arange(PR_DEV, dtype=jnp.int32)
    later_pos = cont_positions(segments[0], gaps[0], prompt_length)
    positions = jnp.concatenate([prompt_pos, later_pos], axis=0)
    cosine, sine = rope_tables(positions, HEAD)
    sine = jnp.where(jnp.arange(HEAD) < HEAD // 2, -sine, sine)
    prompt_query = jnp.arange(token_count, dtype=jnp.int32) < PR_DEV
    prompt_at = jnp.arange(prompt_length, dtype=jnp.int32)
    prompt_keypos = ((dp_index % GROUP) ^ (prompt_at // PR_DEV)) * PR_DEV + prompt_at % PR_DEV
    allowed_prompt = (~prompt_query)[:, None] | (prompt_keypos[None, :] <= positions[:, None])
    query_segment = jnp.concatenate([jnp.full((PR_DEV,), -1, jnp.int32), segments[0]], axis=0)
    allowed_cont = (query_segment[:, None] == segments[0][None, :]) & (
        later_pos[None, :] <= positions[:, None]
    )
    allowed = jnp.concatenate([allowed_prompt, allowed_cont], axis=1)
    bias = jnp.where(allowed, 0.0, -1e30).astype(LOW)
    gathered, cosine, sine, bias, *early = together(
        gathered, cosine, sine, bias, gate_mats[1], up_mats[1]
    )
    gate_mats, up_mats = (gate_mats[0], early[0]), (up_mats[0], early[1])
    rest = gathered[:, 4 * block : 4 * block + 16]
    gain_rows = rest[:, 0].astype(FULL)
    gain_one, gain_two, gain_q, gain_k = (
        gain_rows[:, j * block : (j + 1) * block].reshape(-1) for j in range(4)
    )
    gain_query_local = lax.dynamic_slice_in_dim(gain_q, side * local_width, local_width)
    gain_key_local = lax.dynamic_slice_in_dim(gain_k, side * local_width, local_width)

    names, *parts = (
        rest[:, 8:, j * token_count : (j + 1) * token_count] for j in range(3)
    )
    weights = parts[0].astype(FULL) + parts[1].astype(FULL)
    named = names == dp_index.astype(LOW)
    picked = jnp.sum(named.astype(FULL), axis=1)
    weight = jnp.sum(jnp.where(named, weights, 0.0), axis=1)
    order = jnp.arange(token_count, dtype=jnp.int32)
    earlier = (order[:, None] < order[None, :]).astype(LOW)
    within = dot_nn(picked.astype(LOW), earlier)
    per_row = jnp.sum(picked, axis=1)
    rows_order = jnp.arange(dp_count, dtype=jnp.int32)
    ahead = jnp.sum(
        jnp.where(rows_order[None, :] < rows_order[:, None], per_row[None, :], 0.0), axis=1
    )
    kept = (picked > 0.0) & (within + ahead[:, None] < capacity)
    weight = jnp.where(kept, weight, 0.0)
    weight = lax.dynamic_slice_in_dim(weight, side * half_count, half_count, axis=1)
    if ring:
        blocks, chips = ring_blocks(dp_index), ring_chips(dp_index, HOPS)
        weight = weight[blocks]
    weight = weight.reshape(-1, 1)

    normed_b = rms_norm(tokens_f, gain_one).astype(LOW)
    query_flat, key_flat, values_b, value_prompt = project(
        normed_b, gathered, block, (0, 1, 2), (FULL, FULL, LOW), (2,)
    )
    key_sq = jnp.sum(key_flat * key_flat, axis=1)
    key_sq, value_prompt = together(key_sq, value_prompt)
    value_pieces = collect_prompt(value_prompt, 1, 2)
    query_sq, key_sq = lax.psum(
        (jnp.sum(query_flat * query_flat, axis=1), key_sq), "tensor"
    )
    query_sq, down_mat = lax.optimization_barrier((query_sq, w_down[0]))
    down_mats = (down_mat, swap_tensor(down_mat))
    query_scale = lax.rsqrt(query_sq / column_total + EPSILON)[:, None]
    key_scale = lax.rsqrt(key_sq / column_total + EPSILON)[:, None]
    keys_b, key_prompt = rope_pass(key_flat, gain_key_local[None], key_scale, cosine, sine)
    pieces = (*collect_prompt(key_prompt, 2, 1), *value_pieces)
    turned_by = (gain_query_local[None], query_scale, cosine, sine, bias)
    context_b = attend(query_flat, *turned_by, keys_b, values_b, pieces)
    attn_part = project_back([context_b], gathered, block, (3,))
    attn_part, late, weight = together(attn_part, down_mats[1], weight)
    down_mats = (down_mats[0], late)
    mats = (*gate_mats, *up_mats, *down_mats)
    attn_other = swap_tensor(other_half(attn_part).astype(LOW))
    gathered_back = after(gathered_back, attn_part)
    if ring:
        back_rows = unpack_rows(gathered_back, blocks, 0, model_width)
    else:
        back_rows = gathered_back.reshape(-1, model_width)
    attn_other, back_rows, weight = together(attn_other, back_rows, weight)
    hidden_state = own_half(tokens_f) + own_half(attn_part) + attn_other.astype(FULL)
    normed_two_b = rms_norm(hidden_state, gain_two).astype(LOW)

    low_tn = lambda left, right: dot_tn(left, right).astype(LOW)
    upper = lambda array: array[: array.shape[0] // 2]
    lower = lambda array: array[array.shape[0] // 2 :]
    if ring:
        same, cross, held, hidden_other = expert_ring(
            normed_two_b, back_rows, weight, mats, hidden_state
        )
        expert_in, h0, h1, g0, g1, u0, u1 = held
        late = {}

        def down_stage(gated):
            late["down"] = swap_tensor(low_tn(gated(h1), back_rows))

        def gate_stage(gated):
            late["gate"] = low_tn(gated(expert_in), g1)

        def up_stage(gated):
            late["up"] = low_tn(gated(expert_in), u1)

        def mixed_stage(gated):
            late["mixed"] = mixed_pass(gated(h0), h1, down_mats, chips, core[None])

        fillers = Fillers(late, down_stage, gate_stage, up_stage, mixed_stage)
        normed_two_grad = ring_sum(same, cross, fillers)
        gate_sent, up_sent, mixed_rows = late["gate"], late["up"], late["mixed"]
        down_got = late["down"]
    else:
        hidden_other = swap_tensor(hidden_state)
        expert_in = lax.all_gather(normed_two_b, "dp", axis=0, tiled=True)
        grad_rows, h0, h1, g0, g1, u0, u1 = expert_pass(
            expert_in, back_rows, weight, gate_mats, up_mats, down_mats
        )
        normed_two_grad = lax.psum_scatter(
            grad_rows, "dp", scatter_dimension=0, tiled=True
        ).astype(FULL)
        mixed_rows = (dot_nn(h0, down_mats[0]) + dot_nn(h1, down_mats[1])).astype(LOW)
        down_got = swap_tensor(low_tn(h1, back_rows))
        gate_sent = low_tn(expert_in, g1)
        up_sent = low_tn(expert_in, u1)
    quarter = gate_sent.shape[0] // 4
    gate_first = swap_tensor(gate_sent[:quarter])
    normed_two_grad, down_got, gate_first, mixed_rows, up_sent = together(
        normed_two_grad, down_got, gate_first, mixed_rows, up_sent
    )
    mixed = lax.psum_scatter(mixed_rows, "dp", scatter_dimension=0, tiled=True)

    unused_two, norm_two_back = jax.vjp(rms_norm, hidden_state, gain_two)
    state_part, gain_two_grad = norm_two_back(normed_two_grad)
    state_half = cotangent_half + state_part
    attn_grad_half = state_half.astype(LOW)
    attn_grad_b = both_halves(attn_grad_half, swap_tensor(attn_grad_half))
    attn_grad_b, gate_sent, up_sent = together(attn_grad_b, gate_sent, up_sent)
    (context_grad_b,) = project(attn_grad_b, gathered, block, (3,), (LOW,))
    (gate_middle,) = swap_in_turn([gate_sent[quarter : 3 * quarter]], context_grad_b)
    soon = [
        swap_tensor(after(piece, gate_middle))
        for piece in (gate_sent[3 * quarter :], upper(up_sent))
    ]
    if ring:
        pair = lambda own: (own, swap_bit(own, "dp", 0))
        columns = local_width // 2
        context_sent = lax.dynamic_slice_in_dim(context_b, (1 - core) * columns, columns, axis=1)
        normed_pair, attn_grad_pair = pair(normed_b), pair(attn_grad_b)
        context_got = swap_bit(context_sent, "dp", 0)
    query_normed_grad, query_inner, query_gain_part, key_grad, value_grad, even, *odd = attend_back(
        query_flat, *turned_by, keys_b, values_b, pieces, context_grad_b
    )
    returned = return_prompt(odd, even)
    if ring:
        key_grad, context_got, *pairs = together(
            key_grad, context_got, normed_pair[1], attn_grad_pair[1]
        )
        normed_pair, attn_grad_pair = (normed_b, pairs[0]), (attn_grad_b, pairs[1])
    key_normed_grad, key_inner, key_gain_part, value_pre_grad = key_back(
        key_grad, value_grad, key_flat, gain_key_local[None], key_scale, cosine, sine, returned
    )
    query_inner, *soon = together(query_inner, *soon)
    query_inner, key_inner = lax.psum(
        jnp.stack([query_inner[:, 0], key_inner[:, 0]], axis=0), "tensor"
    )
    query_pre_grad, key_pre_grad, pre_sent = pre_grads_pass(
        core[None],
        (
            query_flat,
            query_normed_grad,
            gain_query_local[None],
            query_scale,
            query_inner[:, None],
        ),
        (key_flat, key_normed_grad, gain_key_local[None], key_scale, key_inner[:, None]),
        value_pre_grad,
    )
    gate_got = jnp.concatenate([gate_first, gate_middle, soon[0]], axis=0)
    pre_grads = (query_pre_grad, key_pre_grad, value_pre_grad)
    grad_sum = lambda left, right, got: dot_tn(left, right) + got.astype(FULL)
    back_all = lambda *grads: project_back(grads, gathered, block, (0, 1, 2))

    wide = lambda part: lax.dynamic_update_slice_in_dim(
        jnp.zeros((column_total,), FULL), part, side * local_width, 0
    )

    def back_shares(*grads):
        part = back_all(*grads)
        return own_half(part), other_half(part).astype(LOW), gain_part(part)

    def input_side(own, other):
        unused_one, norm_one_back = jax.vjp(
            lambda values: rms_norm(values, gain_one), own_half(tokens_f)
        )
        return state_half + norm_one_back(own + other.astype(FULL))[0]

    def gain_part(part):
        return jnp.sum(part * rms_norm(tokens_f, 1.0), axis=0)

    def gain_side(gain_one_grad):
        grads = jnp.stack(
            [gain_one_grad, gain_two_grad, wide(query_gain_part[0]), wide(key_gain_part[0])]
        ).reshape(4, dp_count, block)
        grads = jnp.swapaxes(grads, 0, 1).reshape(dp_count, 1, 4 * block)
        sides = lax.axis_size("tensor")
        grads = jnp.broadcast_to(grads, (dp_count, sides, 4 * block))
        grads = grads.reshape(dp_count * sides, 4 * block)
        sums = lax.all_to_all(grads, ("dp", "tensor"), 0, 0, tiled=True)
        return jnp.sum(sums, axis=0).reshape(4, block)

    if ring:
        pre_got = swap_bit(pre_sent, "dp", 0)
        w_blocks, *far = weight_grads(
            chips,
            core[None],
            normed_pair,
            attn_grad_pair,
            pre_grads,
            pre_got,
            context_b,
            context_got,
        )
        w_blocks, mixed, *far = together(w_blocks, mixed, *far)
        up_pieces = swap_in_turn(cut_rows(lower(up_sent), 2), far[0])
        late, later = {}, {}

        def normed_stage(gated):
            late["own"], late["sent"], late["gain"] = back_shares(*map(gated, pre_grads))

        def gate_product_stage(gated):
            other = swap_tensor(late["sent"])
            late["gate"] = grad_sum(gated(expert_in), g0, gate_got)
            late["mixed"], late["pieces"] = gated(mixed), up_pieces
            later["other"] = other

        def input_stage(gated):
            later["mixed"] = swap_tensor(late["mixed"])
            late["half"] = input_side(late["own"], gated(later["other"]))
            later["half"] = swap_tensor(late["half"])
            late["down"] = grad_sum(gated(h0), back_rows, down_got)
            late["gains"] = gain_side(gated(late["gain"]))

        def up_product_stage(gated):
            up_got = jnp.concatenate([soon[1], *late["pieces"]], axis=0)
            late["up"] = grad_sum(gated(expert_in), u0, up_got)
            late["mixed_other"] = later["mixed"]

        fillers = Fillers(
            late, normed_stage, gate_product_stage, input_stage, up_product_stage
        )
        w_parts = ring_weights(w_blocks, *far, fillers)
        input_half, input_other = late["half"], later["half"]
        gain_sums = late["gains"]
        down_grad, gate_w_grad, up_w_grad = late["down"], late["gate"], late["up"]
        own_w, sent_w = sum_weights(core[None], *w_parts)
        w_sums = place_weights(core[None], own_w, swap_bit(sent_w, "dp", 0))
        mixed_other = late["mixed_other"]
    else:
        w_grads = jnp.concatenate(
            [low_tn(normed_b, g) for g in pre_grads] + [low_tn(attn_grad_b, context_b)], axis=1
        )
        w_sum = lax.psum_scatter(w_grads, "dp", scatter_dimension=0, tiled=True).astype(FULL)
        w_sums = [w_sum[:, j * local_width : (j + 1) * local_width] for j in range(4)]
        w_sums[3] = w_sums[3].T
        down_grad = grad_sum(h0, back_rows, down_got)
        gate_w_grad = grad_sum(expert_in, g0, gate_got)
        up_got = jnp.concatenate([soon[1], swap_tensor(lower(up_sent))], axis=0)
        up_w_grad = grad_sum(expert_in, u0, up_got)
        mixed_other = swap_tensor(mixed)
        normed_own, normed_sent, gain_one_grad = back_shares(*pre_grads)
        gain_sums = gain_side(gain_one_grad)
        input_half = input_side(normed_own, swap_tensor(normed_sent))
        input_other = swap_tensor(input_half)
    input_grad = join_halves(side[None], [input_half], [input_other])
    output = join_halves(side[None], [hidden_state, mixed], [hidden_other, mixed_other])
    return (
        output,
        input_grad,
        gain_sums[0],
        w_sums[0],
        w_sums[1],
        w_sums[2],
        gain_sums[2],
        gain_sums[3],
        w_sums[3],
        gain_sums[1],
        gate_w_grad[None],
        up_w_grad[None],
        down_grad[None],
    )


def solution(mesh):
    return jax.shard_map(
        body,
        mesh=mesh,
        in_specs=(
            P("dp", None),
            P("dp"),
            P("dp", "tensor"),
            P("dp", "tensor"),
            P("dp", "tensor"),
            P("dp"),
            P("dp"),
            P("tensor", "dp"),
            P("dp"),
            P("dp", None, "tensor"),
            P("dp", None, "tensor"),
            P("dp", "tensor", None),
            P("dp", None),
            P("dp", None),
            P("dp", None),
            P("dp", None),
            P("dp", None),
        ),
        out_specs=(
            P("dp", None),
            P("dp", None),
            P("dp"),
            P("dp", "tensor"),
            P("dp", "tensor"),
            P("dp", "tensor"),
            P("dp"),
            P("dp"),
            P("tensor", "dp"),
            P("dp"),
            P("dp", None, "tensor"),
            P("dp", None, "tensor"),
            P("dp", "tensor", None),
        ),
        check_vma=False,
    )
```

```python
import jax
import jax.numpy as jnp
from jax import lax
from jax.experimental import pallas as pl
from jax.experimental.pallas import tpu as pltpu
from jax.sharding import PartitionSpec as P

HEADS = 16
HEAD = 128
GROUP = 8
PR_DEV = 128


EPSILON = 1e-05
VMEM = 60 * 1024 * 1024
LOW = jnp.bfloat16
FULL = jnp.float32


def swap_bit(block, axis, bit):
    count = lax.axis_size(axis)
    return lax.ppermute(block, axis, [(i, i ^ (1 << bit)) for i in range(count)])


def swap_tensor(block):
    return lax.ppermute(block, "tensor", [(0, 1), (1, 0)])


RING = (0, 2, 4, 6, 7, 5, 3, 1)
AHEAD = [
    (RING[p] * 2 + c, RING[(p + 1) % len(RING)] * 2 + c) for p in range(len(RING)) for c in range(2)
]
BEHIND = [(to, at) for at, to in AHEAD]
HOPS = (-1, 1, -2, 2, -3, 3, 0, 4)
LAYOUT = (
    *((-2, 0), (2, 0), (-1, 1), (1, 1)),
    *((-3, 0), (3, 0), (-2, 1), (2, 1)),
    *((4, 0), (4, 1), (-3, 1), (3, 1)),
    *((0, 0), (0, 1)),
    *((-1, 0), (1, 0)),
)


def ahead(block):
    return lax.ppermute(block, "dp", AHEAD)


def behind(block):
    return lax.ppermute(block, "dp", BEHIND)


def ring_chips(dp_index, hops):
    chip = dp_index // 2
    place = jnp.where(chip % 2 == 0, chip // 2, 7 - chip // 2)
    there = (place + jnp.array(hops, jnp.int32)) % len(RING)
    return jnp.where(there < 4, 2 * there, 2 * (7 - there) + 1)


def ring_blocks(dp_index):
    chips = ring_chips(dp_index, [hop for hop, _ in LAYOUT])
    return 2 * chips + (dp_index % 2 ^ jnp.array([cross for _, cross in LAYOUT], jnp.int32))


def add_low(*parts):
    total = parts[0].astype(FULL)
    for part in parts[1:]:
        total = total + part.astype(FULL)
    return total.astype(LOW)


def together(value, *others):
    return lax.optimization_barrier((value, *others))


def after(value, token):
    return lax.optimization_barrier((value, token))[0]


class Fillers:
    def __init__(self, late, *stages):
        self.late, self.stages, self.seen = late, list(stages), set(late)

    def next(self, token):
        if self.stages:
            self.stages.pop(0)(lambda value: after(value, token))

    def settle(self, *blocks):
        due = {key: value for key, value in self.late.items() if key not in self.seen}
        self.seen.update(due)
        *blocks, due = lax.optimization_barrier((*blocks, due))
        self.late.update(due)
        return blocks


def ring_sum(same, cross, fillers):
    both = {hop: add_low(same[hop], swap_bit(cross[hop], "dp", 0)) for hop in (4, 3, 2, 1, 0)}
    rows = both[0].shape[0]
    cut = rows // 2
    fillers.next(both[4])
    right, left = ahead(both[4][:cut]), behind(both[4][cut:])
    fillers.next(left)
    outward, inward = both[3][rows:], both[3][:rows]
    right = jnp.concatenate([add_low(outward[:cut], right), outward[cut:]], axis=0)
    left = jnp.concatenate([inward[:cut], add_low(inward[cut:], left)], axis=0)
    right, left = ahead(right), behind(left)
    fillers.next(left)
    for hop in (2, 1):
        right = ahead(add_low(both[hop][rows:], right))
        left = behind(add_low(both[hop][:rows], left))
        fillers.next(left)
    return both[0].astype(FULL) + right.astype(FULL) + left.astype(FULL)


def swap_in_turn(pieces, token):
    got = []
    for piece in pieces:
        got.append(swap_tensor(after(piece, token)))
        token = got[-1]
    return got


def cut_rows(array, count):
    rows = array.shape[0] // count
    return [array[i * rows : (i + 1) * rows] for i in range(count)]


def rms_norm(values, gain):
    return values * lax.rsqrt(jnp.mean(values * values, axis=-1, keepdims=True) + EPSILON) * gain


def rope_tables(positions, head_size):
    half_size = head_size // 2
    inverse = 10000.0 ** (-(jnp.arange(half_size, dtype=FULL) * 2.0) / head_size)
    angles = positions.astype(FULL)[:, None] * inverse[None, :]
    cosine = jnp.concatenate([jnp.cos(angles), jnp.cos(angles)], axis=-1)
    sine = jnp.concatenate([jnp.sin(angles), jnp.sin(angles)], axis=-1)
    return (cosine, sine)


def cont_positions(segment_row, gap_row, prompt_length):
    order = jnp.arange(segment_row.shape[0], dtype=jnp.int32)
    same = segment_row[:, None] == segment_row[None, :]
    earlier = order[None, :] < order[:, None]
    offset = jnp.sum((same & earlier).astype(jnp.int32), axis=1)
    labels = jnp.arange(gap_row.shape[0], dtype=jnp.int32)
    shifted = jnp.sum(
        jnp.where(segment_row[:, None] == labels[None, :], gap_row[None, :], 0), axis=1
    )
    return prompt_length + shifted + offset


def dot_nn(left, right):
    return jnp.dot(left, right, preferred_element_type=FULL)


def dot_tn(left, right):
    return lax.dot_general(left, right, (((0,), (0,)), ((), ())), preferred_element_type=FULL)


def dot_nt(left, right):
    return lax.dot_general(left, right, (((1,), (1,)), ((), ())), preferred_element_type=FULL)


def collect_prompt(own, first, second):
    near, far = swap_bit(own, "dp", 1), swap_bit(own, "dp", 2)
    last = swap_bit(near if first == 1 else far, "dp", second)
    blocks = []
    for block in (own, near, far, last):
        blocks += [block, swap_bit(block, "dp", 0)]
    return blocks[1:]


SMALL = pl.CostEstimate(flops=1, bytes_accessed=1, transcendentals=0)


def merge_kernel(even_ref, *refs):
    got, (keys_ref, values_ref, far_ref, near_ref) = refs[:3], refs[3:]
    near, far, last = 0, 1, 2
    add = lambda j, which: add_low(even_ref[j, which], got[j][which])
    keys_ref[0], keys_ref[1] = add(near, 0), add(last, 0)
    values_ref[0], values_ref[1] = add(far, 1), add(last, 1)
    far_ref[...], near_ref[...] = add(far, 0), add(near, 1)


def return_prompt(odd, even):
    got = [swap_bit(block, "dp", 0) for block in odd]
    one = jax.ShapeDtypeStruct(even.shape[2:], LOW)
    two = jax.ShapeDtypeStruct(even.shape[1:], LOW)
    keys, values, far, near = pl.pallas_call(
        merge_kernel, out_shape=[two, two, one, one], cost_estimate=SMALL
    )(even, *got[1:])
    keys, values = swap_bit(keys, "dp", 1), swap_bit(values, "dp", 2)
    last_keys = swap_bit(add_low(far, keys[1]), "dp", 2)
    last_values = swap_bit(add_low(near, values[1]), "dp", 1)
    return got[0], keys, values, last_keys, last_values


def turn(values):
    return pltpu.roll(values, HEAD // 2, 1)


def rope_kernel(pre_ref, gain_ref, scale_ref, cos_ref, sin_ref, out_ref, first_ref):
    scale, cosine, sine = scale_ref[...], cos_ref[...], sin_ref[...]
    for at in range(0, pre_ref.shape[1], HEAD):
        span = slice(at, at + HEAD)
        normed = pre_ref[:, span] * scale * gain_ref[:, span]
        out_ref[:, span] = (normed * cosine + turn(normed) * sine).astype(LOW)
    first_ref[...] = out_ref[: first_ref.shape[0]]


def rope_pass(flat, gain, scale, cosine, sine):
    rows, width = flat.shape
    part = width // 2
    wide = lambda rows: pl.BlockSpec((rows, part), lambda h: (0, h))
    return pl.pallas_call(
        rope_kernel,
        grid=(2,),
        in_specs=[wide(rows), wide(1)] + [kept_spec(a) for a in (scale, cosine, sine)],
        out_specs=[wide(rows), wide(PR_DEV)],
        out_shape=[jax.ShapeDtypeStruct((count, width), LOW) for count in (rows, PR_DEV)],
    )(flat, gain, scale, cosine, sine)


PAIR = 2


def head_spec(rows):
    return pl.BlockSpec((rows, PAIR * HEAD), lambda h: (0, h))


def kept_spec(array):
    zeros = (0,) * array.ndim
    return pl.BlockSpec(array.shape, lambda h: zeros, pipeline_mode=pl.Buffered(1))


def all_keys(own_ref, pieces, span):
    return jnp.concatenate(
        [own_ref[:PR_DEV, span]] + [p[:, span] for p in pieces] + [own_ref[PR_DEV:, span]], axis=0
    )


def turned_query(flat_ref, gain_ref, scale, cosine, sine, span):
    normed = flat_ref[:, span] * scale * gain_ref[:, span]
    return (normed * cosine + turn(normed) * sine).astype(LOW)


def softmax_rows(query, keys, bias):
    scores = dot_nt(query, keys) * HEAD ** (-0.5) + bias
    weights = jnp.exp(scores - jnp.max(scores, axis=1, keepdims=True))
    return weights * (1.0 / jnp.sum(weights, axis=1, keepdims=True))


PIECES = GROUP - 1


def attend_kernel(flat_ref, gain_ref, scale_ref, cos_ref, sin_ref, bias_ref, k_ref, v_ref, *refs):
    out_ref = refs[-1]
    bias = bias_ref[...].astype(FULL)
    scale, cosine, sine = scale_ref[...], cos_ref[...], sin_ref[...]
    for at in range(0, PAIR * HEAD, HEAD):
        span = slice(at, at + HEAD)
        query = turned_query(flat_ref, gain_ref, scale, cosine, sine, span)
        probs = softmax_rows(query, all_keys(k_ref, refs[:PIECES], span), bias)
        values = all_keys(v_ref, refs[PIECES : 2 * PIECES], span)
        out_ref[:, span] = dot_nn(probs.astype(LOW), values).astype(LOW)


def attend_specs(rows, scale, cosine, sine, bias):
    return (
        [head_spec(rows), head_spec(1)]
        + [kept_spec(a) for a in (scale, cosine, sine, bias)]
        + [head_spec(rows)] * 2
        + [head_spec(PR_DEV)] * (2 * PIECES)
    )


def attend(flat, gain, scale, cosine, sine, bias, keys, values, pieces):
    rows, width = flat.shape
    return pl.pallas_call(
        attend_kernel,
        grid=(width // HEAD // PAIR,),
        in_specs=attend_specs(rows, scale, cosine, sine, bias),
        out_specs=head_spec(rows),
        out_shape=jax.ShapeDtypeStruct((rows, width), LOW),
        compiler_params=pltpu.CompilerParams(vmem_limit_bytes=VMEM),
    )(flat, gain, scale, cosine, sine, bias, keys, values, *pieces)


def norm_parts(step, at, grad, flat_ref, gain_ref, scale_ref, inner_ref, gain_grad_ref):
    span = slice(at, at + HEAD)
    product = flat_ref[:, span] * grad
    inner = jnp.sum(product * gain_ref[:, span], axis=1, keepdims=True)
    gain_grad_ref[:, span] = jnp.sum(product * scale_ref[...], axis=0, keepdims=True)
    if at:
        inner_ref[...] += inner
    else:
        inner_ref[...] = jnp.where(step == 0, 0.0, inner_ref[...]) + inner


def attend_back_kernel(
    flat_ref, gain_ref, scale_ref, cos_ref, sin_ref, bias_ref, k_ref, v_ref, *refs
):
    back_ref = refs[2 * PIECES]
    qg_ref, inner_ref, gain_grad_ref, kg_ref, vg_ref, even_ref = refs[2 * PIECES + 1 : -4]
    odd_refs = refs[-4:]
    step = pl.program_id(0)
    bias = bias_ref[...].astype(FULL)
    scale, cosine, sine = scale_ref[...], cos_ref[...], sin_ref[...]
    prompt = PR_DEV * GROUP
    for at in range(0, PAIR * HEAD, HEAD):
        span = slice(at, at + HEAD)
        query = turned_query(flat_ref, gain_ref, scale, cosine, sine, span)
        back = back_ref[:, span]
        keys = all_keys(k_ref, refs[:PIECES], span)
        values = all_keys(v_ref, refs[PIECES : 2 * PIECES], span)
        probs = softmax_rows(query, keys, bias)
        prob_grad = dot_nt(back, values)
        value_grad = dot_tn(probs.astype(LOW), back)
        row_dot = jnp.sum(probs * prob_grad, axis=1, keepdims=True)
        score_grad = (probs * (prob_grad - row_dot)).astype(LOW)
        query_grad = dot_nn(score_grad, keys) * HEAD ** (-0.5)
        key_grad = dot_tn(score_grad, query) * HEAD ** (-0.5)
        query_grad = query_grad * cosine - turn(query_grad) * sine
        qg_ref[:, span] = query_grad
        norm_parts(step, at, query_grad, flat_ref, gain_ref, scale_ref, inner_ref, gain_grad_ref)
        for which, grad, own_ref in ((0, key_grad, kg_ref), (1, value_grad, vg_ref)):
            own_ref[:PR_DEV, span] = grad[:PR_DEV]
            own_ref[PR_DEV:, span] = grad[prompt:]
            for j in range(1, GROUP):
                to = odd_refs[j // 2] if j % 2 else even_ref.at[j // 2 - 1]
                to[which, :, span] = grad[j * PR_DEV : (j + 1) * PR_DEV].astype(LOW)


def attend_back(flat, gain, scale, cosine, sine, bias, keys, values, pieces, back):
    rows, width = flat.shape
    wide = jax.ShapeDtypeStruct((rows, width), FULL)
    both = pl.BlockSpec((3, 2, PR_DEV, PAIR * HEAD), lambda h: (0, 0, 0, h))
    return pl.pallas_call(
        attend_back_kernel,
        grid=(width // HEAD // PAIR,),
        in_specs=attend_specs(rows, scale, cosine, sine, bias) + [head_spec(rows)],
        out_specs=[
            head_spec(rows),
            pl.BlockSpec((rows, 1), lambda h: (0, 0)),
            head_spec(1),
            head_spec(rows),
            head_spec(rows),
            both,
        ]
        + [pl.BlockSpec((2, PR_DEV, PAIR * HEAD), lambda h: (0, 0, h))] * 4,
        out_shape=[
            wide,
            jax.ShapeDtypeStruct((rows, 1), FULL),
            jax.ShapeDtypeStruct((1, width), FULL),
            wide,
            wide,
            jax.ShapeDtypeStruct((3, 2, PR_DEV, width), LOW),
        ]
        + [jax.ShapeDtypeStruct((2, PR_DEV, width), LOW)] * 4,
        compiler_params=pltpu.CompilerParams(vmem_limit_bytes=VMEM),
        cost_estimate=pl.CostEstimate(
            flops=20 * 10**9, bytes_accessed=40 * 10**6, transcendentals=4 * 10**6
        ),
    )(flat, gain, scale, cosine, sine, bias, keys, values, *pieces, back)


def key_back_kernel(*refs):
    kg_ref, vg_ref, flat_ref, gain_ref, scale_ref, cos_ref, sin_ref = refs[:7]
    got, keys, values, last_keys, last_values = refs[7:12]
    out_ref, inner_ref, gain_grad_ref, value_ref = refs[12:]
    step = pl.program_id(0)
    for at in range(0, PAIR * HEAD, HEAD):
        span = slice(at, at + HEAD)
        grads = []
        for which, own_ref, near, last in ((0, kg_ref, keys, last_keys), (1, vg_ref, values, last_values)):
            first = own_ref[:PR_DEV, span] + got[which, :, span].astype(FULL)
            first = first + near[0, :, span].astype(FULL) + last[:, span].astype(FULL)
            grads.append(jnp.concatenate([first, own_ref[PR_DEV:, span]], axis=0))
        key_grad = grads[0] * cos_ref[...] - turn(grads[0]) * sin_ref[...]
        out_ref[:, span] = key_grad
        norm_parts(step, at, key_grad, flat_ref, gain_ref, scale_ref, inner_ref, gain_grad_ref)
        value_ref[:, span] = grads[1].astype(LOW)


def key_back(key_grad, value_grad, flat, gain, scale, cosine, sine, returned):
    rows, width = flat.shape
    columns = PAIR * HEAD
    return pl.pallas_call(
        key_back_kernel,
        grid=(width // columns,),
        in_specs=[head_spec(rows)] * 3
        + [head_spec(1)]
        + [kept_spec(a) for a in (scale, cosine, sine)]
        + [pl.BlockSpec((2, PR_DEV, columns), lambda h: (0, 0, h))]
        + [pl.BlockSpec((1, PR_DEV, columns), lambda h: (0, 0, h))] * 2
        + [head_spec(PR_DEV)] * 2,
        out_specs=[
            head_spec(rows),
            pl.BlockSpec((rows, 1), lambda h: (0, 0)),
            head_spec(1),
            head_spec(rows),
        ],
        out_shape=[
            jax.ShapeDtypeStruct((rows, width), FULL),
            jax.ShapeDtypeStruct((rows, 1), FULL),
            jax.ShapeDtypeStruct((1, width), FULL),
            jax.ShapeDtypeStruct((rows, width), LOW),
        ],
        cost_estimate=SMALL,
    )(key_grad, value_grad, flat, gain, scale, cosine, sine, *returned)


def pack_kernel(query, key, value, out, rest, packed):
    at = 0
    for ref in (query, key, value):
        packed[at : at + ref.shape[0]] = ref[...]
        at += ref.shape[0]
    packed[at : at + out.shape[1]] = out[...].T
    packed[at + out.shape[1] :] = rest[...]


def pack_weights(w_query, w_key, w_value, w_out, rest):
    rows = 4 * w_query.shape[0] + rest.shape[0]
    return pl.pallas_call(
        pack_kernel, out_shape=jax.ShapeDtypeStruct((rows, w_query.shape[1]), LOW)
    )(w_query, w_key, w_value, w_out, rest)


def unpack_kernel(first, blocks_ref, packed, out, held, sems):
    width = packed.shape[2]
    parts = out.shape[1] // width
    rows = (packed.shape[1] - first) // parts
    count = packed.shape[0]
    place = lambda i: pl.ds(i * rows, rows)
    loads = [
        pltpu.make_async_copy(
            packed.at[blocks_ref[i], pl.ds(first + j * rows, rows)],
            held.at[place(i), pl.ds(j * width, width)],
            sems.at[i * parts + j],
        )
        for i in range(count)
        for j in range(parts)
    ]
    stores = [
        pltpu.make_async_copy(held.at[place(i)], out.at[place(i)], sems.at[count * parts + i])
        for i in range(count)
    ]
    for one in loads:
        one.start()
    for i, store in enumerate(stores):
        for j in range(parts):
            loads[i * parts + j].wait()
        store.start()
    for store in stores:
        store.wait()


def unpack_rows(packed, blocks, first, width):
    count = packed.shape[0]
    parts = width // packed.shape[2]
    rows = (packed.shape[1] - first) // parts
    return pl.pallas_call(
        lambda *refs: unpack_kernel(first, *refs),
        in_specs=[pl.BlockSpec(memory_space=pltpu.SMEM), pl.BlockSpec(memory_space=pl.ANY)],
        out_specs=pl.BlockSpec(memory_space=pl.ANY),
        out_shape=jax.ShapeDtypeStruct((count * rows, width), LOW),
        scratch_shapes=[
            pltpu.VMEM((count * rows, width), LOW),
            pltpu.SemaphoreType.DMA((count * parts + count,)),
        ],
        compiler_params=pltpu.CompilerParams(vmem_limit_bytes=VMEM),
    )(blocks, packed)


def load_packed(gathered, places, block, held, sems):
    copies = [
        pltpu.make_async_copy(
            gathered.at[:, pl.ds(place * block, block)], held.at[k], sems.at[k]
        )
        for k, place in enumerate(places)
    ]
    for one in copies:
        one.start()
    return copies


def held_pack(gathered, places, block):
    count, columns = gathered.shape[0], gathered.shape[2]
    return [
        pltpu.VMEM((len(places), count, block, columns), LOW),
        pltpu.SemaphoreType.DMA((len(places),)),
    ]


def project_kernel(places, block, heads, rows_ref, gathered, *refs):
    outs, firsts, (held, sems) = refs[: len(places)], refs[len(places) : -2], refs[-2:]
    copies = load_packed(gathered, places, block, held, sems)
    rows = rows_ref[...]
    for k, (one, out) in enumerate(zip(copies, outs)):
        one.wait()
        out[...] = dot_nn(rows, held[k].reshape(-1, out.shape[1])).astype(out.dtype)
    for first, k in zip(firsts, heads):
        first[...] = outs[k][: first.shape[0]]


def project(rows, gathered, block, places, roundings, heads=()):
    count, width = rows.shape
    columns = gathered.shape[2]
    outs = [jax.ShapeDtypeStruct((count, columns), rounding) for rounding in roundings]
    outs += [jax.ShapeDtypeStruct((PR_DEV, columns), roundings[k]) for k in heads]
    fixed = lambda a: pl.BlockSpec(a.shape, lambda i: (0, 0))
    return pl.pallas_call(
        lambda *refs: project_kernel(places, block, heads, *refs),
        grid=(1,),
        in_specs=[fixed(rows), pl.BlockSpec(memory_space=pl.ANY)],
        out_specs=[fixed(out) for out in outs],
        out_shape=outs,
        scratch_shapes=held_pack(gathered, places, block),
        compiler_params=pltpu.CompilerParams(vmem_limit_bytes=VMEM),
        cost_estimate=pl.CostEstimate(
            flops=2 * count * width * columns * len(places),
            bytes_accessed=2 * width * columns * len(places) + 8 * count * columns,
            transcendentals=0,
        ),
    )(rows, gathered)


def pack_specs(gathered, places, steps, at):
    count, width = gathered.shape[0] // steps, gathered.shape[2]
    block = at
    return [
        pl.BlockSpec((count, block, width), lambda i, place=place: (i, place, 0))
        for place in places
    ]


def project_back_kernel(mats, *refs):
    out = refs[-1]
    total = None
    for rows_ref, mat in zip(refs[:mats], refs[mats:-1]):
        part = dot_nt(rows_ref[...], mat[...].reshape(-1, mat.shape[2]))
        total = part if total is None else total + part
    out[...] = total


def project_back(rows, gathered, block, places):
    count, columns = rows[0].shape
    width = gathered.shape[0] * block
    steps = 4 if len(places) > 1 else 2
    fixed = pl.BlockSpec((count, columns), lambda i: (0, 0), pipeline_mode=pl.Buffered(1))
    return pl.pallas_call(
        lambda *refs: project_back_kernel(len(places), *refs),
        grid=(steps,),
        in_specs=[fixed] * len(rows) + pack_specs(gathered, places, steps, block),
        out_specs=pl.BlockSpec((count, width // steps), lambda i: (0, i)),
        out_shape=jax.ShapeDtypeStruct((count, width), FULL),
        compiler_params=pltpu.CompilerParams(vmem_limit_bytes=VMEM),
        cost_estimate=pl.CostEstimate(
            flops=2 * count * width * columns * len(places),
            bytes_accessed=2 * width * columns * len(places) + 4 * count * width,
            transcendentals=0,
        ),
    )(*rows, *[gathered] * len(places))


def pre_kernel(core_ref, *refs):
    inputs, outs = refs[:11], refs[11:]
    step = pl.program_id(0)
    columns = inputs[0].shape[1]
    parts = []
    for flat, grad, gain, scale, inner in (inputs[:5], inputs[5:10]):
        scaled = scale[...]
        mean = inner[...] * (1.0 / (HEADS * HEAD))
        parts.append(
            (
                scaled * gain[...] * grad[...] - flat[...] * (scaled * scaled * scaled) * mean
            ).astype(LOW)
        )
    outs[0][...], outs[1][...] = parts

    @pl.when(step != core_ref[0])
    def _():
        for j, part in enumerate((*parts, inputs[10][...])):
            outs[2][:, j * columns : (j + 1) * columns] = part


def pre_grads_pass(core, query, key, value):
    rows, width = value.shape
    columns = width // 2
    half = lambda rows: pl.BlockSpec((rows, columns), lambda h: (0, h))
    side = [half(rows), half(rows), half(1)] + [pl.BlockSpec((rows, 1), lambda h: (0, 0))] * 2
    return pl.pallas_call(
        pre_kernel,
        grid=(2,),
        in_specs=[pl.BlockSpec(memory_space=pltpu.SMEM)] + side + side + [half(rows)],
        out_specs=[half(rows), half(rows), pl.BlockSpec((rows, 3 * columns), lambda h: (0, 0))],
        out_shape=[jax.ShapeDtypeStruct((rows, width), LOW)] * 2
        + [jax.ShapeDtypeStruct((rows, 3 * columns), LOW)],
    )(core, *query, *key, value)


def weight_kernel(chip_ref, core_ref, *refs):
    normed, normed_got, back, back_got, query, key, value, got, context, context_got = refs[:10]
    out_ref, right_ref, left_ref, pre_both, context_both = refs[10:]
    rows, columns = query.shape

    @pl.when(pl.program_id(0) == 0)
    def _():
        for j, part in enumerate((query, key, value)):
            pre_both[:rows, j * columns : (j + 1) * columns] = part[...]
        pre_both[rows:] = got[...]
        context_both[:rows] = context[...]
        context_both[rows:] = context_got[...]

    left = jnp.concatenate([normed[...], normed_got[...]], axis=0)
    out_ref[0, :, : 3 * columns] = dot_tn(left, pre_both[...]).astype(LOW)
    left = jnp.concatenate([back[...], back_got[...]], axis=0)
    out_ref[0, :, 3 * columns :] = dot_tn(left, context_both[...]).astype(LOW)

    @pl.when(pl.program_id(0) == HOPS.index(4))
    def _():
        right_ref[...] = out_ref[0, :, : 2 * columns]
        left_ref[...] = out_ref[0, :, 2 * columns :]


def weight_grads(chips, core, normed, back, pre_grads, got, context, context_got):
    rows, width = normed[0].shape
    columns = context_got.shape[1]
    count = chips.shape[0]
    block = width // count
    tall = pl.BlockSpec((rows, block), lambda i, chip, core: (0, chip[i]))
    mine = pl.BlockSpec((rows, columns), lambda i, chip, core: (0, core[0]))
    fixed = lambda a: pl.BlockSpec(a.shape, lambda i, chip, core: (0, 0))
    return pl.pallas_call(
        weight_kernel,
        grid_spec=pltpu.PrefetchScalarGridSpec(
            num_scalar_prefetch=2,
            grid=(count,),
            in_specs=[tall] * 4 + [mine] * 3 + [fixed(got), mine, fixed(context_got)],
            out_specs=[pl.BlockSpec((1, block, 4 * columns), lambda i, chip, core: (i, 0, 0))]
            + [pl.BlockSpec((block, 2 * columns), lambda i, chip, core: (0, 0))] * 2,
            scratch_shapes=[
                pltpu.VMEM((2 * rows, 3 * columns), LOW),
                pltpu.VMEM((2 * rows, columns), LOW),
            ],
        ),
        out_shape=[jax.ShapeDtypeStruct((count, block, 4 * columns), LOW)]
        + [jax.ShapeDtypeStruct((block, 2 * columns), LOW)] * 2,
        compiler_params=pltpu.CompilerParams(vmem_limit_bytes=VMEM),
        cost_estimate=pl.CostEstimate(
            flops=16 * rows * width * columns,
            bytes_accessed=2 * (4 * rows * width + 8 * rows * columns + 4 * width * columns),
            transcendentals=0,
        ),
    )(chips, core, *normed, *back, *pre_grads, got, context, context_got)


def ring_weights(blocks, right, left, fillers):
    part = lambda hop: blocks[HOPS.index(hop)]
    cut = blocks.shape[2] // 2
    fillers.next(right)
    right, left = ahead(right), behind(left)
    right, left = fillers.settle(right, left)
    fillers.next(left)
    outward, inward = part(3), part(-3)
    right = jnp.concatenate([add_low(outward[:, :cut], right), outward[:, cut:]], axis=1)
    left = jnp.concatenate([inward[:, :cut], add_low(inward[:, cut:], left)], axis=1)
    right, left = together(right, left)
    right, left = ahead(right), behind(left)
    for hop in (2, 1):
        right, left = fillers.settle(right, left)
        fillers.next(left)
        right, left = together(add_low(part(hop), right), add_low(part(-hop), left))
        right, left = ahead(right), behind(left)
    right, left = fillers.settle(right, left)
    return blocks, right, left


def sum_kernel(core_ref, blocks_ref, right_ref, left_ref, own_ref, sent_ref):
    rows = own_ref.shape[0]
    for k, out in enumerate((own_ref, sent_ref)):
        side = core_ref[0] if k == 0 else 1 - core_ref[0]
        span = pl.ds(pl.multiple_of(side * rows, rows), rows)
        out[...] = (
            blocks_ref[0, span].astype(FULL)
            + right_ref[span].astype(FULL)
            + left_ref[span].astype(FULL)
        )


def sum_weights(core, blocks, right, left):
    rows, width = right.shape
    whole = pl.BlockSpec((rows, width), lambda i: (0, 0))
    half = pl.BlockSpec((rows // 2, width), lambda i: (0, 0))
    return pl.pallas_call(
        sum_kernel,
        grid=(1,),
        in_specs=[
            pl.BlockSpec(memory_space=pltpu.SMEM),
            pl.BlockSpec((1, rows, width), lambda i: (HOPS.index(0), 0, 0)),
            whole,
            whole,
        ],
        out_specs=[half, half],
        out_shape=[jax.ShapeDtypeStruct((rows // 2, width), FULL)] * 2,
    )(core, blocks, right, left)


def place_kernel(core_ref, own_ref, got_ref, *outs):
    columns = own_ref.shape[1] // 4
    first = core_ref[0] == 0
    for k, out in enumerate(outs):
        span = slice(k * columns, (k + 1) * columns)
        own, got = own_ref[:, span], got_ref[:, span]
        left, right = jnp.where(first, own, got), jnp.where(first, got, own)
        if k < 3:
            out[:, :columns], out[:, columns:] = left, right
        else:
            out[:columns], out[columns:] = left.T, right.T


def place_weights(core, own, got):
    rows, width = own.shape
    columns = width // 2
    shapes = [(rows, columns)] * 3 + [(columns, rows)]
    return pl.pallas_call(
        place_kernel,
        grid=(1,),
        in_specs=[pl.BlockSpec(memory_space=pltpu.SMEM)]
        + [pl.BlockSpec((rows, width), lambda i: (0, 0))] * 2,
        out_specs=[pl.BlockSpec(shape, lambda i: (0, 0)) for shape in shapes],
        out_shape=[jax.ShapeDtypeStruct(shape, FULL) for shape in shapes],
    )(core, own, got)


def join_kernel(parts, side_ref, *refs):
    out_ref = refs[-1]
    rows = out_ref.shape[0] // 2
    for k, side in ((0, side_ref[0]), (1, 1 - side_ref[0])):
        total = refs[k * parts][...].astype(FULL)
        for j in range(1, parts):
            total = total + refs[k * parts + j][...].astype(FULL)
        out_ref[pl.ds(pl.multiple_of(side * rows, rows), rows)] = total


def join_halves(side, own, other):
    rows, width = own[0].shape
    columns = width // 2
    half = pl.BlockSpec((rows, columns), lambda i: (0, i))
    return pl.pallas_call(
        lambda *refs: join_kernel(len(own), *refs),
        grid=(2,),
        in_specs=[pl.BlockSpec(memory_space=pltpu.SMEM)] + [half] * (2 * len(own)),
        out_specs=pl.BlockSpec((2 * rows, columns), lambda i: (0, i)),
        out_shape=jax.ShapeDtypeStruct((2 * rows, width), FULL),
    )(side, *own, *other)


def expert_kernel(
    rows_ref, back_ref, gate_ref, wg0, wg1, wu0, wu1, wd0, wd1, grad_ref, h0, h1, g0, g1, u0, u1
):
    rows = rows_ref[...]
    back = back_ref[...]
    gate = gate_ref[...]
    total = None
    for wg, wu, wd, h, g, u in ((wg0, wu0, wd0, h0, g0, u0), (wg1, wu1, wd1, h1, g1, u1)):
        gate_pre = dot_nn(rows, wg[...])
        up_pre = dot_nn(rows, wu[...])
        hidden_grad = gate * dot_nt(back, wd[...])
        sig = 1.0 / (1.0 + jnp.exp(-gate_pre))
        act = gate_pre * sig
        h[...] = (gate * (act * up_pre)).astype(LOW)
        gate_grad = (hidden_grad * up_pre * (sig * (1.0 + gate_pre * (1.0 - sig)))).astype(LOW)
        up_grad = (hidden_grad * act).astype(LOW)
        g[...] = gate_grad
        u[...] = up_grad
        part = dot_nt(gate_grad, wg[...]) + dot_nt(up_grad, wu[...])
        total = part if total is None else total + part
    grad_ref[...] = total.astype(LOW)


def expert_pass(rows, back, gate, gate_mats, up_mats, down_mats):
    count, width = rows.shape
    hidden = gate_mats[0].shape[1]
    tile = 256
    whole = lambda array: pl.BlockSpec(
        array.shape, lambda i: (0, 0), pipeline_mode=pl.Buffered(1)
    )
    tall = lambda columns: pl.BlockSpec((tile, columns), lambda i: (i, 0))
    mats = [*gate_mats, *up_mats, *down_mats]
    flops = 2 * 5 * count * width * hidden * 2
    return pl.pallas_call(
        expert_kernel,
        grid=(count // tile,),
        in_specs=[tall(width), tall(width), tall(1)] + [whole(m) for m in mats],
        out_specs=[tall(width)] + [tall(hidden)] * 6,
        out_shape=[jax.ShapeDtypeStruct((count, width), LOW)]
        + [jax.ShapeDtypeStruct((count, hidden), LOW)] * 6,
        compiler_params=pltpu.CompilerParams(vmem_limit_bytes=VMEM),
        cost_estimate=pl.CostEstimate(
            flops=flops,
            bytes_accessed=2 * (3 * count * width + 6 * count * hidden + 6 * width * hidden),
            transcendentals=2 * count * hidden,
        ),
    )(rows, back, gate, *mats)


def chunk_kernel(pieces, held, at, splits, gate_ref, *refs):
    piece_refs, refs = refs[:pieces], refs[pieces:]
    back_ref, mats, refs = refs[0], refs[1:7], refs[7 + held :]
    grad_outs, refs = refs[: len(splits)], refs[len(splits) :]
    rows_out, outs = refs[0], refs[1:7]
    rows, back, wide, wd, hidden, both_grads, grads, sems = refs[7:]
    count = rows.shape[0]
    part = wd.shape[1]
    slab = wide.shape[0] // 4
    across = lambda k, half: pl.ds((2 * k + half) * part, part)
    place = pl.ds(at * count, count)
    copy = pltpu.make_async_copy
    load_rows, start = [], 0
    for piece in piece_refs:
        span = pl.ds(start, piece.shape[0])
        load_rows.append(copy(piece, rows.at[span], sems.at[len(load_rows)]))
        start += piece.shape[0]
    load_back = copy(back_ref.at[place], back, sems.at[6])
    loads = []
    for half in range(2):
        places = [wide.at[:, across(0, half)], wide.at[:, across(1, half)], wd.at[half]]
        loads.append(
            [copy(mats[2 * k + half], to, sems.at[7 + 3 * half + k]) for k, to in enumerate(places)]
        )
    for one in load_rows + loads[0][:2] + [load_back] + loads[0][2:] + loads[1]:
        one.start()
    gate = gate_ref[...]
    for one in load_rows:
        one.wait()
    stores = [copy(rows, rows_out.at[place], sems.at[13])]
    stores[0].start()
    for half in range(2):
        columns = pl.ds(half * part, part)
        loads[half][0].wait()
        gate_pre = dot_nn(rows[...], wide[:, across(0, half)])
        loads[half][1].wait()
        up_pre = dot_nn(rows[...], wide[:, across(1, half)])
        if half == 0:
            load_back.wait()
        loads[half][2].wait()
        hidden_grad = gate * dot_nt(back[...], wd[half])
        sig = 1.0 / (1.0 + jnp.exp(-gate_pre))
        act = gate_pre * sig
        hidden[:, columns] = (gate * (act * up_pre)).astype(LOW)
        both_grads[:, across(0, half)] = (
            hidden_grad * up_pre * (sig * (1.0 + gate_pre * (1.0 - sig)))
        ).astype(LOW)
        both_grads[:, across(1, half)] = (hidden_grad * act).astype(LOW)
    for half in range(2):
        held_in = (
            hidden.at[:, pl.ds(half * part, part)],
            both_grads.at[:, across(0, half)],
            both_grads.at[:, across(1, half)],
        )
        for k, source in enumerate(held_in):
            stores.append(copy(source, outs[2 * k + half].at[place], sems.at[14 + 3 * half + k]))
            stores[-1].start()

    @pl.loop(0, 4)
    def _(j):
        span = pl.ds(pl.multiple_of(j * slab, slab), slab)
        grads[:, span] = dot_nt(both_grads[...], wide[span]).astype(LOW)

    start = 0
    for k, (split, to) in enumerate(zip(splits, grad_outs)):
        stores.append(copy(grads.at[pl.ds(start, split)], to, sems.at[20 + k]))
        stores[-1].start()
        start += split
    for one in stores:
        one.wait()


def expert_chunk(pieces, back, gate, mats, at, held, splits):
    all_rows, width = back.shape
    part = mats[0].shape[1]
    hidden = 2 * part
    count = sum(piece.shape[0] for piece in pieces)
    anywhere = pl.BlockSpec(memory_space=pl.ANY)
    held = [] if held is None else list(held)
    args = [gate, *pieces, back, *mats, *held]
    out = pl.pallas_call(
        lambda *refs: chunk_kernel(len(pieces), len(held), at, splits, *refs),
        grid=(1,),
        in_specs=[pl.BlockSpec((count, 1), lambda j: (at, 0))] + [anywhere] * (len(args) - 1),
        out_specs=[anywhere] * (len(splits) + 7),
        out_shape=[jax.ShapeDtypeStruct((split, width), LOW) for split in splits]
        + [jax.ShapeDtypeStruct((all_rows, width), LOW)]
        + [jax.ShapeDtypeStruct((all_rows, part), LOW)] * 6,
        scratch_shapes=[
            pltpu.VMEM((count, width), LOW),
            pltpu.VMEM((count, width), LOW),
            pltpu.VMEM((width, 2 * hidden), LOW),
            pltpu.VMEM((2, part, width), LOW),
            pltpu.VMEM((count, hidden), LOW),
            pltpu.VMEM((count, 2 * hidden), LOW),
            pltpu.VMEM((count, width), LOW),
            pltpu.SemaphoreType.DMA((23,)),
        ],
        input_output_aliases={
            len(args) - len(held) + k: len(splits) + k for k in range(len(held))
        },
        compiler_params=pltpu.CompilerParams(vmem_limit_bytes=VMEM),
        cost_estimate=pl.CostEstimate(
            flops=2 * 5 * count * width * hidden,
            bytes_accessed=2 * (4 * count * width + 3 * count * hidden + 3 * width * hidden),
            transcendentals=count * hidden,
        ),
    )(*args)
    return out[: len(splits)], out[len(splits) :]


def mixed_kernel(chip_ref, same_ref, cross_ref, core_ref, *refs):
    first_ref, second_ref, out_ref = refs[4:]
    rows = out_ref.shape[2]
    first, second = (
        jnp.concatenate([refs[k][...], refs[k + 1][...]], axis=0) for k in (0, 2)
    )
    result = (dot_nn(first, first_ref[...]) + dot_nn(second, second_ref[...])).astype(LOW)
    out_ref[0, core_ref[0]] = result[:rows]
    out_ref[0, 1 - core_ref[0]] = result[rows:]


def mixed_pass(h0, h1, down_mats, chips, core):
    count, columns = h0.shape
    width = down_mats[0].shape[1]
    rows = count // len(LAYOUT)
    places = [
        jnp.array([LAYOUT.index((hop, cross)) for hop in HOPS], jnp.int32) for cross in (0, 1)
    ]
    once = pl.Buffered(1)
    fixed = lambda m: pl.BlockSpec(m.shape, lambda i, *tables: (0, 0), pipeline_mode=once)
    block = lambda k: pl.BlockSpec((rows, columns), lambda i, *tables: (tables[k][i], 0))
    out = pl.pallas_call(
        mixed_kernel,
        grid_spec=pltpu.PrefetchScalarGridSpec(
            num_scalar_prefetch=4,
            grid=(len(HOPS),),
            in_specs=[block(1), block(2), block(1), block(2)] + [fixed(m) for m in down_mats],
            out_specs=pl.BlockSpec(
                (1, 2, rows, width), lambda i, chip, *tables: (chip[i], 0, 0, 0)
            ),
        ),
        out_shape=jax.ShapeDtypeStruct((len(HOPS), 2, rows, width), LOW),
        compiler_params=pltpu.CompilerParams(vmem_limit_bytes=VMEM),
        cost_estimate=pl.CostEstimate(
            flops=4 * count * columns * width,
            bytes_accessed=2 * (count * (2 * columns + width) + 2 * columns * width),
            transcendentals=0,
        ),
    )(chips, *places, core, h0, h0, h1, h1, *down_mats)
    return out.reshape(count, width)


def expert_ring(rows, back, gate, mats, waiting):
    size = rows.shape[0]
    cut = size // 2
    swap = lambda block: swap_bit(block, "dp", 0)
    chunk = lambda pieces, at, held, *splits: expert_chunk(
        pieces, back, gate, mats, at, held, splits
    )
    rows, pair = together(rows, swap(rows))
    left, right = ahead(rows), behind(rows)
    parts, crossed = cut_rows(waiting, 4), []
    same, cross = {}, {}
    cross_over = lambda token: crossed.append(swap_tensor(after(parts[len(crossed)], token)))
    cross_over(pair)
    (same[0], cross[0]), held = chunk([rows, pair], 6, None, size, size)
    left, right, same[0] = together(left, right, same[0])
    pieces, got = [left, right], [swap(left), swap(right)]
    left, right = ahead(left), behind(right)
    pieces[0], crossed[0] = together(pieces[0], crossed[0])
    cross_over(pieces[0])
    (same[1],), held = chunk(pieces, 7, held, 2 * size)
    left, right, same[1] = together(left, right, same[1])
    pieces, got = [left, right, *got], [swap(left), swap(right)]
    left, right = ahead(left), behind(right)
    pieces[0], crossed[1] = together(pieces[0], crossed[1])
    cross_over(pieces[0])
    (same[2], cross[1]), held = chunk(pieces, 0, held, 2 * size, 2 * size)
    left, right, same[2] = together(left, right, same[2])
    pieces, got = [left, right, *got], [swap(left), swap(right)]
    left, right = ahead(left[:cut]), behind(right[cut:])
    pieces[0], crossed[2] = together(pieces[0], crossed[2])
    cross_over(pieces[0])
    (same[3], cross[2]), held = chunk(pieces, 1, held, 2 * size, 2 * size)
    left, right, crossed[3], same[3] = together(left, right, crossed[3], same[3])
    pieces = [left, right, swap(left), swap(right), *got]
    (same[4], cross[4], cross[3]), held = chunk(pieces, 2, held, size, size, 2 * size)
    waiting = jnp.concatenate(crossed, axis=0)
    return same, cross, held, waiting


def body(
    inputs,
    attn_gain,
    w_query,
    w_key,
    w_value,
    query_gain,
    key_gain,
    w_out,
    moe_gain,
    w_gate,
    w_up,
    w_down,
    experts,
    gates,
    segments,
    gaps,
    cotangent,
):
    dp_count = lax.axis_size("dp")
    dp_index = lax.axis_index("dp")
    side = lax.axis_index("tensor")
    token_count, model_width = inputs.shape
    half_count = token_count // 2
    top_count = experts.shape[1]
    expert_count = w_gate.shape[0] * dp_count
    capacity = token_count * top_count * dp_count * 9 // (8 * expert_count)
    prompt_length = PR_DEV * GROUP
    column_total = HEADS * HEAD
    block = w_query.shape[0]
    local_width = w_query.shape[1]
    local_heads = local_width // HEAD

    def own_half(array):
        return lax.dynamic_slice_in_dim(array, side * half_count, half_count, axis=0)

    def other_half(array):
        return lax.dynamic_slice_in_dim(array, (1 - side) * half_count, half_count, axis=0)

    def both_halves(own, other):
        first = side == 0
        return jnp.concatenate(
            [jnp.where(first, own, other), jnp.where(first, other, own)], axis=0
        )

    gate_mats = (w_gate[0], swap_tensor(w_gate[0]))
    up_mats = (w_up[0], swap_tensor(w_up[0]))

    ring = dp_count == 2 * len(RING)

    gates_high = gates.astype(LOW)
    gates_low = (gates - gates_high.astype(FULL)).astype(LOW)
    routing = jnp.concatenate([experts.astype(LOW).T, gates_high.T, gates_low.T], axis=1)
    routing = jnp.pad(routing, ((0, 0), (0, local_width - 3 * token_count)))
    gains = jnp.concatenate([attn_gain, moe_gain, query_gain, key_gain])
    gains = jnp.pad(gains[None], ((0, 7), (0, local_width - 4 * block)))
    packed = pack_weights(
        w_query, w_key, w_value, w_out, jnp.concatenate([gains, routing], axis=0)
    )
    gathered = lax.all_gather(packed, "dp", axis=0, tiled=False)
    cotangent_half = own_half(cotangent)
    gathered_back = lax.all_gather(cotangent_half.astype(LOW), "dp", axis=0, tiled=False)
    core = dp_index % 2
    tokens_f = inputs.astype(FULL)
    prompt_pos = dp_index % GROUP * PR_DEV + jnp.arange(PR_DEV, dtype=jnp.int32)
    later_pos = cont_positions(segments[0], gaps[0], prompt_length)
    positions = jnp.concatenate([prompt_pos, later_pos], axis=0)
    cosine, sine = rope_tables(positions, HEAD)
    sine = jnp.where(jnp.arange(HEAD) < HEAD // 2, -sine, sine)
    prompt_query = jnp.arange(token_count, dtype=jnp.int32) < PR_DEV
    prompt_at = jnp.arange(prompt_length, dtype=jnp.int32)
    prompt_keypos = ((dp_index % GROUP) ^ (prompt_at // PR_DEV)) * PR_DEV + prompt_at % PR_DEV
    allowed_prompt = (~prompt_query)[:, None] | (prompt_keypos[None, :] <= positions[:, None])
    query_segment = jnp.concatenate([jnp.full((PR_DEV,), -1, jnp.int32), segments[0]], axis=0)
    allowed_cont = (query_segment[:, None] == segments[0][None, :]) & (
        later_pos[None, :] <= positions[:, None]
    )
    allowed = jnp.concatenate([allowed_prompt, allowed_cont], axis=1)
    bias = jnp.where(allowed, 0.0, -1e30).astype(LOW)
    gathered, cosine, sine, bias, *early = together(
        gathered, cosine, sine, bias, gate_mats[1], up_mats[1]
    )
    gate_mats, up_mats = (gate_mats[0], early[0]), (up_mats[0], early[1])
    rest = gathered[:, 4 * block : 4 * block + 16]
    gain_rows = rest[:, 0].astype(FULL)
    gain_one, gain_two, gain_q, gain_k = (
        gain_rows[:, j * block : (j + 1) * block].reshape(-1) for j in range(4)
    )
    gain_query_local = lax.dynamic_slice_in_dim(gain_q, side * local_width, local_width)
    gain_key_local = lax.dynamic_slice_in_dim(gain_k, side * local_width, local_width)

    names, *parts = (
        rest[:, 8:, j * token_count : (j + 1) * token_count] for j in range(3)
    )
    weights = parts[0].astype(FULL) + parts[1].astype(FULL)
    named = names == dp_index.astype(LOW)
    picked = jnp.sum(named.astype(FULL), axis=1)
    weight = jnp.sum(jnp.where(named, weights, 0.0), axis=1)
    order = jnp.arange(token_count, dtype=jnp.int32)
    earlier = (order[:, None] < order[None, :]).astype(LOW)
    within = dot_nn(picked.astype(LOW), earlier)
    per_row = jnp.sum(picked, axis=1)
    rows_order = jnp.arange(dp_count, dtype=jnp.int32)
    ahead = jnp.sum(
        jnp.where(rows_order[None, :] < rows_order[:, None], per_row[None, :], 0.0), axis=1
    )
    kept = (picked > 0.0) & (within + ahead[:, None] < capacity)
    weight = jnp.where(kept, weight, 0.0)
    weight = lax.dynamic_slice_in_dim(weight, side * half_count, half_count, axis=1)
    if ring:
        blocks, chips = ring_blocks(dp_index), ring_chips(dp_index, HOPS)
        weight = weight[blocks]
    weight = weight.reshape(-1, 1)

    normed_b = rms_norm(tokens_f, gain_one).astype(LOW)
    query_flat, key_flat, values_b, value_prompt = project(
        normed_b, gathered, block, (0, 1, 2), (FULL, FULL, LOW), (2,)
    )
    key_sq = jnp.sum(key_flat * key_flat, axis=1)
    key_sq, value_prompt = together(key_sq, value_prompt)
    value_pieces = collect_prompt(value_prompt, 1, 2)
    query_sq, key_sq = lax.psum(
        (jnp.sum(query_flat * query_flat, axis=1), key_sq), "tensor"
    )
    query_sq, down_mat = lax.optimization_barrier((query_sq, w_down[0]))
    down_mats = (down_mat, swap_tensor(down_mat))
    query_scale = lax.rsqrt(query_sq / column_total + EPSILON)[:, None]
    key_scale = lax.rsqrt(key_sq / column_total + EPSILON)[:, None]
    keys_b, key_prompt = rope_pass(key_flat, gain_key_local[None], key_scale, cosine, sine)
    pieces = (*collect_prompt(key_prompt, 2, 1), *value_pieces)
    turned_by = (gain_query_local[None], query_scale, cosine, sine, bias)
    context_b = attend(query_flat, *turned_by, keys_b, values_b, pieces)
    attn_part = project_back([context_b], gathered, block, (3,))
    attn_part, late, weight = together(attn_part, down_mats[1], weight)
    down_mats = (down_mats[0], late)
    mats = (*gate_mats, *up_mats, *down_mats)
    attn_other = swap_tensor(other_half(attn_part).astype(LOW))
    gathered_back = after(gathered_back, attn_part)
    if ring:
        back_rows = unpack_rows(gathered_back, blocks, 0, model_width)
    else:
        back_rows = gathered_back.reshape(-1, model_width)
    attn_other, back_rows, weight = together(attn_other, back_rows, weight)
    hidden_state = own_half(tokens_f) + own_half(attn_part) + attn_other.astype(FULL)
    normed_two_b = rms_norm(hidden_state, gain_two).astype(LOW)

    low_tn = lambda left, right: dot_tn(left, right).astype(LOW)
    upper = lambda array: array[: array.shape[0] // 2]
    lower = lambda array: array[array.shape[0] // 2 :]
    if ring:
        same, cross, held, hidden_other = expert_ring(
            normed_two_b, back_rows, weight, mats, hidden_state
        )
        expert_in, h0, h1, g0, g1, u0, u1 = held
        late = {}

        def down_stage(gated):
            late["down"] = swap_tensor(low_tn(gated(h1), back_rows))

        def gate_stage(gated):
            late["gate"] = low_tn(gated(expert_in), g1)

        def up_stage(gated):
            late["up"] = low_tn(gated(expert_in), u1)

        def mixed_stage(gated):
            late["mixed"] = mixed_pass(gated(h0), h1, down_mats, chips, core[None])

        fillers = Fillers(late, down_stage, gate_stage, up_stage, mixed_stage)
        normed_two_grad = ring_sum(same, cross, fillers)
        gate_sent, up_sent, mixed_rows = late["gate"], late["up"], late["mixed"]
        down_got = late["down"]
    else:
        hidden_other = swap_tensor(hidden_state)
        expert_in = lax.all_gather(normed_two_b, "dp", axis=0, tiled=True)
        grad_rows, h0, h1, g0, g1, u0, u1 = expert_pass(
            expert_in, back_rows, weight, gate_mats, up_mats, down_mats
        )
        normed_two_grad = lax.psum_scatter(
            grad_rows, "dp", scatter_dimension=0, tiled=True
        ).astype(FULL)
        mixed_rows = (dot_nn(h0, down_mats[0]) + dot_nn(h1, down_mats[1])).astype(LOW)
        down_got = swap_tensor(low_tn(h1, back_rows))
        gate_sent = low_tn(expert_in, g1)
        up_sent = low_tn(expert_in, u1)
    quarter = gate_sent.shape[0] // 4
    gate_first = swap_tensor(gate_sent[:quarter])
    normed_two_grad, down_got, gate_first, mixed_rows, up_sent = together(
        normed_two_grad, down_got, gate_first, mixed_rows, up_sent
    )
    mixed = lax.psum_scatter(mixed_rows, "dp", scatter_dimension=0, tiled=True)

    unused_two, norm_two_back = jax.vjp(rms_norm, hidden_state, gain_two)
    state_part, gain_two_grad = norm_two_back(normed_two_grad)
    state_half = cotangent_half + state_part
    attn_grad_half = state_half.astype(LOW)
    attn_grad_b = both_halves(attn_grad_half, swap_tensor(attn_grad_half))
    attn_grad_b, gate_sent, up_sent = together(attn_grad_b, gate_sent, up_sent)
    (context_grad_b,) = project(attn_grad_b, gathered, block, (3,), (LOW,))
    (gate_middle,) = swap_in_turn([gate_sent[quarter : 3 * quarter]], context_grad_b)
    soon = [
        swap_tensor(after(piece, gate_middle))
        for piece in (gate_sent[3 * quarter :], upper(up_sent))
    ]
    if ring:
        pair = lambda own: (own, swap_bit(own, "dp", 0))
        columns = local_width // 2
        context_sent = lax.dynamic_slice_in_dim(context_b, (1 - core) * columns, columns, axis=1)
        normed_pair, attn_grad_pair = pair(normed_b), pair(attn_grad_b)
        context_got = swap_bit(context_sent, "dp", 0)
    query_normed_grad, query_inner, query_gain_part, key_grad, value_grad, even, *odd = attend_back(
        query_flat, *turned_by, keys_b, values_b, pieces, context_grad_b
    )
    returned = return_prompt(odd, even)
    if ring:
        key_grad, context_got, *pairs = together(
            key_grad, context_got, normed_pair[1], attn_grad_pair[1]
        )
        normed_pair, attn_grad_pair = (normed_b, pairs[0]), (attn_grad_b, pairs[1])
    key_normed_grad, key_inner, key_gain_part, value_pre_grad = key_back(
        key_grad, value_grad, key_flat, gain_key_local[None], key_scale, cosine, sine, returned
    )
    query_inner, *soon = together(query_inner, *soon)
    query_inner, key_inner = lax.psum(
        jnp.stack([query_inner[:, 0], key_inner[:, 0]], axis=0), "tensor"
    )
    query_pre_grad, key_pre_grad, pre_sent = pre_grads_pass(
        core[None],
        (
            query_flat,
            query_normed_grad,
            gain_query_local[None],
            query_scale,
            query_inner[:, None],
        ),
        (key_flat, key_normed_grad, gain_key_local[None], key_scale, key_inner[:, None]),
        value_pre_grad,
    )
    gate_got = jnp.concatenate([gate_first, gate_middle, soon[0]], axis=0)
    pre_grads = (query_pre_grad, key_pre_grad, value_pre_grad)
    grad_sum = lambda left, right, got: dot_tn(left, right) + got.astype(FULL)
    back_all = lambda *grads: project_back(grads, gathered, block, (0, 1, 2))

    wide = lambda part: lax.dynamic_update_slice_in_dim(
        jnp.zeros((column_total,), FULL), part, side * local_width, 0
    )

    def back_shares(*grads):
        part = back_all(*grads)
        return own_half(part), other_half(part).astype(LOW), part

    def input_side(own, other):
        unused_one, norm_one_back = jax.vjp(
            lambda values: rms_norm(values, gain_one), own_half(tokens_f)
        )
        return state_half + norm_one_back(own + other.astype(FULL))[0]

    def gain_part(part):
        return jnp.sum(part * rms_norm(tokens_f, 1.0), axis=0)

    def gain_side(gain_one_grad):
        grads = jnp.stack(
            [gain_one_grad, gain_two_grad, wide(query_gain_part[0]), wide(key_gain_part[0])]
        ).reshape(4, dp_count, block)
        grads = jnp.swapaxes(grads, 0, 1).reshape(dp_count, 1, 4 * block)
        sides = lax.axis_size("tensor")
        grads = jnp.broadcast_to(grads, (dp_count, sides, 4 * block))
        grads = grads.reshape(dp_count * sides, 4 * block)
        sums = lax.all_to_all(grads, ("dp", "tensor"), 0, 0, tiled=True)
        return jnp.sum(sums, axis=0).reshape(4, block)

    if ring:
        pre_got = swap_bit(pre_sent, "dp", 0)
        w_blocks, *far = weight_grads(
            chips,
            core[None],
            normed_pair,
            attn_grad_pair,
            pre_grads,
            pre_got,
            context_b,
            context_got,
        )
        w_blocks, mixed, *far = together(w_blocks, mixed, *far)
        up_pieces = swap_in_turn(cut_rows(lower(up_sent), 2), far[0])
        late, later = {}, {}

        def normed_stage(gated):
            late["own"], late["sent"], late["gain"] = back_shares(*map(gated, pre_grads))

        def gate_product_stage(gated):
            other = swap_tensor(late["sent"])
            late["gate"] = grad_sum(gated(expert_in), g0, gate_got)
            late["mixed"], late["pieces"] = gated(mixed), up_pieces
            later["other"] = other

        def input_stage(gated):
            later["mixed"] = swap_tensor(late["mixed"])
            late["half"] = input_side(late["own"], gated(later["other"]))
            later["half"] = swap_tensor(late["half"])
            late["down"] = grad_sum(gated(h0), back_rows, down_got)

        def up_product_stage(gated):
            up_got = jnp.concatenate([soon[1], *late["pieces"]], axis=0)
            late["up"] = grad_sum(gated(expert_in), u0, up_got)
            late["gains"] = gain_side(gain_part(after(late["gain"], late["up"])))
            late["output"] = join_halves(
                side[None], [gated(hidden_state), mixed], [hidden_other, later["mixed"]]
            )
            late["input"] = join_halves(side[None], [gated(late["half"])], [later["half"]])

        fillers = Fillers(
            late, normed_stage, gate_product_stage, input_stage, up_product_stage
        )
        w_parts = ring_weights(w_blocks, *far, fillers)
        gain_sums, output, input_grad = late["gains"], late["output"], late["input"]
        down_grad, gate_w_grad, up_w_grad = late["down"], late["gate"], late["up"]
        own_w, sent_w = sum_weights(core[None], *w_parts)
        w_sums = place_weights(core[None], own_w, swap_bit(sent_w, "dp", 0))
    else:
        w_grads = jnp.concatenate(
            [low_tn(normed_b, g) for g in pre_grads] + [low_tn(attn_grad_b, context_b)], axis=1
        )
        w_sum = lax.psum_scatter(w_grads, "dp", scatter_dimension=0, tiled=True).astype(FULL)
        w_sums = [w_sum[:, j * local_width : (j + 1) * local_width] for j in range(4)]
        w_sums[3] = w_sums[3].T
        down_grad = grad_sum(h0, back_rows, down_got)
        gate_w_grad = grad_sum(expert_in, g0, gate_got)
        up_got = jnp.concatenate([soon[1], swap_tensor(lower(up_sent))], axis=0)
        up_w_grad = grad_sum(expert_in, u0, up_got)
        mixed_other = swap_tensor(mixed)
        normed_own, normed_sent, part = back_shares(*pre_grads)
        gain_sums = gain_side(gain_part(part))
        input_half = input_side(normed_own, swap_tensor(normed_sent))
        input_other = swap_tensor(input_half)
        input_grad = join_halves(side[None], [input_half], [input_other])
        output = join_halves(side[None], [hidden_state, mixed], [hidden_other, mixed_other])
    return (
        output,
        input_grad,
        gain_sums[0],
        w_sums[0],
        w_sums[1],
        w_sums[2],
        gain_sums[2],
        gain_sums[3],
        w_sums[3],
        gain_sums[1],
        gate_w_grad[None],
        up_w_grad[None],
        down_grad[None],
    )


def solution(mesh):
    return jax.shard_map(
        body,
        mesh=mesh,
        in_specs=(
            P("dp", None),
            P("dp"),
            P("dp", "tensor"),
            P("dp", "tensor"),
            P("dp", "tensor"),
            P("dp"),
            P("dp"),
            P("tensor", "dp"),
            P("dp"),
            P("dp", None, "tensor"),
            P("dp", None, "tensor"),
            P("dp", "tensor", None),
            P("dp", None),
            P("dp", None),
            P("dp", None),
            P("dp", None),
            P("dp", None),
        ),
        out_specs=(
            P("dp", None),
            P("dp", None),
            P("dp"),
            P("dp", "tensor"),
            P("dp", "tensor"),
            P("dp", "tensor"),
            P("dp"),
            P("dp"),
            P("tensor", "dp"),
            P("dp"),
            P("dp", None, "tensor"),
            P("dp", None, "tensor"),
            P("dp", "tensor", None),
        ),
        check_vma=False,
    )
```

```python
import jax
import jax.numpy as jnp
from jax import lax
from jax.experimental import pallas as pl
from jax.experimental.pallas import tpu as pltpu
from jax.sharding import PartitionSpec as P

HEADS = 16
HEAD = 128
GROUP = 8
PR_DEV = 128


EPSILON = 1e-05
VMEM = 60 * 1024 * 1024
LOW = jnp.bfloat16
FULL = jnp.float32


def swap_bit(block, axis, bit):
    count = lax.axis_size(axis)
    return lax.ppermute(block, axis, [(i, i ^ (1 << bit)) for i in range(count)])


def swap_tensor(block):
    return lax.ppermute(block, "tensor", [(0, 1), (1, 0)])


RING = (0, 2, 4, 6, 7, 5, 3, 1)
AHEAD = [
    (RING[p] * 2 + c, RING[(p + 1) % len(RING)] * 2 + c) for p in range(len(RING)) for c in range(2)
]
BEHIND = [(to, at) for at, to in AHEAD]
HOPS = (-1, 1, -2, 2, -3, 3, 0, 4)
LAYOUT = (
    *((-2, 0), (2, 0), (-1, 1), (1, 1)),
    *((-3, 0), (3, 0), (-2, 1), (2, 1)),
    *((4, 0), (4, 1), (-3, 1), (3, 1)),
    *((0, 0), (0, 1)),
    *((-1, 0), (1, 0)),
)


def ahead(block):
    return lax.ppermute(block, "dp", AHEAD)


def behind(block):
    return lax.ppermute(block, "dp", BEHIND)


def ring_chips(dp_index, hops):
    chip = dp_index // 2
    place = jnp.where(chip % 2 == 0, chip // 2, 7 - chip // 2)
    there = (place + jnp.array(hops, jnp.int32)) % len(RING)
    return jnp.where(there < 4, 2 * there, 2 * (7 - there) + 1)


def ring_blocks(dp_index):
    chips = ring_chips(dp_index, [hop for hop, _ in LAYOUT])
    return 2 * chips + (dp_index % 2 ^ jnp.array([cross for _, cross in LAYOUT], jnp.int32))


def add_low(*parts):
    total = parts[0].astype(FULL)
    for part in parts[1:]:
        total = total + part.astype(FULL)
    return total.astype(LOW)


def together(value, *others):
    return lax.optimization_barrier((value, *others))


def after(value, token):
    return lax.optimization_barrier((value, token))[0]


class Fillers:
    def __init__(self, late, *stages):
        self.late, self.stages, self.seen = late, list(stages), set(late)

    def next(self, token):
        if self.stages:
            self.stages.pop(0)(lambda value: after(value, token))

    def settle(self, *blocks):
        due = {key: value for key, value in self.late.items() if key not in self.seen}
        self.seen.update(due)
        *blocks, due = lax.optimization_barrier((*blocks, due))
        self.late.update(due)
        return blocks


def ring_sum(same, cross, fillers):
    both = {hop: add_low(same[hop], swap_bit(cross[hop], "dp", 0)) for hop in (4, 3, 2, 1, 0)}
    rows = both[0].shape[0]
    cut = rows // 2
    fillers.next(both[4])
    right, left = ahead(both[4][:cut]), behind(both[4][cut:])
    fillers.next(left)
    outward, inward = both[3][rows:], both[3][:rows]
    right = jnp.concatenate([add_low(outward[:cut], right), outward[cut:]], axis=0)
    left = jnp.concatenate([inward[:cut], add_low(inward[cut:], left)], axis=0)
    right, left = ahead(right), behind(left)
    fillers.next(left)
    for hop in (2, 1):
        right = ahead(add_low(both[hop][rows:], right))
        left = behind(add_low(both[hop][:rows], left))
        fillers.next(left)
    return both[0].astype(FULL) + right.astype(FULL) + left.astype(FULL)


def swap_in_turn(pieces, token):
    got = []
    for piece in pieces:
        got.append(swap_tensor(after(piece, token)))
        token = got[-1]
    return got


def cut_rows(array, count):
    rows = array.shape[0] // count
    return [array[i * rows : (i + 1) * rows] for i in range(count)]


def rms_norm(values, gain):
    return values * lax.rsqrt(jnp.mean(values * values, axis=-1, keepdims=True) + EPSILON) * gain


def rope_tables(positions, head_size):
    half_size = head_size // 2
    inverse = 10000.0 ** (-(jnp.arange(half_size, dtype=FULL) * 2.0) / head_size)
    angles = positions.astype(FULL)[:, None] * inverse[None, :]
    cosine = jnp.concatenate([jnp.cos(angles), jnp.cos(angles)], axis=-1)
    sine = jnp.concatenate([jnp.sin(angles), jnp.sin(angles)], axis=-1)
    return (cosine, sine)


def cont_positions(segment_row, gap_row, prompt_length):
    order = jnp.arange(segment_row.shape[0], dtype=jnp.int32)
    same = segment_row[:, None] == segment_row[None, :]
    earlier = order[None, :] < order[:, None]
    offset = jnp.sum((same & earlier).astype(jnp.int32), axis=1)
    labels = jnp.arange(gap_row.shape[0], dtype=jnp.int32)
    shifted = jnp.sum(
        jnp.where(segment_row[:, None] == labels[None, :], gap_row[None, :], 0), axis=1
    )
    return prompt_length + shifted + offset


def dot_nn(left, right):
    return jnp.dot(left, right, preferred_element_type=FULL)


def dot_tn(left, right):
    return lax.dot_general(left, right, (((0,), (0,)), ((), ())), preferred_element_type=FULL)


def dot_nt(left, right):
    return lax.dot_general(left, right, (((1,), (1,)), ((), ())), preferred_element_type=FULL)


def collect_prompt(own, first, second):
    near, far = swap_bit(own, "dp", 1), swap_bit(own, "dp", 2)
    last = swap_bit(near if first == 1 else far, "dp", second)
    blocks = []
    for block in (own, near, far, last):
        blocks += [block, swap_bit(block, "dp", 0)]
    return blocks[1:]


SMALL = pl.CostEstimate(flops=1, bytes_accessed=1, transcendentals=0)


def merge_kernel(even_ref, *refs):
    got, (keys_ref, values_ref, far_ref, near_ref) = refs[:3], refs[3:]
    near, far, last = 0, 1, 2
    add = lambda j, which: add_low(even_ref[j, which], got[j][which])
    keys_ref[0], keys_ref[1] = add(near, 0), add(last, 0)
    values_ref[0], values_ref[1] = add(far, 1), add(last, 1)
    far_ref[...], near_ref[...] = add(far, 0), add(near, 1)


def return_prompt(odd, even):
    got = [swap_bit(block, "dp", 0) for block in odd]
    one = jax.ShapeDtypeStruct(even.shape[2:], LOW)
    two = jax.ShapeDtypeStruct(even.shape[1:], LOW)
    keys, values, far, near = pl.pallas_call(
        merge_kernel, out_shape=[two, two, one, one], cost_estimate=SMALL
    )(even, *got[1:])
    keys, values = swap_bit(keys, "dp", 1), swap_bit(values, "dp", 2)
    last_keys = swap_bit(add_low(far, keys[1]), "dp", 2)
    last_values = swap_bit(add_low(near, values[1]), "dp", 1)
    return got[0], keys, values, last_keys, last_values


def turn(values):
    return pltpu.roll(values, HEAD // 2, 1)


def rope_kernel(pre_ref, gain_ref, scale_ref, cos_ref, sin_ref, out_ref, first_ref):
    scale, cosine, sine = scale_ref[...], cos_ref[...], sin_ref[...]
    for at in range(0, pre_ref.shape[1], HEAD):
        span = slice(at, at + HEAD)
        normed = pre_ref[:, span] * scale * gain_ref[:, span]
        out_ref[:, span] = (normed * cosine + turn(normed) * sine).astype(LOW)
    first_ref[...] = out_ref[: first_ref.shape[0]]


def rope_pass(flat, gain, scale, cosine, sine):
    rows, width = flat.shape
    part = width // 2
    wide = lambda rows: pl.BlockSpec((rows, part), lambda h: (0, h))
    return pl.pallas_call(
        rope_kernel,
        grid=(2,),
        in_specs=[wide(rows), wide(1)] + [kept_spec(a) for a in (scale, cosine, sine)],
        out_specs=[wide(rows), wide(PR_DEV)],
        out_shape=[jax.ShapeDtypeStruct((count, width), LOW) for count in (rows, PR_DEV)],
    )(flat, gain, scale, cosine, sine)


PAIR = 2


def head_spec(rows):
    return pl.BlockSpec((rows, PAIR * HEAD), lambda h: (0, h))


def kept_spec(array):
    zeros = (0,) * array.ndim
    return pl.BlockSpec(array.shape, lambda h: zeros, pipeline_mode=pl.Buffered(1))


def all_keys(own_ref, pieces, span):
    return jnp.concatenate(
        [own_ref[:PR_DEV, span]] + [p[:, span] for p in pieces] + [own_ref[PR_DEV:, span]], axis=0
    )


def turned_query(flat_ref, gain_ref, scale, cosine, sine, span):
    normed = flat_ref[:, span] * scale * gain_ref[:, span]
    return (normed * cosine + turn(normed) * sine).astype(LOW)


def softmax_rows(query, keys, bias):
    scores = dot_nt(query, keys) * HEAD ** (-0.5) + bias
    weights = jnp.exp(scores - jnp.max(scores, axis=1, keepdims=True))
    return weights * (1.0 / jnp.sum(weights, axis=1, keepdims=True))


PIECES = GROUP - 1


def attend_kernel(flat_ref, gain_ref, scale_ref, cos_ref, sin_ref, bias_ref, k_ref, v_ref, *refs):
    out_ref = refs[-1]
    bias = bias_ref[...].astype(FULL)
    scale, cosine, sine = scale_ref[...], cos_ref[...], sin_ref[...]
    for at in range(0, PAIR * HEAD, HEAD):
        span = slice(at, at + HEAD)
        query = turned_query(flat_ref, gain_ref, scale, cosine, sine, span)
        probs = softmax_rows(query, all_keys(k_ref, refs[:PIECES], span), bias)
        values = all_keys(v_ref, refs[PIECES : 2 * PIECES], span)
        out_ref[:, span] = dot_nn(probs.astype(LOW), values).astype(LOW)


def attend_specs(rows, scale, cosine, sine, bias):
    return (
        [head_spec(rows), head_spec(1)]
        + [kept_spec(a) for a in (scale, cosine, sine, bias)]
        + [head_spec(rows)] * 2
        + [head_spec(PR_DEV)] * (2 * PIECES)
    )


def attend(flat, gain, scale, cosine, sine, bias, keys, values, pieces):
    rows, width = flat.shape
    return pl.pallas_call(
        attend_kernel,
        grid=(width // HEAD // PAIR,),
        in_specs=attend_specs(rows, scale, cosine, sine, bias),
        out_specs=head_spec(rows),
        out_shape=jax.ShapeDtypeStruct((rows, width), LOW),
        compiler_params=pltpu.CompilerParams(vmem_limit_bytes=VMEM),
    )(flat, gain, scale, cosine, sine, bias, keys, values, *pieces)


def norm_parts(step, at, grad, flat_ref, gain_ref, scale_ref, inner_ref, gain_grad_ref):
    span = slice(at, at + HEAD)
    product = flat_ref[:, span] * grad
    inner = jnp.sum(product * gain_ref[:, span], axis=1, keepdims=True)
    gain_grad_ref[:, span] = jnp.sum(product * scale_ref[...], axis=0, keepdims=True)
    if at:
        inner_ref[...] += inner
    else:
        inner_ref[...] = jnp.where(step == 0, 0.0, inner_ref[...]) + inner


def attend_back_kernel(
    flat_ref, gain_ref, scale_ref, cos_ref, sin_ref, bias_ref, k_ref, v_ref, *refs
):
    back_ref = refs[2 * PIECES]
    qg_ref, inner_ref, gain_grad_ref, kg_ref, vg_ref, even_ref = refs[2 * PIECES + 1 : -4]
    odd_refs = refs[-4:]
    step = pl.program_id(0)
    bias = bias_ref[...].astype(FULL)
    scale, cosine, sine = scale_ref[...], cos_ref[...], sin_ref[...]
    prompt = PR_DEV * GROUP
    for at in range(0, PAIR * HEAD, HEAD):
        span = slice(at, at + HEAD)
        query = turned_query(flat_ref, gain_ref, scale, cosine, sine, span)
        back = back_ref[:, span]
        keys = all_keys(k_ref, refs[:PIECES], span)
        values = all_keys(v_ref, refs[PIECES : 2 * PIECES], span)
        probs = softmax_rows(query, keys, bias)
        prob_grad = dot_nt(back, values)
        value_grad = dot_tn(probs.astype(LOW), back)
        row_dot = jnp.sum(probs * prob_grad, axis=1, keepdims=True)
        score_grad = (probs * (prob_grad - row_dot)).astype(LOW)
        query_grad = dot_nn(score_grad, keys) * HEAD ** (-0.5)
        key_grad = dot_tn(score_grad, query) * HEAD ** (-0.5)
        query_grad = query_grad * cosine - turn(query_grad) * sine
        qg_ref[:, span] = query_grad
        norm_parts(step, at, query_grad, flat_ref, gain_ref, scale_ref, inner_ref, gain_grad_ref)
        for which, grad, own_ref in ((0, key_grad, kg_ref), (1, value_grad, vg_ref)):
            own_ref[:PR_DEV, span] = grad[:PR_DEV]
            own_ref[PR_DEV:, span] = grad[prompt:]
            for j in range(1, GROUP):
                to = odd_refs[j // 2] if j % 2 else even_ref.at[j // 2 - 1]
                to[which, :, span] = grad[j * PR_DEV : (j + 1) * PR_DEV].astype(LOW)


def attend_back(flat, gain, scale, cosine, sine, bias, keys, values, pieces, back):
    rows, width = flat.shape
    wide = jax.ShapeDtypeStruct((rows, width), FULL)
    both = pl.BlockSpec((3, 2, PR_DEV, PAIR * HEAD), lambda h: (0, 0, 0, h))
    return pl.pallas_call(
        attend_back_kernel,
        grid=(width // HEAD // PAIR,),
        in_specs=attend_specs(rows, scale, cosine, sine, bias) + [head_spec(rows)],
        out_specs=[
            head_spec(rows),
            pl.BlockSpec((rows, 1), lambda h: (0, 0)),
            head_spec(1),
            head_spec(rows),
            head_spec(rows),
            both,
        ]
        + [pl.BlockSpec((2, PR_DEV, PAIR * HEAD), lambda h: (0, 0, h))] * 4,
        out_shape=[
            wide,
            jax.ShapeDtypeStruct((rows, 1), FULL),
            jax.ShapeDtypeStruct((1, width), FULL),
            wide,
            wide,
            jax.ShapeDtypeStruct((3, 2, PR_DEV, width), LOW),
        ]
        + [jax.ShapeDtypeStruct((2, PR_DEV, width), LOW)] * 4,
        compiler_params=pltpu.CompilerParams(vmem_limit_bytes=VMEM),
        cost_estimate=pl.CostEstimate(
            flops=20 * 10**9, bytes_accessed=40 * 10**6, transcendentals=4 * 10**6
        ),
    )(flat, gain, scale, cosine, sine, bias, keys, values, *pieces, back)


def key_back_kernel(*refs):
    kg_ref, vg_ref, flat_ref, gain_ref, scale_ref, cos_ref, sin_ref = refs[:7]
    got, keys, values, last_keys, last_values = refs[7:12]
    out_ref, inner_ref, gain_grad_ref, value_ref = refs[12:]
    step = pl.program_id(0)
    for at in range(0, PAIR * HEAD, HEAD):
        span = slice(at, at + HEAD)
        grads = []
        for which, own_ref, near, last in ((0, kg_ref, keys, last_keys), (1, vg_ref, values, last_values)):
            first = own_ref[:PR_DEV, span] + got[which, :, span].astype(FULL)
            first = first + near[0, :, span].astype(FULL) + last[:, span].astype(FULL)
            grads.append(jnp.concatenate([first, own_ref[PR_DEV:, span]], axis=0))
        key_grad = grads[0] * cos_ref[...] - turn(grads[0]) * sin_ref[...]
        out_ref[:, span] = key_grad
        norm_parts(step, at, key_grad, flat_ref, gain_ref, scale_ref, inner_ref, gain_grad_ref)
        value_ref[:, span] = grads[1].astype(LOW)


def key_back(key_grad, value_grad, flat, gain, scale, cosine, sine, returned):
    rows, width = flat.shape
    columns = PAIR * HEAD
    return pl.pallas_call(
        key_back_kernel,
        grid=(width // columns,),
        in_specs=[head_spec(rows)] * 3
        + [head_spec(1)]
        + [kept_spec(a) for a in (scale, cosine, sine)]
        + [pl.BlockSpec((2, PR_DEV, columns), lambda h: (0, 0, h))]
        + [pl.BlockSpec((1, PR_DEV, columns), lambda h: (0, 0, h))] * 2
        + [head_spec(PR_DEV)] * 2,
        out_specs=[
            head_spec(rows),
            pl.BlockSpec((rows, 1), lambda h: (0, 0)),
            head_spec(1),
            head_spec(rows),
        ],
        out_shape=[
            jax.ShapeDtypeStruct((rows, width), FULL),
            jax.ShapeDtypeStruct((rows, 1), FULL),
            jax.ShapeDtypeStruct((1, width), FULL),
            jax.ShapeDtypeStruct((rows, width), LOW),
        ],
        cost_estimate=SMALL,
    )(key_grad, value_grad, flat, gain, scale, cosine, sine, *returned)


def pack_kernel(query, key, value, out, rest, packed):
    at = 0
    for ref in (query, key, value):
        packed[at : at + ref.shape[0]] = ref[...]
        at += ref.shape[0]
    packed[at : at + out.shape[1]] = out[...].T
    packed[at + out.shape[1] :] = rest[...]


def pack_weights(w_query, w_key, w_value, w_out, rest):
    rows = 4 * w_query.shape[0] + rest.shape[0]
    return pl.pallas_call(
        pack_kernel, out_shape=jax.ShapeDtypeStruct((rows, w_query.shape[1]), LOW)
    )(w_query, w_key, w_value, w_out, rest)


def unpack_kernel(first, blocks_ref, packed, out, held, sems):
    width = packed.shape[2]
    parts = out.shape[1] // width
    rows = (packed.shape[1] - first) // parts
    count = packed.shape[0]
    place = lambda i: pl.ds(i * rows, rows)
    loads = [
        pltpu.make_async_copy(
            packed.at[blocks_ref[i], pl.ds(first + j * rows, rows)],
            held.at[place(i), pl.ds(j * width, width)],
            sems.at[i * parts + j],
        )
        for i in range(count)
        for j in range(parts)
    ]
    stores = [
        pltpu.make_async_copy(held.at[place(i)], out.at[place(i)], sems.at[count * parts + i])
        for i in range(count)
    ]
    for one in loads:
        one.start()
    for i, store in enumerate(stores):
        for j in range(parts):
            loads[i * parts + j].wait()
        store.start()
    for store in stores:
        store.wait()


def unpack_rows(packed, blocks, first, width):
    count = packed.shape[0]
    parts = width // packed.shape[2]
    rows = (packed.shape[1] - first) // parts
    return pl.pallas_call(
        lambda *refs: unpack_kernel(first, *refs),
        in_specs=[pl.BlockSpec(memory_space=pltpu.SMEM), pl.BlockSpec(memory_space=pl.ANY)],
        out_specs=pl.BlockSpec(memory_space=pl.ANY),
        out_shape=jax.ShapeDtypeStruct((count * rows, width), LOW),
        scratch_shapes=[
            pltpu.VMEM((count * rows, width), LOW),
            pltpu.SemaphoreType.DMA((count * parts + count,)),
        ],
        compiler_params=pltpu.CompilerParams(vmem_limit_bytes=VMEM),
    )(blocks, packed)


def load_packed(gathered, places, block, held, sems):
    copies = [
        pltpu.make_async_copy(
            gathered.at[:, pl.ds(place * block, block)], held.at[k], sems.at[k]
        )
        for k, place in enumerate(places)
    ]
    for one in copies:
        one.start()
    return copies


def held_pack(gathered, places, block):
    count, columns = gathered.shape[0], gathered.shape[2]
    return [
        pltpu.VMEM((len(places), count, block, columns), LOW),
        pltpu.SemaphoreType.DMA((len(places),)),
    ]


def project_kernel(places, block, heads, rows_ref, gathered, *refs):
    outs, firsts, (held, sems) = refs[: len(places)], refs[len(places) : -2], refs[-2:]
    copies = load_packed(gathered, places, block, held, sems)
    rows = rows_ref[...]
    for k, (one, out) in enumerate(zip(copies, outs)):
        one.wait()
        out[...] = dot_nn(rows, held[k].reshape(-1, out.shape[1])).astype(out.dtype)
    for first, k in zip(firsts, heads):
        first[...] = outs[k][: first.shape[0]]


def project(rows, gathered, block, places, roundings, heads=()):
    count, width = rows.shape
    columns = gathered.shape[2]
    outs = [jax.ShapeDtypeStruct((count, columns), rounding) for rounding in roundings]
    outs += [jax.ShapeDtypeStruct((PR_DEV, columns), roundings[k]) for k in heads]
    fixed = lambda a: pl.BlockSpec(a.shape, lambda i: (0, 0))
    return pl.pallas_call(
        lambda *refs: project_kernel(places, block, heads, *refs),
        grid=(1,),
        in_specs=[fixed(rows), pl.BlockSpec(memory_space=pl.ANY)],
        out_specs=[fixed(out) for out in outs],
        out_shape=outs,
        scratch_shapes=held_pack(gathered, places, block),
        compiler_params=pltpu.CompilerParams(vmem_limit_bytes=VMEM),
        cost_estimate=pl.CostEstimate(
            flops=2 * count * width * columns * len(places),
            bytes_accessed=2 * width * columns * len(places) + 8 * count * columns,
            transcendentals=0,
        ),
    )(rows, gathered)


def pack_specs(gathered, places, steps, at):
    count, width = gathered.shape[0] // steps, gathered.shape[2]
    block = at
    return [
        pl.BlockSpec((count, block, width), lambda i, place=place: (i, place, 0))
        for place in places
    ]


def project_back_kernel(mats, *refs):
    out = refs[-1]
    total = None
    for rows_ref, mat in zip(refs[:mats], refs[mats:-1]):
        part = dot_nt(rows_ref[...], mat[...].reshape(-1, mat.shape[2]))
        total = part if total is None else total + part
    out[...] = total


def project_back(rows, gathered, block, places):
    count, columns = rows[0].shape
    width = gathered.shape[0] * block
    steps = 4 if len(places) > 1 else 2
    fixed = pl.BlockSpec((count, columns), lambda i: (0, 0), pipeline_mode=pl.Buffered(1))
    return pl.pallas_call(
        lambda *refs: project_back_kernel(len(places), *refs),
        grid=(steps,),
        in_specs=[fixed] * len(rows) + pack_specs(gathered, places, steps, block),
        out_specs=pl.BlockSpec((count, width // steps), lambda i: (0, i)),
        out_shape=jax.ShapeDtypeStruct((count, width), FULL),
        compiler_params=pltpu.CompilerParams(vmem_limit_bytes=VMEM),
        cost_estimate=pl.CostEstimate(
            flops=2 * count * width * columns * len(places),
            bytes_accessed=2 * width * columns * len(places) + 4 * count * width,
            transcendentals=0,
        ),
    )(*rows, *[gathered] * len(places))


def pre_kernel(core_ref, *refs):
    inputs, outs = refs[:11], refs[11:]
    step = pl.program_id(0)
    columns = inputs[0].shape[1]
    parts = []
    for flat, grad, gain, scale, inner in (inputs[:5], inputs[5:10]):
        scaled = scale[...]
        mean = inner[...] * (1.0 / (HEADS * HEAD))
        parts.append(
            (
                scaled * gain[...] * grad[...] - flat[...] * (scaled * scaled * scaled) * mean
            ).astype(LOW)
        )
    outs[0][...], outs[1][...] = parts

    @pl.when(step != core_ref[0])
    def _():
        for j, part in enumerate((*parts, inputs[10][...])):
            outs[2][:, j * columns : (j + 1) * columns] = part


def pre_grads_pass(core, query, key, value):
    rows, width = value.shape
    columns = width // 2
    half = lambda rows: pl.BlockSpec((rows, columns), lambda h: (0, h))
    side = [half(rows), half(rows), half(1)] + [pl.BlockSpec((rows, 1), lambda h: (0, 0))] * 2
    return pl.pallas_call(
        pre_kernel,
        grid=(2,),
        in_specs=[pl.BlockSpec(memory_space=pltpu.SMEM)] + side + side + [half(rows)],
        out_specs=[half(rows), half(rows), pl.BlockSpec((rows, 3 * columns), lambda h: (0, 0))],
        out_shape=[jax.ShapeDtypeStruct((rows, width), LOW)] * 2
        + [jax.ShapeDtypeStruct((rows, 3 * columns), LOW)],
    )(core, *query, *key, value)


def weight_kernel(chip_ref, core_ref, *refs):
    normed, normed_got, back, back_got, query, key, value, got, context, context_got = refs[:10]
    out_ref, right_ref, left_ref, pre_both, context_both = refs[10:]
    rows, columns = query.shape

    @pl.when(pl.program_id(0) == 0)
    def _():
        for j, part in enumerate((query, key, value)):
            pre_both[:rows, j * columns : (j + 1) * columns] = part[...]
        pre_both[rows:] = got[...]
        context_both[:rows] = context[...]
        context_both[rows:] = context_got[...]

    left = jnp.concatenate([normed[...], normed_got[...]], axis=0)
    out_ref[0, :, : 3 * columns] = dot_tn(left, pre_both[...]).astype(LOW)
    left = jnp.concatenate([back[...], back_got[...]], axis=0)
    out_ref[0, :, 3 * columns :] = dot_tn(left, context_both[...]).astype(LOW)

    @pl.when(pl.program_id(0) == HOPS.index(4))
    def _():
        right_ref[...] = out_ref[0, :, : 2 * columns]
        left_ref[...] = out_ref[0, :, 2 * columns :]


def weight_grads(chips, core, normed, back, pre_grads, got, context, context_got):
    rows, width = normed[0].shape
    columns = context_got.shape[1]
    count = chips.shape[0]
    block = width // count
    tall = pl.BlockSpec((rows, block), lambda i, chip, core: (0, chip[i]))
    mine = pl.BlockSpec((rows, columns), lambda i, chip, core: (0, core[0]))
    fixed = lambda a: pl.BlockSpec(a.shape, lambda i, chip, core: (0, 0))
    return pl.pallas_call(
        weight_kernel,
        grid_spec=pltpu.PrefetchScalarGridSpec(
            num_scalar_prefetch=2,
            grid=(count,),
            in_specs=[tall] * 4 + [mine] * 3 + [fixed(got), mine, fixed(context_got)],
            out_specs=[pl.BlockSpec((1, block, 4 * columns), lambda i, chip, core: (i, 0, 0))]
            + [pl.BlockSpec((block, 2 * columns), lambda i, chip, core: (0, 0))] * 2,
            scratch_shapes=[
                pltpu.VMEM((2 * rows, 3 * columns), LOW),
                pltpu.VMEM((2 * rows, columns), LOW),
            ],
        ),
        out_shape=[jax.ShapeDtypeStruct((count, block, 4 * columns), LOW)]
        + [jax.ShapeDtypeStruct((block, 2 * columns), LOW)] * 2,
        compiler_params=pltpu.CompilerParams(vmem_limit_bytes=VMEM),
        cost_estimate=pl.CostEstimate(
            flops=16 * rows * width * columns,
            bytes_accessed=2 * (4 * rows * width + 8 * rows * columns + 4 * width * columns),
            transcendentals=0,
        ),
    )(chips, core, *normed, *back, *pre_grads, got, context, context_got)


def ring_weights(blocks, right, left, fillers):
    part = lambda hop: blocks[HOPS.index(hop)]
    cut = blocks.shape[2] // 2
    fillers.next(right)
    right, left = ahead(right), behind(left)
    right, left = fillers.settle(right, left)
    fillers.next(left)
    outward, inward = part(3), part(-3)
    right = jnp.concatenate([add_low(outward[:, :cut], right), outward[:, cut:]], axis=1)
    left = jnp.concatenate([inward[:, :cut], add_low(inward[:, cut:], left)], axis=1)
    right, left = together(right, left)
    right, left = ahead(right), behind(left)
    for hop in (2, 1):
        right, left = fillers.settle(right, left)
        fillers.next(left)
        right, left = together(add_low(part(hop), right), add_low(part(-hop), left))
        right, left = ahead(right), behind(left)
    right, left = fillers.settle(right, left)
    return blocks, right, left


def sum_kernel(core_ref, blocks_ref, right_ref, left_ref, own_ref, sent_ref):
    rows = own_ref.shape[0]
    for k, out in enumerate((own_ref, sent_ref)):
        side = core_ref[0] if k == 0 else 1 - core_ref[0]
        span = pl.ds(pl.multiple_of(side * rows, rows), rows)
        out[...] = (
            blocks_ref[0, span].astype(FULL)
            + right_ref[span].astype(FULL)
            + left_ref[span].astype(FULL)
        )


def sum_weights(core, blocks, right, left):
    rows, width = right.shape
    whole = pl.BlockSpec((rows, width), lambda i: (0, 0))
    half = pl.BlockSpec((rows // 2, width), lambda i: (0, 0))
    return pl.pallas_call(
        sum_kernel,
        grid=(1,),
        in_specs=[
            pl.BlockSpec(memory_space=pltpu.SMEM),
            pl.BlockSpec((1, rows, width), lambda i: (HOPS.index(0), 0, 0)),
            whole,
            whole,
        ],
        out_specs=[half, half],
        out_shape=[jax.ShapeDtypeStruct((rows // 2, width), FULL)] * 2,
    )(core, blocks, right, left)


def place_kernel(core_ref, own_ref, got_ref, *outs):
    columns = own_ref.shape[1] // 4
    first = core_ref[0] == 0
    for k, out in enumerate(outs):
        span = slice(k * columns, (k + 1) * columns)
        own, got = own_ref[:, span], got_ref[:, span]
        left, right = jnp.where(first, own, got), jnp.where(first, got, own)
        if k < 3:
            out[:, :columns], out[:, columns:] = left, right
        else:
            out[:columns], out[columns:] = left.T, right.T


def place_weights(core, own, got):
    rows, width = own.shape
    columns = width // 2
    shapes = [(rows, columns)] * 3 + [(columns, rows)]
    return pl.pallas_call(
        place_kernel,
        grid=(1,),
        in_specs=[pl.BlockSpec(memory_space=pltpu.SMEM)]
        + [pl.BlockSpec((rows, width), lambda i: (0, 0))] * 2,
        out_specs=[pl.BlockSpec(shape, lambda i: (0, 0)) for shape in shapes],
        out_shape=[jax.ShapeDtypeStruct(shape, FULL) for shape in shapes],
    )(core, own, got)


def join_kernel(parts, side_ref, *refs):
    out_ref = refs[-1]
    rows = out_ref.shape[0] // 2
    for k, side in ((0, side_ref[0]), (1, 1 - side_ref[0])):
        total = refs[k * parts][...].astype(FULL)
        for j in range(1, parts):
            total = total + refs[k * parts + j][...].astype(FULL)
        out_ref[pl.ds(pl.multiple_of(side * rows, rows), rows)] = total


def join_halves(side, own, other):
    rows, width = own[0].shape
    columns = width // 2
    half = pl.BlockSpec((rows, columns), lambda i: (0, i))
    return pl.pallas_call(
        lambda *refs: join_kernel(len(own), *refs),
        grid=(2,),
        in_specs=[pl.BlockSpec(memory_space=pltpu.SMEM)] + [half] * (2 * len(own)),
        out_specs=pl.BlockSpec((2 * rows, columns), lambda i: (0, i)),
        out_shape=jax.ShapeDtypeStruct((2 * rows, width), FULL),
    )(side, *own, *other)


def expert_kernel(
    rows_ref, back_ref, gate_ref, wg0, wg1, wu0, wu1, wd0, wd1, grad_ref, h0, h1, g0, g1, u0, u1
):
    rows = rows_ref[...]
    back = back_ref[...]
    gate = gate_ref[...]
    total = None
    for wg, wu, wd, h, g, u in ((wg0, wu0, wd0, h0, g0, u0), (wg1, wu1, wd1, h1, g1, u1)):
        gate_pre = dot_nn(rows, wg[...])
        up_pre = dot_nn(rows, wu[...])
        hidden_grad = gate * dot_nt(back, wd[...])
        sig = 1.0 / (1.0 + jnp.exp(-gate_pre))
        act = gate_pre * sig
        h[...] = (gate * (act * up_pre)).astype(LOW)
        gate_grad = (hidden_grad * up_pre * (sig * (1.0 + gate_pre * (1.0 - sig)))).astype(LOW)
        up_grad = (hidden_grad * act).astype(LOW)
        g[...] = gate_grad
        u[...] = up_grad
        part = dot_nt(gate_grad, wg[...]) + dot_nt(up_grad, wu[...])
        total = part if total is None else total + part
    grad_ref[...] = total.astype(LOW)


def expert_pass(rows, back, gate, gate_mats, up_mats, down_mats):
    count, width = rows.shape
    hidden = gate_mats[0].shape[1]
    tile = 256
    whole = lambda array: pl.BlockSpec(
        array.shape, lambda i: (0, 0), pipeline_mode=pl.Buffered(1)
    )
    tall = lambda columns: pl.BlockSpec((tile, columns), lambda i: (i, 0))
    mats = [*gate_mats, *up_mats, *down_mats]
    flops = 2 * 5 * count * width * hidden * 2
    return pl.pallas_call(
        expert_kernel,
        grid=(count // tile,),
        in_specs=[tall(width), tall(width), tall(1)] + [whole(m) for m in mats],
        out_specs=[tall(width)] + [tall(hidden)] * 6,
        out_shape=[jax.ShapeDtypeStruct((count, width), LOW)]
        + [jax.ShapeDtypeStruct((count, hidden), LOW)] * 6,
        compiler_params=pltpu.CompilerParams(vmem_limit_bytes=VMEM),
        cost_estimate=pl.CostEstimate(
            flops=flops,
            bytes_accessed=2 * (3 * count * width + 6 * count * hidden + 6 * width * hidden),
            transcendentals=2 * count * hidden,
        ),
    )(rows, back, gate, *mats)


def chunk_kernel(pieces, held, at, splits, gate_ref, *refs):
    piece_refs, refs = refs[:pieces], refs[pieces:]
    back_ref, mats, refs = refs[0], refs[1:7], refs[7 + held :]
    grad_outs, refs = refs[: len(splits)], refs[len(splits) :]
    rows_out, outs = refs[0], refs[1:7]
    rows, back, wide, wd, hidden, both_grads, grads, sems = refs[7:]
    count = rows.shape[0]
    part = wd.shape[1]
    slab = wide.shape[0] // 4
    across = lambda k, half: pl.ds((2 * k + half) * part, part)
    place = pl.ds(at * count, count)
    copy = pltpu.make_async_copy
    load_rows, start = [], 0
    for piece in piece_refs:
        span = pl.ds(start, piece.shape[0])
        load_rows.append(copy(piece, rows.at[span], sems.at[len(load_rows)]))
        start += piece.shape[0]
    load_back = copy(back_ref.at[place], back, sems.at[6])
    loads = []
    for half in range(2):
        places = [wide.at[:, across(0, half)], wide.at[:, across(1, half)], wd.at[half]]
        loads.append(
            [copy(mats[2 * k + half], to, sems.at[7 + 3 * half + k]) for k, to in enumerate(places)]
        )
    for one in load_rows + loads[0][:2] + [load_back] + loads[0][2:] + loads[1]:
        one.start()
    gate = gate_ref[...]
    for one in load_rows:
        one.wait()
    stores = [copy(rows, rows_out.at[place], sems.at[13])]
    stores[0].start()
    for half in range(2):
        columns = pl.ds(half * part, part)
        loads[half][0].wait()
        gate_pre = dot_nn(rows[...], wide[:, across(0, half)])
        loads[half][1].wait()
        up_pre = dot_nn(rows[...], wide[:, across(1, half)])
        if half == 0:
            load_back.wait()
        loads[half][2].wait()
        hidden_grad = gate * dot_nt(back[...], wd[half])
        sig = 1.0 / (1.0 + jnp.exp(-gate_pre))
        act = gate_pre * sig
        hidden[:, columns] = (gate * (act * up_pre)).astype(LOW)
        both_grads[:, across(0, half)] = (
            hidden_grad * up_pre * (sig * (1.0 + gate_pre * (1.0 - sig)))
        ).astype(LOW)
        both_grads[:, across(1, half)] = (hidden_grad * act).astype(LOW)
    for half in range(2):
        held_in = (
            hidden.at[:, pl.ds(half * part, part)],
            both_grads.at[:, across(0, half)],
            both_grads.at[:, across(1, half)],
        )
        for k, source in enumerate(held_in):
            stores.append(copy(source, outs[2 * k + half].at[place], sems.at[14 + 3 * half + k]))
            stores[-1].start()

    @pl.loop(0, 4)
    def _(j):
        span = pl.ds(pl.multiple_of(j * slab, slab), slab)
        grads[:, span] = dot_nt(both_grads[...], wide[span]).astype(LOW)

    start = 0
    for k, (split, to) in enumerate(zip(splits, grad_outs)):
        stores.append(copy(grads.at[pl.ds(start, split)], to, sems.at[20 + k]))
        stores[-1].start()
        start += split
    for one in stores:
        one.wait()


def expert_chunk(pieces, back, gate, mats, at, held, splits):
    all_rows, width = back.shape
    part = mats[0].shape[1]
    hidden = 2 * part
    count = sum(piece.shape[0] for piece in pieces)
    anywhere = pl.BlockSpec(memory_space=pl.ANY)
    held = [] if held is None else list(held)
    args = [gate, *pieces, back, *mats, *held]
    out = pl.pallas_call(
        lambda *refs: chunk_kernel(len(pieces), len(held), at, splits, *refs),
        grid=(1,),
        in_specs=[pl.BlockSpec((count, 1), lambda j: (at, 0))] + [anywhere] * (len(args) - 1),
        out_specs=[anywhere] * (len(splits) + 7),
        out_shape=[jax.ShapeDtypeStruct((split, width), LOW) for split in splits]
        + [jax.ShapeDtypeStruct((all_rows, width), LOW)]
        + [jax.ShapeDtypeStruct((all_rows, part), LOW)] * 6,
        scratch_shapes=[
            pltpu.VMEM((count, width), LOW),
            pltpu.VMEM((count, width), LOW),
            pltpu.VMEM((width, 2 * hidden), LOW),
            pltpu.VMEM((2, part, width), LOW),
            pltpu.VMEM((count, hidden), LOW),
            pltpu.VMEM((count, 2 * hidden), LOW),
            pltpu.VMEM((count, width), LOW),
            pltpu.SemaphoreType.DMA((23,)),
        ],
        input_output_aliases={
            len(args) - len(held) + k: len(splits) + k for k in range(len(held))
        },
        compiler_params=pltpu.CompilerParams(vmem_limit_bytes=VMEM),
        cost_estimate=pl.CostEstimate(
            flops=2 * 5 * count * width * hidden,
            bytes_accessed=2 * (4 * count * width + 3 * count * hidden + 3 * width * hidden),
            transcendentals=count * hidden,
        ),
    )(*args)
    return out[: len(splits)], out[len(splits) :]


def mixed_kernel(chip_ref, same_ref, cross_ref, core_ref, *refs):
    first_ref, second_ref, out_ref = refs[4:]
    rows = out_ref.shape[2]
    first, second = (
        jnp.concatenate([refs[k][...], refs[k + 1][...]], axis=0) for k in (0, 2)
    )
    result = (dot_nn(first, first_ref[...]) + dot_nn(second, second_ref[...])).astype(LOW)
    out_ref[0, core_ref[0]] = result[:rows]
    out_ref[0, 1 - core_ref[0]] = result[rows:]


def mixed_pass(h0, h1, down_mats, chips, core):
    count, columns = h0.shape
    width = down_mats[0].shape[1]
    rows = count // len(LAYOUT)
    places = [
        jnp.array([LAYOUT.index((hop, cross)) for hop in HOPS], jnp.int32) for cross in (0, 1)
    ]
    once = pl.Buffered(1)
    fixed = lambda m: pl.BlockSpec(m.shape, lambda i, *tables: (0, 0), pipeline_mode=once)
    block = lambda k: pl.BlockSpec((rows, columns), lambda i, *tables: (tables[k][i], 0))
    out = pl.pallas_call(
        mixed_kernel,
        grid_spec=pltpu.PrefetchScalarGridSpec(
            num_scalar_prefetch=4,
            grid=(len(HOPS),),
            in_specs=[block(1), block(2), block(1), block(2)] + [fixed(m) for m in down_mats],
            out_specs=pl.BlockSpec(
                (1, 2, rows, width), lambda i, chip, *tables: (chip[i], 0, 0, 0)
            ),
        ),
        out_shape=jax.ShapeDtypeStruct((len(HOPS), 2, rows, width), LOW),
        compiler_params=pltpu.CompilerParams(vmem_limit_bytes=VMEM),
        cost_estimate=pl.CostEstimate(
            flops=4 * count * columns * width,
            bytes_accessed=2 * (count * (2 * columns + width) + 2 * columns * width),
            transcendentals=0,
        ),
    )(chips, *places, core, h0, h0, h1, h1, *down_mats)
    return out.reshape(count, width)


def expert_ring(rows, back, gate, mats, waiting):
    size = rows.shape[0]
    cut = size // 2
    swap = lambda block: swap_bit(block, "dp", 0)
    chunk = lambda pieces, at, held, *splits: expert_chunk(
        pieces, back, gate, mats, at, held, splits
    )
    rows, pair = together(rows, swap(rows))
    left, right = ahead(rows), behind(rows)
    parts, crossed = cut_rows(waiting, 4), []
    same, cross = {}, {}
    cross_over = lambda token: crossed.append(swap_tensor(after(parts[len(crossed)], token)))
    cross_over(pair)
    (same[0], cross[0]), held = chunk([rows, pair], 6, None, size, size)
    left, right, same[0] = together(left, right, same[0])
    pieces, got = [left, right], [swap(left), swap(right)]
    left, right = ahead(left), behind(right)
    pieces[0], crossed[0] = together(pieces[0], crossed[0])
    cross_over(pieces[0])
    (same[1],), held = chunk(pieces, 7, held, 2 * size)
    left, right, same[1] = together(left, right, same[1])
    pieces, got = [left, right, *got], [swap(left), swap(right)]
    left, right = ahead(left), behind(right)
    pieces[0], crossed[1] = together(pieces[0], crossed[1])
    cross_over(pieces[0])
    (same[2], cross[1]), held = chunk(pieces, 0, held, 2 * size, 2 * size)
    left, right, same[2] = together(left, right, same[2])
    pieces, got = [left, right, *got], [swap(left), swap(right)]
    left, right = ahead(left[:cut]), behind(right[cut:])
    pieces[0], crossed[2] = together(pieces[0], crossed[2])
    cross_over(pieces[0])
    (same[3], cross[2]), held = chunk(pieces, 1, held, 2 * size, 2 * size)
    left, right, crossed[3], same[3] = together(left, right, crossed[3], same[3])
    pieces = [left, right, swap(left), swap(right), *got]
    (same[4], cross[4], cross[3]), held = chunk(pieces, 2, held, size, size, 2 * size)
    waiting = jnp.concatenate(crossed, axis=0)
    return same, cross, held, waiting


def body(
    inputs,
    attn_gain,
    w_query,
    w_key,
    w_value,
    query_gain,
    key_gain,
    w_out,
    moe_gain,
    w_gate,
    w_up,
    w_down,
    experts,
    gates,
    segments,
    gaps,
    cotangent,
):
    dp_count = lax.axis_size("dp")
    dp_index = lax.axis_index("dp")
    side = lax.axis_index("tensor")
    token_count, model_width = inputs.shape
    half_count = token_count // 2
    top_count = experts.shape[1]
    expert_count = w_gate.shape[0] * dp_count
    capacity = token_count * top_count * dp_count * 9 // (8 * expert_count)
    prompt_length = PR_DEV * GROUP
    column_total = HEADS * HEAD
    block = w_query.shape[0]
    local_width = w_query.shape[1]
    local_heads = local_width // HEAD

    def own_half(array):
        return lax.dynamic_slice_in_dim(array, side * half_count, half_count, axis=0)

    def other_half(array):
        return lax.dynamic_slice_in_dim(array, (1 - side) * half_count, half_count, axis=0)

    def both_halves(own, other):
        first = side == 0
        return jnp.concatenate(
            [jnp.where(first, own, other), jnp.where(first, other, own)], axis=0
        )

    gate_mats = (w_gate[0], swap_tensor(w_gate[0]))
    up_mats = (w_up[0], swap_tensor(w_up[0]))

    ring = dp_count == 2 * len(RING)

    gates_high = gates.astype(LOW)
    gates_low = (gates - gates_high.astype(FULL)).astype(LOW)
    routing = jnp.concatenate([experts.astype(LOW).T, gates_high.T, gates_low.T], axis=1)
    routing = jnp.pad(routing, ((0, 0), (0, local_width - 3 * token_count)))
    gains = jnp.concatenate([attn_gain, moe_gain, query_gain, key_gain])
    gains = jnp.pad(gains[None], ((0, 7), (0, local_width - 4 * block)))
    packed = pack_weights(
        w_query, w_key, w_value, w_out, jnp.concatenate([gains, routing], axis=0)
    )
    gathered = lax.all_gather(packed, "dp", axis=0, tiled=False)
    cotangent_half = own_half(cotangent)
    gathered_back = lax.all_gather(cotangent_half.astype(LOW), "dp", axis=0, tiled=False)
    core = dp_index % 2
    tokens_f = inputs.astype(FULL)
    prompt_pos = dp_index % GROUP * PR_DEV + jnp.arange(PR_DEV, dtype=jnp.int32)
    later_pos = cont_positions(segments[0], gaps[0], prompt_length)
    positions = jnp.concatenate([prompt_pos, later_pos], axis=0)
    cosine, sine = rope_tables(positions, HEAD)
    sine = jnp.where(jnp.arange(HEAD) < HEAD // 2, -sine, sine)
    prompt_query = jnp.arange(token_count, dtype=jnp.int32) < PR_DEV
    prompt_at = jnp.arange(prompt_length, dtype=jnp.int32)
    prompt_keypos = ((dp_index % GROUP) ^ (prompt_at // PR_DEV)) * PR_DEV + prompt_at % PR_DEV
    allowed_prompt = (~prompt_query)[:, None] | (prompt_keypos[None, :] <= positions[:, None])
    query_segment = jnp.concatenate([jnp.full((PR_DEV,), -1, jnp.int32), segments[0]], axis=0)
    allowed_cont = (query_segment[:, None] == segments[0][None, :]) & (
        later_pos[None, :] <= positions[:, None]
    )
    allowed = jnp.concatenate([allowed_prompt, allowed_cont], axis=1)
    bias = jnp.where(allowed, 0.0, -1e30).astype(LOW)
    gathered, cosine, sine, bias, *early = together(
        gathered, cosine, sine, bias, gate_mats[1], up_mats[1]
    )
    gate_mats, up_mats = (gate_mats[0], early[0]), (up_mats[0], early[1])
    rest = gathered[:, 4 * block : 4 * block + 16]
    gain_rows = rest[:, 0].astype(FULL)
    gain_one, gain_two, gain_q, gain_k = (
        gain_rows[:, j * block : (j + 1) * block].reshape(-1) for j in range(4)
    )
    gain_query_local = lax.dynamic_slice_in_dim(gain_q, side * local_width, local_width)
    gain_key_local = lax.dynamic_slice_in_dim(gain_k, side * local_width, local_width)

    names, *parts = (
        rest[:, 8:, j * token_count : (j + 1) * token_count] for j in range(3)
    )
    weights = parts[0].astype(FULL) + parts[1].astype(FULL)
    named = names == dp_index.astype(LOW)
    picked = jnp.sum(named.astype(FULL), axis=1)
    weight = jnp.sum(jnp.where(named, weights, 0.0), axis=1)
    order = jnp.arange(token_count, dtype=jnp.int32)
    earlier = (order[:, None] < order[None, :]).astype(LOW)
    within = dot_nn(picked.astype(LOW), earlier)
    per_row = jnp.sum(picked, axis=1)
    rows_order = jnp.arange(dp_count, dtype=jnp.int32)
    ahead = jnp.sum(
        jnp.where(rows_order[None, :] < rows_order[:, None], per_row[None, :], 0.0), axis=1
    )
    kept = (picked > 0.0) & (within + ahead[:, None] < capacity)
    weight = jnp.where(kept, weight, 0.0)
    weight = lax.dynamic_slice_in_dim(weight, side * half_count, half_count, axis=1)
    if ring:
        blocks, chips = ring_blocks(dp_index), ring_chips(dp_index, HOPS)
        weight = weight[blocks]
    weight = weight.reshape(-1, 1)

    normed_b = rms_norm(tokens_f, gain_one).astype(LOW)
    query_flat, key_flat, values_b, value_prompt = project(
        normed_b, gathered, block, (0, 1, 2), (FULL, FULL, LOW), (2,)
    )
    key_sq = jnp.sum(key_flat * key_flat, axis=1)
    key_sq, value_prompt = together(key_sq, value_prompt)
    value_pieces = collect_prompt(value_prompt, 1, 2)
    query_sq, key_sq = lax.psum(
        (jnp.sum(query_flat * query_flat, axis=1), key_sq), "tensor"
    )
    query_sq, down_mat = lax.optimization_barrier((query_sq, w_down[0]))
    down_mats = (down_mat, swap_tensor(down_mat))
    query_scale = lax.rsqrt(query_sq / column_total + EPSILON)[:, None]
    key_scale = lax.rsqrt(key_sq / column_total + EPSILON)[:, None]
    keys_b, key_prompt = rope_pass(key_flat, gain_key_local[None], key_scale, cosine, sine)
    pieces = (*collect_prompt(key_prompt, 2, 1), *value_pieces)
    turned_by = (gain_query_local[None], query_scale, cosine, sine, bias)
    context_b = attend(query_flat, *turned_by, keys_b, values_b, pieces)
    attn_part = project_back([context_b], gathered, block, (3,))
    attn_part, late, weight = together(attn_part, down_mats[1], weight)
    down_mats = (down_mats[0], late)
    mats = (*gate_mats, *up_mats, *down_mats)
    attn_other = swap_tensor(other_half(attn_part).astype(LOW))
    gathered_back = after(gathered_back, attn_part)
    if ring:
        back_rows = unpack_rows(gathered_back, blocks, 0, model_width)
    else:
        back_rows = gathered_back.reshape(-1, model_width)
    attn_other, back_rows, weight = together(attn_other, back_rows, weight)
    hidden_state = own_half(tokens_f) + own_half(attn_part) + attn_other.astype(FULL)
    normed_two_b = rms_norm(hidden_state, gain_two).astype(LOW)

    low_tn = lambda left, right: dot_tn(left, right).astype(LOW)
    upper = lambda array: array[: array.shape[0] // 2]
    lower = lambda array: array[array.shape[0] // 2 :]
    if ring:
        same, cross, held, hidden_other = expert_ring(
            normed_two_b, back_rows, weight, mats, hidden_state
        )
        expert_in, h0, h1, g0, g1, u0, u1 = held
        late = {}

        def down_stage(gated):
            late["down"] = swap_tensor(low_tn(gated(h1), back_rows))

        def gate_stage(gated):
            late["gate"] = low_tn(gated(expert_in), g1)

        def up_stage(gated):
            late["up"] = low_tn(gated(expert_in), u1)

        def mixed_stage(gated):
            late["mixed"] = mixed_pass(gated(h0), h1, down_mats, chips, core[None])

        fillers = Fillers(late, down_stage, gate_stage, up_stage, mixed_stage)
        normed_two_grad = ring_sum(same, cross, fillers)
        gate_sent, up_sent, mixed_rows = late["gate"], late["up"], late["mixed"]
        down_got = late["down"]
    else:
        hidden_other = swap_tensor(hidden_state)
        expert_in = lax.all_gather(normed_two_b, "dp", axis=0, tiled=True)
        grad_rows, h0, h1, g0, g1, u0, u1 = expert_pass(
            expert_in, back_rows, weight, gate_mats, up_mats, down_mats
        )
        normed_two_grad = lax.psum_scatter(
            grad_rows, "dp", scatter_dimension=0, tiled=True
        ).astype(FULL)
        mixed_rows = (dot_nn(h0, down_mats[0]) + dot_nn(h1, down_mats[1])).astype(LOW)
        down_got = swap_tensor(low_tn(h1, back_rows))
        gate_sent = low_tn(expert_in, g1)
        up_sent = low_tn(expert_in, u1)
    quarter = gate_sent.shape[0] // 4
    gate_first = swap_tensor(gate_sent[:quarter])
    normed_two_grad, down_got, gate_first, mixed_rows, up_sent = together(
        normed_two_grad, down_got, gate_first, mixed_rows, up_sent
    )
    mixed = lax.psum_scatter(mixed_rows, "dp", scatter_dimension=0, tiled=True)

    unused_two, norm_two_back = jax.vjp(rms_norm, hidden_state, gain_two)
    state_part, gain_two_grad = norm_two_back(normed_two_grad)
    state_half = cotangent_half + state_part
    attn_grad_half = state_half.astype(LOW)
    attn_grad_b = both_halves(attn_grad_half, swap_tensor(attn_grad_half))
    attn_grad_b, gate_sent, up_sent = together(attn_grad_b, gate_sent, up_sent)
    (context_grad_b,) = project(attn_grad_b, gathered, block, (3,), (LOW,))
    (gate_middle,) = swap_in_turn([gate_sent[quarter : 3 * quarter]], context_grad_b)
    soon = [
        swap_tensor(after(piece, gate_middle))
        for piece in (gate_sent[3 * quarter :], upper(up_sent))
    ]
    if ring:
        pair = lambda own: (own, swap_bit(own, "dp", 0))
        columns = local_width // 2
        context_sent = lax.dynamic_slice_in_dim(context_b, (1 - core) * columns, columns, axis=1)
        normed_pair, attn_grad_pair = pair(normed_b), pair(attn_grad_b)
        context_got = swap_bit(context_sent, "dp", 0)
    query_normed_grad, query_inner, query_gain_part, key_grad, value_grad, even, *odd = attend_back(
        query_flat, *turned_by, keys_b, values_b, pieces, context_grad_b
    )
    returned = return_prompt(odd, even)
    if ring:
        key_grad, context_got, *pairs = together(
            key_grad, context_got, normed_pair[1], attn_grad_pair[1]
        )
        normed_pair, attn_grad_pair = (normed_b, pairs[0]), (attn_grad_b, pairs[1])
    key_normed_grad, key_inner, key_gain_part, value_pre_grad = key_back(
        key_grad, value_grad, key_flat, gain_key_local[None], key_scale, cosine, sine, returned
    )
    query_inner, *soon = together(query_inner, *soon)
    query_inner, key_inner = lax.psum(
        jnp.stack([query_inner[:, 0], key_inner[:, 0]], axis=0), "tensor"
    )
    query_pre_grad, key_pre_grad, pre_sent = pre_grads_pass(
        core[None],
        (
            query_flat,
            query_normed_grad,
            gain_query_local[None],
            query_scale,
            query_inner[:, None],
        ),
        (key_flat, key_normed_grad, gain_key_local[None], key_scale, key_inner[:, None]),
        value_pre_grad,
    )
    gate_got = jnp.concatenate([gate_first, gate_middle, soon[0]], axis=0)
    pre_grads = (query_pre_grad, key_pre_grad, value_pre_grad)
    grad_sum = lambda left, right, got: dot_tn(left, right) + got.astype(FULL)
    back_all = lambda *grads: project_back(grads, gathered, block, (0, 1, 2))

    wide = lambda part: lax.dynamic_update_slice_in_dim(
        jnp.zeros((column_total,), FULL), part, side * local_width, 0
    )

    def back_shares(*grads):
        part = back_all(*grads)
        return own_half(part), other_half(part).astype(LOW), part

    def input_side(own, other):
        unused_one, norm_one_back = jax.vjp(
            lambda values: rms_norm(values, gain_one), own_half(tokens_f)
        )
        return state_half + norm_one_back(own + other.astype(FULL))[0]

    def gain_part(part):
        return jnp.sum(part * rms_norm(tokens_f, 1.0), axis=0)

    def gain_side(gain_one_grad):
        grads = jnp.stack(
            [gain_one_grad, gain_two_grad, wide(query_gain_part[0]), wide(key_gain_part[0])]
        ).reshape(4, dp_count, block)
        grads = jnp.swapaxes(grads, 0, 1).reshape(dp_count, 1, 4 * block)
        sides = lax.axis_size("tensor")
        grads = jnp.broadcast_to(grads, (dp_count, sides, 4 * block))
        grads = grads.reshape(dp_count * sides, 4 * block)
        sums = lax.all_to_all(grads, ("dp", "tensor"), 0, 0, tiled=True)
        return jnp.sum(sums, axis=0).reshape(4, block)

    if ring:
        pre_got = swap_bit(pre_sent, "dp", 0)
        w_blocks, *far = weight_grads(
            chips,
            core[None],
            normed_pair,
            attn_grad_pair,
            pre_grads,
            pre_got,
            context_b,
            context_got,
        )
        w_blocks, mixed, *far = together(w_blocks, mixed, *far)
        up_pieces = swap_in_turn(cut_rows(lower(up_sent), 2), far[0])
        late, later = {}, {}

        def normed_stage(gated):
            late["part"] = back_all(*map(gated, pre_grads))

        def gate_product_stage(gated):
            later["other"] = swap_tensor(gated(other_half(late["part"]).astype(LOW)))
            late["hidden"] = gated(hidden_other)
            late["gate"] = grad_sum(gated(expert_in), g0, gate_got)
            late["mixed"], late["pieces"] = gated(mixed), up_pieces

        def input_stage(gated):
            later["mixed"] = swap_tensor(late["mixed"])
            late["half"] = input_side(own_half(late["part"]), gated(later["other"]))
            later["half"] = swap_tensor(late["half"])
            late["down"] = grad_sum(gated(h0), back_rows, down_got)

        def up_product_stage(gated):
            up_got = jnp.concatenate([soon[1], *late["pieces"]], axis=0)
            late["up"] = grad_sum(gated(expert_in), u0, up_got)
            late["gains"] = gain_side(gain_part(after(late["part"], late["up"])))
            late["output"] = join_halves(
                side[None], [gated(hidden_state), mixed], [late["hidden"], later["mixed"]]
            )
            late["input"] = join_halves(side[None], [gated(late["half"])], [later["half"]])

        fillers = Fillers(
            late, normed_stage, gate_product_stage, input_stage, up_product_stage
        )
        w_parts = ring_weights(w_blocks, *far, fillers)
        gain_sums, output, input_grad = late["gains"], late["output"], late["input"]
        down_grad, gate_w_grad, up_w_grad = late["down"], late["gate"], late["up"]
        own_w, sent_w = sum_weights(core[None], *w_parts)
        w_sums = place_weights(core[None], own_w, swap_bit(sent_w, "dp", 0))
    else:
        w_grads = jnp.concatenate(
            [low_tn(normed_b, g) for g in pre_grads] + [low_tn(attn_grad_b, context_b)], axis=1
        )
        w_sum = lax.psum_scatter(w_grads, "dp", scatter_dimension=0, tiled=True).astype(FULL)
        w_sums = [w_sum[:, j * local_width : (j + 1) * local_width] for j in range(4)]
        w_sums[3] = w_sums[3].T
        down_grad = grad_sum(h0, back_rows, down_got)
        gate_w_grad = grad_sum(expert_in, g0, gate_got)
        up_got = jnp.concatenate([soon[1], swap_tensor(lower(up_sent))], axis=0)
        up_w_grad = grad_sum(expert_in, u0, up_got)
        mixed_other = swap_tensor(mixed)
        normed_own, normed_sent, part = back_shares(*pre_grads)
        gain_sums = gain_side(gain_part(part))
        input_half = input_side(normed_own, swap_tensor(normed_sent))
        input_other = swap_tensor(input_half)
        input_grad = join_halves(side[None], [input_half], [input_other])
        output = join_halves(side[None], [hidden_state, mixed], [hidden_other, mixed_other])
    return (
        output,
        input_grad,
        gain_sums[0],
        w_sums[0],
        w_sums[1],
        w_sums[2],
        gain_sums[2],
        gain_sums[3],
        w_sums[3],
        gain_sums[1],
        gate_w_grad[None],
        up_w_grad[None],
        down_grad[None],
    )


def solution(mesh):
    return jax.shard_map(
        body,
        mesh=mesh,
        in_specs=(
            P("dp", None),
            P("dp"),
            P("dp", "tensor"),
            P("dp", "tensor"),
            P("dp", "tensor"),
            P("dp"),
            P("dp"),
            P("tensor", "dp"),
            P("dp"),
            P("dp", None, "tensor"),
            P("dp", None, "tensor"),
            P("dp", "tensor", None),
            P("dp", None),
            P("dp", None),
            P("dp", None),
            P("dp", None),
            P("dp", None),
        ),
        out_specs=(
            P("dp", None),
            P("dp", None),
            P("dp"),
            P("dp", "tensor"),
            P("dp", "tensor"),
            P("dp", "tensor"),
            P("dp"),
            P("dp"),
            P("tensor", "dp"),
            P("dp"),
            P("dp", None, "tensor"),
            P("dp", None, "tensor"),
            P("dp", "tensor", None),
        ),
        check_vma=False,
    )
```
